32 devices in a mesh: seq: 8 (over z, y), enc: 4 (over x, core).
Axes of the slice: x: 2, y: 2, z: 4, core: 2. Of those that a mesh axis runs over, the one named last changes fastest.
Arguments:
- tokens: bfloat16 [8192, 1024], P(('seq', 'enc')), may hold values from -6 to 6
- encoder: bfloat16 [8, 4, 2, 128, 1024], P('seq', None, None, 'enc'), may hold values from -6 to 6
- dec_lengths: int32 [64, 2], P(('seq', 'enc')), may hold values from 0 to 128, as said below
- enc_lengths: int32 [64, 2], P(('seq', 'enc')), may hold values from 0 to 128, as said below
- gains: float32 [3, 1024], replicated, may hold values from 0.1 to 1.9
- self_proj: bfloat16 [3, 1024, 1024], P(None, ('seq', 'enc')), may hold values from -0.1875 to 0.1875
- self_out: bfloat16 [1024, 1024], P(('seq', 'enc')), may hold values from -0.75 to 0.75
- cross_proj: bfloat16 [3, 1024, 1024], P(None, ('seq', 'enc')), may hold values from -0.1875 to 0.1875
- cross_out: bfloat16 [1024, 1024], P(('seq', 'enc')), may hold values from -0.75 to 0.75
- ffn_in: bfloat16 [1024, 4096], P(('seq', 'enc')), may hold values from -0.1875 to 0.1875
- ffn_out: bfloat16 [4096, 1024], P(('seq', 'enc')), may hold values from -0.09375 to 0.09375
- adapt_in: bfloat16 [1024, 512], P(('seq', 'enc')), may hold values from -0.1875 to 0.1875
- adapt_out: bfloat16 [512, 1024], P(('seq', 'enc')), may hold values from -0.0625 to 0.0625
- cotangent: bfloat16 [8192, 1024], P(('seq', 'enc')), may hold values from -6 to 6
Outputs:
- layer_out: bfloat16 [8192, 1024], P(('seq', 'enc'))
- grad_tokens: bfloat16 [8192, 1024], P(('seq', 'enc'))
- grad_encoder: bfloat16 [8, 4, 2, 128, 1024], P('seq', None, None, 'enc')
- grad_self_proj: float32 [3, 1024, 1024], P(None, ('seq', 'enc'))
- grad_self_out: float32 [1024, 1024], P(('seq', 'enc'))
- grad_cross_proj: float32 [3, 1024, 1024], P(None, ('seq', 'enc'))
- grad_cross_out: float32 [1024, 1024], P(('seq', 'enc'))
- grad_adapt_in: float32 [1024, 512], P(('seq', 'enc'))
- grad_adapt_out: float32 [512, 1024], P(('seq', 'enc'))
The draws below stay inside these ranges and needn't reach their ends.
Inputs may be any that keep to these rules, and one draw needn't show every extreme that they name: `dec_lengths`: row u describes unit u. If its second value is 0, the unit holds one sequence of bucket 128 from row 0 whose first value of rows are valid, the rest padding; else two sequences of bucket 128 // 2 from rows 0 and 64 with the two valid lengths. A nonzero length is more than half its bucket. `enc_lengths`: valid lengths of the encoder sequences in the same slots of unit u's context; the second value is 0 exactly where that of dec_lengths is, and a nonzero length is more than half its bucket.
All inputs are finite; a program needn't handle non-finite values.
Results may differ from the reference program's by a relative error of at most 0.02.
Values may be sent and summed in bfloat16 or wider, within the bound.
A program may use at most 192 MiB of HBM per device.

```python
import jax
import jax.numpy as jnp
from jax import lax

D = 1024
HEADS = 16
FF = 4096
ADAPT = 512
MB_TOK = 128
MICRO = 2
UNITS = 64
TOKENS = 8192
N_SEQ = 8
N_ENC = 4


def slot_pattern(key):
    paired = jax.random.randint(jax.random.fold_in(key, 5), (UNITS,), 0, 2)
    leading_unit = jnp.arange(UNITS) == 0
    return (jnp.where(leading_unit, 0, paired), leading_unit)


def draw_lengths(key, stream_tag):
    paired, leading_unit = slot_pattern(key)
    bucket = jnp.where(paired == 1, MB_TOK // 2, MB_TOK)
    padding = jax.random.randint(jax.random.fold_in(key, stream_tag), (UNITS, 2), 0, (bucket // 2)[:, None])
    padding = jnp.where(leading_unit[:, None], 0, padding)
    leading = bucket - padding[:, 0]
    trailing = jnp.where(paired == 1, bucket - padding[:, 1], 0)
    return jnp.stack([leading, trailing], axis=1).astype(jnp.int32)


def draw_dec_lengths(key, part):
    return draw_lengths(key, 11)


def draw_enc_lengths(key, part):
    return draw_lengths(key, 13)


def level_of(stream_key, shape, split, least, high):
    level, own = 1.0, jax.random.fold_in(stream_key, 6)
    for dim, blocks in split:
        heights = jnp.exp(jax.random.uniform(jax.random.fold_in(own, dim), (blocks,), jnp.float32, least / len(split), high / len(split)))
        level = level * jnp.repeat(heights, shape[dim] // blocks).reshape([-1 if axis == dim else 1 for axis in range(len(shape))])
    return level


def bell_draw(key, dims, scale, most, cuts=(), held_as=jnp.bfloat16):
    values = scale * jax.random.normal(key, dims, jnp.float32)
    if cuts:
        values = values * level_of(key, dims, cuts, -0.22, 0.18)
    return jnp.clip(values, -most, most).astype(held_as)


def setup_inputs(seed: int = 0) -> dict:
    key_list = jax.random.split(jax.random.key(seed), 15)
    tokens = bell_draw(key_list[0], (TOKENS, D), 1.0, 6.0, ((0, 32),))
    encoder = bell_draw(key_list[1], (N_SEQ, N_ENC, MICRO, MB_TOK, D), 1.0, 6.0, ((0, 8), (3, 4)))
    dec_lengths = draw_dec_lengths(jax.random.fold_in(key_list[14], 71), 0)
    enc_lengths = draw_enc_lengths(jax.random.fold_in(key_list[14], 71), 0)
    gains = jnp.clip(1.0 + 0.18 * jax.random.normal(key_list[4], (3, D), jnp.float32), 0.1, 1.9)
    self_proj = bell_draw(key_list[5], (3, D, D), D ** -0.5, 0.1875, ((1, 32),))
    self_out = bell_draw(key_list[6], (D, D), (D // 16) ** -0.5, 0.75, ((0, 32),))
    cross_proj = bell_draw(key_list[7], (3, D, D), D ** -0.5, 0.1875, ((1, 32),))
    cross_out = bell_draw(key_list[8], (D, D), (D // 16) ** -0.5, 0.75, ((0, 32),))
    ffn_in = bell_draw(key_list[9], (D, FF), D ** -0.5, 0.1875, ((0, 32),))
    ffn_out = bell_draw(key_list[10], (FF, D), FF ** -0.5, 0.09375, ((0, 32),))
    adapt_in = bell_draw(key_list[11], (D, ADAPT), D ** -0.5, 0.1875, ((0, 32),))
    adapt_out = bell_draw(key_list[12], (ADAPT, D), (16 * ADAPT) ** -0.5, 0.0625, ((0, 32),))
    cotangent = bell_draw(key_list[13], (TOKENS, D), 1.0, 6.0, ((0, 32),))
    return {"tokens": tokens, "encoder": encoder, "dec_lengths": dec_lengths, "enc_lengths": enc_lengths, "gains": gains, "self_proj": self_proj, "self_out": self_out, "cross_proj": cross_proj, "cross_out": cross_out, "ffn_in": ffn_in, "ffn_out": ffn_out, "adapt_in": adapt_in, "adapt_out": adapt_out, "cotangent": cotangent}


EPSILON = 1e-05
NEGATIVE = -1e+30
HIGHEST = lax.Precision.HIGHEST

@jax.custom_vjp
def low(v):
    return lax.optimization_barrier(v.astype(jnp.bfloat16)).astype(jnp.float32)

@jax.custom_vjp
def low_back(v):
    return v

def low_keep(v):
    return (low(v), None)

def low_pass(kept, grad):
    return (grad,)

def back_keep(v):
    return (v, None)

def back_low(kept, grad):
    return (low(grad),)
low.defvjp(low_keep, low_pass)
low_back.defvjp(back_keep, back_low)

def matmul(left, right):
    return jnp.dot(left, right, precision=HIGHEST)

def layer_norm(hidden, gain):
    center = hidden - lax.optimization_barrier(jnp.mean(hidden, axis=-1, keepdims=True))
    spread = lax.optimization_barrier(jnp.mean(center * center, axis=-1, keepdims=True))
    return center * lax.rsqrt(spread + EPSILON) * gain

def slot_masks(dec_row, enc_row, rows):
    half_rows = rows // 2
    places = lax.broadcasted_iota(jnp.int32, (rows,), 0)
    paired = dec_row[1] > 0
    second = jnp.logical_and(paired, places >= half_rows)
    anchor = jnp.where(second, half_rows, 0).astype(jnp.int32)
    dec_valid = jnp.where(second, dec_row[1], dec_row[0])
    enc_valid = jnp.where(second, enc_row[1], enc_row[0])
    key_live = places - anchor < dec_valid
    context_live = places - anchor < enc_valid
    same_slot = second[:, None] == second[None, :]
    causal = places[None, :] <= places[:, None]
    self_mask = same_slot & causal & key_live[None, :]
    cross_mask = same_slot & context_live[None, :]
    return (self_mask, cross_mask)

def split_heads(matrix):
    return matrix.reshape(matrix.shape[0], HEADS, matrix.shape[1] // HEADS)

def attention(queries, keys, values, allowed):
    depth = queries.shape[1] // HEADS
    scores = low_back(jnp.einsum('qhd,khd->hqk', split_heads(queries), split_heads(keys), precision=HIGHEST) * float(depth) ** (-0.5))
    masked = jnp.where(allowed[None], scores, NEGATIVE)
    weights = jnp.exp(masked - lax.optimization_barrier(jnp.max(masked, axis=-1, keepdims=True)))
    probs = weights / lax.optimization_barrier(jnp.sum(weights, axis=-1, keepdims=True))
    mixed = jnp.einsum('hqk,khd->qhd', low(probs), split_heads(values), precision=HIGHEST)
    return low(low_back(mixed.reshape(queries.shape)))

def project(rows_in, weight):
    return low(low_back(matmul(rows_in, weight)))

def unit_layer(trained, frozen, pieces):
    self_proj, self_out, cross_proj, cross_out, adapt_in, adapt_out = trained
    ffn_in, ffn_out, gains = frozen
    token_rows, context, dec_row, enc_row = pieces
    self_mask, cross_mask = slot_masks(dec_row, enc_row, token_rows.shape[0])
    self_mix = attention(project(token_rows, self_proj[0]), project(token_rows, self_proj[1]), project(token_rows, self_proj[2]), self_mask)
    first_sum = token_rows + low_back(matmul(self_mix, self_out))
    first_norm = layer_norm(first_sum, gains[0])
    first_low = low(first_norm)
    cross_mix = attention(project(first_low, cross_proj[0]), project(context, cross_proj[1]), project(context, cross_proj[2]), cross_mask)
    second_sum = first_norm + low_back(matmul(cross_mix, cross_out))
    second_norm = layer_norm(second_sum, gains[1])
    second_low = low(second_norm)
    ffn_act = low(jax.nn.gelu(low_back(matmul(second_low, ffn_in)), approximate=False))
    adapt_act = low(jax.nn.silu(low_back(matmul(second_low, adapt_in))))
    branch = low_back(matmul(ffn_act, ffn_out) + 4.0 * matmul(adapt_act, adapt_out))
    return layer_norm(second_norm + branch, gains[2])

def reference(tokens, encoder, dec_lengths, enc_lengths, gains, self_proj, self_out, cross_proj, cross_out, ffn_in, ffn_out, adapt_in, adapt_out, cotangent):
    frozen = (ffn_in.astype(jnp.float32), ffn_out.astype(jnp.float32), gains.astype(jnp.float32))
    trained = tuple((weight.astype(jnp.float32) for weight in (self_proj, self_out, cross_proj, cross_out, adapt_in, adapt_out)))

    def forward(token_all, encoder_all, trained_all):
        units = (token_all.reshape(UNITS, MB_TOK, D), encoder_all.reshape(UNITS, MB_TOK, D), dec_lengths, enc_lengths)
        layer = jax.checkpoint(lambda pieces: unit_layer(trained_all, frozen, pieces))
        return lax.map(layer, units).reshape(TOKENS, D)
    layer_out, pullback = jax.vjp(forward, tokens.astype(jnp.float32), encoder.astype(jnp.float32), trained)
    grad_tokens, grad_encoder, grad_trained = pullback(cotangent.astype(jnp.float32))
    return (layer_out.astype(jnp.bfloat16), grad_tokens.astype(jnp.bfloat16), grad_encoder.astype(jnp.bfloat16), grad_trained[0], grad_trained[1], grad_trained[2], grad_trained[3], grad_trained[4], grad_trained[5])
```

```python
import jax
import jax.numpy as jnp
from jax import lax
from jax.experimental import pallas as pl
from jax.experimental.pallas import tpu as pltpu
from jax.sharding import PartitionSpec as P

HEADS = 16
ADAPT = 512
MICRO = 2


EPSILON = 1e-05
NEGATIVE = -1e30


def matmul(left, right):
    return jnp.dot(left, right, preferred_element_type=jnp.float32)


def matmul_tn(left, right):
    return lax.dot_general(
        left, right, (((0,), (0,)), ((), ())), preferred_element_type=jnp.float32
    )


def matmul_nt(left, right):
    return lax.dot_general(
        left, right, (((1,), (1,)), ((), ())), preferred_element_type=jnp.float32
    )


def layer_norm(hidden, gain):
    center = hidden - jnp.mean(hidden, axis=-1, keepdims=True)
    spread = jnp.mean(center * center, axis=-1, keepdims=True)
    return center * lax.rsqrt(spread + EPSILON) * gain


def norm_back(hidden, gain, grad_out):
    _, pullback = jax.vjp(lambda value: layer_norm(value, gain), hidden)
    return pullback(grad_out)[0]


def gelu_exact(value):
    return jax.nn.gelu(value, approximate=False)


def slot_masks(dec_row, enc_row, rows):
    half_rows = rows // 2
    places = lax.broadcasted_iota(jnp.int32, (rows,), 0)
    paired = dec_row[1] > 0
    second = jnp.logical_and(paired, places >= half_rows)
    anchor = jnp.where(second, half_rows, 0).astype(jnp.int32)
    dec_valid = jnp.where(second, dec_row[1], dec_row[0])
    enc_valid = jnp.where(second, enc_row[1], enc_row[0])
    key_live = places - anchor < dec_valid
    context_live = places - anchor < enc_valid
    same_slot = second[:, None] == second[None, :]
    causal = places[None, :] <= places[:, None]
    self_mask = same_slot & causal & key_live[None, :]
    cross_mask = same_slot & context_live[None, :]
    return (self_mask, cross_mask)


def split_heads(matrix):
    return matrix.reshape(matrix.shape[0], HEADS, matrix.shape[1] // HEADS)


def attend(queries, keys, values, allowed):
    depth = queries.shape[1] // HEADS
    scores = jnp.einsum(
        "qhd,khd->hqk", split_heads(queries), split_heads(keys), preferred_element_type=jnp.float32
    ) * float(depth) ** (-0.5)
    masked = jnp.where(allowed[None], scores, NEGATIVE)
    weights = jnp.exp(masked - jnp.max(masked, axis=-1, keepdims=True))
    probs = weights / jnp.sum(weights, axis=-1, keepdims=True)
    mixed = jnp.einsum(
        "hqk,khd->qhd",
        probs.astype(jnp.bfloat16),
        split_heads(values),
        preferred_element_type=jnp.float32,
    )
    return (mixed.reshape(queries.shape).astype(jnp.bfloat16), probs)


def attend_back(grad_mixed, queries, keys, values, probs):
    depth = queries.shape[1] // HEADS
    factor = float(depth) ** (-0.5)
    grad_heads = split_heads(grad_mixed)
    grad_probs = jnp.einsum(
        "qhd,khd->hqk", grad_heads, split_heads(values), preferred_element_type=jnp.float32
    )
    inner = jnp.sum(probs * grad_probs, axis=-1, keepdims=True)
    grad_scores = (probs * (grad_probs - inner)).astype(jnp.bfloat16)
    grad_query = (
        jnp.einsum(
            "hqk,khd->qhd", grad_scores, split_heads(keys), preferred_element_type=jnp.float32
        )
        * factor
    )
    grad_key = (
        jnp.einsum(
            "hqk,qhd->khd", grad_scores, split_heads(queries), preferred_element_type=jnp.float32
        )
        * factor
    )
    grad_value = jnp.einsum(
        "hqk,qhd->khd", probs.astype(jnp.bfloat16), grad_heads, preferred_element_type=jnp.float32
    )
    return (
        grad_query.reshape(queries.shape).astype(jnp.bfloat16),
        grad_key.reshape(keys.shape).astype(jnp.bfloat16),
        grad_value.reshape(values.shape).astype(jnp.bfloat16),
    )


def per_device(
    tokens,
    encoder,
    dec_lengths,
    enc_lengths,
    gains,
    self_proj,
    self_out,
    cross_proj,
    cross_out,
    ffn_in,
    ffn_out,
    adapt_in,
    adapt_out,
    cotangent,
):
    shards = (self_proj, self_out, cross_proj, cross_out, ffn_in, ffn_out, adapt_in, adapt_out)

    def obtain():
        return (
            lax.all_gather(shards[0], ("seq", "enc"), axis=1, tiled=True),
            lax.all_gather(shards[1], ("seq", "enc"), axis=0, tiled=True),
            lax.all_gather(shards[2], ("seq", "enc"), axis=1, tiled=True),
            lax.all_gather(shards[3], ("seq", "enc"), axis=0, tiled=True),
            lax.all_gather(shards[4], ("seq", "enc"), axis=0, tiled=True),
            lax.all_gather(shards[5], ("seq", "enc"), axis=0, tiled=True),
            lax.all_gather(shards[6], ("seq", "enc"), axis=0, tiled=True),
            lax.all_gather(shards[7], ("seq", "enc"), axis=0, tiled=True),
        )

    rows = tokens.shape[0] // MICRO
    width = tokens.shape[1]
    owner = lax.axis_index("enc")
    acc_self = jnp.zeros((width, 3, width), jnp.float32)
    acc_self_out = jnp.zeros((width, width), jnp.float32)
    acc_cross = jnp.zeros((width, 3, width), jnp.float32)
    acc_cross_out = jnp.zeros((width, width), jnp.float32)
    acc_adapt_in = jnp.zeros((width, ADAPT), jnp.float32)
    acc_adapt_out = jnp.zeros((ADAPT, width), jnp.float32)
    outputs = []
    grad_rows = []
    grad_contexts = []
    for micro_index in range(MICRO):
        w_self, w_self_out, w_cross, w_cross_out, w_ffn_in, w_ffn_out, w_adapt_in, w_adapt_out = (
            obtain()
        )
        lower = micro_index * rows
        token_rows = tokens[lower : lower + rows]
        self_mask, cross_mask = slot_masks(dec_lengths[micro_index], enc_lengths[micro_index], rows)
        pieces = encoder[0, :, micro_index]
        context = lax.dynamic_index_in_dim(
            lax.all_gather(pieces, "enc", axis=1, tiled=True), owner, 0, keepdims=False
        )
        self_query = matmul(token_rows, w_self[0]).astype(jnp.bfloat16)
        self_key = matmul(token_rows, w_self[1]).astype(jnp.bfloat16)
        self_value = matmul(token_rows, w_self[2]).astype(jnp.bfloat16)
        self_mix, self_probs = attend(self_query, self_key, self_value, self_mask)
        first_sum = token_rows.astype(jnp.float32) + matmul(self_mix, w_self_out)
        first_norm = layer_norm(first_sum, gains[0])
        first_low = first_norm.astype(jnp.bfloat16)
        cross_query = matmul(first_low, w_cross[0]).astype(jnp.bfloat16)
        cross_key = matmul(context, w_cross[1]).astype(jnp.bfloat16)
        cross_value = matmul(context, w_cross[2]).astype(jnp.bfloat16)
        cross_mix, cross_probs = attend(cross_query, cross_key, cross_value, cross_mask)
        second_sum = first_norm + matmul(cross_mix, w_cross_out)
        second_norm = layer_norm(second_sum, gains[1])
        second_low = second_norm.astype(jnp.bfloat16)
        ffn_pre = matmul(second_low, w_ffn_in)
        ffn_act = gelu_exact(ffn_pre).astype(jnp.bfloat16)
        adapt_pre = matmul(second_low, w_adapt_in)
        adapt_act = jax.nn.silu(adapt_pre).astype(jnp.bfloat16)
        third_sum = second_norm + matmul(ffn_act, w_ffn_out) + 4.0 * matmul(adapt_act, w_adapt_out)
        outputs.append(layer_norm(third_sum, gains[2]).astype(jnp.bfloat16))
        w_self, w_self_out, w_cross, w_cross_out, w_ffn_in, w_ffn_out, w_adapt_in, w_adapt_out = (
            obtain()
        )
        grad_third = norm_back(
            third_sum, gains[2], cotangent[lower : lower + rows].astype(jnp.float32)
        )
        grad_branch = grad_third.astype(jnp.bfloat16)
        _, gelu_pull = jax.vjp(gelu_exact, ffn_pre)
        grad_ffn_pre = gelu_pull(matmul_nt(grad_branch, w_ffn_out))[0].astype(jnp.bfloat16)
        grad_adapt_act = matmul_nt(grad_branch, w_adapt_out) * 4.0
        _, silu_pull = jax.vjp(jax.nn.silu, adapt_pre)
        grad_adapt_pre = silu_pull(grad_adapt_act)[0].astype(jnp.bfloat16)
        acc_adapt_out = acc_adapt_out + matmul_tn(adapt_act, grad_branch) * 4.0
        acc_adapt_in = acc_adapt_in + matmul_tn(second_low, grad_adapt_pre)
        grad_second = (
            grad_third + matmul_nt(grad_ffn_pre, w_ffn_in) + matmul_nt(grad_adapt_pre, w_adapt_in)
        )
        grad_second_sum = norm_back(second_sum, gains[1], grad_second)
        grad_cross_branch = grad_second_sum.astype(jnp.bfloat16)
        acc_cross_out = acc_cross_out + matmul_tn(cross_mix, grad_cross_branch)
        grad_cross_mix = matmul_nt(grad_cross_branch, w_cross_out).astype(jnp.bfloat16)
        grad_cq, grad_ck, grad_cv = attend_back(
            grad_cross_mix, cross_query, cross_key, cross_value, cross_probs
        )
        acc_cross = acc_cross + jnp.stack(
            [
                matmul_tn(first_low, grad_cq),
                matmul_tn(context, grad_ck),
                matmul_tn(context, grad_cv),
            ],
            axis=1,
        )
        grad_context = matmul_nt(grad_ck, w_cross[1]) + matmul_nt(grad_cv, w_cross[2])
        holder = jnp.zeros((lax.axis_size("enc"),) + grad_context.shape, jnp.float32)
        holder = lax.dynamic_update_index_in_dim(holder, grad_context, owner, 0)
        returned = lax.psum_scatter(
            holder.astype(jnp.bfloat16), "enc", scatter_dimension=1, tiled=True
        )
        grad_contexts.append(returned)
        grad_first = grad_second_sum + matmul_nt(grad_cq, w_cross[0])
        grad_first_sum = norm_back(first_sum, gains[0], grad_first)
        grad_self_branch = grad_first_sum.astype(jnp.bfloat16)
        acc_self_out = acc_self_out + matmul_tn(self_mix, grad_self_branch)
        grad_self_mix = matmul_nt(grad_self_branch, w_self_out).astype(jnp.bfloat16)
        grad_sq, grad_sk, grad_sv = attend_back(
            grad_self_mix, self_query, self_key, self_value, self_probs
        )
        acc_self = acc_self + jnp.stack(
            [
                matmul_tn(token_rows, grad_sq),
                matmul_tn(token_rows, grad_sk),
                matmul_tn(token_rows, grad_sv),
            ],
            axis=1,
        )
        grad_input = (
            grad_first_sum
            + matmul_nt(grad_sq, w_self[0])
            + matmul_nt(grad_sk, w_self[1])
            + matmul_nt(grad_sv, w_self[2])
        )
        grad_rows.append(grad_input.astype(jnp.bfloat16))
    summed = (
        lax.psum_scatter(acc_self, ("seq", "enc"), scatter_dimension=0, tiled=True),
        lax.psum_scatter(acc_self_out, ("seq", "enc"), scatter_dimension=0, tiled=True),
        lax.psum_scatter(acc_cross, ("seq", "enc"), scatter_dimension=0, tiled=True),
        lax.psum_scatter(acc_cross_out, ("seq", "enc"), scatter_dimension=0, tiled=True),
        lax.psum_scatter(acc_adapt_in, ("seq", "enc"), scatter_dimension=0, tiled=True),
        lax.psum_scatter(acc_adapt_out, ("seq", "enc"), scatter_dimension=0, tiled=True),
    )
    layer_out = jnp.concatenate(outputs, axis=0)
    grad_tokens = jnp.concatenate(grad_rows, axis=0)
    grad_encoder = jnp.stack(grad_contexts, axis=1)[None]
    grad_self_proj = jnp.transpose(summed[0], (1, 0, 2))
    grad_cross_proj = jnp.transpose(summed[2], (1, 0, 2))
    return (
        layer_out,
        grad_tokens,
        grad_encoder,
        grad_self_proj,
        summed[1],
        grad_cross_proj,
        summed[3],
        summed[4],
        summed[5],
    )


MESH = pl.DeviceIdType.MESH
AG_GAP = 2
SUBSET = list(range(17))
NOSIB = False

TILES = ["q1", "k1", "v1", "so", "k2", "v2", "q2", "co", "ad", "f0", "f1", "f2", "f3", "o0", "o1", "o2", "o3"]

class Place:
    def __init__(self):
        seq, enc = lax.axis_index("seq"), lax.axis_index("enc")
        self.z, self.y, self.x, self.c = seq // 2, seq % 2, enc // 2, enc % 2
        self.up, self.down = jnp.minimum(self.z + 1, 3), jnp.maximum(self.z - 1, 0)
    def dev(self, z=None, y=None, x=None, c=None):
        z = self.z if z is None else z
        y = self.y if y is None else y
        x = self.x if x is None else x
        c = self.c if c is None else c
        return (z * 2 + y, x * 2 + c)

def entry_barrier(p):
    bar = pltpu.get_barrier_semaphore()
    def sig(d):
        pl.semaphore_signal(bar, inc=1, device_id=d, device_id_type=MESH)
    sig(p.dev(c=1 - p.c)); sig(p.dev(x=1 - p.x)); sig(p.dev(y=1 - p.y)); sig(p.dev(x=1 - p.x, c=1 - p.c))
    @pl.when(p.z < 3)
    def _(): sig(p.dev(z=p.up))
    @pl.when(p.z > 0)
    def _(): sig(p.dev(z=p.down))
    peers = 4 + (p.z < 3).astype(jnp.int32) + (p.z > 0).astype(jnp.int32)
    pl.semaphore_wait(bar, peers)

ALL4 = pl.ds(0, 4)
ALL2 = pl.ds(0, 2)

class Stream:
    def __init__(self, p, view, order, ssem, rsem):
        self.p, self.view, self.order, self.ssem, self.rsem = p, view, order, ssem, rsem
        self.ns = 0
        self.sends = []

    def cut(self, z, y, x, c):
        return self.view(z, y, x, c)

    def copy(self, where, slot, target, guard=None):
        k = self.ns; self.ns += 1
        cp = pltpu.make_async_remote_copy(where, where, self.ssem.at[k], self.rsem.at[slot], device_id=target, device_id_type=MESH)
        if guard is None:
            cp.start()
        else:
            pl.when(guard)(cp.start)
        self.sends.append((cp, guard))

    def arrive(self, where, slot, guard=None):
        cp = pltpu.make_async_remote_copy(where, where, self.ssem.at[0], self.rsem.at[slot], device_id=self.p.dev(), device_id_type=MESH)
        if guard is None:
            cp.wait_recv()
        else:
            pl.when(guard)(cp.wait_recv)

    def finish(self):
        for cp, guard in self.sends:
            if guard is None:
                cp.wait_send()
            else:
                pl.when(guard)(cp.wait_send)

    def at(self, z, own):
        return self.cut(z, own["y"], own["x"], self.p.c)

    def phases(self):
        p = self.p
        if self.order[0] == "z":
            b1, b2 = self.order[1], self.order[2]
            me = {"x": p.x, "y": p.y}
            oth = {"x": 1 - p.x, "y": 1 - p.y}
            part1 = p.dev(**{b1: oth[b1]}); part2 = p.dev(**{b2: oth[b2]})
            sib = p.dev(c=1 - p.c)
            own = dict(me)
            b1o = dict(me); b1o[b1] = oth[b1]
            both = dict(me); both[b1] = ALL2
            allof = {"x": ALL2, "y": ALL2}
            def P0():
                self.copy(self.at(p.z, own), p.z, p.dev(z=p.up), p.z < 3)
                self.copy(self.at(p.z, own), p.z, p.dev(z=p.down), p.z > 0)
                self.copy(self.at(p.z, own), 4 + p.z, part1)
            def hop(t):
                lo, hi = jnp.maximum(p.z - t, 0), jnp.minimum(p.z + t, 3)
                below, above = p.z >= t, p.z + t <= 3
                self.arrive(self.at(lo, own), lo, below)
                if t < 3:
                    self.copy(self.at(lo, own), lo, p.dev(z=p.up), (below) & (p.z < 3))
                self.copy(self.at(lo, own), 4 + lo, part1, below)
                self.arrive(self.at(hi, own), hi, above)
                if t < 3:
                    self.copy(self.at(hi, own), hi, p.dev(z=p.down), (above) & (p.z > 0))
                self.copy(self.at(hi, own), 4 + hi, part1, above)
            def P4():
                for zz in range(4):
                    self.arrive(self.at(zz, b1o), 4 + zz)
                    self.copy(self.at(zz, both), 8 + zz, part2)
            def P5():
                self.copy(self.at(ALL4, both), 12, sib)
                for zz in range(4):
                    self.arrive(self.at(zz, both), 8 + zz)
                b2o = dict(both); b2o[b2] = oth[b2]
                self.copy(self.at(ALL4, b2o), 13, sib)
            def P6():
                b2o = dict(both); b2o[b2] = oth[b2]
                w = lambda s: self.cut(ALL4, s["y"], s["x"], 1 - p.c)
                self.arrive(w(both), 12)
                self.arrive(w(b2o), 13)
            if NOSIB:
                def P5():
                    for zz in range(4):
                        self.arrive(self.at(zz, both), 8 + zz)
                P6 = lambda: None
            return [P0, lambda: hop(1), lambda: hop(2), lambda: hop(3), P4, P5, P6]
        b1, b2 = self.order[0], self.order[2]
        me = {"x": p.x, "y": p.y}
        oth = {"x": 1 - p.x, "y": 1 - p.y}
        part1 = p.dev(**{b1: oth[b1]}); part2 = p.dev(**{b2: oth[b2]})
        sib = p.dev(c=1 - p.c)
        own = dict(me)
        b1o = dict(me); b1o[b1] = oth[b1]
        both = dict(me); both[b1] = ALL2
        b2o = dict(both); b2o[b2] = oth[b2]
        def P0():
            self.copy(self.at(p.z, own), 8, part1)
        def P1():
            self.arrive(self.at(p.z, b1o), 8)
            self.copy(self.at(p.z, both), p.z, p.dev(z=p.up), p.z < 3)
            self.copy(self.at(p.z, both), p.z, p.dev(z=p.down), p.z > 0)
            self.copy(self.at(p.z, both), 4 + p.z, part2)
        def hop(t):
            lo, hi = jnp.maximum(p.z - t, 0), jnp.minimum(p.z + t, 3)
            below, above = p.z >= t, p.z + t <= 3
            self.arrive(self.at(lo, both), lo, below)
            if t < 3:
                self.copy(self.at(lo, both), lo, p.dev(z=p.up), (below) & (p.z < 3))
            self.copy(self.at(lo, both), 4 + lo, part2, below)
            self.arrive(self.at(hi, both), hi, above)
            if t < 3:
                self.copy(self.at(hi, both), hi, p.dev(z=p.down), (above) & (p.z > 0))
            self.copy(self.at(hi, both), 4 + hi, part2, above)
        def P5():
            self.copy(self.at(ALL4, both), 12, sib)
            for zz in range(4):
                self.arrive(self.at(zz, b2o), 4 + zz)
            self.copy(self.at(ALL4, b2o), 13, sib)
        def P6():
            w = lambda s: self.cut(ALL4, s["y"], s["x"], 1 - p.c)
            self.arrive(w(both), 12)
            self.arrive(w(b2o), 13)
        if NOSIB:
            def P5():
                for zz in range(4):
                    self.arrive(self.at(zz, b2o), 4 + zz)
            P6 = lambda: None
        return [P0, P1, lambda: hop(1), lambda: hop(2), lambda: hop(3), P5, P6]
NSLOT = 14
NSEND = 19

def gather_kernel(sp, so, cp, co, fi, fo, ai, ao, en, buf, gfo, ctx, ssem, rsem, lsem, csem, crsem):
    p = Place()
    loc = []
    def put(src, dst):
        k = len(loc)
        c_ = pltpu.make_async_copy(src, dst, lsem.at[k]); c_.start(); loc.append(c_)
    own = lambda t: buf.at[t, p.z, p.y, p.x, p.c]
    for j, t in enumerate((0, 1, 2)): put(sp.at[j], own(t))
    put(so, own(3))
    for j, t in ((1, 4), (2, 5), (0, 6)): put(cp.at[j], own(t))
    put(co, own(7))
    put(ai, buf.at[8, p.z, p.y, p.x, p.c, :, pl.ds(0, 512)])
    put(ao.at[:, pl.ds(0, 512)], buf.at[8, p.z, p.y, p.x, p.c, pl.ds(0, 16), pl.ds(512, 512)])
    put(ao.at[:, pl.ds(512, 512)], buf.at[8, p.z, p.y, p.x, p.c, pl.ds(16, 16), pl.ds(512, 512)])
    for j in range(4): put(fi.at[:, pl.ds(1024 * j, 1024)], own(9 + j))
    put(fo, gfo.at[p.z, p.y, p.x, p.c])
    me = p.x * 2 + p.c
    put(en.at[0, me], ctx.at[:, me])
    entry_barrier(p)
    cs = []
    for k, (dx, dc) in enumerate(((0, 1), (1, 0), (1, 1))):
        tx = (p.x + dx) % 2; tc = (p.c + dc) % 2
        c_ = pltpu.make_async_remote_copy(en.at[0, tx * 2 + tc], ctx.at[:, me], csem.at[k], crsem.at[me], device_id=p.dev(x=tx, c=tc), device_id_type=MESH)
        c_.start(); cs.append(c_)
    for c_ in loc: c_.wait()
    streams = []
    n = 0
    for g in range(6):
        for i in range(3):
            t = 3 * g + i
            if t >= 17 or t not in SUBSET: continue
            rows = [(0, 16, "zxy"), (16, 16, "zyx")] if i == 0 else [(0, 32, "xzy" if i == 1 else "yzx")]
            for r0, nr, order in rows:
                if t < 13:
                    view = lambda z, y, x, c, t=t, r0=r0, nr=nr: buf.at[t, z, y, x, c, pl.ds(r0, nr)]
                else:
                    view = lambda z, y, x, c, j=t - 13, r0=r0, nr=nr: gfo.at[z, y, x, c, pl.ds(32 * j + r0, nr)]
                streams.append((g, Stream(p, view, order, ssem.at[n], rsem.at[n])))
                n += 1
    ph = [(g, s.phases()) for g, s in streams]
    for step in range(6 * AG_GAP + 7):
        for g, f in ph:
            k = step - g * AG_GAP
            if 0 <= k < 7: f[k]()
    for _, s in streams: s.finish()
    for c_ in cs: c_.wait_send()
    for k, (dx, dc) in enumerate(((0, 1), (1, 0), (1, 1))):
        tx = (p.x + dx) % 2; tc = (p.c + dc) % 2
        w = tx * 2 + tc
        pltpu.make_async_remote_copy(en.at[0, w], ctx.at[:, w], csem.at[k], crsem.at[w], device_id=p.dev(), device_id_type=MESH).wait_recv()

N_STREAM = 23
def gather(sp, so, cp, co, fi, fo, ai, ao, en):
    any_ = pl.BlockSpec(memory_space=pl.ANY)
    return pl.pallas_call(gather_kernel,
        out_shape=(jax.ShapeDtypeStruct((13, 4, 2, 2, 2, 32, 1024), jnp.bfloat16),
                   jax.ShapeDtypeStruct((4, 2, 2, 2, 128, 1024), jnp.bfloat16),
                   jax.ShapeDtypeStruct((2, 4, 32, 1024), jnp.bfloat16)),
        in_specs=[any_] * 9, out_specs=(any_,) * 3,
        scratch_shapes=[pltpu.SemaphoreType.DMA((N_STREAM, NSEND)), pltpu.SemaphoreType.DMA((N_STREAM, NSLOT)), pltpu.SemaphoreType.DMA((20,)), pltpu.SemaphoreType.DMA((3,)), pltpu.SemaphoreType.DMA((4,))],
        compiler_params=pltpu.CompilerParams(collective_id=0, has_side_effects=True),
        name="gather")(sp, so, cp, co, fi, fo, ai, ao, en)


NT = 9
ORDERS = ["A", "xzy", "yzx"] * 3
RS_GAP = 0.5
ROW = 1024

class Reduce:
    def __init__(self, p, t, order, PB, L0, L1, L2, UP, DN, LX, ssem, rsem, out):
        self.p, self.t, self.order = p, t, order
        self.PB, self.L0, self.L1, self.L2, self.UP, self.DN, self.LX = PB, L0, L1, L2, UP, DN, LX
        self.ssem, self.rsem, self.out = ssem, rsem, out
        self.ns = 0; self.sends = []
    def copy(self, src, dst, slot, target, guard=None):
        k = self.ns; self.ns += 1
        cp = pltpu.make_async_remote_copy(src, dst, self.ssem.at[k], self.rsem.at[slot], device_id=target, device_id_type=MESH)
        if guard is None: cp.start()
        else: pl.when(guard)(cp.start)
        self.sends.append((cp, guard))
    def arrive(self, dst, slot):
        pltpu.make_async_remote_copy(dst, dst, self.ssem.at[0], self.rsem.at[slot], device_id=self.p.dev(), device_id_type=MESH).wait_recv()
    def finish(self):
        for cp, guard in self.sends:
            if guard is None: cp.wait_send()
            else: pl.when(guard)(cp.wait_send)
    def sib(self, zz):
        p = self.p
        self.copy(self.PB.at[zz, :, :, 1 - p.c], self.L0.at[zz], zz, p.dev(c=1 - p.c))
    def merge(self, zz):
        p = self.p
        self.arrive(self.L0.at[zz], zz)
        for yy in range(2):
            for xx in range(2):
                self.PB[zz, yy, xx, p.c] = self.PB[zz, yy, xx, p.c] + self.L0[zz, yy, xx]
    def pair(self, ref, zz, b2name, b2v, r=None):
        if b2name == "y": return ref.at[zz, b2v, :, self.p.c] if r is None else ref.at[zz, b2v, :, self.p.c, r]
        return ref.at[zz, :, b2v, self.p.c] if r is None else ref.at[zz, :, b2v, self.p.c, r]

    def phases(self):
        return self.phases_c() if self.order != "A" else self.phases_a()

    def phases_c(self):
        p = self.p
        b1, b2 = self.order[0], self.order[2]
        me = {"x": p.x, "y": p.y}
        part1 = p.dev(**{b1: 1 - me[b1]}); part2 = p.dev(**{b2: 1 - me[b2]})
        own = lambda zz: self.pair(self.PB, zz, b2, me[b2])
        def R1():
            for zz in range(4):
                self.merge(zz)
                self.copy(self.pair(self.PB, zz, b2, 1 - me[b2]), self.L1.at[zz], 4 + zz, part2)
        def R2():
            for zz in range(4):
                self.arrive(self.L1.at[zz], 4 + zz)
                o = own(zz)
                o[...] = o[...] + self.L1[zz]
        def hop(zu, zd):
            def up_add():
                self.arrive(self.UP.at[zu], 8 + zu)
                o = own(zu); o[...] = o[...] + self.UP[zu]
            pl.when((p.z < zu) & (p.z > 0))(up_add)
            self.copy(own(zu), self.UP.at[zu], 8 + zu, p.dev(z=p.up), p.z < zu)
            def dn_add():
                self.arrive(self.DN.at[zd], 12 + zd)
                o = own(zd); o[...] = o[...] + self.DN[zd]
            pl.when((p.z > zd) & (p.z < 3))(dn_add)
            self.copy(own(zd), self.DN.at[zd], 12 + zd, p.dev(z=p.down), p.z > zd)
        def Z3():
            o = own(p.z)
            @pl.when(p.z > 0)
            def _():
                self.arrive(self.UP.at[p.z], 8 + p.z)
                o[...] = o[...] + self.UP[p.z]
            @pl.when(p.z < 3)
            def _():
                self.arrive(self.DN.at[p.z], 12 + p.z)
                o[...] = o[...] + self.DN[p.z]
            ob1 = dict(me); ob1[b1] = 1 - me[b1]
            self.copy(self.PB.at[p.z, ob1["y"], ob1["x"], p.c], self.LX, 16, part1)
        def FIN():
            self.arrive(self.LX, 16)
            v = self.PB[p.z, p.y, p.x, p.c].astype(jnp.float32) + self.LX[...].astype(jnp.float32)
            self.out(v)
        return dict(R1=R1, R2=R2, Z0=lambda: hop(3, 0), Z1=lambda: hop(2, 1), Z2=lambda: hop(1, 2), Z3=Z3, FIN=FIN)

    def phases_a(self):
        p = self.p
        me = {"x": p.x, "y": p.y}
        halves = []
        for h, (b1, b2) in enumerate((("x", "y"), ("y", "x"))):
            r = pl.ds(16 * h, 16)
            halves.append((h, b1, b2, r, p.dev(**{b1: 1 - me[b1]}), p.dev(**{b2: 1 - me[b2]})))
        def at(zz, b1, b1v, r):
            d = dict(me); d[b1] = b1v
            return self.PB.at[zz, d["y"], d["x"], p.c, r]
        def R1():
            for zz in range(4):
                self.merge(zz)
                for h, b1, b2, r, part1, part2 in halves:
                    self.copy(self.pair(self.PB, zz, b2, 1 - me[b2], r), self.L1.at[zz, :, r], 17 + 4 * h + zz, part2)
        def R2():
            for zz in range(4):
                for h, b1, b2, r, part1, part2 in halves:
                    self.arrive(self.L1.at[zz, :, r], 17 + 4 * h + zz)
                    o = self.pair(self.PB, zz, b2, me[b2], r)
                    o[...] = o[...] + self.L1[zz, :, r]
                    self.copy(at(zz, b1, 1 - me[b1], r), self.L2.at[zz, r], 25 + 4 * h + zz, part1)
        def R3():
            for zz in range(4):
                for h, b1, b2, r, part1, part2 in halves:
                    self.arrive(self.L2.at[zz, r], 25 + 4 * h + zz)
                    o = at(zz, b1, me[b1], r)
                    o[...] = o[...] + self.L2[zz, r]
        blk = lambda zz: self.PB.at[zz, p.y, p.x, p.c]
        def hop(zu, zd):
            def up_add():
                self.arrive(self.UP.at[zu, 0], 8 + zu)
                o = blk(zu); o[...] = o[...] + self.UP[zu, 0]
            pl.when((p.z < zu) & (p.z > 0))(up_add)
            self.copy(blk(zu), self.UP.at[zu, 0], 8 + zu, p.dev(z=p.up), p.z < zu)
            def dn_add():
                self.arrive(self.DN.at[zd, 0], 12 + zd)
                o = blk(zd); o[...] = o[...] + self.DN[zd, 0]
            pl.when((p.z > zd) & (p.z < 3))(dn_add)
            self.copy(blk(zd), self.DN.at[zd, 0], 12 + zd, p.dev(z=p.down), p.z > zd)
        def FIN():
            o = blk(p.z)
            @pl.when(p.z > 0)
            def _():
                self.arrive(self.UP.at[p.z, 0], 8 + p.z)
                o[...] = o[...] + self.UP[p.z, 0]
            @pl.when(p.z < 3)
            def _():
                self.arrive(self.DN.at[p.z, 0], 12 + p.z)
                o[...] = o[...] + self.DN[p.z, 0]
            self.out(o[...].astype(jnp.float32))
        return dict(R1=R1, R2=R2, Z3=R3, Z0=lambda: hop(3, 0), Z1=lambda: hop(2, 1), Z2=lambda: hop(1, 2), FIN=FIN)

NS, NR = 32, 33
OFF_C = dict(LD=0, R1=1, R2=2, Z0=3, Z1=3.4, Z2=3.8, Z3=4.4, FIN=6)
OFF_A = dict(LD=0, R1=1, R2=2, Z3=3, Z0=4, Z1=4.4, Z2=4.8, FIN=6)

def scatter_kernel(*refs):
    g = refs[:9]; gctx = refs[9]
    osp, oso, ocp, oco, oai, oao, oen = refs[10:17]
    PB, L0, L1, L2, UP, DN, LX, ssem, rsem, lsem, csem, crsem = refs[17:]
    p = Place()
    loads = []
    for t in range(NT):
        cp = pltpu.make_async_copy(g[t], PB.at[t], lsem.at[t]); cp.start(); loads.append(cp)
    entry_barrier(p)
    me = p.x * 2 + p.c
    cs = []
    for k, (dx, dc) in enumerate(((0, 1), (1, 0), (1, 1))):
        tx = (p.x + dx) % 2; tc = (p.c + dc) % 2
        w = tx * 2 + tc
        c_ = pltpu.make_async_remote_copy(gctx.at[:, w], oen.at[0, me], csem.at[k], crsem.at[me], device_id=p.dev(x=tx, c=tc), device_id_type=MESH)
        c_.start(); cs.append(c_)
    lc = pltpu.make_async_copy(gctx.at[:, me], oen.at[0, me], lsem.at[9]); lc.start()
    def o_ad(v):
        oai[...] = v[:, :512]
        oao[:, 0:512] = v[0:16, 512:]
        oao[:, 512:1024] = v[16:32, 512:]
    def put(ref, j=None):
        def f(v):
            if j is None: ref[...] = v
            else: ref[j] = v
        return f
    outs = [o_ad, put(oco), put(ocp, 1), put(ocp, 2), put(ocp, 0), put(oso), put(osp, 1), put(osp, 2), put(osp, 0)]
    items = []
    reds = []
    for t in range(NT):
        r = Reduce(p, t, ORDERS[t], PB.at[t], L0.at[t], L1.at[t], L2.at[t], UP.at[t], DN.at[t], LX.at[t], ssem.at[t], rsem.at[t], outs[t])
        reds.append(r)
        ph = r.phases()
        def LD(t=t, r=r):
            loads[t].wait()
            for zz in range(4): r.sib(zz)
        ph["LD"] = LD
        for name, off in (OFF_A if ORDERS[t] == "A" else OFF_C).items():
            items.append((t * RS_GAP + off, t, len(items), ph[name]))
    items.sort(key=lambda q: q[:3])
    for it in items: it[3]()
    for r in reds: r.finish()
    lc.wait()
    for c_ in cs: c_.wait_send()
    for k, (dx, dc) in enumerate(((0, 1), (1, 0), (1, 1))):
        tx = (p.x + dx) % 2; tc = (p.c + dc) % 2
        w = tx * 2 + tc
        pltpu.make_async_remote_copy(gctx.at[:, w], oen.at[0, w], csem.at[k], crsem.at[w], device_id=p.dev(), device_id_type=MESH).wait_recv()

def scatter(tiles, gctx):
    any_ = pl.BlockSpec(memory_space=pl.ANY)
    vm = pl.BlockSpec(memory_space=pltpu.VMEM)
    f32, bf = jnp.float32, jnp.bfloat16
    return pl.pallas_call(scatter_kernel,
        out_shape=(jax.ShapeDtypeStruct((3, 32, 1024), f32), jax.ShapeDtypeStruct((32, 1024), f32), jax.ShapeDtypeStruct((3, 32, 1024), f32), jax.ShapeDtypeStruct((32, 1024), f32), jax.ShapeDtypeStruct((32, 512), f32), jax.ShapeDtypeStruct((16, 1024), f32), jax.ShapeDtypeStruct((1, 4, 2, 32, 1024), bf)),
        in_specs=[any_] * 10, out_specs=(vm,) * 6 + (any_,),
        scratch_shapes=[pltpu.VMEM((NT, 4, 2, 2, 2, 32, ROW), bf), pltpu.VMEM((NT, 4, 2, 2, 32, ROW), bf), pltpu.VMEM((NT, 4, 2, 32, ROW), bf), pltpu.VMEM((NT, 4, 32, ROW), bf),
                        pltpu.VMEM((NT, 4, 2, 32, ROW), bf), pltpu.VMEM((NT, 4, 2, 32, ROW), bf), pltpu.VMEM((NT, 32, ROW), bf),
                        pltpu.SemaphoreType.DMA((NT, NS)), pltpu.SemaphoreType.DMA((NT, NR)), pltpu.SemaphoreType.DMA((10,)), pltpu.SemaphoreType.DMA((3,)), pltpu.SemaphoreType.DMA((4,))],
        compiler_params=pltpu.CompilerParams(collective_id=1, has_side_effects=True, vmem_limit_bytes=62 << 20),
        name="scatter")(*tiles, gctx)


def device_program(tokens, encoder, dec_lengths, enc_lengths, gains, self_proj, self_out, cross_proj, cross_out, ffn_in, ffn_out, adapt_in, adapt_out, cotangent):
    bf = jnp.bfloat16
    buf, gfo, ctx = gather(self_proj, self_out, cross_proj, cross_out, ffn_in, ffn_out, adapt_in, adapt_out, encoder)
    w = lambda t: buf[t].reshape(1024, 1024)
    wq1, wk1, wv1, wso, wk2, wv2, wq2, wco = (w(t) for t in range(8))
    ad = buf[8].reshape(32, 32, 1024)
    wai = ad[:, :, :512].reshape(1024, 512)
    wao = jnp.concatenate([ad[:, :16, 512:].reshape(512, 512), ad[:, 16:, 512:].reshape(512, 512)], axis=1)
    wfi = [w(9 + j) for j in range(4)]
    wfo = gfo.reshape(4096, 1024)
    context = ctx.reshape(256, 1024)
    masks = [slot_masks(dec_lengths[m], enc_lengths[m], 128) for m in range(2)]
    smask = jnp.stack([a for a, _ in masks]); cmask = jnp.stack([b for _, b in masks])
    r16 = lambda v: v.astype(bf)
    sq, sk, sv = (r16(matmul(tokens, m)) for m in (wq1, wk1, wv1))
    att = lambda q, k, v, m: attend2(q, k, v, m)
    self_mix, p1 = att(sq, sk, sv, smask)
    h1 = tokens.astype(jnp.float32) + matmul(self_mix, wso)
    y1 = layer_norm(h1, gains[0])
    y1l = r16(y1)
    cq = r16(matmul(y1l, wq2)); ck = r16(matmul(context, wk2)); cv = r16(matmul(context, wv2))
    cross_mix, p2 = att(cq, ck, cv, cmask)
    h2 = y1 + matmul(cross_mix, wco)
    y2 = layer_norm(h2, gains[1])
    y2l = r16(y2)
    u = jnp.concatenate([matmul(y2l, m) for m in wfi], axis=1)
    af = r16(gelu_exact(u))
    r = matmul(y2l, wai)
    ar = r16(jax.nn.silu(r))
    h3 = y2 + matmul(af, wfo) + 4.0 * matmul(ar, wao)
    layer_out = r16(layer_norm(h3, gains[2]))
    g3 = norm_back(h3, gains[2], cotangent.astype(jnp.float32))
    gb = r16(g3)
    gu = r16(jax.vjp(gelu_exact, u)[1](matmul_nt(gb, wfo))[0])
    gr = r16(jax.vjp(jax.nn.silu, r)[1](matmul_nt(gb, wao) * 4.0)[0])
    dao = matmul_tn(ar, gb) * 4.0
    dai = matmul_tn(y2l, gr)
    gy2 = g3 + matmul_nt(gr, wai)
    for j in range(4):
        gy2 = gy2 + matmul_nt(gu[:, 1024 * j:1024 * j + 1024], wfi[j])
    g2 = norm_back(h2, gains[1], gy2)
    gc2 = r16(g2)
    dco = matmul_tn(cross_mix, gc2)
    gx2 = r16(matmul_nt(gc2, wco))
    gq2, gk2, gv2 = attend_back2(gx2, cq, ck, cv, p2)
    dq2 = matmul_tn(y1l, gq2); dk2 = matmul_tn(context, gk2); dv2 = matmul_tn(context, gv2)
    gctx = r16(matmul_nt(gk2, wk2) + matmul_nt(gv2, wv2)).reshape(2, 4, 32, 1024)
    gy1 = g2 + matmul_nt(gq2, wq2)
    g1 = norm_back(h1, gains[0], gy1)
    gc1 = r16(g1)
    dso = matmul_tn(self_mix, gc1)
    gx1 = r16(matmul_nt(gc1, wso))
    gq1, gk1, gv1 = attend_back2(gx1, sq, sk, sv, p1)
    dq1, dk1, dv1 = (matmul_tn(tokens, g) for g in (gq1, gk1, gv1))
    gtok = r16(g1 + matmul_nt(gq1, wq1) + matmul_nt(gk1, wk1) + matmul_nt(gv1, wv1))
    dad = jnp.concatenate([dai, dao.reshape(32, 16, 2, 512).transpose(0, 2, 1, 3).reshape(1024, 512)], axis=1)
    tiles = [r16(v).reshape(4, 2, 2, 2, 32, 1024) for v in (dad, dco, dk2, dv2, dq2, dso, dk1, dv1, dq1)]
    osp, oso, ocp, oco, oai, oao, oen = scatter(tiles, gctx)
    return (layer_out, gtok, oen, osp, oso, ocp, oco, oai, oao)


def heads(m):
    return m.reshape(2, 128, HEADS, 64)


def attend2(q, k, v, allowed):
    s = jnp.einsum("uqhd,ukhd->uhqk", heads(q), heads(k), preferred_element_type=jnp.float32) * 0.125
    s = jnp.where(allowed[:, None], s, NEGATIVE)
    e = jnp.exp(s - jnp.max(s, axis=-1, keepdims=True))
    p = e / jnp.sum(e, axis=-1, keepdims=True)
    mixed = jnp.einsum("uhqk,ukhd->uqhd", p.astype(jnp.bfloat16), heads(v), preferred_element_type=jnp.float32)
    return mixed.reshape(q.shape).astype(jnp.bfloat16), p


def attend_back2(g, q, k, v, p):
    gh = heads(g)
    dp = jnp.einsum("uqhd,ukhd->uhqk", gh, heads(v), preferred_element_type=jnp.float32)
    ds = (p * (dp - jnp.sum(p * dp, axis=-1, keepdims=True))).astype(jnp.bfloat16)
    dq = jnp.einsum("uhqk,ukhd->uqhd", ds, heads(k), preferred_element_type=jnp.float32) * 0.125
    dk = jnp.einsum("uhqk,uqhd->ukhd", ds, heads(q), preferred_element_type=jnp.float32) * 0.125
    dv = jnp.einsum("uhqk,uqhd->ukhd", p.astype(jnp.bfloat16), gh, preferred_element_type=jnp.float32)
    return tuple(t.reshape(q.shape).astype(jnp.bfloat16) for t in (dq, dk, dv))


def solution(mesh):
    in_specs = (
        P(("seq", "enc"), None),
        P("seq", None, None, "enc", None),
        P(("seq", "enc"), None),
        P(("seq", "enc"), None),
        P(),
        P(None, ("seq", "enc"), None),
        P(("seq", "enc"), None),
        P(None, ("seq", "enc"), None),
        P(("seq", "enc"), None),
        P(("seq", "enc"), None),
        P(("seq", "enc"), None),
        P(("seq", "enc"), None),
        P(("seq", "enc"), None),
        P(("seq", "enc"), None),
    )
    out_specs = (
        P(("seq", "enc"), None),
        P(("seq", "enc"), None),
        P("seq", None, None, "enc", None),
        P(None, ("seq", "enc"), None),
        P(("seq", "enc"), None),
        P(None, ("seq", "enc"), None),
        P(("seq", "enc"), None),
        P(("seq", "enc"), None),
        P(("seq", "enc"), None),
    )
    fast = (mesh.shape["seq"], mesh.shape["enc"]) == (8, 4)
    return jax.shard_map(
        device_program if fast else per_device, mesh=mesh, in_specs=in_specs, out_specs=out_specs, check_vma=False
    )
```

```python
import jax
import jax.numpy as jnp
from jax import lax
from jax.experimental import pallas as pl
from jax.experimental.pallas import tpu as pltpu
from jax.sharding import PartitionSpec as P

HEADS = 16
ADAPT = 512
MICRO = 2


EPSILON = 1e-05
NEGATIVE = -1e30


def matmul(left, right):
    return jnp.dot(left, right, preferred_element_type=jnp.float32)


def matmul_tn(left, right):
    return lax.dot_general(
        left, right, (((0,), (0,)), ((), ())), preferred_element_type=jnp.float32
    )


def matmul_nt(left, right):
    return lax.dot_general(
        left, right, (((1,), (1,)), ((), ())), preferred_element_type=jnp.float32
    )


def layer_norm(hidden, gain):
    center = hidden - jnp.mean(hidden, axis=-1, keepdims=True)
    spread = jnp.mean(center * center, axis=-1, keepdims=True)
    return center * lax.rsqrt(spread + EPSILON) * gain


def norm_back(hidden, gain, grad_out):
    _, pullback = jax.vjp(lambda value: layer_norm(value, gain), hidden)
    return pullback(grad_out)[0]


def gelu_exact(value):
    return jax.nn.gelu(value, approximate=False)


def slot_masks(dec_row, enc_row, rows):
    half_rows = rows // 2
    places = lax.broadcasted_iota(jnp.int32, (rows,), 0)
    paired = dec_row[1] > 0
    second = jnp.logical_and(paired, places >= half_rows)
    anchor = jnp.where(second, half_rows, 0).astype(jnp.int32)
    dec_valid = jnp.where(second, dec_row[1], dec_row[0])
    enc_valid = jnp.where(second, enc_row[1], enc_row[0])
    key_live = places - anchor < dec_valid
    context_live = places - anchor < enc_valid
    same_slot = second[:, None] == second[None, :]
    causal = places[None, :] <= places[:, None]
    self_mask = same_slot & causal & key_live[None, :]
    cross_mask = same_slot & context_live[None, :]
    return (self_mask, cross_mask)


def split_heads(matrix):
    return matrix.reshape(matrix.shape[0], HEADS, matrix.shape[1] // HEADS)


def attend(queries, keys, values, allowed):
    depth = queries.shape[1] // HEADS
    scores = jnp.einsum(
        "qhd,khd->hqk", split_heads(queries), split_heads(keys), preferred_element_type=jnp.float32
    ) * float(depth) ** (-0.5)
    masked = jnp.where(allowed[None], scores, NEGATIVE)
    weights = jnp.exp(masked - jnp.max(masked, axis=-1, keepdims=True))
    probs = weights / jnp.sum(weights, axis=-1, keepdims=True)
    mixed = jnp.einsum(
        "hqk,khd->qhd",
        probs.astype(jnp.bfloat16),
        split_heads(values),
        preferred_element_type=jnp.float32,
    )
    return (mixed.reshape(queries.shape).astype(jnp.bfloat16), probs)


def attend_back(grad_mixed, queries, keys, values, probs):
    depth = queries.shape[1] // HEADS
    factor = float(depth) ** (-0.5)
    grad_heads = split_heads(grad_mixed)
    grad_probs = jnp.einsum(
        "qhd,khd->hqk", grad_heads, split_heads(values), preferred_element_type=jnp.float32
    )
    inner = jnp.sum(probs * grad_probs, axis=-1, keepdims=True)
    grad_scores = (probs * (grad_probs - inner)).astype(jnp.bfloat16)
    grad_query = (
        jnp.einsum(
            "hqk,khd->qhd", grad_scores, split_heads(keys), preferred_element_type=jnp.float32
        )
        * factor
    )
    grad_key = (
        jnp.einsum(
            "hqk,qhd->khd", grad_scores, split_heads(queries), preferred_element_type=jnp.float32
        )
        * factor
    )
    grad_value = jnp.einsum(
        "hqk,qhd->khd", probs.astype(jnp.bfloat16), grad_heads, preferred_element_type=jnp.float32
    )
    return (
        grad_query.reshape(queries.shape).astype(jnp.bfloat16),
        grad_key.reshape(keys.shape).astype(jnp.bfloat16),
        grad_value.reshape(values.shape).astype(jnp.bfloat16),
    )


def per_device(
    tokens,
    encoder,
    dec_lengths,
    enc_lengths,
    gains,
    self_proj,
    self_out,
    cross_proj,
    cross_out,
    ffn_in,
    ffn_out,
    adapt_in,
    adapt_out,
    cotangent,
):
    shards = (self_proj, self_out, cross_proj, cross_out, ffn_in, ffn_out, adapt_in, adapt_out)

    def obtain():
        return (
            lax.all_gather(shards[0], ("seq", "enc"), axis=1, tiled=True),
            lax.all_gather(shards[1], ("seq", "enc"), axis=0, tiled=True),
            lax.all_gather(shards[2], ("seq", "enc"), axis=1, tiled=True),
            lax.all_gather(shards[3], ("seq", "enc"), axis=0, tiled=True),
            lax.all_gather(shards[4], ("seq", "enc"), axis=0, tiled=True),
            lax.all_gather(shards[5], ("seq", "enc"), axis=0, tiled=True),
            lax.all_gather(shards[6], ("seq", "enc"), axis=0, tiled=True),
            lax.all_gather(shards[7], ("seq", "enc"), axis=0, tiled=True),
        )

    rows = tokens.shape[0] // MICRO
    width = tokens.shape[1]
    owner = lax.axis_index("enc")
    acc_self = jnp.zeros((width, 3, width), jnp.float32)
    acc_self_out = jnp.zeros((width, width), jnp.float32)
    acc_cross = jnp.zeros((width, 3, width), jnp.float32)
    acc_cross_out = jnp.zeros((width, width), jnp.float32)
    acc_adapt_in = jnp.zeros((width, ADAPT), jnp.float32)
    acc_adapt_out = jnp.zeros((ADAPT, width), jnp.float32)
    outputs = []
    grad_rows = []
    grad_contexts = []
    for micro_index in range(MICRO):
        w_self, w_self_out, w_cross, w_cross_out, w_ffn_in, w_ffn_out, w_adapt_in, w_adapt_out = (
            obtain()
        )
        lower = micro_index * rows
        token_rows = tokens[lower : lower + rows]
        self_mask, cross_mask = slot_masks(dec_lengths[micro_index], enc_lengths[micro_index], rows)
        pieces = encoder[0, :, micro_index]
        context = lax.dynamic_index_in_dim(
            lax.all_gather(pieces, "enc", axis=1, tiled=True), owner, 0, keepdims=False
        )
        self_query = matmul(token_rows, w_self[0]).astype(jnp.bfloat16)
        self_key = matmul(token_rows, w_self[1]).astype(jnp.bfloat16)
        self_value = matmul(token_rows, w_self[2]).astype(jnp.bfloat16)
        self_mix, self_probs = attend(self_query, self_key, self_value, self_mask)
        first_sum = token_rows.astype(jnp.float32) + matmul(self_mix, w_self_out)
        first_norm = layer_norm(first_sum, gains[0])
        first_low = first_norm.astype(jnp.bfloat16)
        cross_query = matmul(first_low, w_cross[0]).astype(jnp.bfloat16)
        cross_key = matmul(context, w_cross[1]).astype(jnp.bfloat16)
        cross_value = matmul(context, w_cross[2]).astype(jnp.bfloat16)
        cross_mix, cross_probs = attend(cross_query, cross_key, cross_value, cross_mask)
        second_sum = first_norm + matmul(cross_mix, w_cross_out)
        second_norm = layer_norm(second_sum, gains[1])
        second_low = second_norm.astype(jnp.bfloat16)
        ffn_pre = matmul(second_low, w_ffn_in)
        ffn_act = gelu_exact(ffn_pre).astype(jnp.bfloat16)
        adapt_pre = matmul(second_low, w_adapt_in)
        adapt_act = jax.nn.silu(adapt_pre).astype(jnp.bfloat16)
        third_sum = second_norm + matmul(ffn_act, w_ffn_out) + 4.0 * matmul(adapt_act, w_adapt_out)
        outputs.append(layer_norm(third_sum, gains[2]).astype(jnp.bfloat16))
        w_self, w_self_out, w_cross, w_cross_out, w_ffn_in, w_ffn_out, w_adapt_in, w_adapt_out = (
            obtain()
        )
        grad_third = norm_back(
            third_sum, gains[2], cotangent[lower : lower + rows].astype(jnp.float32)
        )
        grad_branch = grad_third.astype(jnp.bfloat16)
        _, gelu_pull = jax.vjp(gelu_exact, ffn_pre)
        grad_ffn_pre = gelu_pull(matmul_nt(grad_branch, w_ffn_out))[0].astype(jnp.bfloat16)
        grad_adapt_act = matmul_nt(grad_branch, w_adapt_out) * 4.0
        _, silu_pull = jax.vjp(jax.nn.silu, adapt_pre)
        grad_adapt_pre = silu_pull(grad_adapt_act)[0].astype(jnp.bfloat16)
        acc_adapt_out = acc_adapt_out + matmul_tn(adapt_act, grad_branch) * 4.0
        acc_adapt_in = acc_adapt_in + matmul_tn(second_low, grad_adapt_pre)
        grad_second = (
            grad_third + matmul_nt(grad_ffn_pre, w_ffn_in) + matmul_nt(grad_adapt_pre, w_adapt_in)
        )
        grad_second_sum = norm_back(second_sum, gains[1], grad_second)
        grad_cross_branch = grad_second_sum.astype(jnp.bfloat16)
        acc_cross_out = acc_cross_out + matmul_tn(cross_mix, grad_cross_branch)
        grad_cross_mix = matmul_nt(grad_cross_branch, w_cross_out).astype(jnp.bfloat16)
        grad_cq, grad_ck, grad_cv = attend_back(
            grad_cross_mix, cross_query, cross_key, cross_value, cross_probs
        )
        acc_cross = acc_cross + jnp.stack(
            [
                matmul_tn(first_low, grad_cq),
                matmul_tn(context, grad_ck),
                matmul_tn(context, grad_cv),
            ],
            axis=1,
        )
        grad_context = matmul_nt(grad_ck, w_cross[1]) + matmul_nt(grad_cv, w_cross[2])
        holder = jnp.zeros((lax.axis_size("enc"),) + grad_context.shape, jnp.float32)
        holder = lax.dynamic_update_index_in_dim(holder, grad_context, owner, 0)
        returned = lax.psum_scatter(
            holder.astype(jnp.bfloat16), "enc", scatter_dimension=1, tiled=True
        )
        grad_contexts.append(returned)
        grad_first = grad_second_sum + matmul_nt(grad_cq, w_cross[0])
        grad_first_sum = norm_back(first_sum, gains[0], grad_first)
        grad_self_branch = grad_first_sum.astype(jnp.bfloat16)
        acc_self_out = acc_self_out + matmul_tn(self_mix, grad_self_branch)
        grad_self_mix = matmul_nt(grad_self_branch, w_self_out).astype(jnp.bfloat16)
        grad_sq, grad_sk, grad_sv = attend_back(
            grad_self_mix, self_query, self_key, self_value, self_probs
        )
        acc_self = acc_self + jnp.stack(
            [
                matmul_tn(token_rows, grad_sq),
                matmul_tn(token_rows, grad_sk),
                matmul_tn(token_rows, grad_sv),
            ],
            axis=1,
        )
        grad_input = (
            grad_first_sum
            + matmul_nt(grad_sq, w_self[0])
            + matmul_nt(grad_sk, w_self[1])
            + matmul_nt(grad_sv, w_self[2])
        )
        grad_rows.append(grad_input.astype(jnp.bfloat16))
    summed = (
        lax.psum_scatter(acc_self, ("seq", "enc"), scatter_dimension=0, tiled=True),
        lax.psum_scatter(acc_self_out, ("seq", "enc"), scatter_dimension=0, tiled=True),
        lax.psum_scatter(acc_cross, ("seq", "enc"), scatter_dimension=0, tiled=True),
        lax.psum_scatter(acc_cross_out, ("seq", "enc"), scatter_dimension=0, tiled=True),
        lax.psum_scatter(acc_adapt_in, ("seq", "enc"), scatter_dimension=0, tiled=True),
        lax.psum_scatter(acc_adapt_out, ("seq", "enc"), scatter_dimension=0, tiled=True),
    )
    layer_out = jnp.concatenate(outputs, axis=0)
    grad_tokens = jnp.concatenate(grad_rows, axis=0)
    grad_encoder = jnp.stack(grad_contexts, axis=1)[None]
    grad_self_proj = jnp.transpose(summed[0], (1, 0, 2))
    grad_cross_proj = jnp.transpose(summed[2], (1, 0, 2))
    return (
        layer_out,
        grad_tokens,
        grad_encoder,
        grad_self_proj,
        summed[1],
        grad_cross_proj,
        summed[3],
        summed[4],
        summed[5],
    )


MESH = pl.DeviceIdType.MESH
AG_GAP = 2

TILES = ["q1", "k1", "v1", "so", "k2", "v2", "q2", "co", "ad", "f0", "f1", "f2", "f3", "o0", "o1", "o2", "o3"]

class Place:
    def __init__(self):
        seq, enc = lax.axis_index("seq"), lax.axis_index("enc")
        self.z, self.y, self.x, self.c = seq // 2, seq % 2, enc // 2, enc % 2
        self.up, self.down = jnp.minimum(self.z + 1, 3), jnp.maximum(self.z - 1, 0)
    def dev(self, z=None, y=None, x=None, c=None):
        z = self.z if z is None else z
        y = self.y if y is None else y
        x = self.x if x is None else x
        c = self.c if c is None else c
        return (z * 2 + y, x * 2 + c)

def entry_barrier(p):
    bar = pltpu.get_barrier_semaphore()
    def sig(d):
        pl.semaphore_signal(bar, inc=1, device_id=d, device_id_type=MESH)
    sig(p.dev(c=1 - p.c)); sig(p.dev(x=1 - p.x)); sig(p.dev(y=1 - p.y)); sig(p.dev(x=1 - p.x, c=1 - p.c))
    @pl.when(p.z < 3)
    def _(): sig(p.dev(z=p.up))
    @pl.when(p.z > 0)
    def _(): sig(p.dev(z=p.down))
    peers = 4 + (p.z < 3).astype(jnp.int32) + (p.z > 0).astype(jnp.int32)
    pl.semaphore_wait(bar, peers)

ALL4 = pl.ds(0, 4)
ALL2 = pl.ds(0, 2)

class Stream:
    def __init__(self, p, view, order, ssem, rsem):
        self.p, self.view, self.order, self.ssem, self.rsem = p, view, order, ssem, rsem
        self.ns = 0
        self.sends = []

    def cut(self, z, y, x, c):
        return self.view(z, y, x, c)

    def copy(self, where, slot, target, guard=None):
        k = self.ns; self.ns += 1
        cp = pltpu.make_async_remote_copy(where, where, self.ssem.at[k], self.rsem.at[slot], device_id=target, device_id_type=MESH)
        if guard is None:
            cp.start()
        else:
            pl.when(guard)(cp.start)
        self.sends.append((cp, guard))

    def arrive(self, where, slot, guard=None):
        cp = pltpu.make_async_remote_copy(where, where, self.ssem.at[0], self.rsem.at[slot], device_id=self.p.dev(), device_id_type=MESH)
        if guard is None:
            cp.wait_recv()
        else:
            pl.when(guard)(cp.wait_recv)

    def finish(self):
        for cp, guard in self.sends:
            if guard is None:
                cp.wait_send()
            else:
                pl.when(guard)(cp.wait_send)

    def at(self, z, own):
        return self.cut(z, own["y"], own["x"], self.p.c)

    def phases(self):
        p = self.p
        if self.order[0] == "z":
            b1, b2 = self.order[1], self.order[2]
            me = {"x": p.x, "y": p.y}
            oth = {"x": 1 - p.x, "y": 1 - p.y}
            part1 = p.dev(**{b1: oth[b1]}); part2 = p.dev(**{b2: oth[b2]})
            sib = p.dev(c=1 - p.c)
            own = dict(me)
            b1o = dict(me); b1o[b1] = oth[b1]
            both = dict(me); both[b1] = ALL2
            allof = {"x": ALL2, "y": ALL2}
            def P0():
                self.copy(self.at(p.z, own), p.z, p.dev(z=p.up), p.z < 3)
                self.copy(self.at(p.z, own), p.z, p.dev(z=p.down), p.z > 0)
                self.copy(self.at(p.z, own), 4 + p.z, part1)
            def hop(t):
                lo, hi = jnp.maximum(p.z - t, 0), jnp.minimum(p.z + t, 3)
                below, above = p.z >= t, p.z + t <= 3
                self.arrive(self.at(lo, own), lo, below)
                if t < 3:
                    self.copy(self.at(lo, own), lo, p.dev(z=p.up), (below) & (p.z < 3))
                self.copy(self.at(lo, own), 4 + lo, part1, below)
                self.arrive(self.at(hi, own), hi, above)
                if t < 3:
                    self.copy(self.at(hi, own), hi, p.dev(z=p.down), (above) & (p.z > 0))
                self.copy(self.at(hi, own), 4 + hi, part1, above)
            def P4():
                for zz in range(4):
                    self.arrive(self.at(zz, b1o), 4 + zz)
                    self.copy(self.at(zz, both), 8 + zz, part2)
            def P5():
                self.copy(self.at(ALL4, both), 12, sib)
                for zz in range(4):
                    self.arrive(self.at(zz, both), 8 + zz)
                b2o = dict(both); b2o[b2] = oth[b2]
                self.copy(self.at(ALL4, b2o), 13, sib)
            def P6():
                b2o = dict(both); b2o[b2] = oth[b2]
                w = lambda s: self.cut(ALL4, s["y"], s["x"], 1 - p.c)
                self.arrive(w(both), 12)
                self.arrive(w(b2o), 13)
            return [P0, lambda: hop(1), lambda: hop(2), lambda: hop(3), P4, P5, P6]
        b1, b2 = self.order[0], self.order[2]
        me = {"x": p.x, "y": p.y}
        oth = {"x": 1 - p.x, "y": 1 - p.y}
        part1 = p.dev(**{b1: oth[b1]}); part2 = p.dev(**{b2: oth[b2]})
        sib = p.dev(c=1 - p.c)
        own = dict(me)
        b1o = dict(me); b1o[b1] = oth[b1]
        both = dict(me); both[b1] = ALL2
        b2o = dict(both); b2o[b2] = oth[b2]
        def P0():
            self.copy(self.at(p.z, own), 8, part1)
        def P1():
            self.arrive(self.at(p.z, b1o), 8)
            self.copy(self.at(p.z, both), p.z, p.dev(z=p.up), p.z < 3)
            self.copy(self.at(p.z, both), p.z, p.dev(z=p.down), p.z > 0)
            self.copy(self.at(p.z, both), 4 + p.z, part2)
        def hop(t):
            lo, hi = jnp.maximum(p.z - t, 0), jnp.minimum(p.z + t, 3)
            below, above = p.z >= t, p.z + t <= 3
            self.arrive(self.at(lo, both), lo, below)
            if t < 3:
                self.copy(self.at(lo, both), lo, p.dev(z=p.up), (below) & (p.z < 3))
            self.copy(self.at(lo, both), 4 + lo, part2, below)
            self.arrive(self.at(hi, both), hi, above)
            if t < 3:
                self.copy(self.at(hi, both), hi, p.dev(z=p.down), (above) & (p.z > 0))
            self.copy(self.at(hi, both), 4 + hi, part2, above)
        def P5():
            self.copy(self.at(ALL4, both), 12, sib)
            for zz in range(4):
                self.arrive(self.at(zz, b2o), 4 + zz)
            self.copy(self.at(ALL4, b2o), 13, sib)
        def P6():
            w = lambda s: self.cut(ALL4, s["y"], s["x"], 1 - p.c)
            self.arrive(w(both), 12)
            self.arrive(w(b2o), 13)
        return [P0, P1, lambda: hop(1), lambda: hop(2), lambda: hop(3), P5, P6]

F32, BF = jnp.float32, jnp.bfloat16
NSLOT, NSEND = 14, 19
N_STREAM = 23
EPS = 1e-05

def dot(a, b):
    return jnp.dot(a, b, preferred_element_type=F32)

def dot_nt(a, b):
    return lax.dot_general(a, b, (((1,), (1,)), ((), ())), preferred_element_type=F32)

def dot_tn(a, b):
    return lax.dot_general(a, b, (((0,), (0,)), ((), ())), preferred_element_type=F32)

def cols(n, width):
    return pl.ds(pl.multiple_of(n * width, width), width)

def norm_rows(h):
    center = h - jnp.mean(h, axis=-1, keepdims=True)
    spread = jnp.mean(center * center, axis=-1, keepdims=True)
    return center * lax.rsqrt(spread + EPS)

def half_masks():
    lane = lax.broadcasted_iota(jnp.int32, (1, 128), 1)
    lo = jnp.where(lane < 64, 1.0, 0.0)
    return lo.astype(BF), (1.0 - lo).astype(BF)

def pair_up(m, lo, hi):
    return jnp.concatenate([m * lo, m * hi], axis=0)

def side(m):
    return jnp.concatenate([m[:128], m[128:]], axis=1)

def forward_kernel(x, gains, bias, sp, so, cp, co, fi, fo, ai, ao, en,
                   buf, gfo, o_qkv, o_p, o_h, o_t, o_at, o_gp, o_sr, o_out,
                   qkv, P, H, T, AT, GP, SR, OUT, ctx, wbuf, wo, own, ownf, y, yl, mix, af, ar,
                   ssem, rsem, lsem, csem, crsem, wsem, osem):
    p = Place()
    loc = []
    def put(src, dst):
        c_ = pltpu.make_async_copy(src, dst, lsem.at[len(loc)]); c_.start(); loc.append(c_)
    for j, t in enumerate((0, 1, 2)): put(sp.at[j], own.at[t])
    put(so, own.at[3])
    for j, t in ((1, 4), (2, 5), (0, 6)): put(cp.at[j], own.at[t])
    put(co, own.at[7])
    put(ai, own.at[8, :, pl.ds(0, 512)])
    put(ao.at[:, pl.ds(0, 512)], own.at[8, pl.ds(0, 16), pl.ds(512, 512)])
    put(ao.at[:, pl.ds(512, 512)], own.at[8, pl.ds(16, 16), pl.ds(512, 512)])
    for j in range(4): put(fi.at[:, pl.ds(1024 * j, 1024)], own.at[9 + j])
    put(fo, ownf)
    me = p.x * 2 + p.c
    put(en.at[0, me], ctx.at[:, me])
    entry_barrier(p)
    for c_ in loc: c_.wait()
    n_in = len(loc)
    c1 = pltpu.make_async_copy(own, buf.at[:, p.z, p.y, p.x, p.c], lsem.at[n_in]); c1.start()
    c2 = pltpu.make_async_copy(ownf, gfo.at[p.z, p.y, p.x, p.c], lsem.at[n_in + 1]); c2.start()
    cs = []
    for k, (dx, dc) in enumerate(((0, 1), (1, 0), (1, 1))):
        tx = (p.x + dx) % 2; tc = (p.c + dc) % 2
        c_ = pltpu.make_async_remote_copy(en.at[0, tx * 2 + tc], ctx.at[:, me], csem.at[k], crsem.at[me], device_id=p.dev(x=tx, c=tc), device_id_type=MESH)
        c_.start(); cs.append(c_)
    c1.wait(); c2.wait()
    streams = []
    for g in range(6):
        for i in range(3):
            t = 3 * g + i
            if t >= 17: continue
            R = 32 if t < 13 else 128
            rows = [(0, R // 2, "zxy"), (R // 2, R // 2, "zyx")] if i == 0 else [(0, R, "xzy" if i == 1 else "yzx")]
            for r0, nr, order in rows:
                n = len(streams)
                if t < 13:
                    view = lambda z, y_, x_, c, t=t, r0=r0, nr=nr: buf.at[t, z, y_, x_, c, pl.ds(r0, nr)]
                else:
                    view = lambda z, y_, x_, c, j=t - 13, r0=r0, nr=nr: gfo.at[z, y_, x_, c, pl.ds(r0, nr), pl.ds(256 * j, 256)]
                streams.append((g, i, Stream(p, view, order, ssem.at[n], rsem.at[n])))
    items = []
    def add(pos, fn): items.append((pos, len(items), fn))
    for g, i, s in streams:
        for k, fn in enumerate(s.phases()): add(g * AG_GAP + k + 0.25 * i, fn)

    def fetch(t):
        if t < 13: return pltpu.make_async_copy(buf.at[t], wbuf.at[t % 4], wsem.at[t])
        j = t - 13
        return pltpu.make_async_copy(gfo.at[:, :, :, :, :, pl.ds(256 * j, 256)], wo.at[j % 2], wsem.at[t])
    def start(t): return lambda: fetch(t).start()
    outs = []
    def keep(src, dst):
        c_ = pltpu.make_async_copy(src, dst, osem.at[len(outs)]); c_.start(); outs.append(c_)
    lo, hi = half_masks()

    def mm(lhs, t, fn, width=1024, first=0):
        @pl.loop(0, width // 256)
        def _(n):
            ds = cols(n, 256)
            w = wbuf[t % 4, :, :, :, :, :, ds].reshape(1024, 256)
            fn(ds, dot(lhs[...], w))

    def proj(lhs, t, slot):
        def run():
            fetch(t).wait()
            def st(ds, v): qkv[slot, :, ds] = v.astype(BF)
            mm(lhs, t, st)
            keep(qkv.at[slot], o_qkv.at[slot])
        return run

    def flip(src, slot):
        def run():
            @pl.loop(0, 4)
            def _(n):
                T[slot, cols(n, 256), :] = src[:, cols(n, 256)].T
            keep(T.at[slot], o_t.at[slot])
        return run

    def attend(a, part):
        def run():
            u = part // 2
            @pl.loop(0, 4)
            def _(n):
                pr = (part % 2) * 4 + n
                r, cc = pl.ds(u * 128, 128), cols(pr, 128)
                q, k, v = (qkv[3 * a + j, r, cc] for j in range(3))
                b = bias[a, u]
                s = dot_nt(pair_up(q, lo, hi), k) * 0.125 + jnp.concatenate([b, b], axis=0)
                e = jnp.exp(s - jnp.max(s, axis=-1, keepdims=True))
                pr_ = e / jnp.sum(e, axis=-1, keepdims=True)
                P[a, u * 8 + pr] = pr_
                mix[r, cc] = dot(side(pr_.astype(BF)), pair_up(v, lo, hi)).astype(BF)
            if part == 3: keep(P.at[a], o_p.at[a])
        return run

    def branch(t, base, slot):
        def run():
            fetch(t).wait()
            def st(ds, v): H[slot, :, ds] = base[:, ds].astype(F32) + v
            mm(mix, t, st)
        return run

    def norm(slot):
        def run():
            keep(H.at[slot], o_h.at[slot])
            @pl.loop(0, 8)
            def _(n):
                r = pl.ds(pl.multiple_of(n * 32, 32), 32)
                v = norm_rows(H[slot, r, :]) * gains[slot, :][None]
                if slot < 2:
                    y[r, :] = v
                    yl[r, :] = v.astype(BF)
                else:
                    OUT[r, :] = v.astype(BF)
            if slot == 2: keep(OUT, o_out)
        return run

    def context_in():
        for k, (dx, dc) in enumerate(((0, 1), (1, 0), (1, 1))):
            tx = (p.x + dx) % 2; tc = (p.c + dc) % 2
            w = tx * 2 + tc
            pltpu.make_async_remote_copy(en.at[0, w], ctx.at[:, w], csem.at[k], crsem.at[w], device_id=p.dev(), device_id_type=MESH).wait_recv()

    class Ctx:
        def __getitem__(self, idx):
            if idx is Ellipsis: return ctx[...].reshape(256, 1024)
            return ctx[:, :, :, idx[1]].reshape(256, -1)
    cref = Ctx()
    def adapter():
        fetch(8).wait()
        w = wbuf[0, :, :, :, :, :, pl.ds(0, 512)].reshape(1024, 512)
        r = dot(yl[...], w)
        s = 1.0 / (1.0 + jnp.exp(-r))
        a = (r * s).astype(BF)
        ar[...] = a
        SR[...] = s * (1.0 + r * (1.0 - s))
        AT[...] = a.T
        keep(SR, o_sr); keep(AT, o_at)
    def adapter_out():
        top = wbuf[0, :, :, :, :, pl.ds(0, 16), pl.ds(512, 512)].reshape(512, 512)
        bot = wbuf[0, :, :, :, :, pl.ds(16, 16), pl.ds(512, 512)].reshape(512, 512)
        H[2, :, 0:512] = y[:, 0:512] + 4.0 * dot(ar[...], top)
        H[2, :, 512:1024] = y[:, 512:1024] + 4.0 * dot(ar[...], bot)
    def hidden(j, part):
        def run():
            t = 9 + j
            if part == 0: fetch(t).wait()
            @pl.loop(2 * part, 2 * part + 2)
            def _(n):
                ds = cols(n, 256)
                @pl.loop(0, 4)
                def _(m):
                    r = pl.ds(pl.multiple_of(m * 64, 64), 64)
                    u = dot(yl[r, :], wbuf[t % 4, :, :, :, :, :, ds].reshape(1024, 256))
                    half = 0.5 + 0.5 * lax.erf(u * 0.7071067811865476)
                    af[j, r, ds] = (u * half).astype(BF)
                    GP[j, r, ds] = half + u * (0.3989422804014327 * jnp.exp(-0.5 * u * u))
            if part == 1: keep(GP.at[j], o_gp.at[j])
        return run
    def out_cols(j):
        def run():
            fetch(13 + j).wait()
            acc = H[2, :, pl.ds(256 * j, 256)]
            for f in range(4):
                w = wo[j % 2, f].reshape(1024, 256)
                acc = acc + dot(af[f], w)
            H[2, :, pl.ds(256 * j, 256)] = acc
        return run

    E = lambda g: g * AG_GAP + 6 + 0.6
    add(1.4, flip(x, 0))
    g0 = E(0)
    for t in (0, 1, 2): add(g0, start(t))
    for t in (0, 1, 2): add(g0 + 0.2 * t, proj(x, t, t))
    for part in range(4): add(g0 + 0.8 + 0.25 * part, attend(0, part))
    add(g0 + 1.8, flip(mix, 3))
    g1 = E(1)
    add(1.6, context_in); add(1.7, flip(cref, 1))
    for t in (3, 4, 5): add(g1, start(t))
    add(g1 + 0.1, branch(3, x, 0)); add(g1 + 0.2, norm(0)); add(g1 + 0.3, flip(yl, 2))
    add(g1 + 0.5, proj(cref, 4, 4)); add(g1 + 0.7, proj(cref, 5, 5))
    g2 = E(2)
    for t in (6, 7): add(g2, start(t))
    add(g2 + 0.01, start(8))
    add(g2 + 0.1, proj(yl, 6, 3))
    for part in range(4): add(g2 + 0.3 + 0.25 * part, attend(1, part))
    add(g2 + 1.3, flip(mix, 4)); add(g2 + 1.4, branch(7, y, 1)); add(g2 + 1.5, norm(1)); add(g2 + 1.6, flip(yl, 5))
    add(g2 + 1.7, adapter); add(g2 + 1.8, adapter_out)
    g3 = max(E(3), g2 + 1.9)
    for t in (9, 10, 11): add(g3, start(t))
    for j in range(3):
        for part in range(2): add(g3 + 0.1 + 0.3 * j + 0.15 * part, hidden(j, part))
    g4 = max(E(4), g3 + 1.1)
    add(g4, start(12)); add(g4, start(13)); add(g4, start(14))
    for part in range(2): add(g4 + 0.1 + 0.2 * part, hidden(3, part))
    add(g4 + 0.5, out_cols(0)); add(g4 + 0.7, out_cols(1))
    g5 = max(E(5), g4 + 0.9)
    add(g5, start(15)); add(g5 + 0.01, out_cols(2)); add(g5 + 0.02, start(16)); add(g5 + 0.03, out_cols(3)); add(g5 + 0.04, norm(2))
    items.sort(key=lambda q: q[:2])
    for it in items: it[2]()
    for _, _, s in streams: s.finish()
    for c_ in cs: c_.wait_send()
    for c_ in outs: c_.wait()

def forward(tokens, gains, bias, shards, encoder):
    any_ = pl.BlockSpec(memory_space=pl.ANY)
    vm = pl.BlockSpec(memory_space=pltpu.VMEM)
    V, S, D = pltpu.VMEM, jax.ShapeDtypeStruct, pltpu.SemaphoreType.DMA
    tile = (4, 2, 2, 2, 32, 1024)
    return pl.pallas_call(forward_kernel,
        out_shape=(S((13,) + tile, BF), S((4, 2, 2, 2, 128, 1024), BF), S((6, 256, 1024), BF), S((2, 16, 256, 128), F32), S((3, 256, 1024), F32),
                   S((6, 1024, 256), BF), S((512, 256), BF), S((4, 256, 1024), F32), S((256, 512), F32), S((256, 1024), BF)),
        in_specs=[vm] * 3 + [any_] * 9, out_specs=(any_,) * 10,
        scratch_shapes=[V((6, 256, 1024), BF), V((2, 16, 256, 128), F32), V((3, 256, 1024), F32), V((6, 1024, 256), BF), V((512, 256), BF),
                        V((4, 256, 1024), F32), V((256, 512), F32), V((256, 1024), BF), V((2, 4, 32, 1024), BF), V((4,) + tile, BF),
                        V((2, 4, 2, 2, 2, 128, 256), BF), V((13, 32, 1024), BF), V((128, 1024), BF), V((256, 1024), F32), V((256, 1024), BF),
                        V((256, 1024), BF), V((4, 256, 1024), BF), V((256, 512), BF),
                        D((N_STREAM, NSEND)), D((N_STREAM, NSLOT)), D((20,)), D((3,)), D((4,)), D((17,)), D((26,))],
        compiler_params=pltpu.CompilerParams(collective_id=0, has_side_effects=True, vmem_limit_bytes=60 << 20),
        name="forward")(tokens, gains, bias, *shards, encoder)


NT = 9
ORDERS = ["A", "xzy", "yzx"] * 3
RS_GAP = 0.5
ROW = 1024

class Reduce:
    def __init__(self, p, t, order, PB, L0, L1, L2, UP, DN, LX, ssem, rsem, out):
        self.p, self.t, self.order = p, t, order
        self.PB, self.L0, self.L1, self.L2, self.UP, self.DN, self.LX = PB, L0, L1, L2, UP, DN, LX
        self.ssem, self.rsem, self.out = ssem, rsem, out
        self.ns = 0; self.sends = []
    def copy(self, src, dst, slot, target, guard=None):
        k = self.ns; self.ns += 1
        cp = pltpu.make_async_remote_copy(src, dst, self.ssem.at[k], self.rsem.at[slot], device_id=target, device_id_type=MESH)
        if guard is None: cp.start()
        else: pl.when(guard)(cp.start)
        self.sends.append((cp, guard))
    def arrive(self, dst, slot):
        pltpu.make_async_remote_copy(dst, dst, self.ssem.at[0], self.rsem.at[slot], device_id=self.p.dev(), device_id_type=MESH).wait_recv()
    def finish(self):
        for cp, guard in self.sends:
            if guard is None: cp.wait_send()
            else: pl.when(guard)(cp.wait_send)
    def sib(self, zz):
        p = self.p
        self.copy(self.PB.at[zz, :, :, 1 - p.c], self.L0.at[zz], zz, p.dev(c=1 - p.c))
    def merge(self, zz):
        p = self.p
        self.arrive(self.L0.at[zz], zz)
        for yy in range(2):
            for xx in range(2):
                self.PB[zz, yy, xx, p.c] = self.PB[zz, yy, xx, p.c] + self.L0[zz, yy, xx]
    def pair(self, ref, zz, b2name, b2v, r=None):
        if b2name == "y": return ref.at[zz, b2v, :, self.p.c] if r is None else ref.at[zz, b2v, :, self.p.c, r]
        return ref.at[zz, :, b2v, self.p.c] if r is None else ref.at[zz, :, b2v, self.p.c, r]

    def phases(self):
        return self.phases_c() if self.order != "A" else self.phases_a()

    def phases_c(self):
        p = self.p
        b1, b2 = self.order[0], self.order[2]
        me = {"x": p.x, "y": p.y}
        part1 = p.dev(**{b1: 1 - me[b1]}); part2 = p.dev(**{b2: 1 - me[b2]})
        own = lambda zz: self.pair(self.PB, zz, b2, me[b2])
        def R1():
            for zz in range(4):
                self.merge(zz)
                self.copy(self.pair(self.PB, zz, b2, 1 - me[b2]), self.L1.at[zz], 4 + zz, part2)
        def R2():
            for zz in range(4):
                self.arrive(self.L1.at[zz], 4 + zz)
                o = own(zz)
                o[...] = o[...] + self.L1[zz]
        def hop(zu, zd):
            def up_add():
                self.arrive(self.UP.at[zu], 8 + zu)
                o = own(zu); o[...] = o[...] + self.UP[zu]
            pl.when((p.z < zu) & (p.z > 0))(up_add)
            self.copy(own(zu), self.UP.at[zu], 8 + zu, p.dev(z=p.up), p.z < zu)
            def dn_add():
                self.arrive(self.DN.at[zd], 12 + zd)
                o = own(zd); o[...] = o[...] + self.DN[zd]
            pl.when((p.z > zd) & (p.z < 3))(dn_add)
            self.copy(own(zd), self.DN.at[zd], 12 + zd, p.dev(z=p.down), p.z > zd)
        def Z3():
            o = own(p.z)
            @pl.when(p.z > 0)
            def _():
                self.arrive(self.UP.at[p.z], 8 + p.z)
                o[...] = o[...] + self.UP[p.z]
            @pl.when(p.z < 3)
            def _():
                self.arrive(self.DN.at[p.z], 12 + p.z)
                o[...] = o[...] + self.DN[p.z]
            ob1 = dict(me); ob1[b1] = 1 - me[b1]
            self.copy(self.PB.at[p.z, ob1["y"], ob1["x"], p.c], self.LX, 16, part1)
        def FIN():
            self.arrive(self.LX, 16)
            v = self.PB[p.z, p.y, p.x, p.c].astype(jnp.float32) + self.LX[...].astype(jnp.float32)
            self.out(v)
        return dict(R1=R1, R2=R2, Z0=lambda: hop(3, 0), Z1=lambda: hop(2, 1), Z2=lambda: hop(1, 2), Z3=Z3, FIN=FIN)

    def phases_a(self):
        p = self.p
        me = {"x": p.x, "y": p.y}
        halves = []
        for h, (b1, b2) in enumerate((("x", "y"), ("y", "x"))):
            r = pl.ds(16 * h, 16)
            halves.append((h, b1, b2, r, p.dev(**{b1: 1 - me[b1]}), p.dev(**{b2: 1 - me[b2]})))
        def at(zz, b1, b1v, r):
            d = dict(me); d[b1] = b1v
            return self.PB.at[zz, d["y"], d["x"], p.c, r]
        def R1():
            for zz in range(4):
                self.merge(zz)
                for h, b1, b2, r, part1, part2 in halves:
                    self.copy(self.pair(self.PB, zz, b2, 1 - me[b2], r), self.L1.at[zz, :, r], 17 + 4 * h + zz, part2)
        def R2():
            for zz in range(4):
                for h, b1, b2, r, part1, part2 in halves:
                    self.arrive(self.L1.at[zz, :, r], 17 + 4 * h + zz)
                    o = self.pair(self.PB, zz, b2, me[b2], r)
                    o[...] = o[...] + self.L1[zz, :, r]
                    self.copy(at(zz, b1, 1 - me[b1], r), self.L2.at[zz, r], 25 + 4 * h + zz, part1)
        def R3():
            for zz in range(4):
                for h, b1, b2, r, part1, part2 in halves:
                    self.arrive(self.L2.at[zz, r], 25 + 4 * h + zz)
                    o = at(zz, b1, me[b1], r)
                    o[...] = o[...] + self.L2[zz, r]
        blk = lambda zz: self.PB.at[zz, p.y, p.x, p.c]
        def hop(zu, zd):
            def up_add():
                self.arrive(self.UP.at[zu, 0], 8 + zu)
                o = blk(zu); o[...] = o[...] + self.UP[zu, 0]
            pl.when((p.z < zu) & (p.z > 0))(up_add)
            self.copy(blk(zu), self.UP.at[zu, 0], 8 + zu, p.dev(z=p.up), p.z < zu)
            def dn_add():
                self.arrive(self.DN.at[zd, 0], 12 + zd)
                o = blk(zd); o[...] = o[...] + self.DN[zd, 0]
            pl.when((p.z > zd) & (p.z < 3))(dn_add)
            self.copy(blk(zd), self.DN.at[zd, 0], 12 + zd, p.dev(z=p.down), p.z > zd)
        def FIN():
            o = blk(p.z)
            @pl.when(p.z > 0)
            def _():
                self.arrive(self.UP.at[p.z, 0], 8 + p.z)
                o[...] = o[...] + self.UP[p.z, 0]
            @pl.when(p.z < 3)
            def _():
                self.arrive(self.DN.at[p.z, 0], 12 + p.z)
                o[...] = o[...] + self.DN[p.z, 0]
            self.out(o[...].astype(jnp.float32))
        return dict(R1=R1, R2=R2, Z3=R3, Z0=lambda: hop(3, 0), Z1=lambda: hop(2, 1), Z2=lambda: hop(1, 2), FIN=FIN)

NS, NR = 32, 33
OFF_C = dict(LD=0, R1=1, R2=2, Z0=3, Z1=3.4, Z2=3.8, Z3=4.4, FIN=6)
OFF_A = dict(LD=0, R1=1, R2=2, Z3=3, Z0=4, Z1=4.4, Z2=4.8, FIN=6)

def scatter_kernel(*refs):
    g = refs[:9]; gctx = refs[9]
    osp, oso, ocp, oco, oai, oao, oen = refs[10:17]
    PB, L0, L1, L2, UP, DN, LX, ssem, rsem, lsem, csem, crsem = refs[17:]
    p = Place()
    loads = []
    for t in range(NT):
        cp = pltpu.make_async_copy(g[t], PB.at[t], lsem.at[t]); cp.start(); loads.append(cp)
    entry_barrier(p)
    me = p.x * 2 + p.c
    cs = []
    for k, (dx, dc) in enumerate(((0, 1), (1, 0), (1, 1))):
        tx = (p.x + dx) % 2; tc = (p.c + dc) % 2
        w = tx * 2 + tc
        c_ = pltpu.make_async_remote_copy(gctx.at[:, w], oen.at[0, me], csem.at[k], crsem.at[me], device_id=p.dev(x=tx, c=tc), device_id_type=MESH)
        c_.start(); cs.append(c_)
    lc = pltpu.make_async_copy(gctx.at[:, me], oen.at[0, me], lsem.at[9]); lc.start()
    def o_ad(v):
        oai[...] = v[:, :512]
        oao[:, 0:512] = v[0:16, 512:]
        oao[:, 512:1024] = v[16:32, 512:]
    def put(ref, j=None):
        def f(v):
            if j is None: ref[...] = v
            else: ref[j] = v
        return f
    outs = [o_ad, put(oco), put(ocp, 1), put(ocp, 2), put(ocp, 0), put(oso), put(osp, 1), put(osp, 2), put(osp, 0)]
    items = []
    reds = []
    for t in range(NT):
        r = Reduce(p, t, ORDERS[t], PB.at[t], L0.at[t], L1.at[t], L2.at[t], UP.at[t], DN.at[t], LX.at[t], ssem.at[t], rsem.at[t], outs[t])
        reds.append(r)
        ph = r.phases()
        def LD(t=t, r=r):
            loads[t].wait()
            for zz in range(4): r.sib(zz)
        ph["LD"] = LD
        for name, off in (OFF_A if ORDERS[t] == "A" else OFF_C).items():
            items.append((t * RS_GAP + off, t, len(items), ph[name]))
    items.sort(key=lambda q: q[:3])
    for it in items: it[3]()
    for r in reds: r.finish()
    lc.wait()
    for c_ in cs: c_.wait_send()
    for k, (dx, dc) in enumerate(((0, 1), (1, 0), (1, 1))):
        tx = (p.x + dx) % 2; tc = (p.c + dc) % 2
        w = tx * 2 + tc
        pltpu.make_async_remote_copy(gctx.at[:, w], oen.at[0, w], csem.at[k], crsem.at[w], device_id=p.dev(), device_id_type=MESH).wait_recv()

def scatter(tiles, gctx):
    any_ = pl.BlockSpec(memory_space=pl.ANY)
    vm = pl.BlockSpec(memory_space=pltpu.VMEM)
    f32, bf = jnp.float32, jnp.bfloat16
    return pl.pallas_call(scatter_kernel,
        out_shape=(jax.ShapeDtypeStruct((3, 32, 1024), f32), jax.ShapeDtypeStruct((32, 1024), f32), jax.ShapeDtypeStruct((3, 32, 1024), f32), jax.ShapeDtypeStruct((32, 1024), f32), jax.ShapeDtypeStruct((32, 512), f32), jax.ShapeDtypeStruct((16, 1024), f32), jax.ShapeDtypeStruct((1, 4, 2, 32, 1024), bf)),
        in_specs=[any_] * 10, out_specs=(vm,) * 6 + (any_,),
        scratch_shapes=[pltpu.VMEM((NT, 4, 2, 2, 2, 32, ROW), bf), pltpu.VMEM((NT, 4, 2, 2, 32, ROW), bf), pltpu.VMEM((NT, 4, 2, 32, ROW), bf), pltpu.VMEM((NT, 4, 32, ROW), bf),
                        pltpu.VMEM((NT, 4, 2, 32, ROW), bf), pltpu.VMEM((NT, 4, 2, 32, ROW), bf), pltpu.VMEM((NT, 32, ROW), bf),
                        pltpu.SemaphoreType.DMA((NT, NS)), pltpu.SemaphoreType.DMA((NT, NR)), pltpu.SemaphoreType.DMA((10,)), pltpu.SemaphoreType.DMA((3,)), pltpu.SemaphoreType.DMA((4,))],
        compiler_params=pltpu.CompilerParams(collective_id=1, has_side_effects=True, vmem_limit_bytes=62 << 20),
        name="scatter")(*tiles, gctx)


def device_program(tokens, encoder, dec_lengths, enc_lengths, gains, self_proj, self_out, cross_proj, cross_out, ffn_in, ffn_out, adapt_in, adapt_out, cotangent):
    bf = jnp.bfloat16
    masks = [slot_masks(dec_lengths[m], enc_lengths[m], 128) for m in range(2)]
    bias = jnp.where(jnp.stack([jnp.stack([masks[u][a] for u in range(2)]) for a in range(2)]), 0.0, NEGATIVE)
    buf, gfo, qkv, pp, hh, tt, at, gp, sr, layer_out = forward(tokens, gains, bias, (self_proj, self_out, cross_proj, cross_out, ffn_in, ffn_out, adapt_in, adapt_out), encoder)
    w = lambda t: buf[t].reshape(1024, 1024)
    wq1, wk1, wv1, wso, wk2, wv2, wq2, wco = (w(t) for t in range(8))
    ad = buf[8].reshape(32, 32, 1024)
    wai = ad[:, :, :512].reshape(1024, 512)
    wao = jnp.concatenate([ad[:, :16, 512:].reshape(512, 512), ad[:, 16:, 512:].reshape(512, 512)], axis=1)
    wfi = [w(9 + j) for j in range(4)]
    wfo = gfo.reshape(4096, 1024)
    r16 = lambda v: v.astype(bf)
    sq, sk, sv, cq, ck, cv = (qkv[j] for j in range(6))
    p1, p2 = (pp[a].reshape(2, 8, 2, 128, 128).reshape(2, 16, 128, 128) for a in range(2))
    h1, h2, h3 = (hh[j] for j in range(3))
    xT, cT, y1T, m1T, m2T, y2T = (tt[j] for j in range(6))
    gu_ = jnp.concatenate([gp[j] for j in range(4)], axis=1)
    g3 = norm_back(h3, gains[2], cotangent.astype(jnp.float32))
    gb = r16(g3)
    gu = r16(gu_ * matmul_nt(gb, wfo))
    gr = r16(sr * (matmul_nt(gb, wao) * 4.0))
    dao = matmul(at, gb) * 4.0
    dai = matmul(y2T, gr)
    gy2 = g3 + matmul_nt(gr, wai)
    for j in range(4):
        gy2 = gy2 + matmul_nt(gu[:, 1024 * j:1024 * j + 1024], wfi[j])
    g2 = norm_back(h2, gains[1], gy2)
    gc2 = r16(g2)
    dco = matmul(m2T, gc2)
    gx2 = r16(matmul_nt(gc2, wco))
    gq2, gk2, gv2 = attend_back2(gx2, cq, ck, cv, p2)
    dq2 = matmul(y1T, gq2); dk2 = matmul(cT, gk2); dv2 = matmul(cT, gv2)
    gctx = r16(matmul_nt(gk2, wk2) + matmul_nt(gv2, wv2)).reshape(2, 4, 32, 1024)
    gy1 = g2 + matmul_nt(gq2, wq2)
    g1 = norm_back(h1, gains[0], gy1)
    gc1 = r16(g1)
    dso = matmul(m1T, gc1)
    gx1 = r16(matmul_nt(gc1, wso))
    gq1, gk1, gv1 = attend_back2(gx1, sq, sk, sv, p1)
    dq1, dk1, dv1 = (matmul(xT, g) for g in (gq1, gk1, gv1))
    gtok = r16(g1 + matmul_nt(gq1, wq1) + matmul_nt(gk1, wk1) + matmul_nt(gv1, wv1))
    dad = jnp.concatenate([dai, dao.reshape(32, 16, 2, 512).transpose(0, 2, 1, 3).reshape(1024, 512)], axis=1)
    tiles = [r16(v).reshape(4, 2, 2, 2, 32, 1024) for v in (dad, dco, dk2, dv2, dq2, dso, dk1, dv1, dq1)]
    osp, oso, ocp, oco, oai, oao, oen = scatter(tiles, gctx)
    return (layer_out, gtok, oen, osp, oso, ocp, oco, oai, oao)


def heads(m):
    return m.reshape(2, 128, HEADS, 64)


def attend2(q, k, v, allowed):
    s = jnp.einsum("uqhd,ukhd->uhqk", heads(q), heads(k), preferred_element_type=jnp.float32) * 0.125
    s = jnp.where(allowed[:, None], s, NEGATIVE)
    e = jnp.exp(s - jnp.max(s, axis=-1, keepdims=True))
    p = e / jnp.sum(e, axis=-1, keepdims=True)
    mixed = jnp.einsum("uhqk,ukhd->uqhd", p.astype(jnp.bfloat16), heads(v), preferred_element_type=jnp.float32)
    return mixed.reshape(q.shape).astype(jnp.bfloat16), p


def attend_back2(g, q, k, v, p):
    gh = heads(g)
    dp = jnp.einsum("uqhd,ukhd->uhqk", gh, heads(v), preferred_element_type=jnp.float32)
    ds = (p * (dp - jnp.sum(p * dp, axis=-1, keepdims=True))).astype(jnp.bfloat16)
    dq = jnp.einsum("uhqk,ukhd->uqhd", ds, heads(k), preferred_element_type=jnp.float32) * 0.125
    dk = jnp.einsum("uhqk,uqhd->ukhd", ds, heads(q), preferred_element_type=jnp.float32) * 0.125
    dv = jnp.einsum("uhqk,uqhd->ukhd", p.astype(jnp.bfloat16), gh, preferred_element_type=jnp.float32)
    return tuple(t.reshape(q.shape).astype(jnp.bfloat16) for t in (dq, dk, dv))


def solution(mesh):
    in_specs = (
        P(("seq", "enc"), None),
        P("seq", None, None, "enc", None),
        P(("seq", "enc"), None),
        P(("seq", "enc"), None),
        P(),
        P(None, ("seq", "enc"), None),
        P(("seq", "enc"), None),
        P(None, ("seq", "enc"), None),
        P(("seq", "enc"), None),
        P(("seq", "enc"), None),
        P(("seq", "enc"), None),
        P(("seq", "enc"), None),
        P(("seq", "enc"), None),
        P(("seq", "enc"), None),
    )
    out_specs = (
        P(("seq", "enc"), None),
        P(("seq", "enc"), None),
        P("seq", None, None, "enc", None),
        P(None, ("seq", "enc"), None),
        P(("seq", "enc"), None),
        P(None, ("seq", "enc"), None),
        P(("seq", "enc"), None),
        P(("seq", "enc"), None),
        P(("seq", "enc"), None),
    )
    fast = (mesh.shape["seq"], mesh.shape["enc"]) == (8, 4)
    return jax.shard_map(
        device_program if fast else per_device, mesh=mesh, in_specs=in_specs, out_specs=out_specs, check_vma=False
    )
```

```python
import jax
import jax.numpy as jnp
from jax import lax
from jax.experimental import pallas as pl
from jax.experimental.pallas import tpu as pltpu
from jax.sharding import PartitionSpec as P

HEADS = 16
ADAPT = 512
MICRO = 2


EPSILON = 1e-05
NEGATIVE = -1e30


def matmul(left, right):
    return jnp.dot(left, right, preferred_element_type=jnp.float32)


def matmul_tn(left, right):
    return lax.dot_general(
        left, right, (((0,), (0,)), ((), ())), preferred_element_type=jnp.float32
    )


def matmul_nt(left, right):
    return lax.dot_general(
        left, right, (((1,), (1,)), ((), ())), preferred_element_type=jnp.float32
    )


def layer_norm(hidden, gain):
    center = hidden - jnp.mean(hidden, axis=-1, keepdims=True)
    spread = jnp.mean(center * center, axis=-1, keepdims=True)
    return center * lax.rsqrt(spread + EPSILON) * gain


def norm_back(hidden, gain, grad_out):
    _, pullback = jax.vjp(lambda value: layer_norm(value, gain), hidden)
    return pullback(grad_out)[0]


def gelu_exact(value):
    return jax.nn.gelu(value, approximate=False)


def slot_masks(dec_row, enc_row, rows):
    half_rows = rows // 2
    places = lax.broadcasted_iota(jnp.int32, (rows,), 0)
    paired = dec_row[1] > 0
    second = jnp.logical_and(paired, places >= half_rows)
    anchor = jnp.where(second, half_rows, 0).astype(jnp.int32)
    dec_valid = jnp.where(second, dec_row[1], dec_row[0])
    enc_valid = jnp.where(second, enc_row[1], enc_row[0])
    key_live = places - anchor < dec_valid
    context_live = places - anchor < enc_valid
    same_slot = second[:, None] == second[None, :]
    causal = places[None, :] <= places[:, None]
    self_mask = same_slot & causal & key_live[None, :]
    cross_mask = same_slot & context_live[None, :]
    return (self_mask, cross_mask)


def split_heads(matrix):
    return matrix.reshape(matrix.shape[0], HEADS, matrix.shape[1] // HEADS)


def attend(queries, keys, values, allowed):
    depth = queries.shape[1] // HEADS
    scores = jnp.einsum(
        "qhd,khd->hqk", split_heads(queries), split_heads(keys), preferred_element_type=jnp.float32
    ) * float(depth) ** (-0.5)
    masked = jnp.where(allowed[None], scores, NEGATIVE)
    weights = jnp.exp(masked - jnp.max(masked, axis=-1, keepdims=True))
    probs = weights / jnp.sum(weights, axis=-1, keepdims=True)
    mixed = jnp.einsum(
        "hqk,khd->qhd",
        probs.astype(jnp.bfloat16),
        split_heads(values),
        preferred_element_type=jnp.float32,
    )
    return (mixed.reshape(queries.shape).astype(jnp.bfloat16), probs)


def attend_back(grad_mixed, queries, keys, values, probs):
    depth = queries.shape[1] // HEADS
    factor = float(depth) ** (-0.5)
    grad_heads = split_heads(grad_mixed)
    grad_probs = jnp.einsum(
        "qhd,khd->hqk", grad_heads, split_heads(values), preferred_element_type=jnp.float32
    )
    inner = jnp.sum(probs * grad_probs, axis=-1, keepdims=True)
    grad_scores = (probs * (grad_probs - inner)).astype(jnp.bfloat16)
    grad_query = (
        jnp.einsum(
            "hqk,khd->qhd", grad_scores, split_heads(keys), preferred_element_type=jnp.float32
        )
        * factor
    )
    grad_key = (
        jnp.einsum(
            "hqk,qhd->khd", grad_scores, split_heads(queries), preferred_element_type=jnp.float32
        )
        * factor
    )
    grad_value = jnp.einsum(
        "hqk,qhd->khd", probs.astype(jnp.bfloat16), grad_heads, preferred_element_type=jnp.float32
    )
    return (
        grad_query.reshape(queries.shape).astype(jnp.bfloat16),
        grad_key.reshape(keys.shape).astype(jnp.bfloat16),
        grad_value.reshape(values.shape).astype(jnp.bfloat16),
    )


def per_device(
    tokens,
    encoder,
    dec_lengths,
    enc_lengths,
    gains,
    self_proj,
    self_out,
    cross_proj,
    cross_out,
    ffn_in,
    ffn_out,
    adapt_in,
    adapt_out,
    cotangent,
):
    shards = (self_proj, self_out, cross_proj, cross_out, ffn_in, ffn_out, adapt_in, adapt_out)

    def obtain():
        return (
            lax.all_gather(shards[0], ("seq", "enc"), axis=1, tiled=True),
            lax.all_gather(shards[1], ("seq", "enc"), axis=0, tiled=True),
            lax.all_gather(shards[2], ("seq", "enc"), axis=1, tiled=True),
            lax.all_gather(shards[3], ("seq", "enc"), axis=0, tiled=True),
            lax.all_gather(shards[4], ("seq", "enc"), axis=0, tiled=True),
            lax.all_gather(shards[5], ("seq", "enc"), axis=0, tiled=True),
            lax.all_gather(shards[6], ("seq", "enc"), axis=0, tiled=True),
            lax.all_gather(shards[7], ("seq", "enc"), axis=0, tiled=True),
        )

    rows = tokens.shape[0] // MICRO
    width = tokens.shape[1]
    owner = lax.axis_index("enc")
    acc_self = jnp.zeros((width, 3, width), jnp.float32)
    acc_self_out = jnp.zeros((width, width), jnp.float32)
    acc_cross = jnp.zeros((width, 3, width), jnp.float32)
    acc_cross_out = jnp.zeros((width, width), jnp.float32)
    acc_adapt_in = jnp.zeros((width, ADAPT), jnp.float32)
    acc_adapt_out = jnp.zeros((ADAPT, width), jnp.float32)
    outputs = []
    grad_rows = []
    grad_contexts = []
    for micro_index in range(MICRO):
        w_self, w_self_out, w_cross, w_cross_out, w_ffn_in, w_ffn_out, w_adapt_in, w_adapt_out = (
            obtain()
        )
        lower = micro_index * rows
        token_rows = tokens[lower : lower + rows]
        self_mask, cross_mask = slot_masks(dec_lengths[micro_index], enc_lengths[micro_index], rows)
        pieces = encoder[0, :, micro_index]
        context = lax.dynamic_index_in_dim(
            lax.all_gather(pieces, "enc", axis=1, tiled=True), owner, 0, keepdims=False
        )
        self_query = matmul(token_rows, w_self[0]).astype(jnp.bfloat16)
        self_key = matmul(token_rows, w_self[1]).astype(jnp.bfloat16)
        self_value = matmul(token_rows, w_self[2]).astype(jnp.bfloat16)
        self_mix, self_probs = attend(self_query, self_key, self_value, self_mask)
        first_sum = token_rows.astype(jnp.float32) + matmul(self_mix, w_self_out)
        first_norm = layer_norm(first_sum, gains[0])
        first_low = first_norm.astype(jnp.bfloat16)
        cross_query = matmul(first_low, w_cross[0]).astype(jnp.bfloat16)
        cross_key = matmul(context, w_cross[1]).astype(jnp.bfloat16)
        cross_value = matmul(context, w_cross[2]).astype(jnp.bfloat16)
        cross_mix, cross_probs = attend(cross_query, cross_key, cross_value, cross_mask)
        second_sum = first_norm + matmul(cross_mix, w_cross_out)
        second_norm = layer_norm(second_sum, gains[1])
        second_low = second_norm.astype(jnp.bfloat16)
        ffn_pre = matmul(second_low, w_ffn_in)
        ffn_act = gelu_exact(ffn_pre).astype(jnp.bfloat16)
        adapt_pre = matmul(second_low, w_adapt_in)
        adapt_act = jax.nn.silu(adapt_pre).astype(jnp.bfloat16)
        third_sum = second_norm + matmul(ffn_act, w_ffn_out) + 4.0 * matmul(adapt_act, w_adapt_out)
        outputs.append(layer_norm(third_sum, gains[2]).astype(jnp.bfloat16))
        w_self, w_self_out, w_cross, w_cross_out, w_ffn_in, w_ffn_out, w_adapt_in, w_adapt_out = (
            obtain()
        )
        grad_third = norm_back(
            third_sum, gains[2], cotangent[lower : lower + rows].astype(jnp.float32)
        )
        grad_branch = grad_third.astype(jnp.bfloat16)
        _, gelu_pull = jax.vjp(gelu_exact, ffn_pre)
        grad_ffn_pre = gelu_pull(matmul_nt(grad_branch, w_ffn_out))[0].astype(jnp.bfloat16)
        grad_adapt_act = matmul_nt(grad_branch, w_adapt_out) * 4.0
        _, silu_pull = jax.vjp(jax.nn.silu, adapt_pre)
        grad_adapt_pre = silu_pull(grad_adapt_act)[0].astype(jnp.bfloat16)
        acc_adapt_out = acc_adapt_out + matmul_tn(adapt_act, grad_branch) * 4.0
        acc_adapt_in = acc_adapt_in + matmul_tn(second_low, grad_adapt_pre)
        grad_second = (
            grad_third + matmul_nt(grad_ffn_pre, w_ffn_in) + matmul_nt(grad_adapt_pre, w_adapt_in)
        )
        grad_second_sum = norm_back(second_sum, gains[1], grad_second)
        grad_cross_branch = grad_second_sum.astype(jnp.bfloat16)
        acc_cross_out = acc_cross_out + matmul_tn(cross_mix, grad_cross_branch)
        grad_cross_mix = matmul_nt(grad_cross_branch, w_cross_out).astype(jnp.bfloat16)
        grad_cq, grad_ck, grad_cv = attend_back(
            grad_cross_mix, cross_query, cross_key, cross_value, cross_probs
        )
        acc_cross = acc_cross + jnp.stack(
            [
                matmul_tn(first_low, grad_cq),
                matmul_tn(context, grad_ck),
                matmul_tn(context, grad_cv),
            ],
            axis=1,
        )
        grad_context = matmul_nt(grad_ck, w_cross[1]) + matmul_nt(grad_cv, w_cross[2])
        holder = jnp.zeros((lax.axis_size("enc"),) + grad_context.shape, jnp.float32)
        holder = lax.dynamic_update_index_in_dim(holder, grad_context, owner, 0)
        returned = lax.psum_scatter(
            holder.astype(jnp.bfloat16), "enc", scatter_dimension=1, tiled=True
        )
        grad_contexts.append(returned)
        grad_first = grad_second_sum + matmul_nt(grad_cq, w_cross[0])
        grad_first_sum = norm_back(first_sum, gains[0], grad_first)
        grad_self_branch = grad_first_sum.astype(jnp.bfloat16)
        acc_self_out = acc_self_out + matmul_tn(self_mix, grad_self_branch)
        grad_self_mix = matmul_nt(grad_self_branch, w_self_out).astype(jnp.bfloat16)
        grad_sq, grad_sk, grad_sv = attend_back(
            grad_self_mix, self_query, self_key, self_value, self_probs
        )
        acc_self = acc_self + jnp.stack(
            [
                matmul_tn(token_rows, grad_sq),
                matmul_tn(token_rows, grad_sk),
                matmul_tn(token_rows, grad_sv),
            ],
            axis=1,
        )
        grad_input = (
            grad_first_sum
            + matmul_nt(grad_sq, w_self[0])
            + matmul_nt(grad_sk, w_self[1])
            + matmul_nt(grad_sv, w_self[2])
        )
        grad_rows.append(grad_input.astype(jnp.bfloat16))
    summed = (
        lax.psum_scatter(acc_self, ("seq", "enc"), scatter_dimension=0, tiled=True),
        lax.psum_scatter(acc_self_out, ("seq", "enc"), scatter_dimension=0, tiled=True),
        lax.psum_scatter(acc_cross, ("seq", "enc"), scatter_dimension=0, tiled=True),
        lax.psum_scatter(acc_cross_out, ("seq", "enc"), scatter_dimension=0, tiled=True),
        lax.psum_scatter(acc_adapt_in, ("seq", "enc"), scatter_dimension=0, tiled=True),
        lax.psum_scatter(acc_adapt_out, ("seq", "enc"), scatter_dimension=0, tiled=True),
    )
    layer_out = jnp.concatenate(outputs, axis=0)
    grad_tokens = jnp.concatenate(grad_rows, axis=0)
    grad_encoder = jnp.stack(grad_contexts, axis=1)[None]
    grad_self_proj = jnp.transpose(summed[0], (1, 0, 2))
    grad_cross_proj = jnp.transpose(summed[2], (1, 0, 2))
    return (
        layer_out,
        grad_tokens,
        grad_encoder,
        grad_self_proj,
        summed[1],
        grad_cross_proj,
        summed[3],
        summed[4],
        summed[5],
    )


MESH = pl.DeviceIdType.MESH
GAP = 2

TILES = ["q1", "k1", "v1", "so", "k2", "v2", "q2", "co", "ad", "f0", "f1", "f2", "f3", "o0", "o1", "o2", "o3"]

class Place:
    def __init__(self):
        seq, enc = lax.axis_index("seq"), lax.axis_index("enc")
        self.z, self.y, self.x, self.c = seq // 2, seq % 2, enc // 2, enc % 2
        self.up, self.down = jnp.minimum(self.z + 1, 3), jnp.maximum(self.z - 1, 0)
    def dev(self, z=None, y=None, x=None, c=None):
        z = self.z if z is None else z
        y = self.y if y is None else y
        x = self.x if x is None else x
        c = self.c if c is None else c
        return (z * 2 + y, x * 2 + c)

def entry_barrier(p):
    bar = pltpu.get_barrier_semaphore()
    def sig(d):
        pl.semaphore_signal(bar, inc=1, device_id=d, device_id_type=MESH)
    sig(p.dev(c=1 - p.c)); sig(p.dev(x=1 - p.x)); sig(p.dev(y=1 - p.y)); sig(p.dev(x=1 - p.x, c=1 - p.c))
    @pl.when(p.z < 3)
    def _(): sig(p.dev(z=p.up))
    @pl.when(p.z > 0)
    def _(): sig(p.dev(z=p.down))
    peers = 4 + (p.z < 3).astype(jnp.int32) + (p.z > 0).astype(jnp.int32)
    pl.semaphore_wait(bar, peers)

ALL4 = pl.ds(0, 4)
ALL2 = pl.ds(0, 2)

class Stream:
    def __init__(self, p, view, order, ssem, rsem):
        self.p, self.view, self.order, self.ssem, self.rsem = p, view, order, ssem, rsem
        self.ns = 0
        self.sends = []

    def cut(self, z, y, x, c):
        return self.view(z, y, x, c)

    def copy(self, where, slot, target, guard=None):
        k = self.ns; self.ns += 1
        cp = pltpu.make_async_remote_copy(where, where, self.ssem.at[k], self.rsem.at[slot], device_id=target, device_id_type=MESH)
        if guard is None:
            cp.start()
        else:
            pl.when(guard)(cp.start)
        self.sends.append((cp, guard))

    def arrive(self, where, slot, guard=None):
        cp = pltpu.make_async_remote_copy(where, where, self.ssem.at[0], self.rsem.at[slot], device_id=self.p.dev(), device_id_type=MESH)
        if guard is None:
            cp.wait_recv()
        else:
            pl.when(guard)(cp.wait_recv)

    def finish(self):
        for cp, guard in self.sends:
            if guard is None:
                cp.wait_send()
            else:
                pl.when(guard)(cp.wait_send)

    def at(self, z, own):
        return self.cut(z, own["y"], own["x"], self.p.c)

    def phases(self):
        p = self.p
        if self.order[0] == "z":
            b1, b2 = self.order[1], self.order[2]
            me = {"x": p.x, "y": p.y}
            oth = {"x": 1 - p.x, "y": 1 - p.y}
            part1 = p.dev(**{b1: oth[b1]}); part2 = p.dev(**{b2: oth[b2]})
            sib = p.dev(c=1 - p.c)
            own = dict(me)
            b1o = dict(me); b1o[b1] = oth[b1]
            both = dict(me); both[b1] = ALL2
            allof = {"x": ALL2, "y": ALL2}
            def P0():
                self.copy(self.at(p.z, own), p.z, p.dev(z=p.up), p.z < 3)
                self.copy(self.at(p.z, own), p.z, p.dev(z=p.down), p.z > 0)
                self.copy(self.at(p.z, own), 4 + p.z, part1)
            def hop(t):
                lo, hi = jnp.maximum(p.z - t, 0), jnp.minimum(p.z + t, 3)
                below, above = p.z >= t, p.z + t <= 3
                self.arrive(self.at(lo, own), lo, below)
                if t < 3:
                    self.copy(self.at(lo, own), lo, p.dev(z=p.up), (below) & (p.z < 3))
                self.copy(self.at(lo, own), 4 + lo, part1, below)
                self.arrive(self.at(hi, own), hi, above)
                if t < 3:
                    self.copy(self.at(hi, own), hi, p.dev(z=p.down), (above) & (p.z > 0))
                self.copy(self.at(hi, own), 4 + hi, part1, above)
            def P4():
                for zz in range(4):
                    self.arrive(self.at(zz, b1o), 4 + zz)
                    self.copy(self.at(zz, both), 8 + zz, part2)
            def P5():
                self.copy(self.at(ALL4, both), 12, sib)
                for zz in range(4):
                    self.arrive(self.at(zz, both), 8 + zz)
                b2o = dict(both); b2o[b2] = oth[b2]
                self.copy(self.at(ALL4, b2o), 13, sib)
            def P6():
                b2o = dict(both); b2o[b2] = oth[b2]
                w = lambda s: self.cut(ALL4, s["y"], s["x"], 1 - p.c)
                self.arrive(w(both), 12)
                self.arrive(w(b2o), 13)
            return [P0, lambda: hop(1), lambda: hop(2), lambda: hop(3), P4, P5, P6]
        b1, b2 = self.order[0], self.order[2]
        me = {"x": p.x, "y": p.y}
        oth = {"x": 1 - p.x, "y": 1 - p.y}
        part1 = p.dev(**{b1: oth[b1]}); part2 = p.dev(**{b2: oth[b2]})
        sib = p.dev(c=1 - p.c)
        own = dict(me)
        b1o = dict(me); b1o[b1] = oth[b1]
        both = dict(me); both[b1] = ALL2
        b2o = dict(both); b2o[b2] = oth[b2]
        def P0():
            self.copy(self.at(p.z, own), 8, part1)
        def P1():
            self.arrive(self.at(p.z, b1o), 8)
            self.copy(self.at(p.z, both), p.z, p.dev(z=p.up), p.z < 3)
            self.copy(self.at(p.z, both), p.z, p.dev(z=p.down), p.z > 0)
            self.copy(self.at(p.z, both), 4 + p.z, part2)
        def hop(t):
            lo, hi = jnp.maximum(p.z - t, 0), jnp.minimum(p.z + t, 3)
            below, above = p.z >= t, p.z + t <= 3
            self.arrive(self.at(lo, both), lo, below)
            if t < 3:
                self.copy(self.at(lo, both), lo, p.dev(z=p.up), (below) & (p.z < 3))
            self.copy(self.at(lo, both), 4 + lo, part2, below)
            self.arrive(self.at(hi, both), hi, above)
            if t < 3:
                self.copy(self.at(hi, both), hi, p.dev(z=p.down), (above) & (p.z > 0))
            self.copy(self.at(hi, both), 4 + hi, part2, above)
        def P5():
            self.copy(self.at(ALL4, both), 12, sib)
            for zz in range(4):
                self.arrive(self.at(zz, b2o), 4 + zz)
            self.copy(self.at(ALL4, b2o), 13, sib)
        def P6():
            w = lambda s: self.cut(ALL4, s["y"], s["x"], 1 - p.c)
            self.arrive(w(both), 12)
            self.arrive(w(b2o), 13)
        return [P0, P1, lambda: hop(1), lambda: hop(2), lambda: hop(3), P5, P6]

F32, BF = jnp.float32, jnp.bfloat16
NSLOT, NSEND = 14, 19
N_STREAM = 23
EPS = 1e-05

def dot(a, b):
    return jnp.dot(a, b, preferred_element_type=F32)

def dot_nt(a, b):
    return lax.dot_general(a, b, (((1,), (1,)), ((), ())), preferred_element_type=F32)

def dot_tn(a, b):
    return lax.dot_general(a, b, (((0,), (0,)), ((), ())), preferred_element_type=F32)

def cols(n, width):
    return pl.ds(pl.multiple_of(n * width, width), width)

def norm_rows(h):
    center = h - jnp.mean(h, axis=-1, keepdims=True)
    spread = jnp.mean(center * center, axis=-1, keepdims=True)
    return center * lax.rsqrt(spread + EPS)

def half_masks():
    lane = lax.broadcasted_iota(jnp.int32, (1, 128), 1)
    lo = jnp.where(lane < 64, 1.0, 0.0)
    return lo.astype(BF), (1.0 - lo).astype(BF)

def pair_up(m, lo, hi):
    return jnp.concatenate([m * lo, m * hi], axis=0)

def side(m):
    return jnp.concatenate([m[:128], m[128:]], axis=1)

def forward_kernel(x, gains, bias, sp, so, cp, co, fi, fo, ai, ao, en,
                   buf, gfo, o_qkv, o_p, o_h, o_t, o_at, o_gp, o_sr, o_out,
                   qkv, P, H, T, AT, GP, SR, OUT, ctx, wbuf, wo, own, ownf, y, yl, mix, af, ar,
                   ssem, rsem, lsem, csem, crsem, wsem, osem):
    p = Place()
    loc = []
    def put(src, dst):
        c_ = pltpu.make_async_copy(src, dst, lsem.at[len(loc)]); c_.start(); loc.append(c_)
    for j, t in enumerate((0, 1, 2)): put(sp.at[j], own.at[t])
    put(so, own.at[3])
    for j, t in ((1, 4), (2, 5), (0, 6)): put(cp.at[j], own.at[t])
    put(co, own.at[7])
    put(ai, own.at[8, :, pl.ds(0, 512)])
    put(ao.at[:, pl.ds(0, 512)], own.at[8, pl.ds(0, 16), pl.ds(512, 512)])
    put(ao.at[:, pl.ds(512, 512)], own.at[8, pl.ds(16, 16), pl.ds(512, 512)])
    for j in range(4): put(fi.at[:, pl.ds(1024 * j, 1024)], own.at[9 + j])
    put(fo, ownf)
    me = p.x * 2 + p.c
    put(en.at[0, me], ctx.at[:, me])
    entry_barrier(p)
    for c_ in loc: c_.wait()
    n_in = len(loc)
    c1 = pltpu.make_async_copy(own, buf.at[:, p.z, p.y, p.x, p.c], lsem.at[n_in]); c1.start()
    c2 = pltpu.make_async_copy(ownf, gfo.at[p.z, p.y, p.x, p.c], lsem.at[n_in + 1]); c2.start()
    cs = []
    for k, (dx, dc) in enumerate(((0, 1), (1, 0), (1, 1))):
        tx = (p.x + dx) % 2; tc = (p.c + dc) % 2
        c_ = pltpu.make_async_remote_copy(en.at[0, tx * 2 + tc], ctx.at[:, me], csem.at[k], crsem.at[me], device_id=p.dev(x=tx, c=tc), device_id_type=MESH)
        c_.start(); cs.append(c_)
    c1.wait(); c2.wait()
    streams = []
    for g in range(6):
        for i in range(3):
            t = 3 * g + i
            if t >= 17: continue
            R = 32 if t < 13 else 128
            rows = [(0, R // 2, "zxy"), (R // 2, R // 2, "zyx")] if i == 0 else [(0, R, "xzy" if i == 1 else "yzx")]
            for r0, nr, order in rows:
                n = len(streams)
                if t < 13:
                    view = lambda z, y_, x_, c, t=t, r0=r0, nr=nr: buf.at[t, z, y_, x_, c, pl.ds(r0, nr)]
                else:
                    view = lambda z, y_, x_, c, j=t - 13, r0=r0, nr=nr: gfo.at[z, y_, x_, c, pl.ds(r0, nr), pl.ds(256 * j, 256)]
                streams.append((g, i, Stream(p, view, order, ssem.at[n], rsem.at[n])))
    items = []
    def add(pos, fn): items.append((pos, len(items), fn))
    for g, i, s in streams:
        for k, fn in enumerate(s.phases()): add(g * GAP + k + 0.25 * i, fn)

    def fetch(t):
        if t < 13: return pltpu.make_async_copy(buf.at[t], wbuf.at[t % 4], wsem.at[t])
        j = t - 13
        return pltpu.make_async_copy(gfo.at[:, :, :, :, :, pl.ds(256 * j, 256)], wo.at[j % 2], wsem.at[t])
    def start(t): return lambda: fetch(t).start()
    outs = []
    def keep(src, dst):
        c_ = pltpu.make_async_copy(src, dst, osem.at[len(outs)]); c_.start(); outs.append(c_)
    lo, hi = half_masks()

    def mm(lhs, t, fn, width=1024, first=0):
        @pl.loop(0, width // 256)
        def _(n):
            ds = cols(n, 256)
            w = wbuf[t % 4, :, :, :, :, :, ds].reshape(1024, 256)
            fn(ds, dot(lhs[...], w))

    def proj(lhs, t, slot):
        def run():
            fetch(t).wait()
            def st(ds, v): qkv[slot, :, ds] = v.astype(BF)
            mm(lhs, t, st)
            keep(qkv.at[slot], o_qkv.at[slot])
        return run

    def flip(src, slot):
        def run():
            @pl.loop(0, 4)
            def _(n):
                T[slot, cols(n, 256), :] = src[:, cols(n, 256)].T
            keep(T.at[slot], o_t.at[slot])
        return run

    def attend(a, part):
        def run():
            u = part // 2
            @pl.loop(0, 4)
            def _(n):
                pr = (part % 2) * 4 + n
                r, cc = pl.ds(u * 128, 128), cols(pr, 128)
                q, k, v = (qkv[3 * a + j, r, cc] for j in range(3))
                b = bias[a, u]
                s = dot_nt(pair_up(q, lo, hi), k) * 0.125 + jnp.concatenate([b, b], axis=0)
                e = jnp.exp(s - jnp.max(s, axis=-1, keepdims=True))
                pr_ = e / jnp.sum(e, axis=-1, keepdims=True)
                P[a, u * 8 + pr] = pr_
                mix[r, cc] = dot(side(pr_.astype(BF)), pair_up(v, lo, hi)).astype(BF)
            if part == 3: keep(P.at[a], o_p.at[a])
        return run

    def branch(t, base, slot):
        def run():
            fetch(t).wait()
            def st(ds, v): H[slot, :, ds] = base[:, ds].astype(F32) + v
            mm(mix, t, st)
        return run

    def norm(slot):
        def run():
            keep(H.at[slot], o_h.at[slot])
            @pl.loop(0, 8)
            def _(n):
                r = pl.ds(pl.multiple_of(n * 32, 32), 32)
                v = norm_rows(H[slot, r, :]) * gains[slot, :][None]
                if slot < 2:
                    y[r, :] = v
                    yl[r, :] = v.astype(BF)
                else:
                    OUT[r, :] = v.astype(BF)
            if slot == 2: keep(OUT, o_out)
        return run

    def context_in():
        for k, (dx, dc) in enumerate(((0, 1), (1, 0), (1, 1))):
            tx = (p.x + dx) % 2; tc = (p.c + dc) % 2
            w = tx * 2 + tc
            pltpu.make_async_remote_copy(en.at[0, w], ctx.at[:, w], csem.at[k], crsem.at[w], device_id=p.dev(), device_id_type=MESH).wait_recv()

    class Ctx:
        def __getitem__(self, idx):
            if idx is Ellipsis: return ctx[...].reshape(256, 1024)
            return ctx[:, :, :, idx[1]].reshape(256, -1)
    cref = Ctx()
    def adapter():
        fetch(8).wait()
        w = wbuf[0, :, :, :, :, :, pl.ds(0, 512)].reshape(1024, 512)
        r = dot(yl[...], w)
        s = 1.0 / (1.0 + jnp.exp(-r))
        a = (r * s).astype(BF)
        ar[...] = a
        SR[...] = s * (1.0 + r * (1.0 - s))
        AT[...] = a.T
        keep(SR, o_sr); keep(AT, o_at)
    def adapter_out():
        top = wbuf[0, :, :, :, :, pl.ds(0, 16), pl.ds(512, 512)].reshape(512, 512)
        bot = wbuf[0, :, :, :, :, pl.ds(16, 16), pl.ds(512, 512)].reshape(512, 512)
        H[2, :, 0:512] = y[:, 0:512] + 4.0 * dot(ar[...], top)
        H[2, :, 512:1024] = y[:, 512:1024] + 4.0 * dot(ar[...], bot)
    def hidden(j, part):
        def run():
            t = 9 + j
            if part == 0: fetch(t).wait()
            @pl.loop(2 * part, 2 * part + 2)
            def _(n):
                ds = cols(n, 256)
                @pl.loop(0, 4)
                def _(m):
                    r = pl.ds(pl.multiple_of(m * 64, 64), 64)
                    u = dot(yl[r, :], wbuf[t % 4, :, :, :, :, :, ds].reshape(1024, 256))
                    half = 0.5 + 0.5 * lax.erf(u * 0.7071067811865476)
                    af[j, r, ds] = (u * half).astype(BF)
                    GP[j, r, ds] = half + u * (0.3989422804014327 * jnp.exp(-0.5 * u * u))
            if part == 1: keep(GP.at[j], o_gp.at[j])
        return run
    def out_cols(j):
        def run():
            fetch(13 + j).wait()
            acc = H[2, :, pl.ds(256 * j, 256)]
            for f in range(4):
                w = wo[j % 2, f].reshape(1024, 256)
                acc = acc + dot(af[f], w)
            H[2, :, pl.ds(256 * j, 256)] = acc
        return run

    E = lambda g: g * GAP + 6 + 0.6
    add(1.4, flip(x, 0))
    g0 = E(0)
    for t in (0, 1, 2): add(g0, start(t))
    for t in (0, 1, 2): add(g0 + 0.2 * t, proj(x, t, t))
    for part in range(4): add(g0 + 0.8 + 0.25 * part, attend(0, part))
    add(g0 + 1.8, flip(mix, 3))
    g1 = E(1)
    add(1.6, context_in); add(1.7, flip(cref, 1))
    for t in (3, 4, 5): add(g1, start(t))
    add(g1 + 0.1, branch(3, x, 0)); add(g1 + 0.2, norm(0)); add(g1 + 0.3, flip(yl, 2))
    add(g1 + 0.5, proj(cref, 4, 4)); add(g1 + 0.7, proj(cref, 5, 5))
    g2 = E(2)
    for t in (6, 7): add(g2, start(t))
    add(g2 + 0.01, start(8))
    add(g2 + 0.1, proj(yl, 6, 3))
    for part in range(4): add(g2 + 0.3 + 0.25 * part, attend(1, part))
    add(g2 + 1.3, flip(mix, 4)); add(g2 + 1.4, branch(7, y, 1)); add(g2 + 1.5, norm(1)); add(g2 + 1.6, flip(yl, 5))
    add(g2 + 1.7, adapter); add(g2 + 1.8, adapter_out)
    g3 = max(E(3), g2 + 1.9)
    for t in (9, 10, 11): add(g3, start(t))
    for j in range(3):
        for part in range(2): add(g3 + 0.1 + 0.3 * j + 0.15 * part, hidden(j, part))
    g4 = max(E(4), g3 + 1.1)
    add(g4, start(12)); add(g4, start(13)); add(g4, start(14))
    for part in range(2): add(g4 + 0.1 + 0.2 * part, hidden(3, part))
    add(g4 + 0.5, out_cols(0)); add(g4 + 0.7, out_cols(1))
    g5 = max(E(5), g4 + 0.9)
    add(g5, start(15)); add(g5 + 0.01, out_cols(2)); add(g5 + 0.02, start(16)); add(g5 + 0.03, out_cols(3)); add(g5 + 0.04, norm(2))
    items.sort(key=lambda q: q[:2])
    for it in items: it[2]()
    for _, _, s in streams: s.finish()
    for c_ in cs: c_.wait_send()
    for c_ in outs: c_.wait()

def forward(tokens, gains, bias, shards, encoder):
    any_ = pl.BlockSpec(memory_space=pl.ANY)
    vm = pl.BlockSpec(memory_space=pltpu.VMEM)
    V, S, D = pltpu.VMEM, jax.ShapeDtypeStruct, pltpu.SemaphoreType.DMA
    tile = (4, 2, 2, 2, 32, 1024)
    return pl.pallas_call(forward_kernel,
        out_shape=(S((13,) + tile, BF), S((4, 2, 2, 2, 128, 1024), BF), S((6, 256, 1024), BF), S((2, 16, 256, 128), F32), S((3, 256, 1024), F32),
                   S((6, 1024, 256), BF), S((512, 256), BF), S((4, 256, 1024), F32), S((256, 512), F32), S((256, 1024), BF)),
        in_specs=[vm] * 3 + [any_] * 9, out_specs=(any_,) * 10,
        scratch_shapes=[V((6, 256, 1024), BF), V((2, 16, 256, 128), F32), V((3, 256, 1024), F32), V((6, 1024, 256), BF), V((512, 256), BF),
                        V((4, 256, 1024), F32), V((256, 512), F32), V((256, 1024), BF), V((2, 4, 32, 1024), BF), V((4,) + tile, BF),
                        V((2, 4, 2, 2, 2, 128, 256), BF), V((13, 32, 1024), BF), V((128, 1024), BF), V((256, 1024), F32), V((256, 1024), BF),
                        V((256, 1024), BF), V((4, 256, 1024), BF), V((256, 512), BF),
                        D((N_STREAM, NSEND)), D((N_STREAM, NSLOT)), D((20,)), D((3,)), D((4,)), D((17,)), D((26,))],
        compiler_params=pltpu.CompilerParams(collective_id=0, has_side_effects=True, vmem_limit_bytes=60 << 20),
        name="forward")(tokens, gains, bias, *shards, encoder)


NT = 9
ORDERS = ["A", "xzy", "yzx"] * 3
NS, NR = 27, 33
LAG_C = dict(R1=4.0, R2=8.0, Z0=9.0, Z1=11.0, Z2=13.0, Z3=15.0, FIN=18.0)
LAG_A = dict(R1=4.0, R2=8.0, R3=11.0, Z0=12.0, Z1=14.0, Z2=16.0, FIN=18.0)

class Reduce:
    def __init__(self, p, t, order, PB, L0, L1, L2, UP, DN, LX, ssem, rsem, out):
        self.p, self.t, self.order = p, t, order
        self.PB, self.L0, self.L1, self.L2, self.UP, self.DN, self.LX = PB, L0, L1, L2, UP, DN, LX
        self.ssem, self.rsem, self.out = ssem, rsem, out
        self.sends = []
    def desc(self, src, dst, k, slot, target):
        return pltpu.make_async_remote_copy(src, dst, self.ssem.at[k], self.rsem.at[slot], device_id=target, device_id_type=MESH)
    def copy(self, src, dst, k, slot, target, guard=None):
        cp = self.desc(src, dst, k, slot, target)
        if guard is None: cp.start()
        else: pl.when(guard)(cp.start)
        self.sends.append((cp, guard))
    def arrive(self, dst, slot):
        self.desc(dst, dst, 0, slot, self.p.dev()).wait_recv()
    def finish(self):
        for cp, guard in self.sends:
            if guard is None: cp.wait_send()
            else: pl.when(guard)(cp.wait_send)
    def sib(self, zz):
        p = self.p
        self.desc(self.PB.at[zz, :, :, 1 - p.c], self.L0.at[zz], zz, zz, p.dev(c=1 - p.c)).start()
    def sib_note(self):
        p = self.p
        for zz in range(4):
            self.sends.append((self.desc(self.PB.at[zz, :, :, 1 - p.c], self.L0.at[zz], zz, zz, p.dev(c=1 - p.c)), None))
    def merge(self, zz):
        p = self.p
        self.arrive(self.L0.at[zz], zz)
        for yy in range(2):
            for xx in range(2):
                self.PB[zz, yy, xx, p.c] = self.PB[zz, yy, xx, p.c] + self.L0[zz, yy, xx]
    def pair(self, zz, b2name, b2v, r=pl.ds(0, 32)):
        if b2name == "y": return self.PB.at[zz, b2v, :, self.p.c, r]
        return self.PB.at[zz, :, b2v, self.p.c, r]
    def block(self, zz, r=pl.ds(0, 32), **where):
        p = self.p
        return self.PB.at[zz, where.get("y", p.y), where.get("x", p.x), p.c, r]

    def hop(self, own, up, dn, zu, zd):
        p = self.p
        @pl.when((p.z < zu) & (p.z > 0))
        def _():
            self.arrive(up(zu), 8 + zu)
            o = own(zu); o[...] = o[...] + up(zu)[...]
        self.copy(own(zu), up(zu), 20 + zu - 1, 8 + zu, p.dev(z=p.up), p.z < zu)
        @pl.when((p.z > zd) & (p.z < 3))
        def _():
            self.arrive(dn(zd), 12 + zd)
            o = own(zd); o[...] = o[...] + dn(zd)[...]
        self.copy(own(zd), dn(zd), 23 + zd, 12 + zd, p.dev(z=p.down), p.z > zd)
    def meet(self, own, up, dn):
        p = self.p
        o = own(p.z)
        @pl.when(p.z > 0)
        def _():
            zu = jnp.maximum(p.z, 1)
            self.arrive(up(zu), 8 + zu)
            o[...] = o[...] + up(zu)[...]
        @pl.when(p.z < 3)
        def _():
            zd = jnp.minimum(p.z, 2)
            self.arrive(dn(zd), 12 + zd)
            o[...] = o[...] + dn(zd)[...]

    def phases(self):
        return self.phases_c() if self.order != "A" else self.phases_a()

    def phases_c(self):
        p = self.p
        b1, b2 = self.order[0], self.order[2]
        me = {"x": p.x, "y": p.y}
        part1 = p.dev(**{b1: 1 - me[b1]}); part2 = p.dev(**{b2: 1 - me[b2]})
        own = lambda zz: self.pair(zz, b2, me[b2])
        up = lambda zz: self.UP.at[zz - 1]
        dn = lambda zz: self.DN.at[zz]
        def R1():
            for zz in range(4):
                self.merge(zz)
                self.copy(self.pair(zz, b2, 1 - me[b2]), self.L1.at[zz], 4 + zz, 4 + zz, part2)
        def R2():
            for zz in range(4):
                self.arrive(self.L1.at[zz], 4 + zz)
                o = own(zz)
                o[...] = o[...] + self.L1[zz]
        def Z3():
            self.meet(own, up, dn)
            self.copy(self.block(p.z, **{b1: 1 - me[b1]}), self.LX, 26, 16, part1)
        def FIN():
            self.arrive(self.LX, 16)
            self.out(self.block(p.z)[...].astype(F32) + self.LX[...].astype(F32))
        return dict(R1=R1, R2=R2, Z0=lambda: self.hop(own, up, dn, 3, 0), Z1=lambda: self.hop(own, up, dn, 2, 1), Z2=lambda: self.hop(own, up, dn, 1, 2), Z3=Z3, FIN=FIN)

    def phases_a(self):
        p = self.p
        me = {"x": p.x, "y": p.y}
        halves = [(h, b1, b2, pl.ds(16 * h, 16), p.dev(**{b1: 1 - me[b1]}), p.dev(**{b2: 1 - me[b2]})) for h, (b1, b2) in enumerate((("x", "y"), ("y", "x")))]
        own = lambda zz: self.block(zz)
        up = lambda zz: self.UP.at[zz - 1]
        dn = lambda zz: self.DN.at[zz]
        def R1():
            for zz in range(4):
                self.merge(zz)
                for h, b1, b2, r, part1, part2 in halves:
                    self.copy(self.pair(zz, b2, 1 - me[b2], r), self.L1.at[zz, :, r], 4 + 4 * h + zz, 17 + 4 * h + zz, part2)
        def R2():
            for zz in range(4):
                for h, b1, b2, r, part1, part2 in halves:
                    self.arrive(self.L1.at[zz, :, r], 17 + 4 * h + zz)
                    o = self.pair(zz, b2, me[b2], r)
                    o[...] = o[...] + self.L1[zz, :, r]
                    self.copy(self.block(zz, r, **{b1: 1 - me[b1]}), self.L2.at[zz, r], 12 + 4 * h + zz, 25 + 4 * h + zz, part1)
        def R3():
            for zz in range(4):
                for h, b1, b2, r, part1, part2 in halves:
                    self.arrive(self.L2.at[zz, r], 25 + 4 * h + zz)
                    o = self.block(zz, r)
                    o[...] = o[...] + self.L2[zz, r]
        def FIN():
            self.meet(own, up, dn)
            self.out(own(p.z)[...].astype(F32))
        return dict(R1=R1, R2=R2, R3=R3, Z0=lambda: self.hop(own, up, dn, 3, 0), Z1=lambda: self.hop(own, up, dn, 2, 1), Z2=lambda: self.hop(own, up, dn, 1, 2), FIN=FIN)

W_ORDER = ["o0", "o1", "o2", "o3", 8, 9, 10, 11, 12, 7, 4, 5, 6, 3, 0, 1, 2]
T_ORDER = [5, 4, 1, 2, 3, 0]
NW = 3

def backward_kernel(gains, buf, gfo, qkv, P, H, T, AT, GP, SR, cot,
                    o_tok, osp, oso, ocp, oco, oai, oao, oen,
                    PB, L0, L1, L2, UPC, DNC, UPA, DNA, LX, wbuf, hb, gpb, tb, atb, srb, pb, cotb, g, gb, gr, gx, gqkv, gtok,
                    ssem, rsem, csem, crsem, wsem, hsem, gpsem, tsem, msem, qsem, psem, osem):
    p = Place()
    lo, hi = half_masks()
    def w_copy(i):
        n = W_ORDER[i]
        src = gfo.at[int(n[1])] if isinstance(n, str) else buf.at[n]
        return pltpu.make_async_copy(src, wbuf.at[i % NW], wsem.at[i])
    h_copy = lambda i: pltpu.make_async_copy(H.at[2 - i], hb.at[i % 2], hsem.at[i])
    gp_copy = lambda j: pltpu.make_async_copy(GP.at[j], gpb.at[j % 2], gpsem.at[j])
    t_copy = lambda i: pltpu.make_async_copy(T.at[T_ORDER[i]], tb.at[i % 3], tsem.at[i])
    q_copy = lambda a, j: pltpu.make_async_copy(qkv.at[3 * a + j], PB.at[6 + a, j], qsem.at[3 * a + j])
    p_copy = lambda a: pltpu.make_async_copy(P.at[a], pb, psem.at[a])
    m_copy = [pltpu.make_async_copy(cot, cotb, msem.at[0]), pltpu.make_async_copy(SR, srb, msem.at[1]), pltpu.make_async_copy(AT, atb, msem.at[2])]
    h_copy(0).start(); m_copy[0].start(); w_copy(0).start(); gp_copy(0).start(); w_copy(1).start(); gp_copy(1).start(); w_copy(2).start()
    h_copy(1).start(); m_copy[1].start(); m_copy[2].start()
    for i in range(3): t_copy(i).start()
    for j in range(3): q_copy(1, j).start()
    p_copy(1).start()
    for j in range(3): q_copy(0, j).start()
    entry_barrier(p)

    def o_ad(v):
        oai[...] = v[:, :512]
        oao[:, 0:512] = v[0:16, 512:]
        oao[:, 512:1024] = v[16:32, 512:]
    def put(ref, j=None):
        def f(v):
            if j is None: ref[...] = v
            else: ref[j] = v
        return f
    finals = [o_ad, put(oco), put(ocp, 1), put(ocp, 2), put(ocp, 0), put(oso), put(osp, 1), put(osp, 2), put(osp, 0)]
    reds = []
    nc = na = 0
    for t in range(NT):
        if ORDERS[t] == "A":
            up, dn, l2 = UPA.at[na], DNA.at[na], L2.at[na]; na += 1
        else:
            up, dn, l2 = UPC.at[nc], DNC.at[nc], None; nc += 1
        reds.append(Reduce(p, t, ORDERS[t], PB.at[t], L0.at[t], L1.at[t], l2, up, dn, LX.at[t], ssem.at[t], rsem.at[t], finals[t]))

    items = []
    clock = [0.0]
    def add(pos, fn): items.append((pos, len(items), fn))
    def work(us, fn, made=None):
        add(clock[0], fn)
        clock[0] += us
        if made is not None:
            r = reds[made]
            ph = r.phases()
            for name, off in (LAG_A if ORDERS[made] == "A" else LAG_C).items():
                add(clock[0] + off, ph[name])

    def norm_back(i, first=False):
        def run():
            h_copy(i).wait()
            if first: m_copy[0].wait()
            @pl.loop(0, 8)
            def _(n):
                r = pl.ds(pl.multiple_of(n * 32, 32), 32)
                h = hb[i % 2, r, :]
                center = h - jnp.mean(h, axis=-1, keepdims=True)
                inv = lax.rsqrt(jnp.mean(center * center, axis=-1, keepdims=True) + EPS)
                nrm = center * inv
                gy = cotb[r, :].astype(F32) if first else g[r, :]
                a = gy * gains[2 - i, :][None]
                v = (a - jnp.mean(a, axis=-1, keepdims=True) - nrm * jnp.mean(a * nrm, axis=-1, keepdims=True)) * inv
                g[r, :] = v
                gb[r, :] = v.astype(BF)
            if i == 0: h_copy(2).start()
        return run

    def used(i):
        if i + NW < len(W_ORDER): w_copy(i + NW).start()

    def nt(lhs, i, fn):
        @pl.loop(0, 4)
        def _(n):
            ds = cols(n, 256)
            fn(ds, dot_nt(lhs(), wbuf[i % NW, ds, :]))

    def gu_ref(j, r=pl.ds(0, 2)): return PB.at[8, j]
    def hidden_back(j):
        def run():
            w_copy(j).wait(); gp_copy(j).wait()
            def st(ds, v):
                PB[8, j, :, :, :, :, ds] = (gpb[j % 2, :, ds] * v).astype(BF).reshape(2, 2, 2, 32, 256)
            nt(lambda: gb[...], j, st)
            used(j)
            if j + 2 < 4: gp_copy(j + 2).start()
        return run

    def adapter_back():
        i = 4
        w_copy(i).wait(); m_copy[1].wait(); m_copy[2].wait()
        v = wbuf[i % NW, :, 512:1024].reshape(32, 32, 512)
        top, bot = v[:, :16].reshape(512, 512), v[:, 16:].reshape(512, 512)
        s = dot_nt(gb[:, 0:512], top) + dot_nt(gb[:, 512:1024], bot)
        gr[...] = (srb[...] * (4.0 * s)).astype(BF)
        wai = wbuf[i % NW, :, 0:512]
        g[...] = g[...] + dot_nt(gr[...], wai)
        used(i)

    def adapter_grads():
        r = reds[0]
        for h in range(2):
            v = 4.0 * dot(atb[...], gb[:, 512 * h:512 * h + 512])
            PB[0, :, :, :, :, 16 * h:16 * h + 16, 512:1024] = v.astype(BF).reshape(4, 2, 2, 2, 16, 512)
        t_copy(0).wait()
        @pl.loop(0, 4)
        def _(zz):
            v = dot(tb[0, cols(zz, 256), :], gr[...])
            PB[0, zz, :, :, :, :, 0:512] = v.astype(BF).reshape(2, 2, 2, 32, 512)
            r.sib(zz)
        r.sib_note()
        t_copy(3).start()

    def hidden_in_back(j):
        def run():
            i = 5 + j
            w_copy(i).wait()
            def st(ds, v): g[:, ds] = g[:, ds] + v
            nt(lambda: PB[8, j].reshape(256, 1024), i, st)
            used(i)
        return run

    def grad_tile(t, ti, rhs, last):
        def run():
            r = reds[t]
            if t in (1, 2, 4, 5, 6): t_copy(ti).wait()
            @pl.loop(0, 4)
            def _(zz):
                lhs = tb[ti % 3, cols(zz, 256), :]
                @pl.loop(0, 4)
                def _(n):
                    ds = cols(n, 256)
                    PB[t, zz, :, :, :, :, ds] = dot(lhs, rhs(ds)).astype(BF).reshape(2, 2, 2, 32, 256)
                r.sib(zz)
            r.sib_note()
            if last and ti + 3 < 6: t_copy(ti + 3).start()
        return run

    def mix_back(i):
        def run():
            w_copy(i).wait()
            def st(ds, v): gx[:, ds] = v.astype(BF)
            nt(lambda: gb[...], i, st)
            used(i)
        return run

    def attend_back(a, part):
        def run():
            if part == 0:
                p_copy(a).wait()
                for j in range(3): q_copy(a, j).wait()
            u = part // 2
            @pl.loop(0, 4)
            def _(n):
                pr = (part % 2) * 4 + n
                r, cc = pl.ds(u * 128, 128), cols(pr, 128)
                q, k, v = (PB[6 + a, j, u, :, :, :, cc].reshape(128, 128) for j in range(3))
                go = pair_up(gx[r, cc], lo, hi)
                prob = pb[u * 8 + pr]
                dp = dot_nt(go, v)
                ds = (prob * (dp - jnp.sum(prob * dp, axis=-1, keepdims=True))).astype(BF)
                gqkv[0, r, cc] = (dot(side(ds), pair_up(k, lo, hi)) * 0.125).astype(BF)
                gqkv[1, r, cc] = (dot_tn(ds, pair_up(q, lo, hi)) * 0.125).astype(BF)
                gqkv[2, r, cc] = dot_tn(prob.astype(BF), go).astype(BF)
            if part == 3 and a == 1: p_copy(0).start()
        return run

    def row_back(i, j, dst):
        def run():
            w_copy(i).wait()
            nt(lambda: gqkv[j], i, dst)
            used(i)
        return run
    def to_g(ds, v): g[:, ds] = g[:, ds] + v
    def ctx_first(ds, v): hb[0, :, ds] = v
    cs = []
    me = p.x * 2 + p.c
    def context_back():
        i = 11
        w_copy(i).wait()
        def st(ds, v): PB[8, 0, :, :, :, :, ds] = (ctxf[:, ds] + v).astype(BF).reshape(2, 2, 2, 32, 256)
        nt(lambda: gqkv[2], i, st)
        used(i)
        for k, (dx, dc) in enumerate(((0, 1), (1, 0), (1, 1))):
            tx = (p.x + dx) % 2; tc = (p.c + dc) % 2
            c_ = pltpu.make_async_remote_copy(PB.at[8, 0, :, tx, tc], oen.at[0, me], csem.at[k], crsem.at[me], device_id=p.dev(x=tx, c=tc), device_id_type=MESH)
            c_.start(); cs.append(c_)
        c_ = pltpu.make_async_copy(PB.at[8, 0, :, p.x, p.c], oen.at[0, me], osem.at[0]); c_.start(); cs.append(c_)

    ctxf = gpb.at[0]
    def ctx_part(ds, v): ctxf[:, ds] = v
    def context_sent():
        for c_ in cs[:3]: c_.wait_send()
        cs[3].wait()
    def tokens_back():
        i = 16
        w_copy(i).wait()
        def st(ds, v): gtok[:, ds] = (g[:, ds] + v).astype(BF)
        nt(lambda: gqkv[2], i, st)
        pltpu.make_async_copy(gtok, o_tok, osem.at[1]).start()

    work(1.5, norm_back(0, True))
    for j in range(4): work(1.3, hidden_back(j))
    work(1.2, adapter_back)
    work(1.2, adapter_grads, 0)
    for j in range(4): work(1.2, hidden_in_back(j))
    work(1.5, norm_back(1))
    work(1.3, grad_tile(1, 1, lambda ds: gb[:, ds], True), 1)
    work(1.2, mix_back(9))
    for part in range(4): work(2.5, attend_back(1, part))
    work(1.3, grad_tile(2, 2, lambda ds: gqkv[1, :, ds], False), 2)
    work(1.3, grad_tile(3, 2, lambda ds: gqkv[2, :, ds], True), 3)
    work(1.3, grad_tile(4, 3, lambda ds: gqkv[0, :, ds], True), 4)
    work(1.2, row_back(10, 1, ctx_part))
    work(1.4, context_back)
    work(1.2, row_back(12, 0, to_g))
    work(1.5, norm_back(2))
    work(1.3, grad_tile(5, 4, lambda ds: gb[:, ds], True), 5)
    work(1.2, mix_back(13))
    for part in range(4): work(2.5, attend_back(0, part))
    work(0.2, context_sent)
    work(1.3, grad_tile(6, 5, lambda ds: gqkv[1, :, ds], False), 6)
    work(1.3, grad_tile(7, 5, lambda ds: gqkv[2, :, ds], False), 7)
    work(1.3, grad_tile(8, 5, lambda ds: gqkv[0, :, ds], True), 8)
    work(1.2, row_back(14, 0, to_g))
    work(1.2, row_back(15, 1, to_g))
    work(1.2, tokens_back)
    items.sort(key=lambda q: q[:2])
    for it in items: it[2]()
    for r in reds: r.finish()
    pltpu.make_async_copy(gtok, o_tok, osem.at[1]).wait()
    for k, (dx, dc) in enumerate(((0, 1), (1, 0), (1, 1))):
        tx = (p.x + dx) % 2; tc = (p.c + dc) % 2
        w = tx * 2 + tc
        pltpu.make_async_remote_copy(PB.at[8, 0, :, tx, tc], oen.at[0, w], csem.at[k], crsem.at[w], device_id=p.dev(), device_id_type=MESH).wait_recv()

def backward(gains, buf, gfo, qkv, P, H, T, AT, GP, SR, cot):
    any_ = pl.BlockSpec(memory_space=pl.ANY)
    vm = pl.BlockSpec(memory_space=pltpu.VMEM)
    V, S, D = pltpu.VMEM, jax.ShapeDtypeStruct, pltpu.SemaphoreType.DMA
    ops = (gains, buf.reshape(13, 1024, 1024), gfo.reshape(4, 1024, 1024), qkv.reshape(6, 2, 2, 2, 32, 1024), P, H, T, AT, GP, SR, cot)
    return pl.pallas_call(backward_kernel,
        out_shape=(S((256, 1024), BF), S((3, 32, 1024), F32), S((32, 1024), F32), S((3, 32, 1024), F32), S((32, 1024), F32), S((32, 512), F32), S((16, 1024), F32), S((1, 4, 2, 32, 1024), BF)),
        in_specs=[vm] + [any_] * 10, out_specs=(any_,) + (vm,) * 6 + (any_,),
        scratch_shapes=[V((NT, 4, 2, 2, 2, 32, 1024), BF), V((NT, 4, 2, 2, 32, 1024), BF), V((NT, 4, 2, 32, 1024), BF), V((3, 4, 32, 1024), BF),
                        V((6, 3, 2, 32, 1024), BF), V((6, 3, 2, 32, 1024), BF), V((3, 3, 32, 1024), BF), V((3, 3, 32, 1024), BF), V((NT, 32, 1024), BF),
                        V((NW, 1024, 1024), BF), V((2, 256, 1024), F32), V((2, 256, 1024), F32), V((3, 1024, 256), BF), V((512, 256), BF), V((256, 512), F32),
                        V((16, 256, 128), F32), V((256, 1024), BF), V((256, 1024), F32), V((256, 1024), BF), V((256, 512), BF), V((256, 1024), BF),
                        V((3, 256, 1024), BF), V((256, 1024), BF),
                        D((NT, NS)), D((NT, NR)), D((3,)), D((4,)), D((17,)), D((3,)), D((4,)), D((6,)), D((3,)), D((6,)), D((2,)), D((2,))],
        compiler_params=pltpu.CompilerParams(collective_id=1, has_side_effects=True, vmem_limit_bytes=63 << 20),
        name="backward")(*ops)


def device_program(tokens, encoder, dec_lengths, enc_lengths, gains, self_proj, self_out, cross_proj, cross_out, ffn_in, ffn_out, adapt_in, adapt_out, cotangent):
    masks = [slot_masks(dec_lengths[m], enc_lengths[m], 128) for m in range(2)]
    bias = jnp.where(jnp.stack([jnp.stack([masks[u][a] for u in range(2)]) for a in range(2)]), 0.0, NEGATIVE)
    shards = (self_proj, self_out, cross_proj, cross_out, ffn_in, ffn_out, adapt_in, adapt_out)
    buf, gfo, qkv, probs, hidden, turned, act_turned, gelu_slope, silu_slope, layer_out = forward(tokens, gains, bias, shards, encoder)
    gtok, osp, oso, ocp, oco, oai, oao, oen = backward(gains, buf, gfo, qkv, probs, hidden, turned, act_turned, gelu_slope, silu_slope, cotangent)
    return (layer_out, gtok, oen, osp, oso, ocp, oco, oai, oao)


def solution(mesh):
    in_specs = (
        P(("seq", "enc"), None),
        P("seq", None, None, "enc", None),
        P(("seq", "enc"), None),
        P(("seq", "enc"), None),
        P(),
        P(None, ("seq", "enc"), None),
        P(("seq", "enc"), None),
        P(None, ("seq", "enc"), None),
        P(("seq", "enc"), None),
        P(("seq", "enc"), None),
        P(("seq", "enc"), None),
        P(("seq", "enc"), None),
        P(("seq", "enc"), None),
        P(("seq", "enc"), None),
    )
    out_specs = (
        P(("seq", "enc"), None),
        P(("seq", "enc"), None),
        P("seq", None, None, "enc", None),
        P(None, ("seq", "enc"), None),
        P(("seq", "enc"), None),
        P(None, ("seq", "enc"), None),
        P(("seq", "enc"), None),
        P(("seq", "enc"), None),
        P(("seq", "enc"), None),
    )
    fast = (mesh.shape["seq"], mesh.shape["enc"]) == (8, 4)
    return jax.shard_map(
        device_program if fast else per_device, mesh=mesh, in_specs=in_specs, out_specs=out_specs, check_vma=False
    )
```

```python
import jax
import jax.numpy as jnp
from jax import lax
from jax.experimental import pallas as pl
from jax.experimental.pallas import tpu as pltpu
from jax.sharding import PartitionSpec as P

HEADS = 16
ADAPT = 512
MICRO = 2


EPSILON = 1e-05
NEGATIVE = -1e30


def matmul(left, right):
    return jnp.dot(left, right, preferred_element_type=jnp.float32)


def matmul_tn(left, right):
    return lax.dot_general(
        left, right, (((0,), (0,)), ((), ())), preferred_element_type=jnp.float32
    )


def matmul_nt(left, right):
    return lax.dot_general(
        left, right, (((1,), (1,)), ((), ())), preferred_element_type=jnp.float32
    )


def layer_norm(hidden, gain):
    center = hidden - jnp.mean(hidden, axis=-1, keepdims=True)
    spread = jnp.mean(center * center, axis=-1, keepdims=True)
    return center * lax.rsqrt(spread + EPSILON) * gain


def norm_back(hidden, gain, grad_out):
    _, pullback = jax.vjp(lambda value: layer_norm(value, gain), hidden)
    return pullback(grad_out)[0]


def gelu_exact(value):
    return jax.nn.gelu(value, approximate=False)


def slot_masks(dec_row, enc_row, rows):
    half_rows = rows // 2
    places = lax.broadcasted_iota(jnp.int32, (rows,), 0)
    paired = dec_row[1] > 0
    second = jnp.logical_and(paired, places >= half_rows)
    anchor = jnp.where(second, half_rows, 0).astype(jnp.int32)
    dec_valid = jnp.where(second, dec_row[1], dec_row[0])
    enc_valid = jnp.where(second, enc_row[1], enc_row[0])
    key_live = places - anchor < dec_valid
    context_live = places - anchor < enc_valid
    same_slot = second[:, None] == second[None, :]
    causal = places[None, :] <= places[:, None]
    self_mask = same_slot & causal & key_live[None, :]
    cross_mask = same_slot & context_live[None, :]
    return (self_mask, cross_mask)


def split_heads(matrix):
    return matrix.reshape(matrix.shape[0], HEADS, matrix.shape[1] // HEADS)


def attend(queries, keys, values, allowed):
    depth = queries.shape[1] // HEADS
    scores = jnp.einsum(
        "qhd,khd->hqk", split_heads(queries), split_heads(keys), preferred_element_type=jnp.float32
    ) * float(depth) ** (-0.5)
    masked = jnp.where(allowed[None], scores, NEGATIVE)
    weights = jnp.exp(masked - jnp.max(masked, axis=-1, keepdims=True))
    probs = weights / jnp.sum(weights, axis=-1, keepdims=True)
    mixed = jnp.einsum(
        "hqk,khd->qhd",
        probs.astype(jnp.bfloat16),
        split_heads(values),
        preferred_element_type=jnp.float32,
    )
    return (mixed.reshape(queries.shape).astype(jnp.bfloat16), probs)


def attend_back(grad_mixed, queries, keys, values, probs):
    depth = queries.shape[1] // HEADS
    factor = float(depth) ** (-0.5)
    grad_heads = split_heads(grad_mixed)
    grad_probs = jnp.einsum(
        "qhd,khd->hqk", grad_heads, split_heads(values), preferred_element_type=jnp.float32
    )
    inner = jnp.sum(probs * grad_probs, axis=-1, keepdims=True)
    grad_scores = (probs * (grad_probs - inner)).astype(jnp.bfloat16)
    grad_query = (
        jnp.einsum(
            "hqk,khd->qhd", grad_scores, split_heads(keys), preferred_element_type=jnp.float32
        )
        * factor
    )
    grad_key = (
        jnp.einsum(
            "hqk,qhd->khd", grad_scores, split_heads(queries), preferred_element_type=jnp.float32
        )
        * factor
    )
    grad_value = jnp.einsum(
        "hqk,qhd->khd", probs.astype(jnp.bfloat16), grad_heads, preferred_element_type=jnp.float32
    )
    return (
        grad_query.reshape(queries.shape).astype(jnp.bfloat16),
        grad_key.reshape(keys.shape).astype(jnp.bfloat16),
        grad_value.reshape(values.shape).astype(jnp.bfloat16),
    )


def per_device(
    tokens,
    encoder,
    dec_lengths,
    enc_lengths,
    gains,
    self_proj,
    self_out,
    cross_proj,
    cross_out,
    ffn_in,
    ffn_out,
    adapt_in,
    adapt_out,
    cotangent,
):
    shards = (self_proj, self_out, cross_proj, cross_out, ffn_in, ffn_out, adapt_in, adapt_out)

    def obtain():
        return (
            lax.all_gather(shards[0], ("seq", "enc"), axis=1, tiled=True),
            lax.all_gather(shards[1], ("seq", "enc"), axis=0, tiled=True),
            lax.all_gather(shards[2], ("seq", "enc"), axis=1, tiled=True),
            lax.all_gather(shards[3], ("seq", "enc"), axis=0, tiled=True),
            lax.all_gather(shards[4], ("seq", "enc"), axis=0, tiled=True),
            lax.all_gather(shards[5], ("seq", "enc"), axis=0, tiled=True),
            lax.all_gather(shards[6], ("seq", "enc"), axis=0, tiled=True),
            lax.all_gather(shards[7], ("seq", "enc"), axis=0, tiled=True),
        )

    rows = tokens.shape[0] // MICRO
    width = tokens.shape[1]
    owner = lax.axis_index("enc")
    acc_self = jnp.zeros((width, 3, width), jnp.float32)
    acc_self_out = jnp.zeros((width, width), jnp.float32)
    acc_cross = jnp.zeros((width, 3, width), jnp.float32)
    acc_cross_out = jnp.zeros((width, width), jnp.float32)
    acc_adapt_in = jnp.zeros((width, ADAPT), jnp.float32)
    acc_adapt_out = jnp.zeros((ADAPT, width), jnp.float32)
    outputs = []
    grad_rows = []
    grad_contexts = []
    for micro_index in range(MICRO):
        w_self, w_self_out, w_cross, w_cross_out, w_ffn_in, w_ffn_out, w_adapt_in, w_adapt_out = (
            obtain()
        )
        lower = micro_index * rows
        token_rows = tokens[lower : lower + rows]
        self_mask, cross_mask = slot_masks(dec_lengths[micro_index], enc_lengths[micro_index], rows)
        pieces = encoder[0, :, micro_index]
        context = lax.dynamic_index_in_dim(
            lax.all_gather(pieces, "enc", axis=1, tiled=True), owner, 0, keepdims=False
        )
        self_query = matmul(token_rows, w_self[0]).astype(jnp.bfloat16)
        self_key = matmul(token_rows, w_self[1]).astype(jnp.bfloat16)
        self_value = matmul(token_rows, w_self[2]).astype(jnp.bfloat16)
        self_mix, self_probs = attend(self_query, self_key, self_value, self_mask)
        first_sum = token_rows.astype(jnp.float32) + matmul(self_mix, w_self_out)
        first_norm = layer_norm(first_sum, gains[0])
        first_low = first_norm.astype(jnp.bfloat16)
        cross_query = matmul(first_low, w_cross[0]).astype(jnp.bfloat16)
        cross_key = matmul(context, w_cross[1]).astype(jnp.bfloat16)
        cross_value = matmul(context, w_cross[2]).astype(jnp.bfloat16)
        cross_mix, cross_probs = attend(cross_query, cross_key, cross_value, cross_mask)
        second_sum = first_norm + matmul(cross_mix, w_cross_out)
        second_norm = layer_norm(second_sum, gains[1])
        second_low = second_norm.astype(jnp.bfloat16)
        ffn_pre = matmul(second_low, w_ffn_in)
        ffn_act = gelu_exact(ffn_pre).astype(jnp.bfloat16)
        adapt_pre = matmul(second_low, w_adapt_in)
        adapt_act = jax.nn.silu(adapt_pre).astype(jnp.bfloat16)
        third_sum = second_norm + matmul(ffn_act, w_ffn_out) + 4.0 * matmul(adapt_act, w_adapt_out)
        outputs.append(layer_norm(third_sum, gains[2]).astype(jnp.bfloat16))
        w_self, w_self_out, w_cross, w_cross_out, w_ffn_in, w_ffn_out, w_adapt_in, w_adapt_out = (
            obtain()
        )
        grad_third = norm_back(
            third_sum, gains[2], cotangent[lower : lower + rows].astype(jnp.float32)
        )
        grad_branch = grad_third.astype(jnp.bfloat16)
        _, gelu_pull = jax.vjp(gelu_exact, ffn_pre)
        grad_ffn_pre = gelu_pull(matmul_nt(grad_branch, w_ffn_out))[0].astype(jnp.bfloat16)
        grad_adapt_act = matmul_nt(grad_branch, w_adapt_out) * 4.0
        _, silu_pull = jax.vjp(jax.nn.silu, adapt_pre)
        grad_adapt_pre = silu_pull(grad_adapt_act)[0].astype(jnp.bfloat16)
        acc_adapt_out = acc_adapt_out + matmul_tn(adapt_act, grad_branch) * 4.0
        acc_adapt_in = acc_adapt_in + matmul_tn(second_low, grad_adapt_pre)
        grad_second = (
            grad_third + matmul_nt(grad_ffn_pre, w_ffn_in) + matmul_nt(grad_adapt_pre, w_adapt_in)
        )
        grad_second_sum = norm_back(second_sum, gains[1], grad_second)
        grad_cross_branch = grad_second_sum.astype(jnp.bfloat16)
        acc_cross_out = acc_cross_out + matmul_tn(cross_mix, grad_cross_branch)
        grad_cross_mix = matmul_nt(grad_cross_branch, w_cross_out).astype(jnp.bfloat16)
        grad_cq, grad_ck, grad_cv = attend_back(
            grad_cross_mix, cross_query, cross_key, cross_value, cross_probs
        )
        acc_cross = acc_cross + jnp.stack(
            [
                matmul_tn(first_low, grad_cq),
                matmul_tn(context, grad_ck),
                matmul_tn(context, grad_cv),
            ],
            axis=1,
        )
        grad_context = matmul_nt(grad_ck, w_cross[1]) + matmul_nt(grad_cv, w_cross[2])
        holder = jnp.zeros((lax.axis_size("enc"),) + grad_context.shape, jnp.float32)
        holder = lax.dynamic_update_index_in_dim(holder, grad_context, owner, 0)
        returned = lax.psum_scatter(
            holder.astype(jnp.bfloat16), "enc", scatter_dimension=1, tiled=True
        )
        grad_contexts.append(returned)
        grad_first = grad_second_sum + matmul_nt(grad_cq, w_cross[0])
        grad_first_sum = norm_back(first_sum, gains[0], grad_first)
        grad_self_branch = grad_first_sum.astype(jnp.bfloat16)
        acc_self_out = acc_self_out + matmul_tn(self_mix, grad_self_branch)
        grad_self_mix = matmul_nt(grad_self_branch, w_self_out).astype(jnp.bfloat16)
        grad_sq, grad_sk, grad_sv = attend_back(
            grad_self_mix, self_query, self_key, self_value, self_probs
        )
        acc_self = acc_self + jnp.stack(
            [
                matmul_tn(token_rows, grad_sq),
                matmul_tn(token_rows, grad_sk),
                matmul_tn(token_rows, grad_sv),
            ],
            axis=1,
        )
        grad_input = (
            grad_first_sum
            + matmul_nt(grad_sq, w_self[0])
            + matmul_nt(grad_sk, w_self[1])
            + matmul_nt(grad_sv, w_self[2])
        )
        grad_rows.append(grad_input.astype(jnp.bfloat16))
    summed = (
        lax.psum_scatter(acc_self, ("seq", "enc"), scatter_dimension=0, tiled=True),
        lax.psum_scatter(acc_self_out, ("seq", "enc"), scatter_dimension=0, tiled=True),
        lax.psum_scatter(acc_cross, ("seq", "enc"), scatter_dimension=0, tiled=True),
        lax.psum_scatter(acc_cross_out, ("seq", "enc"), scatter_dimension=0, tiled=True),
        lax.psum_scatter(acc_adapt_in, ("seq", "enc"), scatter_dimension=0, tiled=True),
        lax.psum_scatter(acc_adapt_out, ("seq", "enc"), scatter_dimension=0, tiled=True),
    )
    layer_out = jnp.concatenate(outputs, axis=0)
    grad_tokens = jnp.concatenate(grad_rows, axis=0)
    grad_encoder = jnp.stack(grad_contexts, axis=1)[None]
    grad_self_proj = jnp.transpose(summed[0], (1, 0, 2))
    grad_cross_proj = jnp.transpose(summed[2], (1, 0, 2))
    return (
        layer_out,
        grad_tokens,
        grad_encoder,
        grad_self_proj,
        summed[1],
        grad_cross_proj,
        summed[3],
        summed[4],
        summed[5],
    )


MESH = pl.DeviceIdType.MESH
GAP = 2

TILES = ["q1", "k1", "v1", "so", "k2", "v2", "q2", "co", "ad", "f0", "f1", "f2", "f3", "o0", "o1", "o2", "o3"]

class Place:
    def __init__(self):
        seq, enc = lax.axis_index("seq"), lax.axis_index("enc")
        self.z, self.y, self.x, self.c = seq // 2, seq % 2, enc // 2, enc % 2
        self.up, self.down = jnp.minimum(self.z + 1, 3), jnp.maximum(self.z - 1, 0)
    def dev(self, z=None, y=None, x=None, c=None):
        z = self.z if z is None else z
        y = self.y if y is None else y
        x = self.x if x is None else x
        c = self.c if c is None else c
        return (z * 2 + y, x * 2 + c)

def entry_barrier(p):
    bar = pltpu.get_barrier_semaphore()
    def sig(d):
        pl.semaphore_signal(bar, inc=1, device_id=d, device_id_type=MESH)
    sig(p.dev(c=1 - p.c)); sig(p.dev(x=1 - p.x)); sig(p.dev(y=1 - p.y)); sig(p.dev(x=1 - p.x, c=1 - p.c))
    @pl.when(p.z < 3)
    def _(): sig(p.dev(z=p.up))
    @pl.when(p.z > 0)
    def _(): sig(p.dev(z=p.down))
    peers = 4 + (p.z < 3).astype(jnp.int32) + (p.z > 0).astype(jnp.int32)
    pl.semaphore_wait(bar, peers)

ALL4 = pl.ds(0, 4)
ALL2 = pl.ds(0, 2)

class Stream:
    def __init__(self, p, view, order, ssem, rsem):
        self.p, self.view, self.order, self.ssem, self.rsem = p, view, order, ssem, rsem
        self.ns = 0
        self.sends = []

    def cut(self, z, y, x, c):
        return self.view(z, y, x, c)

    def copy(self, where, slot, target, guard=None):
        k = self.ns; self.ns += 1
        cp = pltpu.make_async_remote_copy(where, where, self.ssem.at[k], self.rsem.at[slot], device_id=target, device_id_type=MESH)
        if guard is None:
            cp.start()
        else:
            pl.when(guard)(cp.start)
        self.sends.append((cp, guard))

    def arrive(self, where, slot, guard=None):
        cp = pltpu.make_async_remote_copy(where, where, self.ssem.at[0], self.rsem.at[slot], device_id=self.p.dev(), device_id_type=MESH)
        if guard is None:
            cp.wait_recv()
        else:
            pl.when(guard)(cp.wait_recv)

    def finish(self):
        for cp, guard in self.sends:
            if guard is None:
                cp.wait_send()
            else:
                pl.when(guard)(cp.wait_send)

    def at(self, z, own):
        return self.cut(z, own["y"], own["x"], self.p.c)

    def phases(self):
        p = self.p
        if self.order[0] == "z":
            b1, b2 = self.order[1], self.order[2]
            me = {"x": p.x, "y": p.y}
            oth = {"x": 1 - p.x, "y": 1 - p.y}
            part1 = p.dev(**{b1: oth[b1]}); part2 = p.dev(**{b2: oth[b2]})
            sib = p.dev(c=1 - p.c)
            own = dict(me)
            b1o = dict(me); b1o[b1] = oth[b1]
            both = dict(me); both[b1] = ALL2
            allof = {"x": ALL2, "y": ALL2}
            def P0():
                self.copy(self.at(p.z, own), p.z, p.dev(z=p.up), p.z < 3)
                self.copy(self.at(p.z, own), p.z, p.dev(z=p.down), p.z > 0)
                self.copy(self.at(p.z, own), 4 + p.z, part1)
            def hop(t):
                lo, hi = jnp.maximum(p.z - t, 0), jnp.minimum(p.z + t, 3)
                below, above = p.z >= t, p.z + t <= 3
                self.arrive(self.at(lo, own), lo, below)
                if t < 3:
                    self.copy(self.at(lo, own), lo, p.dev(z=p.up), (below) & (p.z < 3))
                self.copy(self.at(lo, own), 4 + lo, part1, below)
                self.arrive(self.at(hi, own), hi, above)
                if t < 3:
                    self.copy(self.at(hi, own), hi, p.dev(z=p.down), (above) & (p.z > 0))
                self.copy(self.at(hi, own), 4 + hi, part1, above)
            def P4():
                for zz in range(4):
                    self.arrive(self.at(zz, b1o), 4 + zz)
                    self.copy(self.at(zz, both), 8 + zz, part2)
            def P5():
                self.copy(self.at(ALL4, both), 12, sib)
                for zz in range(4):
                    self.arrive(self.at(zz, both), 8 + zz)
                b2o = dict(both); b2o[b2] = oth[b2]
                self.copy(self.at(ALL4, b2o), 13, sib)
            def P6():
                b2o = dict(both); b2o[b2] = oth[b2]
                w = lambda s: self.cut(ALL4, s["y"], s["x"], 1 - p.c)
                self.arrive(w(both), 12)
                self.arrive(w(b2o), 13)
            return [P0, lambda: hop(1), lambda: hop(2), lambda: hop(3), P4, P5, P6]
        b1, b2 = self.order[0], self.order[2]
        me = {"x": p.x, "y": p.y}
        oth = {"x": 1 - p.x, "y": 1 - p.y}
        part1 = p.dev(**{b1: oth[b1]}); part2 = p.dev(**{b2: oth[b2]})
        sib = p.dev(c=1 - p.c)
        own = dict(me)
        b1o = dict(me); b1o[b1] = oth[b1]
        both = dict(me); both[b1] = ALL2
        b2o = dict(both); b2o[b2] = oth[b2]
        def P0():
            self.copy(self.at(p.z, own), 8, part1)
        def P1():
            self.arrive(self.at(p.z, b1o), 8)
            self.copy(self.at(p.z, both), p.z, p.dev(z=p.up), p.z < 3)
            self.copy(self.at(p.z, both), p.z, p.dev(z=p.down), p.z > 0)
            self.copy(self.at(p.z, both), 4 + p.z, part2)
        def hop(t):
            lo, hi = jnp.maximum(p.z - t, 0), jnp.minimum(p.z + t, 3)
            below, above = p.z >= t, p.z + t <= 3
            self.arrive(self.at(lo, both), lo, below)
            if t < 3:
                self.copy(self.at(lo, both), lo, p.dev(z=p.up), (below) & (p.z < 3))
            self.copy(self.at(lo, both), 4 + lo, part2, below)
            self.arrive(self.at(hi, both), hi, above)
            if t < 3:
                self.copy(self.at(hi, both), hi, p.dev(z=p.down), (above) & (p.z > 0))
            self.copy(self.at(hi, both), 4 + hi, part2, above)
        def P5():
            self.copy(self.at(ALL4, both), 12, sib)
            for zz in range(4):
                self.arrive(self.at(zz, b2o), 4 + zz)
            self.copy(self.at(ALL4, b2o), 13, sib)
        def P6():
            w = lambda s: self.cut(ALL4, s["y"], s["x"], 1 - p.c)
            self.arrive(w(both), 12)
            self.arrive(w(b2o), 13)
        return [P0, P1, lambda: hop(1), lambda: hop(2), lambda: hop(3), P5, P6]

F32, BF = jnp.float32, jnp.bfloat16
NSLOT, NSEND = 14, 19
N_STREAM = 23
EPS = 1e-05

def dot(a, b):
    return jnp.dot(a, b, preferred_element_type=F32)

def dot_nt(a, b):
    return lax.dot_general(a, b, (((1,), (1,)), ((), ())), preferred_element_type=F32)

def dot_tn(a, b):
    return lax.dot_general(a, b, (((0,), (0,)), ((), ())), preferred_element_type=F32)

def cols(n, width):
    return pl.ds(pl.multiple_of(n * width, width), width)

def norm_rows(h):
    center = h - jnp.mean(h, axis=-1, keepdims=True)
    spread = jnp.mean(center * center, axis=-1, keepdims=True)
    return center * lax.rsqrt(spread + EPS)

def half_masks():
    lane = lax.broadcasted_iota(jnp.int32, (1, 128), 1)
    lo = jnp.where(lane < 64, 1.0, 0.0)
    return lo.astype(BF), (1.0 - lo).astype(BF)

def pair_up(m, lo, hi):
    return jnp.concatenate([m * lo, m * hi], axis=0)

def side(m):
    return jnp.concatenate([m[:128], m[128:]], axis=1)

def forward_kernel(x, gains, bias, sp, so, cp, co, fi, fo, ai, ao, en,
                   buf, gfo, o_qkv, o_p, o_h, o_t, o_at, o_gp, o_sr, o_out,
                   qkv, P, H, T, AT, GP, SR, OUT, ctx, wbuf, wo, own, ownf, y, yl, mix, af, ar,
                   ssem, rsem, lsem, csem, crsem, wsem, osem):
    p = Place()
    loc = []
    def put(src, dst):
        c_ = pltpu.make_async_copy(src, dst, lsem.at[len(loc)]); c_.start(); loc.append(c_)
    for j, t in enumerate((0, 1, 2)): put(sp.at[j], own.at[t])
    put(so, own.at[3])
    for j, t in ((1, 4), (2, 5), (0, 6)): put(cp.at[j], own.at[t])
    put(co, own.at[7])
    put(ai, own.at[8, :, pl.ds(0, 512)])
    put(ao.at[:, pl.ds(0, 512)], own.at[8, pl.ds(0, 16), pl.ds(512, 512)])
    put(ao.at[:, pl.ds(512, 512)], own.at[8, pl.ds(16, 16), pl.ds(512, 512)])
    for j in range(4): put(fi.at[:, pl.ds(1024 * j, 1024)], own.at[9 + j])
    put(fo, ownf)
    me = p.x * 2 + p.c
    put(en.at[0, me], ctx.at[:, me])
    entry_barrier(p)
    for c_ in loc: c_.wait()
    n_in = len(loc)
    c1 = pltpu.make_async_copy(own, buf.at[:, p.z, p.y, p.x, p.c], lsem.at[n_in]); c1.start()
    c2 = pltpu.make_async_copy(ownf, gfo.at[p.z, p.y, p.x, p.c], lsem.at[n_in + 1]); c2.start()
    cs = []
    for k, (dx, dc) in enumerate(((0, 1), (1, 0), (1, 1))):
        tx = (p.x + dx) % 2; tc = (p.c + dc) % 2
        c_ = pltpu.make_async_remote_copy(en.at[0, tx * 2 + tc], ctx.at[:, me], csem.at[k], crsem.at[me], device_id=p.dev(x=tx, c=tc), device_id_type=MESH)
        c_.start(); cs.append(c_)
    c1.wait(); c2.wait()
    streams = []
    for g in range(6):
        for i in range(3):
            t = 3 * g + i
            if t >= 17: continue
            R = 32 if t < 13 else 128
            rows = [(0, R // 2, "zxy"), (R // 2, R // 2, "zyx")] if i == 0 else [(0, R, "xzy" if i == 1 else "yzx")]
            for r0, nr, order in rows:
                n = len(streams)
                if t < 13:
                    view = lambda z, y_, x_, c, t=t, r0=r0, nr=nr: buf.at[t, z, y_, x_, c, pl.ds(r0, nr)]
                else:
                    view = lambda z, y_, x_, c, j=t - 13, r0=r0, nr=nr: gfo.at[z, y_, x_, c, pl.ds(r0, nr), pl.ds(256 * j, 256)]
                streams.append((g, i, Stream(p, view, order, ssem.at[n], rsem.at[n])))
    items = []
    def add(pos, fn): items.append((pos, len(items), fn))
    for g, i, s in streams:
        for k, fn in enumerate(s.phases()): add(g * GAP + k + 0.25 * i, fn)

    def fetch(t):
        if t < 13: return pltpu.make_async_copy(buf.at[t], wbuf.at[t % 4], wsem.at[t])
        j = t - 13
        return pltpu.make_async_copy(gfo.at[:, :, :, :, :, pl.ds(256 * j, 256)], wo.at[j % 2], wsem.at[t])
    def start(t): return lambda: fetch(t).start()
    outs = []
    def keep(src, dst):
        c_ = pltpu.make_async_copy(src, dst, osem.at[len(outs)]); c_.start(); outs.append(c_)
    lo, hi = half_masks()

    def mm(lhs, t, fn, width=1024, first=0):
        @pl.loop(0, width // 256)
        def _(n):
            ds = cols(n, 256)
            w = wbuf[t % 4, :, :, :, :, :, ds].reshape(1024, 256)
            fn(ds, dot(lhs[...], w))

    def proj(lhs, t, slot):
        def run():
            fetch(t).wait()
            def st(ds, v): qkv[slot, :, ds] = v.astype(BF)
            mm(lhs, t, st)
            keep(qkv.at[slot], o_qkv.at[slot])
        return run

    def flip(src, slot):
        def run():
            @pl.loop(0, 4)
            def _(n):
                T[slot, cols(n, 256), :] = src[:, cols(n, 256)].T
            keep(T.at[slot], o_t.at[slot])
        return run

    def attend(a, part):
        def run():
            u = part // 2
            @pl.loop(0, 4)
            def _(n):
                pr = (part % 2) * 4 + n
                r, cc = pl.ds(u * 128, 128), cols(pr, 128)
                q, k, v = (qkv[3 * a + j, r, cc] for j in range(3))
                b = bias[a, u]
                s = dot_nt(pair_up(q, lo, hi), k) * 0.125 + jnp.concatenate([b, b], axis=0)
                e = jnp.exp(s - jnp.max(s, axis=-1, keepdims=True))
                pr_ = e / jnp.sum(e, axis=-1, keepdims=True)
                P[a, u * 8 + pr] = pr_
                mix[r, cc] = dot(side(pr_.astype(BF)), pair_up(v, lo, hi)).astype(BF)
            if part == 3: keep(P.at[a], o_p.at[a])
        return run

    def branch(t, base, slot):
        def run():
            fetch(t).wait()
            def st(ds, v): H[slot, :, ds] = base[:, ds].astype(F32) + v
            mm(mix, t, st)
        return run

    def norm(slot):
        def run():
            keep(H.at[slot], o_h.at[slot])
            @pl.loop(0, 8)
            def _(n):
                r = pl.ds(pl.multiple_of(n * 32, 32), 32)
                v = norm_rows(H[slot, r, :]) * gains[slot, :][None]
                if slot < 2:
                    y[r, :] = v
                    yl[r, :] = v.astype(BF)
                else:
                    OUT[r, :] = v.astype(BF)
            if slot == 2: keep(OUT, o_out)
        return run

    def context_in():
        for k, (dx, dc) in enumerate(((0, 1), (1, 0), (1, 1))):
            tx = (p.x + dx) % 2; tc = (p.c + dc) % 2
            w = tx * 2 + tc
            pltpu.make_async_remote_copy(en.at[0, w], ctx.at[:, w], csem.at[k], crsem.at[w], device_id=p.dev(), device_id_type=MESH).wait_recv()

    class Ctx:
        def __getitem__(self, idx):
            if idx is Ellipsis: return ctx[...].reshape(256, 1024)
            return ctx[:, :, :, idx[1]].reshape(256, -1)
    cref = Ctx()
    def adapter():
        fetch(8).wait()
        w = wbuf[0, :, :, :, :, :, pl.ds(0, 512)].reshape(1024, 512)
        r = dot(yl[...], w)
        s = 1.0 / (1.0 + jnp.exp(-r))
        a = (r * s).astype(BF)
        ar[...] = a
        SR[...] = s * (1.0 + r * (1.0 - s))
        AT[...] = a.T
        keep(SR, o_sr); keep(AT, o_at)
    def adapter_out():
        top = wbuf[0, :, :, :, :, pl.ds(0, 16), pl.ds(512, 512)].reshape(512, 512)
        bot = wbuf[0, :, :, :, :, pl.ds(16, 16), pl.ds(512, 512)].reshape(512, 512)
        H[2, :, 0:512] = y[:, 0:512] + 4.0 * dot(ar[...], top)
        H[2, :, 512:1024] = y[:, 512:1024] + 4.0 * dot(ar[...], bot)
    def hidden(j, part):
        def run():
            t = 9 + j
            if part == 0: fetch(t).wait()
            @pl.loop(2 * part, 2 * part + 2)
            def _(n):
                ds = cols(n, 256)
                @pl.loop(0, 4)
                def _(m):
                    r = pl.ds(pl.multiple_of(m * 64, 64), 64)
                    u = dot(yl[r, :], wbuf[t % 4, :, :, :, :, :, ds].reshape(1024, 256))
                    half = 0.5 + 0.5 * lax.erf(u * 0.7071067811865476)
                    af[j, r, ds] = (u * half).astype(BF)
                    GP[j, r, ds] = half + u * (0.3989422804014327 * jnp.exp(-0.5 * u * u))
            if part == 1: keep(GP.at[j], o_gp.at[j])
        return run
    def out_cols(j):
        def run():
            fetch(13 + j).wait()
            acc = H[2, :, pl.ds(256 * j, 256)]
            for f in range(4):
                w = wo[j % 2, f].reshape(1024, 256)
                acc = acc + dot(af[f], w)
            H[2, :, pl.ds(256 * j, 256)] = acc
        return run

    E = lambda g: g * GAP + 6 + 0.6
    add(1.4, flip(x, 0))
    g0 = E(0)
    for t in (0, 1, 2): add(g0, start(t))
    for t in (0, 1, 2): add(g0 + 0.2 * t, proj(x, t, t))
    for part in range(4): add(g0 + 0.8 + 0.25 * part, attend(0, part))
    add(g0 + 1.8, flip(mix, 3))
    g1 = E(1)
    add(1.6, context_in); add(1.7, flip(cref, 1))
    for t in (3, 4, 5): add(g1, start(t))
    add(g1 + 0.1, branch(3, x, 0)); add(g1 + 0.2, norm(0)); add(g1 + 0.3, flip(yl, 2))
    add(g1 + 0.5, proj(cref, 4, 4)); add(g1 + 0.7, proj(cref, 5, 5))
    g2 = E(2)
    for t in (6, 7): add(g2, start(t))
    add(g2 + 0.01, start(8))
    add(g2 + 0.1, proj(yl, 6, 3))
    for part in range(4): add(g2 + 0.3 + 0.25 * part, attend(1, part))
    add(g2 + 1.3, flip(mix, 4)); add(g2 + 1.4, branch(7, y, 1)); add(g2 + 1.5, norm(1)); add(g2 + 1.6, flip(yl, 5))
    add(g2 + 1.7, adapter); add(g2 + 1.8, adapter_out)
    g3 = max(E(3), g2 + 1.9)
    for t in (9, 10, 11): add(g3, start(t))
    for j in range(3):
        for part in range(2): add(g3 + 0.1 + 0.3 * j + 0.15 * part, hidden(j, part))
    g4 = max(E(4), g3 + 1.1)
    add(g4, start(12)); add(g4, start(13)); add(g4, start(14))
    for part in range(2): add(g4 + 0.1 + 0.2 * part, hidden(3, part))
    add(g4 + 0.5, out_cols(0)); add(g4 + 0.7, out_cols(1))
    g5 = max(E(5), g4 + 0.9)
    add(g5, start(15)); add(g5 + 0.01, out_cols(2)); add(g5 + 0.02, start(16)); add(g5 + 0.03, out_cols(3)); add(g5 + 0.04, norm(2))
    items.sort(key=lambda q: q[:2])
    for it in items: it[2]()
    for _, _, s in streams: s.finish()
    for c_ in cs: c_.wait_send()
    for c_ in outs: c_.wait()

def forward(tokens, gains, bias, shards, encoder):
    any_ = pl.BlockSpec(memory_space=pl.ANY)
    vm = pl.BlockSpec(memory_space=pltpu.VMEM)
    V, S, D = pltpu.VMEM, jax.ShapeDtypeStruct, pltpu.SemaphoreType.DMA
    tile = (4, 2, 2, 2, 32, 1024)
    return pl.pallas_call(forward_kernel,
        out_shape=(S((13,) + tile, BF), S((4, 2, 2, 2, 128, 1024), BF), S((6, 256, 1024), BF), S((2, 16, 256, 128), F32), S((3, 256, 1024), F32),
                   S((6, 1024, 256), BF), S((512, 256), BF), S((4, 256, 1024), F32), S((256, 512), F32), S((256, 1024), BF)),
        in_specs=[vm] * 3 + [any_] * 9, out_specs=(any_,) * 10,
        scratch_shapes=[V((6, 256, 1024), BF), V((2, 16, 256, 128), F32), V((3, 256, 1024), F32), V((6, 1024, 256), BF), V((512, 256), BF),
                        V((4, 256, 1024), F32), V((256, 512), F32), V((256, 1024), BF), V((2, 4, 32, 1024), BF), V((4,) + tile, BF),
                        V((2, 4, 2, 2, 2, 128, 256), BF), V((13, 32, 1024), BF), V((128, 1024), BF), V((256, 1024), F32), V((256, 1024), BF),
                        V((256, 1024), BF), V((4, 256, 1024), BF), V((256, 512), BF),
                        D((N_STREAM, NSEND)), D((N_STREAM, NSLOT)), D((20,)), D((3,)), D((4,)), D((17,)), D((26,))],
        compiler_params=pltpu.CompilerParams(collective_id=0, has_side_effects=True, vmem_limit_bytes=60 << 20),
        name="forward")(tokens, gains, bias, *shards, encoder)

PLAN_B = [
    "nb0", "hb0", "hb1", "hb2", "hb3", "adb", "adg.0", "adg.1", "adg.2", "adg.3", "hi0", (0, "R1", 0, None), "hi1", (0, "R1", 1, None), "hi2", "hi3",
    (0, "R1", 2, None), (0, "R2", 0, None), (0, "R1", 3, None), "nb1", "t1.0", "t1.1", (0, "R2", 1, None), "t1.2", "t1.3", "mb9", (0, "R3", 0, None),
    (0, "D", 0, 3), (0, "D", 0, 2), (0, "R2", 2, None), "at10", (0, "R2", 3, None), (0, "R3", 1, None), (0, "D", 1, 3), (0, "D", 1, 2), "at11",
    (1, "R1", 0, None), (0, "R3", 2, None), (0, "D", 2, 3), (1, "R1", 1, None), (0, "U", 2, 0), "at12", (0, "D", 0, 1), (1, "R1", 2, None),
    (1, "R1", 3, None), (0, "R3", 3, None), (0, "U", 3, 0), "at13", "t2.0", "t2.1", (0, "U", 1, 0), (0, "U", 3, 1), (1, "R2", 0, None), (1, "D", 0, 3),
    "t2.2", "t2.3", "t3.0", (0, "U", 2, 1), (1, "D", 0, 2), (2, "R1", 0, None), "t3.1", "t3.2", "t3.3", "t4.0", (1, "R2", 1, None), (1, "U", 1, 0),
    (1, "D", 1, 2), (2, "R1", 1, None), (1, "D", 1, 3), (0, "U", 3, 2), (2, "R1", 2, None), (1, "D", 0, 1), "t4.1", "t4.2", (2, "R1", 3, None),
    (3, "R1", 0, None), "t4.3", (4, "R1", 0, None), (1, "R2", 2, None), (1, "D", 2, 3), (1, "U", 2, 0), (3, "R1", 3, None), (2, "R2", 0, None),
    (2, "D", 0, 3), (1, "R2", 3, None), (1, "U", 3, 0), (3, "R1", 1, None), "rb10", "cb", "rb12", (2, "D", 0, 2), (4, "R1", 1, None), (1, "U", 2, 1),
    (4, "R1", 3, None), (1, "U", 3, 1), (2, "R2", 1, None), (2, "U", 1, 0), (2, "D", 1, 3), (4, "R2", 0, None), (1, "Z3", 0, 0), (2, "D", 1, 2), "nb2",
    "t5.0", "t5.1", (0, "FIN", 0, 0), (0, "FIN", 0, 1), (2, "R2", 3, None), (2, "R2", 2, None), "t5.2", "t5.3", (2, "U", 3, 0), (1, "Z3", 0, 1),
    (4, "R1", 2, None), (1, "Z3", 0, 2), (2, "D", 0, 1), (3, "R1", 2, None), (0, "FIN", 0, 3), (2, "U", 2, 0), (2, "D", 2, 3), (4, "D", 0, 3), "mb13",
    "at00", (2, "U", 3, 1), (5, "R1", 0, None), (4, "R2", 1, None), (1, "U", 3, 2), (3, "R2", 0, None), (2, "Z3", 0, 0), (2, "U", 2, 1),
    (5, "R1", 1, None), (5, "R1", 2, None), (4, "U", 1, 0), (1, "FIN", 0, 0), (3, "R2", 1, None), (2, "Z3", 0, 1), (0, "FIN", 0, 2), "at01",
    (4, "D", 0, 2), (2, "U", 3, 2), "at02", (4, "D", 1, 3), (4, "R2", 2, None), (4, "R2", 3, None), (4, "U", 2, 0), (4, "U", 3, 0), "at03", "cs",
    "t6.0", "t6.1", (5, "R2", 0, None), (5, "D", 0, 3), (5, "D", 0, 2), (1, "Z3", 0, 3), (4, "D", 1, 2), (5, "R1", 3, None), (3, "R2", 3, None),
    (3, "R2", 2, None), (3, "R3", 0, None), (3, "D", 0, 3), "t6.2", "t6.3", (4, "D", 0, 1), (4, "U", 3, 1), "t7.0", (5, "R2", 2, None), (5, "U", 2, 1),
    (5, "U", 2, 0), (5, "D", 2, 3), (4, "U", 2, 1), (6, "R1", 0, None), "t7.1", "t7.2", "t7.3", "t8.0", "t8.1", (5, "D", 0, 1), (2, "Z3", 0, 3),
    (6, "R1", 2, None), (4, "U", 3, 2), (3, "D", 0, 2), (2, "Z3", 0, 2), (5, "R2", 1, None), (5, "D", 1, 3), (5, "U", 1, 0), (4, "Z3", 0, 1),
    (5, "R2", 3, None), (5, "U", 3, 0), (4, "Z3", 0, 0), (3, "R3", 3, None), (3, "U", 3, 0), (6, "R1", 1, None), (4, "D", 2, 3), (2, "FIN", 0, 0),
    (7, "R1", 0, None), (1, "FIN", 0, 1), (3, "D", 0, 1), (3, "R3", 2, None), (7, "R1", 2, None), (8, "R1", 0, None), (5, "U", 3, 1),
    (7, "R1", 1, None), (3, "U", 3, 1), (3, "U", 2, 0), (5, "D", 1, 2), "t8.2", "t8.3", "rb14", (4, "Z3", 0, 2), "rb15", (5, "U", 3, 2), "tok",
    (5, "Z3", 0, 0), (6, "R1", 3, None), (7, "R1", 3, None), (2, "FIN", 0, 1), (8, "R1", 1, None), (3, "U", 2, 1), (1, "FIN", 0, 2),
    (8, "R1", 2, None), (7, "R2", 0, None), (3, "R3", 1, None), (3, "U", 1, 0), (3, "D", 1, 2), (3, "D", 1, 3), (7, "D", 0, 2), (7, "D", 0, 3),
    (5, "Z3", 0, 2), (5, "Z3", 0, 1), (3, "D", 2, 3), (7, "D", 0, 1), (7, "R2", 2, None), (7, "U", 2, 1), (7, "U", 2, 0), (8, "R1", 3, None),
    (7, "R2", 1, None), (7, "U", 1, 0), (7, "D", 1, 3), (7, "D", 2, 3), (7, "D", 1, 2), (8, "R2", 0, None), (7, "R2", 3, None), (7, "U", 3, 1),
    (7, "U", 3, 0), (2, "FIN", 0, 3), (3, "U", 3, 2), (5, "FIN", 0, 2), (5, "FIN", 0, 1), (1, "FIN", 0, 3), (8, "D", 0, 2), (4, "Z3", 0, 3),
    (4, "FIN", 0, 1), (8, "D", 0, 3), (7, "Z3", 0, 2), (3, "FIN", 0, 1), (8, "R2", 3, None), (5, "Z3", 0, 3), (8, "R2", 1, None), (8, "D", 1, 2),
    (5, "FIN", 0, 0), (8, "R2", 2, None), (8, "U", 2, 0), (8, "D", 1, 3), (5, "FIN", 0, 3), (6, "R2", 1, None), (3, "FIN", 0, 2), (6, "R2", 0, None),
    (8, "U", 1, 0), (7, "U", 3, 2), (8, "D", 0, 1), (4, "FIN", 0, 2), (3, "FIN", 0, 0), (8, "D", 2, 3), (6, "R2", 2, None), (2, "FIN", 0, 2),
    (7, "Z3", 0, 0), (8, "U", 2, 1), (6, "R2", 3, None), (7, "Z3", 0, 1), (8, "U", 3, 0), (4, "FIN", 0, 3), (6, "R3", 0, None), (6, "R3", 1, None),
    (6, "R3", 2, None), (6, "D", 0, 3), (6, "D", 0, 2), (6, "D", 1, 3), (6, "D", 1, 2), (7, "FIN", 0, 1), (8, "U", 3, 2), (8, "U", 3, 1),
    (7, "Z3", 0, 3), (6, "D", 2, 3), (6, "D", 0, 1), (3, "FIN", 0, 3), (6, "U", 1, 0), (6, "R3", 3, None), (7, "FIN", 0, 2), (6, "U", 2, 0),
    (7, "FIN", 0, 3), (8, "Z3", 0, 1), (6, "U", 3, 1), (6, "U", 3, 0), (8, "Z3", 0, 0), (6, "U", 2, 1), (8, "Z3", 0, 2), (6, "FIN", 0, 0),
    (7, "FIN", 0, 0), (8, "FIN", 0, 2), (8, "FIN", 0, 1), (6, "U", 3, 2), (8, "Z3", 0, 3), (4, "FIN", 0, 0), (8, "FIN", 0, 0), (6, "FIN", 0, 3),
    (6, "FIN", 0, 1), (6, "FIN", 0, 2), (8, "FIN", 0, 3),
]


NT = 9
ORDERS = ["A", "xzy", "yzx"] * 3
NS, NR = 27, 33

class Reduce:
    def __init__(self, p, t, order, PB, L0, L1, L2, UP, DN, LX, ssem, rsem, out):
        self.p, self.t, self.order = p, t, order
        self.PB, self.L0, self.L1, self.L2, self.UP, self.DN, self.LX = PB, L0, L1, L2, UP, DN, LX
        self.ssem, self.rsem, self.out = ssem, rsem, out
        self.sends = []
        self.me = {"x": p.x, "y": p.y}
        self.flat = order == "A"
        if not self.flat: self.b1, self.b2 = order[0], order[2]
    def partner(self, b):
        return self.p.dev(**{b: 1 - self.me[b]})
    def desc(self, src, dst, k, slot, target):
        return pltpu.make_async_remote_copy(src, dst, self.ssem.at[k], self.rsem.at[slot], device_id=target, device_id_type=MESH)
    def copy(self, what, k, slot, z=None):
        def make():
            src, dst, target = what()
            return self.desc(src, dst, k, slot, target)
        make().start()
        self.sends.append((make, z))
    def arrive(self, dst, slot):
        self.desc(dst, dst, 0, slot, self.p.dev()).wait_recv()
    def finish(self, z):
        for make, at in self.sends:
            if at == z: make().wait_send()
    def sib(self, zz):
        self.copy(lambda: (self.PB.at[zz, :, :, 1 - self.p.c], self.L0.at[zz], self.p.dev(c=1 - self.p.c)), zz, zz)
    def pair(self, zz, b2name, b2v, r=pl.ds(0, 32)):
        if b2name == "y": return self.PB.at[zz, b2v, :, self.p.c, r]
        return self.PB.at[zz, :, b2v, self.p.c, r]
    def block(self, zz, r=pl.ds(0, 32), **where):
        return self.PB.at[zz, where.get("y", self.p.y), where.get("x", self.p.x), self.p.c, r]
    def mine(self, zz):
        return self.block(zz) if self.flat else self.pair(zz, self.b2, self.me[self.b2])
    def halves(self):
        return [(h, b1, b2, pl.ds(16 * h, 16)) for h, (b1, b2) in enumerate((("x", "y"), ("y", "x")))]

    def R1(self, zz):
        p = self.p
        self.arrive(self.L0.at[zz], zz)
        for yy in range(2):
            for xx in range(2):
                self.PB[zz, yy, xx, p.c] = self.PB[zz, yy, xx, p.c] + self.L0[zz, yy, xx]
        if self.flat:
            for h, b1, b2, r in self.halves():
                self.copy(lambda b2=b2, r=r: (self.pair(zz, b2, 1 - self.me[b2], r), self.L1.at[zz, :, r], self.partner(b2)), 4 + 4 * h + zz, 17 + 4 * h + zz)
        else:
            self.copy(lambda: (self.pair(zz, self.b2, 1 - self.me[self.b2]), self.L1.at[zz], self.partner(self.b2)), 4 + zz, 4 + zz)
    def R2(self, zz):
        if self.flat:
            for h, b1, b2, r in self.halves():
                self.arrive(self.L1.at[zz, :, r], 17 + 4 * h + zz)
                o = self.pair(zz, b2, self.me[b2], r)
                o[...] = o[...] + self.L1[zz, :, r]
                self.copy(lambda b1=b1, r=r: (self.block(zz, r, **{b1: 1 - self.me[b1]}), self.L2.at[zz, r], self.partner(b1)), 12 + 4 * h + zz, 25 + 4 * h + zz)
        else:
            self.arrive(self.L1.at[zz], 4 + zz)
            o = self.mine(zz)
            o[...] = o[...] + self.L1[zz]
    def R3(self, zz):
        for h, b1, b2, r in self.halves():
            self.arrive(self.L2.at[zz, r], 25 + 4 * h + zz)
            o = self.block(zz, r)
            o[...] = o[...] + self.L2[zz, r]
    def U(self, zu, z):
        o, land = self.mine(zu), self.UP.at[zu - 1]
        if 0 < z <= zu:
            self.arrive(land, 8 + zu)
            o[...] = o[...] + land[...]
        if z < zu: self.copy(lambda: (self.mine(zu), self.UP.at[zu - 1], self.p.dev(z=z + 1)), 20 + zu - 1, 8 + zu, z)
    def D(self, zd, z):
        o, land = self.mine(zd), self.DN.at[zd]
        if zd <= z < 3:
            self.arrive(land, 12 + zd)
            o[...] = o[...] + land[...]
        if z > zd: self.copy(lambda: (self.mine(zd), self.DN.at[zd], self.p.dev(z=z - 1)), 23 + zd, 12 + zd, z)
    def Z3(self, k, z):
        if z > 0: self.U(z, z)
        if z < 3: self.D(z, z)
        self.copy(lambda: (self.block(z, **{self.b1: 1 - self.me[self.b1]}), self.LX, self.partner(self.b1)), 26, 16, z)
    def FIN(self, k, z):
        v = self.block(z)
        if self.flat:
            if z > 0: self.U(z, z)
            if z < 3: self.D(z, z)
            self.out(v[...].astype(F32))
        else:
            self.arrive(self.LX, 16)
            self.out(v[...].astype(F32) + self.LX[...].astype(F32))

def run_plan(p, plan, compute, movers):
    i = 0
    while i < len(plan):
        it = plan[i]
        if isinstance(it, str):
            compute[it]()
            i += 1
        elif it[3] is None:
            getattr(movers[it[0]], it[1])(it[2])
            i += 1
        else:
            z, j = it[3], i
            while j < len(plan) and not isinstance(plan[j], str) and plan[j][3] == z: j += 1
            @pl.when(p.z == z)
            def _():
                for m, name, k, _z in plan[i:j]: getattr(movers[m], name)(k, z)
            i = j

W_ORDER = ["o0", "o1", "o2", "o3", 8, 9, 10, 11, 12, 7, 4, 5, 6, 3, 0, 1, 2]
T_ORDER = [5, 4, 1, 2, 3, 0]
NW = 3

def backward_kernel(gains, buf, gfo, qkv, P, H, T, AT, GP, SR, cot,
                    o_tok, osp, oso, ocp, oco, oai, oao, oen,
                    PB, L0, L1, L2, UPC, DNC, UPA, DNA, LX, wbuf, hb, gpb, tb, atb, srb, pb, cotb, g, gb, gr, gx, gqkv, gtok,
                    ssem, rsem, csem, crsem, wsem, hsem, gpsem, tsem, msem, qsem, psem, osem):
    p = Place()
    lo, hi = half_masks()
    def w_copy(i):
        n = W_ORDER[i]
        src = gfo.at[int(n[1])] if isinstance(n, str) else buf.at[n]
        return pltpu.make_async_copy(src, wbuf.at[i % NW], wsem.at[i])
    h_copy = lambda i: pltpu.make_async_copy(H.at[2 - i], hb.at[i % 2], hsem.at[i])
    gp_copy = lambda j: pltpu.make_async_copy(GP.at[j], gpb.at[j % 2], gpsem.at[j])
    t_copy = lambda i: pltpu.make_async_copy(T.at[T_ORDER[i]], tb.at[i % 3], tsem.at[i])
    q_copy = lambda a, j: pltpu.make_async_copy(qkv.at[3 * a + j], PB.at[6 + a, j], qsem.at[3 * a + j])
    p_copy = lambda a: pltpu.make_async_copy(P.at[a], pb, psem.at[a])
    m_copy = [pltpu.make_async_copy(cot, cotb, msem.at[0]), pltpu.make_async_copy(SR, srb, msem.at[1]), pltpu.make_async_copy(AT, atb, msem.at[2])]
    h_copy(0).start(); m_copy[0].start(); w_copy(0).start(); gp_copy(0).start(); w_copy(1).start(); gp_copy(1).start(); w_copy(2).start()
    h_copy(1).start(); m_copy[1].start(); m_copy[2].start()
    for i in range(3): t_copy(i).start()
    for j in range(3): q_copy(1, j).start()
    p_copy(1).start()
    for j in range(3): q_copy(0, j).start()
    entry_barrier(p)

    def o_ad(v):
        oai[...] = v[:, :512]
        oao[:, 0:512] = v[0:16, 512:]
        oao[:, 512:1024] = v[16:32, 512:]
    def put(ref, j=None):
        def f(v):
            if j is None: ref[...] = v
            else: ref[j] = v
        return f
    finals = [o_ad, put(oco), put(ocp, 1), put(ocp, 2), put(ocp, 0), put(oso), put(osp, 1), put(osp, 2), put(osp, 0)]
    reds = []
    nc = na = 0
    for t in range(NT):
        if ORDERS[t] == "A":
            up, dn, l2 = UPA.at[na], DNA.at[na], L2.at[na]; na += 1
        else:
            up, dn, l2 = UPC.at[nc], DNC.at[nc], None; nc += 1
        reds.append(Reduce(p, t, ORDERS[t], PB.at[t], L0.at[t], L1.at[t], l2, up, dn, LX.at[t], ssem.at[t], rsem.at[t], finals[t]))

    compute = {}
    def work(name, fn): compute[name] = fn

    def norm_back(i, first=False):
        def run():
            h_copy(i).wait()
            if first: m_copy[0].wait()
            @pl.loop(0, 8)
            def _(n):
                r = pl.ds(pl.multiple_of(n * 32, 32), 32)
                h = hb[i % 2, r, :]
                center = h - jnp.mean(h, axis=-1, keepdims=True)
                inv = lax.rsqrt(jnp.mean(center * center, axis=-1, keepdims=True) + EPS)
                nrm = center * inv
                gy = cotb[r, :].astype(F32) if first else g[r, :]
                a = gy * gains[2 - i, :][None]
                v = (a - jnp.mean(a, axis=-1, keepdims=True) - nrm * jnp.mean(a * nrm, axis=-1, keepdims=True)) * inv
                g[r, :] = v
                gb[r, :] = v.astype(BF)
            if i == 0: h_copy(2).start()
        return run

    def used(i):
        if i + NW < len(W_ORDER): w_copy(i + NW).start()

    def nt(lhs, i, fn):
        fn(dot_nt(lhs(), wbuf[i % NW]))

    def hidden_back(j):
        def run():
            w_copy(j).wait(); gp_copy(j).wait()
            def st(v):
                PB[8, j] = (gpb[j % 2] * v).astype(BF).reshape(2, 2, 2, 32, 1024)
            nt(lambda: gb[...], j, st)
            used(j)
            if j + 2 < 4: gp_copy(j + 2).start()
        return run

    def adapter_back():
        i = 4
        w_copy(i).wait(); m_copy[1].wait(); m_copy[2].wait()
        v = wbuf[i % NW, :, 512:1024].reshape(32, 32, 512)
        top, bot = v[:, :16].reshape(512, 512), v[:, 16:].reshape(512, 512)
        s = dot_nt(gb[:, 0:512], top) + dot_nt(gb[:, 512:1024], bot)
        gr[...] = (srb[...] * (4.0 * s)).astype(BF)
        wai = wbuf[i % NW, :, 0:512]
        g[...] = g[...] + dot_nt(gr[...], wai)
        used(i)

    def adapter_grads(zz):
        def run():
            if zz == 0:
                for h in range(2):
                    v = 4.0 * dot(atb[...], gb[:, 512 * h:512 * h + 512])
                    PB[0, :, :, :, :, 16 * h:16 * h + 16, 512:1024] = v.astype(BF).reshape(4, 2, 2, 2, 16, 512)
                t_copy(0).wait()
            v = dot(tb[0, pl.ds(256 * zz, 256), :], gr[...])
            PB[0, zz, :, :, :, :, 0:512] = v.astype(BF).reshape(2, 2, 2, 32, 512)
            reds[0].sib(zz)
            if zz == 3: t_copy(3).start()
        return run

    def hidden_in_back(j):
        def run():
            i = 5 + j
            w_copy(i).wait()
            def st(v): g[...] = g[...] + v
            nt(lambda: PB[8, j].reshape(256, 1024), i, st)
            used(i)
        return run

    def grad_tile(t, ti, rhs, last, zz):
        def run():
            if zz == 0 and t in (1, 2, 4, 5, 6): t_copy(ti).wait()
            PB[t, zz] = dot(tb[ti % 3, pl.ds(256 * zz, 256), :], rhs()).astype(BF).reshape(2, 2, 2, 32, 1024)
            reds[t].sib(zz)
            if zz == 3 and last and ti + 3 < 6: t_copy(ti + 3).start()
        return run

    def mix_back(i):
        def run():
            w_copy(i).wait()
            def st(v): gx[...] = v.astype(BF)
            nt(lambda: gb[...], i, st)
            used(i)
        return run

    def attend_back(a, part):
        def run():
            if part == 0:
                p_copy(a).wait()
                for j in range(3): q_copy(a, j).wait()
            u = part // 2
            @pl.loop(0, 4)
            def _(n):
                pr = (part % 2) * 4 + n
                r, cc = pl.ds(u * 128, 128), cols(pr, 128)
                q, k, v = (PB[6 + a, j, u, :, :, :, cc].reshape(128, 128) for j in range(3))
                go = pair_up(gx[r, cc], lo, hi)
                prob = pb[u * 8 + pr]
                dp = dot_nt(go, v)
                ds = (prob * (dp - jnp.sum(prob * dp, axis=-1, keepdims=True))).astype(BF)
                gqkv[0, r, cc] = (dot(side(ds), pair_up(k, lo, hi)) * 0.125).astype(BF)
                gqkv[1, r, cc] = (dot_tn(ds, pair_up(q, lo, hi)) * 0.125).astype(BF)
                gqkv[2, r, cc] = dot_tn(prob.astype(BF), go).astype(BF)
            if part == 3 and a == 1: p_copy(0).start()
        return run

    def row_back(i, j, dst):
        def run():
            w_copy(i).wait()
            nt(lambda: gqkv[j], i, dst)
            used(i)
        return run
    def to_g(v): g[...] = g[...] + v
    cs = []
    me = p.x * 2 + p.c
    def context_back():
        i = 11
        w_copy(i).wait()
        def st(v): PB[8, 0] = (ctxf[...] + v).astype(BF).reshape(2, 2, 2, 32, 1024)
        nt(lambda: gqkv[2], i, st)
        used(i)
        for k, (dx, dc) in enumerate(((0, 1), (1, 0), (1, 1))):
            tx = (p.x + dx) % 2; tc = (p.c + dc) % 2
            c_ = pltpu.make_async_remote_copy(PB.at[8, 0, :, tx, tc], oen.at[0, me], csem.at[k], crsem.at[me], device_id=p.dev(x=tx, c=tc), device_id_type=MESH)
            c_.start(); cs.append(c_)
        c_ = pltpu.make_async_copy(PB.at[8, 0, :, p.x, p.c], oen.at[0, me], osem.at[0]); c_.start(); cs.append(c_)

    ctxf = gpb.at[0]
    def ctx_part(v): ctxf[...] = v
    def context_sent():
        for c_ in cs[:3]: c_.wait_send()
        cs[3].wait()
    def tokens_back():
        i = 16
        w_copy(i).wait()
        def st(v): gtok[...] = (g[...] + v).astype(BF)
        nt(lambda: gqkv[2], i, st)
        pltpu.make_async_copy(gtok, o_tok, osem.at[1]).start()

    def tile(t, ti, rhs, last):
        for zz in range(4): work(f"t{t}.{zz}", grad_tile(t, ti, rhs, last, zz))
    work("nb0", norm_back(0, True))
    for j in range(4): work(f"hb{j}", hidden_back(j))
    work("adb", adapter_back)
    for zz in range(4): work(f"adg.{zz}", adapter_grads(zz))
    for j in range(4): work(f"hi{j}", hidden_in_back(j))
    work("nb1", norm_back(1))
    tile(1, 1, lambda: gb[...], True)
    work("mb9", mix_back(9))
    for part in range(4): work(f"at1{part}", attend_back(1, part))
    tile(2, 2, lambda: gqkv[1], False)
    tile(3, 2, lambda: gqkv[2], True)
    tile(4, 3, lambda: gqkv[0], True)
    work("rb10", row_back(10, 1, ctx_part))
    work("cb", context_back)
    work("rb12", row_back(12, 0, to_g))
    work("nb2", norm_back(2))
    tile(5, 4, lambda: gb[...], True)
    work("mb13", mix_back(13))
    for part in range(4): work(f"at0{part}", attend_back(0, part))
    work("cs", context_sent)
    tile(6, 5, lambda: gqkv[1], False)
    tile(7, 5, lambda: gqkv[2], False)
    tile(8, 5, lambda: gqkv[0], True)
    work("rb14", row_back(14, 0, to_g))
    work("rb15", row_back(15, 1, to_g))
    work("tok", tokens_back)
    run_plan(p, PLAN_B, compute, reds)
    for r in reds: r.finish(None)
    for z in range(4):
        @pl.when(p.z == z)
        def _():
            for r in reds: r.finish(z)
    pltpu.make_async_copy(gtok, o_tok, osem.at[1]).wait()
    for k, (dx, dc) in enumerate(((0, 1), (1, 0), (1, 1))):
        tx = (p.x + dx) % 2; tc = (p.c + dc) % 2
        w = tx * 2 + tc
        pltpu.make_async_remote_copy(PB.at[8, 0, :, tx, tc], oen.at[0, w], csem.at[k], crsem.at[w], device_id=p.dev(), device_id_type=MESH).wait_recv()

def backward(gains, buf, gfo, qkv, P, H, T, AT, GP, SR, cot):
    any_ = pl.BlockSpec(memory_space=pl.ANY)
    vm = pl.BlockSpec(memory_space=pltpu.VMEM)
    V, S, D = pltpu.VMEM, jax.ShapeDtypeStruct, pltpu.SemaphoreType.DMA
    ops = (gains, buf.reshape(13, 1024, 1024), gfo.reshape(4, 1024, 1024), qkv.reshape(6, 2, 2, 2, 32, 1024), P, H, T, AT, GP, SR, cot)
    return pl.pallas_call(backward_kernel,
        out_shape=(S((256, 1024), BF), S((3, 32, 1024), F32), S((32, 1024), F32), S((3, 32, 1024), F32), S((32, 1024), F32), S((32, 512), F32), S((16, 1024), F32), S((1, 4, 2, 32, 1024), BF)),
        in_specs=[vm] + [any_] * 10, out_specs=(any_,) + (vm,) * 6 + (any_,),
        scratch_shapes=[V((NT, 4, 2, 2, 2, 32, 1024), BF), V((NT, 4, 2, 2, 32, 1024), BF), V((NT, 4, 2, 32, 1024), BF), V((3, 4, 32, 1024), BF),
                        V((6, 3, 2, 32, 1024), BF), V((6, 3, 2, 32, 1024), BF), V((3, 3, 32, 1024), BF), V((3, 3, 32, 1024), BF), V((NT, 32, 1024), BF),
                        V((NW, 1024, 1024), BF), V((2, 256, 1024), F32), V((2, 256, 1024), F32), V((3, 1024, 256), BF), V((512, 256), BF), V((256, 512), F32),
                        V((16, 256, 128), F32), V((256, 1024), BF), V((256, 1024), F32), V((256, 1024), BF), V((256, 512), BF), V((256, 1024), BF),
                        V((3, 256, 1024), BF), V((256, 1024), BF),
                        D((NT, NS)), D((NT, NR)), D((3,)), D((4,)), D((17,)), D((3,)), D((4,)), D((6,)), D((3,)), D((6,)), D((2,)), D((2,))],
        compiler_params=pltpu.CompilerParams(collective_id=1, has_side_effects=True, vmem_limit_bytes=63 << 20),
        name="backward")(*ops)


def device_program(tokens, encoder, dec_lengths, enc_lengths, gains, self_proj, self_out, cross_proj, cross_out, ffn_in, ffn_out, adapt_in, adapt_out, cotangent):
    masks = [slot_masks(dec_lengths[m], enc_lengths[m], 128) for m in range(2)]
    bias = jnp.where(jnp.stack([jnp.stack([masks[u][a] for u in range(2)]) for a in range(2)]), 0.0, NEGATIVE)
    shards = (self_proj, self_out, cross_proj, cross_out, ffn_in, ffn_out, adapt_in, adapt_out)
    buf, gfo, qkv, probs, hidden, turned, act_turned, gelu_slope, silu_slope, layer_out = forward(tokens, gains, bias, shards, encoder)
    gtok, osp, oso, ocp, oco, oai, oao, oen = backward(gains, buf, gfo, qkv, probs, hidden, turned, act_turned, gelu_slope, silu_slope, cotangent)
    return (layer_out, gtok, oen, osp, oso, ocp, oco, oai, oao)


def solution(mesh):
    in_specs = (
        P(("seq", "enc"), None),
        P("seq", None, None, "enc", None),
        P(("seq", "enc"), None),
        P(("seq", "enc"), None),
        P(),
        P(None, ("seq", "enc"), None),
        P(("seq", "enc"), None),
        P(None, ("seq", "enc"), None),
        P(("seq", "enc"), None),
        P(("seq", "enc"), None),
        P(("seq", "enc"), None),
        P(("seq", "enc"), None),
        P(("seq", "enc"), None),
        P(("seq", "enc"), None),
    )
    out_specs = (
        P(("seq", "enc"), None),
        P(("seq", "enc"), None),
        P("seq", None, None, "enc", None),
        P(None, ("seq", "enc"), None),
        P(("seq", "enc"), None),
        P(None, ("seq", "enc"), None),
        P(("seq", "enc"), None),
        P(("seq", "enc"), None),
        P(("seq", "enc"), None),
    )
    fast = (mesh.shape["seq"], mesh.shape["enc"]) == (8, 4)
    return jax.shard_map(
        device_program if fast else per_device, mesh=mesh, in_specs=in_specs, out_specs=out_specs, check_vma=False
    )
```

```python
import jax
import jax.numpy as jnp
from jax import lax
from jax.experimental import pallas as pl
from jax.experimental.pallas import tpu as pltpu
from jax.sharding import PartitionSpec as P

HEADS = 16
ADAPT = 512
MICRO = 2


EPSILON = 1e-05
NEGATIVE = -1e30


def matmul(left, right):
    return jnp.dot(left, right, preferred_element_type=jnp.float32)


def matmul_tn(left, right):
    return lax.dot_general(
        left, right, (((0,), (0,)), ((), ())), preferred_element_type=jnp.float32
    )


def matmul_nt(left, right):
    return lax.dot_general(
        left, right, (((1,), (1,)), ((), ())), preferred_element_type=jnp.float32
    )


def layer_norm(hidden, gain):
    center = hidden - jnp.mean(hidden, axis=-1, keepdims=True)
    spread = jnp.mean(center * center, axis=-1, keepdims=True)
    return center * lax.rsqrt(spread + EPSILON) * gain


def norm_back(hidden, gain, grad_out):
    _, pullback = jax.vjp(lambda value: layer_norm(value, gain), hidden)
    return pullback(grad_out)[0]


def gelu_exact(value):
    return jax.nn.gelu(value, approximate=False)


def slot_masks(dec_row, enc_row, rows):
    half_rows = rows // 2
    places = lax.broadcasted_iota(jnp.int32, (rows,), 0)
    paired = dec_row[1] > 0
    second = jnp.logical_and(paired, places >= half_rows)
    anchor = jnp.where(second, half_rows, 0).astype(jnp.int32)
    dec_valid = jnp.where(second, dec_row[1], dec_row[0])
    enc_valid = jnp.where(second, enc_row[1], enc_row[0])
    key_live = places - anchor < dec_valid
    context_live = places - anchor < enc_valid
    same_slot = second[:, None] == second[None, :]
    causal = places[None, :] <= places[:, None]
    self_mask = same_slot & causal & key_live[None, :]
    cross_mask = same_slot & context_live[None, :]
    return (self_mask, cross_mask)


def split_heads(matrix):
    return matrix.reshape(matrix.shape[0], HEADS, matrix.shape[1] // HEADS)


def attend(queries, keys, values, allowed):
    depth = queries.shape[1] // HEADS
    scores = jnp.einsum(
        "qhd,khd->hqk", split_heads(queries), split_heads(keys), preferred_element_type=jnp.float32
    ) * float(depth) ** (-0.5)
    masked = jnp.where(allowed[None], scores, NEGATIVE)
    weights = jnp.exp(masked - jnp.max(masked, axis=-1, keepdims=True))
    probs = weights / jnp.sum(weights, axis=-1, keepdims=True)
    mixed = jnp.einsum(
        "hqk,khd->qhd",
        probs.astype(jnp.bfloat16),
        split_heads(values),
        preferred_element_type=jnp.float32,
    )
    return (mixed.reshape(queries.shape).astype(jnp.bfloat16), probs)


def attend_back(grad_mixed, queries, keys, values, probs):
    depth = queries.shape[1] // HEADS
    factor = float(depth) ** (-0.5)
    grad_heads = split_heads(grad_mixed)
    grad_probs = jnp.einsum(
        "qhd,khd->hqk", grad_heads, split_heads(values), preferred_element_type=jnp.float32
    )
    inner = jnp.sum(probs * grad_probs, axis=-1, keepdims=True)
    grad_scores = (probs * (grad_probs - inner)).astype(jnp.bfloat16)
    grad_query = (
        jnp.einsum(
            "hqk,khd->qhd", grad_scores, split_heads(keys), preferred_element_type=jnp.float32
        )
        * factor
    )
    grad_key = (
        jnp.einsum(
            "hqk,qhd->khd", grad_scores, split_heads(queries), preferred_element_type=jnp.float32
        )
        * factor
    )
    grad_value = jnp.einsum(
        "hqk,qhd->khd", probs.astype(jnp.bfloat16), grad_heads, preferred_element_type=jnp.float32
    )
    return (
        grad_query.reshape(queries.shape).astype(jnp.bfloat16),
        grad_key.reshape(keys.shape).astype(jnp.bfloat16),
        grad_value.reshape(values.shape).astype(jnp.bfloat16),
    )


def per_device(
    tokens,
    encoder,
    dec_lengths,
    enc_lengths,
    gains,
    self_proj,
    self_out,
    cross_proj,
    cross_out,
    ffn_in,
    ffn_out,
    adapt_in,
    adapt_out,
    cotangent,
):
    shards = (self_proj, self_out, cross_proj, cross_out, ffn_in, ffn_out, adapt_in, adapt_out)

    def obtain():
        return (
            lax.all_gather(shards[0], ("seq", "enc"), axis=1, tiled=True),
            lax.all_gather(shards[1], ("seq", "enc"), axis=0, tiled=True),
            lax.all_gather(shards[2], ("seq", "enc"), axis=1, tiled=True),
            lax.all_gather(shards[3], ("seq", "enc"), axis=0, tiled=True),
            lax.all_gather(shards[4], ("seq", "enc"), axis=0, tiled=True),
            lax.all_gather(shards[5], ("seq", "enc"), axis=0, tiled=True),
            lax.all_gather(shards[6], ("seq", "enc"), axis=0, tiled=True),
            lax.all_gather(shards[7], ("seq", "enc"), axis=0, tiled=True),
        )

    rows = tokens.shape[0] // MICRO
    width = tokens.shape[1]
    owner = lax.axis_index("enc")
    acc_self = jnp.zeros((width, 3, width), jnp.float32)
    acc_self_out = jnp.zeros((width, width), jnp.float32)
    acc_cross = jnp.zeros((width, 3, width), jnp.float32)
    acc_cross_out = jnp.zeros((width, width), jnp.float32)
    acc_adapt_in = jnp.zeros((width, ADAPT), jnp.float32)
    acc_adapt_out = jnp.zeros((ADAPT, width), jnp.float32)
    outputs = []
    grad_rows = []
    grad_contexts = []
    for micro_index in range(MICRO):
        w_self, w_self_out, w_cross, w_cross_out, w_ffn_in, w_ffn_out, w_adapt_in, w_adapt_out = (
            obtain()
        )
        lower = micro_index * rows
        token_rows = tokens[lower : lower + rows]
        self_mask, cross_mask = slot_masks(dec_lengths[micro_index], enc_lengths[micro_index], rows)
        pieces = encoder[0, :, micro_index]
        context = lax.dynamic_index_in_dim(
            lax.all_gather(pieces, "enc", axis=1, tiled=True), owner, 0, keepdims=False
        )
        self_query = matmul(token_rows, w_self[0]).astype(jnp.bfloat16)
        self_key = matmul(token_rows, w_self[1]).astype(jnp.bfloat16)
        self_value = matmul(token_rows, w_self[2]).astype(jnp.bfloat16)
        self_mix, self_probs = attend(self_query, self_key, self_value, self_mask)
        first_sum = token_rows.astype(jnp.float32) + matmul(self_mix, w_self_out)
        first_norm = layer_norm(first_sum, gains[0])
        first_low = first_norm.astype(jnp.bfloat16)
        cross_query = matmul(first_low, w_cross[0]).astype(jnp.bfloat16)
        cross_key = matmul(context, w_cross[1]).astype(jnp.bfloat16)
        cross_value = matmul(context, w_cross[2]).astype(jnp.bfloat16)
        cross_mix, cross_probs = attend(cross_query, cross_key, cross_value, cross_mask)
        second_sum = first_norm + matmul(cross_mix, w_cross_out)
        second_norm = layer_norm(second_sum, gains[1])
        second_low = second_norm.astype(jnp.bfloat16)
        ffn_pre = matmul(second_low, w_ffn_in)
        ffn_act = gelu_exact(ffn_pre).astype(jnp.bfloat16)
        adapt_pre = matmul(second_low, w_adapt_in)
        adapt_act = jax.nn.silu(adapt_pre).astype(jnp.bfloat16)
        third_sum = second_norm + matmul(ffn_act, w_ffn_out) + 4.0 * matmul(adapt_act, w_adapt_out)
        outputs.append(layer_norm(third_sum, gains[2]).astype(jnp.bfloat16))
        w_self, w_self_out, w_cross, w_cross_out, w_ffn_in, w_ffn_out, w_adapt_in, w_adapt_out = (
            obtain()
        )
        grad_third = norm_back(
            third_sum, gains[2], cotangent[lower : lower + rows].astype(jnp.float32)
        )
        grad_branch = grad_third.astype(jnp.bfloat16)
        _, gelu_pull = jax.vjp(gelu_exact, ffn_pre)
        grad_ffn_pre = gelu_pull(matmul_nt(grad_branch, w_ffn_out))[0].astype(jnp.bfloat16)
        grad_adapt_act = matmul_nt(grad_branch, w_adapt_out) * 4.0
        _, silu_pull = jax.vjp(jax.nn.silu, adapt_pre)
        grad_adapt_pre = silu_pull(grad_adapt_act)[0].astype(jnp.bfloat16)
        acc_adapt_out = acc_adapt_out + matmul_tn(adapt_act, grad_branch) * 4.0
        acc_adapt_in = acc_adapt_in + matmul_tn(second_low, grad_adapt_pre)
        grad_second = (
            grad_third + matmul_nt(grad_ffn_pre, w_ffn_in) + matmul_nt(grad_adapt_pre, w_adapt_in)
        )
        grad_second_sum = norm_back(second_sum, gains[1], grad_second)
        grad_cross_branch = grad_second_sum.astype(jnp.bfloat16)
        acc_cross_out = acc_cross_out + matmul_tn(cross_mix, grad_cross_branch)
        grad_cross_mix = matmul_nt(grad_cross_branch, w_cross_out).astype(jnp.bfloat16)
        grad_cq, grad_ck, grad_cv = attend_back(
            grad_cross_mix, cross_query, cross_key, cross_value, cross_probs
        )
        acc_cross = acc_cross + jnp.stack(
            [
                matmul_tn(first_low, grad_cq),
                matmul_tn(context, grad_ck),
                matmul_tn(context, grad_cv),
            ],
            axis=1,
        )
        grad_context = matmul_nt(grad_ck, w_cross[1]) + matmul_nt(grad_cv, w_cross[2])
        holder = jnp.zeros((lax.axis_size("enc"),) + grad_context.shape, jnp.float32)
        holder = lax.dynamic_update_index_in_dim(holder, grad_context, owner, 0)
        returned = lax.psum_scatter(
            holder.astype(jnp.bfloat16), "enc", scatter_dimension=1, tiled=True
        )
        grad_contexts.append(returned)
        grad_first = grad_second_sum + matmul_nt(grad_cq, w_cross[0])
        grad_first_sum = norm_back(first_sum, gains[0], grad_first)
        grad_self_branch = grad_first_sum.astype(jnp.bfloat16)
        acc_self_out = acc_self_out + matmul_tn(self_mix, grad_self_branch)
        grad_self_mix = matmul_nt(grad_self_branch, w_self_out).astype(jnp.bfloat16)
        grad_sq, grad_sk, grad_sv = attend_back(
            grad_self_mix, self_query, self_key, self_value, self_probs
        )
        acc_self = acc_self + jnp.stack(
            [
                matmul_tn(token_rows, grad_sq),
                matmul_tn(token_rows, grad_sk),
                matmul_tn(token_rows, grad_sv),
            ],
            axis=1,
        )
        grad_input = (
            grad_first_sum
            + matmul_nt(grad_sq, w_self[0])
            + matmul_nt(grad_sk, w_self[1])
            + matmul_nt(grad_sv, w_self[2])
        )
        grad_rows.append(grad_input.astype(jnp.bfloat16))
    summed = (
        lax.psum_scatter(acc_self, ("seq", "enc"), scatter_dimension=0, tiled=True),
        lax.psum_scatter(acc_self_out, ("seq", "enc"), scatter_dimension=0, tiled=True),
        lax.psum_scatter(acc_cross, ("seq", "enc"), scatter_dimension=0, tiled=True),
        lax.psum_scatter(acc_cross_out, ("seq", "enc"), scatter_dimension=0, tiled=True),
        lax.psum_scatter(acc_adapt_in, ("seq", "enc"), scatter_dimension=0, tiled=True),
        lax.psum_scatter(acc_adapt_out, ("seq", "enc"), scatter_dimension=0, tiled=True),
    )
    layer_out = jnp.concatenate(outputs, axis=0)
    grad_tokens = jnp.concatenate(grad_rows, axis=0)
    grad_encoder = jnp.stack(grad_contexts, axis=1)[None]
    grad_self_proj = jnp.transpose(summed[0], (1, 0, 2))
    grad_cross_proj = jnp.transpose(summed[2], (1, 0, 2))
    return (
        layer_out,
        grad_tokens,
        grad_encoder,
        grad_self_proj,
        summed[1],
        grad_cross_proj,
        summed[3],
        summed[4],
        summed[5],
    )


MESH = pl.DeviceIdType.MESH
class Place:
    def __init__(self):
        seq, enc = lax.axis_index("seq"), lax.axis_index("enc")
        self.z, self.y, self.x, self.c = seq // 2, seq % 2, enc // 2, enc % 2
        self.up, self.down = jnp.minimum(self.z + 1, 3), jnp.maximum(self.z - 1, 0)
        self.step = jnp.where(self.z < 2, 1, -1)
    def dev(self, z=None, y=None, x=None, c=None):
        z = self.z if z is None else z
        y = self.y if y is None else y
        x = self.x if x is None else x
        c = self.c if c is None else c
        return (z * 2 + y, x * 2 + c)

def entry_barrier(p):
    bar = pltpu.get_barrier_semaphore()
    def sig(d):
        pl.semaphore_signal(bar, inc=1, device_id=d, device_id_type=MESH)
    sig(p.dev(c=1 - p.c)); sig(p.dev(x=1 - p.x)); sig(p.dev(y=1 - p.y)); sig(p.dev(x=1 - p.x, c=1 - p.c))
    @pl.when(p.z < 3)
    def _(): sig(p.dev(z=p.up))
    @pl.when(p.z > 0)
    def _(): sig(p.dev(z=p.down))
    peers = 4 + (p.z < 3).astype(jnp.int32) + (p.z > 0).astype(jnp.int32)
    return lambda: pl.semaphore_wait(bar, peers)

ALL4 = pl.ds(0, 4)
ALL2 = pl.ds(0, 2)

class Stream:
    def __init__(self, p, own, view, order, ssem, rsem):
        self.p, self.own, self.view, self.order, self.ssem, self.rsem = p, own, view, order, ssem, rsem
        self.flat = order[0] == "z"
        self.b1, self.b2 = (order[1], order[2]) if self.flat else (order[0], order[2])
        self.me = {"x": p.x, "y": p.y}
        self.sends = [[], []]

    def source(self, r, kind):
        p = self.p
        return p.z - p.step if kind == 1 and r == 3 else p.z + p.step * r

    def unit(self, z, c=None, **where):
        w = dict(self.me) if self.flat else {**self.me, self.b1: ALL2}
        w.update(where)
        return self.view(z, w["y"], w["x"], self.p.c if c is None else c)

    def partner(self, b):
        return self.p.dev(**{b: 1 - self.me[b]})

    def copy(self, kind, slot, what):
        k = len(self.sends[kind])
        def make():
            src, dst, target = what()
            return pltpu.make_async_remote_copy(src, dst, self.ssem.at[k], self.rsem.at[slot()], device_id=target, device_id_type=MESH)
        make().start()
        self.sends[kind].append(make)

    def arrive(self, where, slot):
        pltpu.make_async_remote_copy(where, where, self.ssem.at[0], self.rsem.at[slot], device_id=self.p.dev(), device_id_type=MESH).wait_recv()

    def finish(self, kind):
        for make in self.sends[kind]: make().wait_send()

    def along(self, kind, r, way, src=None):
        p = self.p
        def what():
            u = self.unit(self.source(r, kind))
            return u if src is None else src, u, p.dev(z=p.z + way * p.step)
        self.copy(kind, lambda: self.source(r, kind), what)

    def across(self, kind, r, src=None):
        b = self.b1 if self.flat else self.b2
        def what():
            u = self.unit(self.source(r, kind))
            return u if src is None else src, u, self.partner(b)
        self.copy(kind, lambda: 4 + self.source(r, kind), what)

    def P0(self, r, kind):
        if self.flat:
            self.along(kind, 0, 1, self.own)
            if kind == 1: self.along(kind, 0, -1, self.own)
            self.across(kind, 0, self.own)
        else:
            self.copy(kind, lambda: 8, lambda: (self.own, self.unit(self.p.z, **self.me), self.partner(self.b1)))
    def E0(self, r, kind):
        self.arrive(self.unit(self.p.z, **{self.b1: 1 - self.me[self.b1]}), 8)
        self.along(kind, 0, 1)
        if kind == 1: self.along(kind, 0, -1)
        self.across(kind, 0)
    def H(self, r, kind):
        z = self.source(r, kind)
        self.arrive(self.unit(z), z)
        if kind == 1: self.along(kind, r, -1 if r < 3 else 1)
        self.across(kind, r)
    def E(self, r, kind):
        z = self.source(r, kind)
        self.arrive(self.unit(z, **{self.b1: 1 - self.me[self.b1]}), 4 + z)
        def what():
            u = self.unit(self.source(r, kind), **{self.b1: ALL2})
            return u, u, self.partner(self.b2)
        self.copy(kind, lambda: 8 + self.source(r, kind), what)
    def plane(self, far, c=None):
        return self.unit(ALL4, c, **{self.b1: ALL2, self.b2: 1 - self.me[self.b2] if far else self.me[self.b2]})
    def F0(self, r, kind):
        self.copy(kind, lambda: 12, lambda: (self.plane(False), self.plane(False), self.p.dev(c=1 - self.p.c)))
    def F5(self, r, kind):
        for zz in range(4):
            self.arrive(self.unit(zz, **{self.b1: ALL2, self.b2: 1 - self.me[self.b2]}), (8 if self.flat else 4) + zz)
        self.copy(kind, lambda: 13, lambda: (self.plane(True), self.plane(True), self.p.dev(c=1 - self.p.c)))
    def L(self, r, kind):
        self.arrive(self.plane(False, 1 - self.p.c), 12)
        self.arrive(self.plane(True, 1 - self.p.c), 13)

def run_plan(plan, compute, movers, guards):
    i = 0
    while i < len(plan):
        it = plan[i]
        if isinstance(it, str):
            compute[it]()
            i += 1
        elif it[3] is None:
            getattr(movers[it[0]], it[1])(it[2])
            i += 1
        else:
            j = i
            while j < len(plan) and not isinstance(plan[j], str) and plan[j][3] == it[3]: j += 1
            @pl.when(guards[it[3]])
            def _():
                for m, name, k, kind in plan[i:j]: getattr(movers[m], name)(k, kind)
            i = j


PLAN_F = [
    (0, "P0", 0, 0), (0, "P0", 0, 1), (1, "P0", 0, 0), (1, "P0", 0, 1), (2, "P0", 0, 0), (3, "P0", 0, 0), (2, "P0", 0, 1), (4, "P0", 0, 0),
    (3, "P0", 0, 1), (4, "P0", 0, 1), (5, "P0", 0, 0), (6, "P0", 0, 0), (5, "P0", 0, 1), (7, "P0", 0, 0), (8, "P0", 0, 0), (6, "P0", 0, 1),
    (7, "P0", 0, 1), (9, "P0", 0, 0), (0, "H", 1, 1), (0, "H", 1, 0), "own", (0, "E", 0, 0), (0, "H", 3, 1), (1, "E", 0, 0), (0, "E", 0, 1),
    (10, "P0", 0, 0), (1, "E", 0, 1), (11, "P0", 0, 0), (1, "H", 1, 1), (1, "H", 1, 0), (12, "P0", 0, 0), (1, "H", 3, 1), (13, "P0", 0, 0),
    (8, "P0", 0, 1), (2, "E0", 0, 0), (2, "E0", 0, 1), (4, "H", 1, 0), (3, "E0", 0, 0), (3, "E0", 0, 1), (14, "P0", 0, 0), (4, "E", 0, 0),
    (4, "H", 1, 1), (5, "H", 1, 0), (5, "E", 0, 0), (4, "H", 3, 1), (15, "P0", 0, 0), (4, "E", 0, 1), (16, "P0", 0, 0), (0, "H", 2, 1), (0, "H", 2, 0),
    (5, "H", 1, 1), (17, "P0", 0, 0), (5, "H", 3, 1), (18, "P0", 0, 0), (1, "H", 2, 0), (1, "H", 2, 1), (6, "E0", 0, 0), (5, "E", 0, 1),
    (7, "E0", 0, 0), (6, "E0", 0, 1), (19, "P0", 0, 0), (8, "H", 1, 0), (7, "E0", 0, 1), (8, "E", 0, 0), (9, "E", 0, 0), (0, "E", 1, 1),
    (20, "P0", 0, 0), (8, "H", 1, 1), (0, "E", 1, 0), (0, "E", 3, 1), (21, "P0", 0, 0), (8, "H", 3, 1), (22, "P0", 0, 0), (9, "P0", 0, 1),
    (23, "P0", 0, 0), (9, "H", 3, 1), (10, "P0", 0, 1), (1, "E", 1, 1), (11, "P0", 0, 1), (12, "P0", 0, 1), (1, "E", 3, 1), (12, "H", 3, 1),
    (2, "H", 1, 0), (2, "H", 1, 1), (11, "E0", 0, 0), (8, "E", 0, 1), (13, "P0", 0, 1), (10, "E0", 0, 0), (2, "H", 3, 1), (1, "E", 1, 0),
    (13, "H", 3, 1), (14, "P0", 0, 1), (12, "E", 0, 0), (15, "P0", 0, 1), (13, "E", 0, 0), (16, "P0", 0, 1), (17, "P0", 0, 1), (4, "E", 1, 0),
    (18, "P0", 0, 1), (19, "P0", 0, 1), (20, "P0", 0, 1), (3, "H", 1, 0), (3, "H", 1, 1), (21, "P0", 0, 1), (4, "H", 2, 0), (3, "H", 3, 1),
    (4, "H", 2, 1), (4, "E", 1, 1), (0, "H", 3, 0), (5, "H", 2, 1), (4, "E", 3, 1), (16, "H", 3, 1), (5, "E", 1, 1), (5, "H", 2, 0), (17, "H", 3, 1),
    (0, "E", 2, 1), (0, "F0", 0, 1), (5, "E", 3, 1), (1, "H", 3, 0), (22, "P0", 0, 1), (23, "P0", 0, 1), "flip0", (14, "E0", 0, 0), (1, "E", 2, 1),
    (1, "F0", 0, 1), (5, "E", 1, 0), "ctxsend", (6, "H", 1, 1), "masks", (6, "H", 3, 1), (15, "E0", 0, 0), (6, "H", 1, 0), (16, "E", 0, 0),
    (17, "E", 0, 0), (0, "E", 2, 0), (1, "E", 2, 0), (7, "H", 1, 1), (8, "E", 1, 1), (7, "H", 3, 1), (18, "E0", 0, 0), (8, "H", 2, 1), (8, "E", 3, 1),
    (9, "H", 1, 1), (7, "H", 1, 0), (20, "H", 3, 1), (9, "H", 2, 1), (8, "H", 2, 0), (10, "E0", 0, 1), (9, "E", 0, 1), (12, "H", 1, 1), (9, "H", 1, 0),
    (21, "H", 3, 1), (9, "E", 3, 1), (12, "H", 2, 1), (12, "H", 1, 0), (19, "E0", 0, 0), (13, "H", 1, 1), (8, "E", 1, 0), (12, "E", 0, 1),
    (11, "E0", 0, 1), (11, "H", 3, 1), (2, "H", 2, 0), (12, "E", 3, 1), (20, "E", 0, 0), (2, "H", 2, 1), (13, "H", 1, 0), (22, "E0", 0, 0),
    (2, "F0", 0, 1), (21, "E", 0, 0), (10, "H", 3, 1), (16, "H", 1, 0), (13, "H", 2, 1), (23, "E0", 0, 0), (14, "E0", 0, 1), (17, "H", 1, 0),
    (16, "H", 1, 1), (16, "E", 0, 1), (17, "H", 1, 1), (20, "H", 1, 0), (13, "E", 0, 1), (20, "H", 1, 1), (18, "E0", 0, 1), (14, "H", 3, 1),
    (20, "E", 0, 1), (21, "H", 1, 1), (3, "H", 2, 0), (21, "H", 1, 0), (13, "E", 3, 1), (3, "H", 2, 1), (4, "H", 3, 0), (3, "F0", 0, 1),
    (16, "H", 2, 1), (5, "H", 3, 0), (15, "E0", 0, 1), (15, "H", 3, 1), (17, "H", 2, 1), (17, "E", 0, 1), (18, "H", 3, 1), (19, "E0", 0, 1),
    (6, "H", 2, 0), (4, "E", 2, 1), (4, "F0", 0, 1), (5, "E", 2, 0), (21, "E", 0, 1), (6, "H", 2, 1), (6, "F0", 0, 1), (1, "E", 3, 0), (16, "E", 3, 1),
    (1, "F0", 0, 0), (19, "H", 3, 1), (5, "E", 2, 1), (5, "F0", 0, 1), (7, "H", 2, 0), (7, "H", 2, 1), (8, "H", 3, 0), (7, "F0", 0, 1),
    (20, "H", 2, 1), (9, "H", 2, 0), (22, "E0", 0, 1), (17, "E", 3, 1), (22, "H", 3, 1), (4, "E", 2, 0), (9, "H", 3, 0), (0, "E", 3, 0),
    (1, "F5", 0, 1), (0, "F0", 0, 0), (0, "F5", 0, 1), (23, "E0", 0, 1), (10, "H", 1, 1), (23, "H", 3, 1), (1, "L", 0, 1), (21, "H", 2, 1),
    (10, "H", 1, 0), (0, "L", 0, 1), (12, "H", 2, 0), (12, "H", 3, 0), (13, "H", 2, 0), (11, "H", 1, 1), "ctxin", "flip1", (11, "H", 1, 0),
    (9, "E", 1, 0), (11, "H", 2, 1), (11, "F0", 0, 1), (2, "H", 3, 0), (2, "F0", 0, 0), (9, "E", 1, 1), (10, "H", 2, 1), (8, "E", 2, 0),
    (13, "H", 3, 0), (10, "F0", 0, 1), (9, "E", 2, 1), (9, "F0", 0, 1), (12, "E", 1, 0), (8, "E", 2, 1), (8, "F0", 0, 1), (20, "E", 3, 1),
    (14, "H", 1, 1), (14, "H", 1, 0), (13, "E", 1, 0), (16, "H", 2, 0), (21, "E", 3, 1), (17, "H", 2, 0), (12, "E", 1, 1), (13, "E", 1, 1),
    (20, "H", 2, 0), (17, "E", 1, 0), (18, "H", 1, 1), (16, "E", 1, 0), (21, "E", 1, 0), (12, "E", 2, 1), (12, "F0", 0, 1), (5, "E", 3, 0),
    (5, "F0", 0, 0), (18, "H", 1, 0), (20, "E", 1, 0), (14, "H", 2, 1), (21, "H", 2, 0), (14, "F0", 0, 1), (9, "E", 2, 0), (2, "F5", 0, 1),
    (15, "H", 1, 1), (3, "H", 3, 0), (3, "F0", 0, 0), (4, "E", 3, 0), (4, "F0", 0, 0), (16, "H", 3, 0), (9, "E", 3, 0), (9, "F0", 0, 0),
    (16, "E", 1, 1), (2, "L", 0, 1), (0, "F5", 0, 0), (13, "E", 2, 1), (13, "F0", 0, 1), (1, "F5", 0, 0), (15, "H", 2, 1), (15, "F0", 0, 1),
    (15, "H", 1, 0), (20, "E", 1, 1), (17, "H", 3, 0), (0, "L", 0, 0), (1, "L", 0, 0), "w0", (18, "H", 2, 1), (18, "F0", 0, 1), (13, "E", 2, 0),
    (8, "E", 3, 0), (8, "F0", 0, 0), "proj0", (17, "E", 1, 1), (12, "E", 2, 0), (19, "H", 1, 0), (12, "E", 3, 0), (3, "F5", 0, 1), (12, "F0", 0, 0),
    (19, "H", 1, 1), (16, "E", 2, 1), (2, "F5", 0, 0), (16, "F0", 0, 1), (6, "H", 3, 0), (6, "F0", 0, 0), (3, "L", 0, 1), (13, "E", 3, 0),
    (13, "F0", 0, 0), (19, "H", 2, 1), (2, "L", 0, 0), "w1", (19, "F0", 0, 1), (7, "H", 3, 0), (7, "F0", 0, 0), (22, "H", 1, 1), "proj1",
    (20, "H", 3, 0), (16, "E", 2, 0), (20, "E", 2, 0), (22, "H", 2, 1), (22, "H", 1, 0), (22, "F0", 0, 1), (17, "E", 2, 0), (23, "H", 1, 0),
    (17, "E", 2, 1), (17, "F0", 0, 1), (21, "E", 1, 1), (23, "H", 1, 1), (23, "H", 2, 1), (23, "F0", 0, 1), (5, "F5", 0, 0), (10, "H", 2, 0),
    (21, "H", 3, 0), (5, "L", 0, 0), (4, "F5", 0, 1), (21, "E", 2, 0), (11, "H", 2, 0), (6, "F5", 0, 1), (3, "F5", 0, 0), (4, "L", 0, 1),
    (4, "F5", 0, 0), (16, "E", 3, 0), (5, "F5", 0, 1), (16, "F0", 0, 0), (17, "E", 3, 0), (17, "F0", 0, 0), (9, "F5", 0, 0), (6, "L", 0, 1),
    (11, "H", 3, 0), (8, "F5", 0, 0), (3, "L", 0, 0), (11, "F0", 0, 0), "w2", (5, "L", 0, 1), (4, "L", 0, 0), "w3", (7, "F5", 0, 1), "proj2",
    (20, "E", 2, 1), (20, "F0", 0, 1), (9, "L", 0, 0), (10, "H", 3, 0), (10, "F0", 0, 0), (8, "L", 0, 0), (12, "F5", 0, 0), "at00", (7, "L", 0, 1),
    "at01", (21, "E", 2, 1), (21, "F0", 0, 1), (6, "F5", 0, 0), (12, "L", 0, 0), (14, "H", 2, 0), "at02", (10, "F5", 0, 1), (13, "F5", 0, 0),
    (18, "H", 2, 0), (8, "F5", 0, 1), "at03", (10, "L", 0, 1), (6, "L", 0, 0), (8, "L", 0, 1), (7, "F5", 0, 0), (13, "L", 0, 0), (14, "H", 3, 0),
    (14, "F0", 0, 0), (20, "E", 3, 0), (11, "F5", 0, 1), (20, "F0", 0, 0), "flip3", "branch3", "norm0", (11, "L", 0, 1), (9, "F5", 0, 1),
    (7, "L", 0, 0), (15, "H", 2, 0), (16, "F5", 0, 0), (21, "E", 3, 0), (21, "F0", 0, 0), "flip2", "w4", "w5", (9, "L", 0, 1), "w6", (15, "H", 3, 0),
    (15, "F0", 0, 0), (16, "L", 0, 0), "proj4", (10, "F5", 0, 0), "proj5", "proj6", (18, "H", 3, 0), (18, "F0", 0, 0), (17, "F5", 0, 0), "at10",
    (12, "F5", 0, 1), (10, "L", 0, 0), "at11", (12, "L", 0, 1), (13, "F5", 0, 1), (14, "F5", 0, 1), (11, "F5", 0, 0), (17, "L", 0, 0), (19, "H", 2, 0),
    "at12", (13, "L", 0, 1), (15, "F5", 0, 1), (14, "F5", 0, 0), (19, "H", 3, 0), (19, "F0", 0, 0), (11, "L", 0, 0), (22, "H", 2, 0), "at13",
    (14, "L", 0, 1), (15, "L", 0, 1), (18, "F5", 0, 1), (20, "F5", 0, 0), (14, "L", 0, 0), (21, "F5", 0, 0), (22, "H", 3, 0), (22, "F0", 0, 0),
    "flip4", (23, "H", 2, 0), "w7", (16, "F5", 0, 1), "w8", (15, "F5", 0, 0), (18, "F5", 0, 0), (20, "L", 0, 0), (23, "H", 3, 0), (23, "F0", 0, 0),
    (21, "L", 0, 0), (18, "L", 0, 1), "branch7", (16, "L", 0, 1), (19, "F5", 0, 1), "norm1", (22, "F5", 0, 1), "w9", "w10", (17, "F5", 0, 1),
    (20, "F5", 0, 1), (15, "L", 0, 0), (22, "F5", 0, 0), "flip5", (18, "L", 0, 0), "adapter", (19, "L", 0, 1), "adapter_out", (19, "F5", 0, 0),
    (17, "L", 0, 1), (22, "L", 0, 0), (22, "L", 0, 1), "hid0", "hid1", (20, "L", 0, 1), (23, "F5", 0, 1), "w11", "w12", "w13", (19, "L", 0, 0),
    (23, "F5", 0, 0), (21, "F5", 0, 1), "w14", "hid2", (23, "L", 0, 1), (23, "L", 0, 0), "hid3", (21, "L", 0, 1), "out0", "out1", "w15", "w16", "out2",
    "out3", "norm2",
]

F32, BF = jnp.float32, jnp.bfloat16
NSLOT, NSEND = 14, 19
N_STREAM = 24
EPS = 1e-05

def dot(a, b):
    return jnp.dot(a, b, preferred_element_type=F32)

def dot_nt(a, b):
    return lax.dot_general(a, b, (((1,), (1,)), ((), ())), preferred_element_type=F32)

def dot_tn(a, b):
    return lax.dot_general(a, b, (((0,), (0,)), ((), ())), preferred_element_type=F32)

def cols(n, width):
    return pl.ds(pl.multiple_of(n * width, width), width)

def norm_rows(h):
    center = h - jnp.mean(h, axis=-1, keepdims=True)
    spread = jnp.mean(center * center, axis=-1, keepdims=True)
    return center * lax.rsqrt(spread + EPS)

def half_masks():
    lane = lax.broadcasted_iota(jnp.int32, (1, 128), 1)
    lo = jnp.where(lane < 64, 1.0, 0.0)
    return lo.astype(BF), (1.0 - lo).astype(BF)

def pair_up(m, lo, hi):
    return jnp.concatenate([m * lo, m * hi], axis=0)

def side(m):
    return jnp.concatenate([m[:128], m[128:]], axis=1)

def forward_kernel(x, gains, dlen, elen, sp, so, cp, co, fi, fo, ai, ao, en,
                   buf, gfo, o_qkv, o_p, o_h, o_t, o_at, o_gp, o_sr, o_out,
                   qkv, P, H, T, AT, GP, SR, OUT, ctx, wbuf, wo, own, ownf, y, yl, mix, af, ar, bias,
                   ssem, rsem, lsem, csem, crsem, wsem, osem):
    p = Place()
    neighbours_in = entry_barrier(p)
    loc = []
    def put(src, dst):
        c_ = pltpu.make_async_copy(src, dst, lsem.at[len(loc)]); c_.start(); loc.append(c_)
    for j, t in enumerate((0, 1, 2)): put(sp.at[j], own.at[t])
    put(so, own.at[3])
    for j, t in ((1, 4), (2, 5), (0, 6)): put(cp.at[j], own.at[t])
    put(co, own.at[7])
    put(ai, own.at[8, :, pl.ds(0, 512)])
    put(ao.at[:, pl.ds(0, 512)], own.at[8, pl.ds(0, 16), pl.ds(512, 512)])
    put(ao.at[:, pl.ds(512, 512)], own.at[8, pl.ds(16, 16), pl.ds(512, 512)])
    for j in range(4): put(fi.at[:, pl.ds(1024 * j, 1024)], own.at[9 + j])
    put(fo, ownf)
    me = p.x * 2 + p.c
    put(en.at[0, me], ctx.at[:, me])
    for c_ in loc: c_.wait()
    n_in = len(loc)
    c1 = pltpu.make_async_copy(own, buf.at[:, p.z, p.y, p.x, p.c], lsem.at[n_in]); c1.start()
    c2 = pltpu.make_async_copy(ownf, gfo.at[p.z, p.y, p.x, p.c], lsem.at[n_in + 1]); c2.start()
    neighbours_in()
    streams = []
    for t in range(17):
        R = 32 if t < 13 else 128
        i = t % 3
        rows = [(0, R // 2, "zxy"), (R // 2, R // 2, "zyx")] if i == 0 else [(0, R, "xzy" if i == 1 else "yzx")]
        if t == 16: rows = [(0, R // 2, "xzy"), (R // 2, R // 2, "yzx")]
        for r0, nr, order in rows:
            n = len(streams)
            if t < 13:
                mine = own.at[t, pl.ds(r0, nr)]
                view = lambda z, y_, x_, c, t=t, r0=r0, nr=nr: buf.at[t, z, y_, x_, c, pl.ds(r0, nr)]
            else:
                mine = ownf.at[pl.ds(r0, nr), pl.ds(256 * (t - 13), 256)]
                view = lambda z, y_, x_, c, j=t - 13, r0=r0, nr=nr: gfo.at[z, y_, x_, c, pl.ds(r0, nr), pl.ds(256 * j, 256)]
            streams.append(Stream(p, mine, view, order, ssem.at[n], rsem.at[n]))
    ends = (p.z == 0) | (p.z == 3)
    guards = [ends, jnp.logical_not(ends)]

    def fetch(t):
        if t < 13: return pltpu.make_async_copy(buf.at[t], wbuf.at[t % 4], wsem.at[t])
        j = t - 13
        return pltpu.make_async_copy(gfo.at[:, :, :, :, :, pl.ds(256 * j, 256)], wo.at[j % 2], wsem.at[t])
    def start(t): return lambda: fetch(t).start()
    outs = []
    def keep(src, dst):
        c_ = pltpu.make_async_copy(src, dst, osem.at[len(outs)]); c_.start(); outs.append(c_)
    lo, hi = half_masks()

    def mm(lhs, t, fn):
        fn(dot(lhs[...], wbuf[t % 4].reshape(1024, 1024)))

    def proj(lhs, t, slot):
        def run():
            fetch(t).wait()
            def st(v): qkv[slot] = v.astype(BF)
            mm(lhs, t, st)
            keep(qkv.at[slot], o_qkv.at[slot])
        return run

    def flip(src, slot):
        def run():
            @pl.loop(0, 4)
            def _(n):
                T[slot, cols(n, 256), :] = src[:, cols(n, 256)].T
            keep(T.at[slot], o_t.at[slot])
        return run

    def attend(a, part):
        def run():
            u = part // 2
            @pl.loop(0, 4)
            def _(n):
                pr = (part % 2) * 4 + n
                r, cc = pl.ds(u * 128, 128), cols(pr, 128)
                q, k, v = (qkv[3 * a + j, r, cc] for j in range(3))
                b = bias[a, u]
                s = dot_nt(pair_up(q, lo, hi), k) * 0.125 + jnp.concatenate([b, b], axis=0)
                e = jnp.exp(s - jnp.max(s, axis=-1, keepdims=True))
                pr_ = e / jnp.sum(e, axis=-1, keepdims=True)
                P[a, u * 8 + pr] = pr_
                mix[r, cc] = dot(side(pr_.astype(BF)), pair_up(v, lo, hi)).astype(BF)
            if part == 3: keep(P.at[a], o_p.at[a])
        return run

    def branch(t, base, slot):
        def run():
            fetch(t).wait()
            def st(v): H[slot] = base[...].astype(F32) + v
            mm(mix, t, st)
        return run

    def norm(slot):
        def run():
            keep(H.at[slot], o_h.at[slot])
            @pl.loop(0, 8)
            def _(n):
                r = pl.ds(pl.multiple_of(n * 32, 32), 32)
                v = norm_rows(H[slot, r, :]) * gains[slot, :][None]
                if slot < 2:
                    y[r, :] = v
                    yl[r, :] = v.astype(BF)
                else:
                    OUT[r, :] = v.astype(BF)
            if slot == 2: keep(OUT, o_out)
        return run

    cs = []
    def context_out():
        for k, (dx, dc) in enumerate(((0, 1), (1, 0), (1, 1))):
            tx = (p.x + dx) % 2; tc = (p.c + dc) % 2
            c_ = pltpu.make_async_remote_copy(en.at[0, tx * 2 + tc], ctx.at[:, me], csem.at[k], crsem.at[me], device_id=p.dev(x=tx, c=tc), device_id_type=MESH)
            c_.start(); cs.append(c_)
    def context_in():
        for k, (dx, dc) in enumerate(((0, 1), (1, 0), (1, 1))):
            tx = (p.x + dx) % 2; tc = (p.c + dc) % 2
            w = tx * 2 + tc
            pltpu.make_async_remote_copy(en.at[0, w], ctx.at[:, w], csem.at[k], crsem.at[w], device_id=p.dev(), device_id_type=MESH).wait_recv()

    class Ctx:
        def __getitem__(self, idx):
            if idx is Ellipsis: return ctx[...].reshape(256, 1024)
            return ctx[:, :, :, idx[1]].reshape(256, -1)
    cref = Ctx()
    def adapter():
        fetch(8).wait()
        w = wbuf[0, :, :, :, :, :, pl.ds(0, 512)].reshape(1024, 512)
        r = dot(yl[...], w)
        s = 1.0 / (1.0 + jnp.exp(-r))
        a = (r * s).astype(BF)
        ar[...] = a
        SR[...] = s * (1.0 + r * (1.0 - s))
        AT[...] = a.T
        keep(SR, o_sr); keep(AT, o_at)
    def adapter_out():
        top = wbuf[0, :, :, :, :, pl.ds(0, 16), pl.ds(512, 512)].reshape(512, 512)
        bot = wbuf[0, :, :, :, :, pl.ds(16, 16), pl.ds(512, 512)].reshape(512, 512)
        H[2, :, 0:512] = y[:, 0:512] + 4.0 * dot(ar[...], top)
        H[2, :, 512:1024] = y[:, 512:1024] + 4.0 * dot(ar[...], bot)
    def hidden(j):
        def run():
            t = 9 + j
            fetch(t).wait()
            @pl.loop(0, 4)
            def _(n):
                ds = cols(n, 256)
                u = dot(yl[...], wbuf[t % 4, :, :, :, :, :, ds].reshape(1024, 256))
                half = 0.5 + 0.5 * lax.erf(u * 0.7071067811865476)
                af[j, :, ds] = (u * half).astype(BF)
                GP[j, :, ds] = half + u * (0.3989422804014327 * jnp.exp(-0.5 * u * u))
            keep(GP.at[j], o_gp.at[j])
        return run
    def out_cols(j):
        def run():
            fetch(13 + j).wait()
            acc = H[2, :, pl.ds(256 * j, 256)]
            for f in range(4):
                w = wo[j % 2, f].reshape(1024, 256)
                acc = acc + dot(af[f], w)
            H[2, :, pl.ds(256 * j, 256)] = acc
        return run

    def masks():
        row = lax.broadcasted_iota(jnp.int32, (128, 128), 0)
        col = lax.broadcasted_iota(jnp.int32, (128, 128), 1)
        for u in range(2):
            wide = lambda ref, j: jnp.broadcast_to(ref[u:u + 1, j:j + 1], (128, 128))
            paired = wide(dlen, 1) > 0
            far = jnp.where(paired, 64, 128)
            second = col >= far
            place = jnp.where(second, col - 64, col)
            same = (row >= far) == second
            dec = jnp.where(second, wide(dlen, 1), wide(dlen, 0))
            enc = jnp.where(second, wide(elen, 1), wide(elen, 0))
            bias[0, u] = jnp.where(same & (col <= row) & (place < dec), 0.0, -1e30)
            bias[1, u] = jnp.where(same & (place < enc), 0.0, -1e30)

    compute = {}
    for t in range(17): compute[f"w{t}"] = start(t)
    compute["masks"] = masks
    compute["own"] = lambda: (c1.wait(), c2.wait())
    for k, src in ((0, x), (1, cref), (2, yl), (3, mix), (4, mix), (5, yl)): compute[f"flip{k}"] = flip(src, k)
    for t, lhs, slot in ((0, x, 0), (1, x, 1), (2, x, 2), (4, cref, 4), (5, cref, 5), (6, yl, 3)): compute[f"proj{t}"] = proj(lhs, t, slot)
    for a in range(2):
        for part in range(4): compute[f"at{a}{part}"] = attend(a, part)
    compute.update(branch3=branch(3, x, 0), branch7=branch(7, y, 1), norm0=norm(0), norm1=norm(1), norm2=norm(2),
                   ctxsend=context_out, ctxin=context_in, adapter=adapter, adapter_out=adapter_out)
    for j in range(4): compute.update({f"hid{j}": hidden(j), f"out{j}": out_cols(j)})
    run_plan(PLAN_F, compute, streams, guards)
    for k in range(2):
        @pl.when(guards[k])
        def _():
            for s in streams: s.finish(k)
    for c_ in cs: c_.wait_send()
    for c_ in outs: c_.wait()

def forward(tokens, gains, dec_lengths, enc_lengths, shards, encoder):
    any_ = pl.BlockSpec(memory_space=pl.ANY)
    vm = pl.BlockSpec(memory_space=pltpu.VMEM)
    V, S, D = pltpu.VMEM, jax.ShapeDtypeStruct, pltpu.SemaphoreType.DMA
    tile = (4, 2, 2, 2, 32, 1024)
    return pl.pallas_call(forward_kernel,
        out_shape=(S((13,) + tile, BF), S((4, 2, 2, 2, 128, 1024), BF), S((6, 256, 1024), BF), S((2, 16, 256, 128), F32), S((3, 256, 1024), F32),
                   S((6, 1024, 256), BF), S((512, 256), BF), S((4, 256, 1024), F32), S((256, 512), F32), S((256, 1024), BF)),
        in_specs=[vm] * 4 + [any_] * 9, out_specs=(any_,) * 10,
        scratch_shapes=[V((6, 256, 1024), BF), V((2, 16, 256, 128), F32), V((3, 256, 1024), F32), V((6, 1024, 256), BF), V((512, 256), BF),
                        V((4, 256, 1024), F32), V((256, 512), F32), V((256, 1024), BF), V((2, 4, 32, 1024), BF), V((4,) + tile, BF),
                        V((2, 4, 2, 2, 2, 128, 256), BF), V((13, 32, 1024), BF), V((128, 1024), BF), V((256, 1024), F32), V((256, 1024), BF),
                        V((256, 1024), BF), V((4, 256, 1024), BF), V((256, 512), BF), V((2, 2, 128, 128), F32),
                        D((N_STREAM, NSEND)), D((N_STREAM, NSLOT)), D((20,)), D((3,)), D((4,)), D((17,)), D((26,))],
        compiler_params=pltpu.CompilerParams(collective_id=0, has_side_effects=True, vmem_limit_bytes=60 << 20),
        name="forward")(tokens, gains, dec_lengths, enc_lengths, *shards, encoder)

PLAN_B = [
    "nb0", "hb0", "hb1", "hb2", "hb3", "adb", "adg.0", "adg.1", "adg.2", "adg.3", "hi0", (0, "R1", 0, None), "hi1", (0, "R1", 1, None), "hi2", "hi3",
    (0, "R1", 2, None), (0, "R2", 0, None), (0, "R1", 3, None), "nb1", "t1.0", "t1.1", (0, "R2", 1, None), "t1.2", "t1.3", "mb9", (0, "R3", 0, None),
    (0, "D", 0, 3), (0, "D", 0, 2), (0, "R2", 2, None), "at10", (0, "R2", 3, None), (0, "R3", 1, None), (0, "D", 1, 3), (0, "D", 1, 2), "at11",
    (1, "R1", 0, None), (0, "R3", 2, None), (0, "D", 2, 3), (1, "R1", 1, None), (0, "U", 2, 0), "at12", (0, "D", 0, 1), (1, "R1", 2, None),
    (1, "R1", 3, None), (0, "R3", 3, None), (0, "U", 3, 0), "at13", "t2.0", "t2.1", (0, "U", 1, 0), (0, "U", 3, 1), (1, "R2", 0, None), (1, "D", 0, 3),
    "t2.2", "t2.3", "t3.0", (0, "U", 2, 1), (1, "D", 0, 2), (2, "R1", 0, None), "t3.1", "t3.2", "t3.3", "t4.0", (1, "R2", 1, None), (1, "U", 1, 0),
    (1, "D", 1, 2), (2, "R1", 1, None), (1, "D", 1, 3), (0, "U", 3, 2), (2, "R1", 2, None), (1, "D", 0, 1), "t4.1", "t4.2", (2, "R1", 3, None),
    (3, "R1", 0, None), "t4.3", (4, "R1", 0, None), (1, "R2", 2, None), (1, "D", 2, 3), (1, "U", 2, 0), (3, "R1", 3, None), (2, "R2", 0, None),
    (2, "D", 0, 3), (1, "R2", 3, None), (1, "U", 3, 0), (3, "R1", 1, None), "rb10", "cb", "rb12", (2, "D", 0, 2), (4, "R1", 1, None), (1, "U", 2, 1),
    (4, "R1", 3, None), (1, "U", 3, 1), (2, "R2", 1, None), (2, "U", 1, 0), (2, "D", 1, 3), (4, "R2", 0, None), (1, "Z3", 0, 0), (2, "D", 1, 2), "nb2",
    "t5.0", "t5.1", (0, "FIN", 0, 0), (0, "FIN", 0, 1), (2, "R2", 3, None), (2, "R2", 2, None), "t5.2", "t5.3", (2, "U", 3, 0), (1, "Z3", 0, 1),
    (4, "R1", 2, None), (1, "Z3", 0, 2), (2, "D", 0, 1), (3, "R1", 2, None), (0, "FIN", 0, 3), (2, "U", 2, 0), (2, "D", 2, 3), (4, "D", 0, 3), "mb13",
    "at00", (2, "U", 3, 1), (5, "R1", 0, None), (4, "R2", 1, None), (1, "U", 3, 2), (3, "R2", 0, None), (2, "Z3", 0, 0), (2, "U", 2, 1),
    (5, "R1", 1, None), (5, "R1", 2, None), (4, "U", 1, 0), (1, "FIN", 0, 0), (3, "R2", 1, None), (2, "Z3", 0, 1), (0, "FIN", 0, 2), "at01",
    (4, "D", 0, 2), (2, "U", 3, 2), "at02", (4, "D", 1, 3), (4, "R2", 2, None), (4, "R2", 3, None), (4, "U", 2, 0), (4, "U", 3, 0), "at03", "cs",
    "t6.0", "t6.1", (5, "R2", 0, None), (5, "D", 0, 3), (5, "D", 0, 2), (1, "Z3", 0, 3), (4, "D", 1, 2), (5, "R1", 3, None), (3, "R2", 3, None),
    (3, "R2", 2, None), (3, "R3", 0, None), (3, "D", 0, 3), "t6.2", "t6.3", (4, "D", 0, 1), (4, "U", 3, 1), "t7.0", (5, "R2", 2, None), (5, "U", 2, 1),
    (5, "U", 2, 0), (5, "D", 2, 3), (4, "U", 2, 1), (6, "R1", 0, None), "t7.1", "t7.2", "t7.3", "t8.0", "t8.1", (5, "D", 0, 1), (2, "Z3", 0, 3),
    (6, "R1", 2, None), (4, "U", 3, 2), (3, "D", 0, 2), (2, "Z3", 0, 2), (5, "R2", 1, None), (5, "D", 1, 3), (5, "U", 1, 0), (4, "Z3", 0, 1),
    (5, "R2", 3, None), (5, "U", 3, 0), (4, "Z3", 0, 0), (3, "R3", 3, None), (3, "U", 3, 0), (6, "R1", 1, None), (4, "D", 2, 3), (2, "FIN", 0, 0),
    (7, "R1", 0, None), (1, "FIN", 0, 1), (3, "D", 0, 1), (3, "R3", 2, None), (7, "R1", 2, None), (8, "R1", 0, None), (5, "U", 3, 1),
    (7, "R1", 1, None), (3, "U", 3, 1), (3, "U", 2, 0), (5, "D", 1, 2), "t8.2", "t8.3", "rb14", (4, "Z3", 0, 2), "rb15", (5, "U", 3, 2), "tok",
    (5, "Z3", 0, 0), (6, "R1", 3, None), (7, "R1", 3, None), (2, "FIN", 0, 1), (8, "R1", 1, None), (3, "U", 2, 1), (1, "FIN", 0, 2),
    (8, "R1", 2, None), (7, "R2", 0, None), (3, "R3", 1, None), (3, "U", 1, 0), (3, "D", 1, 2), (3, "D", 1, 3), (7, "D", 0, 2), (7, "D", 0, 3),
    (5, "Z3", 0, 2), (5, "Z3", 0, 1), (3, "D", 2, 3), (7, "D", 0, 1), (7, "R2", 2, None), (7, "U", 2, 1), (7, "U", 2, 0), (8, "R1", 3, None),
    (7, "R2", 1, None), (7, "U", 1, 0), (7, "D", 1, 3), (7, "D", 2, 3), (7, "D", 1, 2), (8, "R2", 0, None), (7, "R2", 3, None), (7, "U", 3, 1),
    (7, "U", 3, 0), (2, "FIN", 0, 3), (3, "U", 3, 2), (5, "FIN", 0, 2), (5, "FIN", 0, 1), (1, "FIN", 0, 3), (8, "D", 0, 2), (4, "Z3", 0, 3),
    (4, "FIN", 0, 1), (8, "D", 0, 3), (7, "Z3", 0, 2), (3, "FIN", 0, 1), (8, "R2", 3, None), (5, "Z3", 0, 3), (8, "R2", 1, None), (8, "D", 1, 2),
    (5, "FIN", 0, 0), (8, "R2", 2, None), (8, "U", 2, 0), (8, "D", 1, 3), (5, "FIN", 0, 3), (6, "R2", 1, None), (3, "FIN", 0, 2), (6, "R2", 0, None),
    (8, "U", 1, 0), (7, "U", 3, 2), (8, "D", 0, 1), (4, "FIN", 0, 2), (3, "FIN", 0, 0), (8, "D", 2, 3), (6, "R2", 2, None), (2, "FIN", 0, 2),
    (7, "Z3", 0, 0), (8, "U", 2, 1), (6, "R2", 3, None), (7, "Z3", 0, 1), (8, "U", 3, 0), (4, "FIN", 0, 3), (6, "R3", 0, None), (6, "R3", 1, None),
    (6, "R3", 2, None), (6, "D", 0, 3), (6, "D", 0, 2), (6, "D", 1, 3), (6, "D", 1, 2), (7, "FIN", 0, 1), (8, "U", 3, 2), (8, "U", 3, 1),
    (7, "Z3", 0, 3), (6, "D", 2, 3), (6, "D", 0, 1), (3, "FIN", 0, 3), (6, "U", 1, 0), (6, "R3", 3, None), (7, "FIN", 0, 2), (6, "U", 2, 0),
    (7, "FIN", 0, 3), (8, "Z3", 0, 1), (6, "U", 3, 1), (6, "U", 3, 0), (8, "Z3", 0, 0), (6, "U", 2, 1), (8, "Z3", 0, 2), (6, "FIN", 0, 0),
    (7, "FIN", 0, 0), (8, "FIN", 0, 2), (8, "FIN", 0, 1), (6, "U", 3, 2), (8, "Z3", 0, 3), (4, "FIN", 0, 0), (8, "FIN", 0, 0), (6, "FIN", 0, 3),
    (6, "FIN", 0, 1), (6, "FIN", 0, 2), (8, "FIN", 0, 3),
]


NT = 9
ORDERS = ["A", "xzy", "yzx"] * 3
NS, NR = 27, 33

class Reduce:
    def __init__(self, p, t, order, PB, L0, L1, L2, UP, DN, LX, ssem, rsem, out):
        self.p, self.t, self.order = p, t, order
        self.PB, self.L0, self.L1, self.L2, self.UP, self.DN, self.LX = PB, L0, L1, L2, UP, DN, LX
        self.ssem, self.rsem, self.out = ssem, rsem, out
        self.sends = []
        self.me = {"x": p.x, "y": p.y}
        self.flat = order == "A"
        if not self.flat: self.b1, self.b2 = order[0], order[2]
    def partner(self, b):
        return self.p.dev(**{b: 1 - self.me[b]})
    def desc(self, src, dst, k, slot, target):
        return pltpu.make_async_remote_copy(src, dst, self.ssem.at[k], self.rsem.at[slot], device_id=target, device_id_type=MESH)
    def copy(self, what, k, slot, z=None):
        def make():
            src, dst, target = what()
            return self.desc(src, dst, k, slot, target)
        make().start()
        self.sends.append((make, z))
    def arrive(self, dst, slot):
        self.desc(dst, dst, 0, slot, self.p.dev()).wait_recv()
    def finish(self, z):
        for make, at in self.sends:
            if at == z: make().wait_send()
    def sib(self, zz):
        self.copy(lambda: (self.PB.at[zz, :, :, 1 - self.p.c], self.L0.at[zz], self.p.dev(c=1 - self.p.c)), zz, zz)
    def pair(self, zz, b2name, b2v, r=pl.ds(0, 32)):
        if b2name == "y": return self.PB.at[zz, b2v, :, self.p.c, r]
        return self.PB.at[zz, :, b2v, self.p.c, r]
    def block(self, zz, r=pl.ds(0, 32), **where):
        return self.PB.at[zz, where.get("y", self.p.y), where.get("x", self.p.x), self.p.c, r]
    def mine(self, zz):
        return self.block(zz) if self.flat else self.pair(zz, self.b2, self.me[self.b2])
    def halves(self):
        return [(h, b1, b2, pl.ds(16 * h, 16)) for h, (b1, b2) in enumerate((("x", "y"), ("y", "x")))]

    def R1(self, zz):
        p = self.p
        self.arrive(self.L0.at[zz], zz)
        for yy in range(2):
            for xx in range(2):
                self.PB[zz, yy, xx, p.c] = self.PB[zz, yy, xx, p.c] + self.L0[zz, yy, xx]
        if self.flat:
            for h, b1, b2, r in self.halves():
                self.copy(lambda b2=b2, r=r: (self.pair(zz, b2, 1 - self.me[b2], r), self.L1.at[zz, :, r], self.partner(b2)), 4 + 4 * h + zz, 17 + 4 * h + zz)
        else:
            self.copy(lambda: (self.pair(zz, self.b2, 1 - self.me[self.b2]), self.L1.at[zz], self.partner(self.b2)), 4 + zz, 4 + zz)
    def R2(self, zz):
        if self.flat:
            for h, b1, b2, r in self.halves():
                self.arrive(self.L1.at[zz, :, r], 17 + 4 * h + zz)
                o = self.pair(zz, b2, self.me[b2], r)
                o[...] = o[...] + self.L1[zz, :, r]
                self.copy(lambda b1=b1, r=r: (self.block(zz, r, **{b1: 1 - self.me[b1]}), self.L2.at[zz, r], self.partner(b1)), 12 + 4 * h + zz, 25 + 4 * h + zz)
        else:
            self.arrive(self.L1.at[zz], 4 + zz)
            o = self.mine(zz)
            o[...] = o[...] + self.L1[zz]
    def R3(self, zz):
        for h, b1, b2, r in self.halves():
            self.arrive(self.L2.at[zz, r], 25 + 4 * h + zz)
            o = self.block(zz, r)
            o[...] = o[...] + self.L2[zz, r]
    def U(self, zu, z):
        o, land = self.mine(zu), self.UP.at[zu - 1]
        if 0 < z <= zu:
            self.arrive(land, 8 + zu)
            o[...] = o[...] + land[...]
        if z < zu: self.copy(lambda: (self.mine(zu), self.UP.at[zu - 1], self.p.dev(z=z + 1)), 20 + zu - 1, 8 + zu, z)
    def D(self, zd, z):
        o, land = self.mine(zd), self.DN.at[zd]
        if zd <= z < 3:
            self.arrive(land, 12 + zd)
            o[...] = o[...] + land[...]
        if z > zd: self.copy(lambda: (self.mine(zd), self.DN.at[zd], self.p.dev(z=z - 1)), 23 + zd, 12 + zd, z)
    def Z3(self, k, z):
        if z > 0: self.U(z, z)
        if z < 3: self.D(z, z)
        self.copy(lambda: (self.block(z, **{self.b1: 1 - self.me[self.b1]}), self.LX, self.partner(self.b1)), 26, 16, z)
    def FIN(self, k, z):
        v = self.block(z)
        if self.flat:
            if z > 0: self.U(z, z)
            if z < 3: self.D(z, z)
            self.out(v[...].astype(F32))
        else:
            self.arrive(self.LX, 16)
            self.out(v[...].astype(F32) + self.LX[...].astype(F32))

W_ORDER = ["o0", "o1", "o2", "o3", 8, 9, 10, 11, 12, 7, 4, 5, 6, 3, 0, 1, 2]
T_ORDER = [5, 4, 1, 2, 3, 0]
NW = 3

def backward_kernel(gains, buf, gfo, qkv, P, H, T, AT, GP, SR, cot,
                    o_tok, osp, oso, ocp, oco, oai, oao, oen,
                    PB, L0, L1, L2, UPC, DNC, UPA, DNA, LX, wbuf, hb, gpb, tb, atb, srb, pb, cotb, g, gb, gr, gx, gqkv, gtok,
                    ssem, rsem, csem, crsem, wsem, hsem, gpsem, tsem, msem, qsem, psem, osem):
    p = Place()
    neighbours_in = entry_barrier(p)
    lo, hi = half_masks()
    def w_copy(i):
        n = W_ORDER[i]
        src = gfo.at[int(n[1])] if isinstance(n, str) else buf.at[n]
        return pltpu.make_async_copy(src, wbuf.at[i % NW], wsem.at[i])
    h_copy = lambda i: pltpu.make_async_copy(H.at[2 - i], hb.at[i % 2], hsem.at[i])
    gp_copy = lambda j: pltpu.make_async_copy(GP.at[j], gpb.at[j % 2], gpsem.at[j])
    t_copy = lambda i: pltpu.make_async_copy(T.at[T_ORDER[i]], tb.at[i % 3], tsem.at[i])
    q_copy = lambda a, j: pltpu.make_async_copy(qkv.at[3 * a + j], PB.at[6 + a, j], qsem.at[3 * a + j])
    p_copy = lambda a: pltpu.make_async_copy(P.at[a], pb, psem.at[a])
    m_copy = [pltpu.make_async_copy(cot, cotb, msem.at[0]), pltpu.make_async_copy(SR, srb, msem.at[1]), pltpu.make_async_copy(AT, atb, msem.at[2])]
    h_copy(0).start(); m_copy[0].start(); w_copy(0).start(); gp_copy(0).start(); w_copy(1).start(); gp_copy(1).start(); w_copy(2).start()
    h_copy(1).start(); m_copy[1].start(); m_copy[2].start()
    for i in range(3): t_copy(i).start()
    for j in range(3): q_copy(1, j).start()
    p_copy(1).start()
    for j in range(3): q_copy(0, j).start()

    def o_ad(v):
        oai[...] = v[:, :512]
        oao[:, 0:512] = v[0:16, 512:]
        oao[:, 512:1024] = v[16:32, 512:]
    def put(ref, j=None):
        def f(v):
            if j is None: ref[...] = v
            else: ref[j] = v
        return f
    finals = [o_ad, put(oco), put(ocp, 1), put(ocp, 2), put(ocp, 0), put(oso), put(osp, 1), put(osp, 2), put(osp, 0)]
    reds = []
    nc = na = 0
    for t in range(NT):
        if ORDERS[t] == "A":
            up, dn, l2 = UPA.at[na], DNA.at[na], L2.at[na]; na += 1
        else:
            up, dn, l2 = UPC.at[nc], DNC.at[nc], None; nc += 1
        reds.append(Reduce(p, t, ORDERS[t], PB.at[t], L0.at[t], L1.at[t], l2, up, dn, LX.at[t], ssem.at[t], rsem.at[t], finals[t]))

    compute = {}
    def work(name, fn): compute[name] = fn

    def norm_back(i, first=False):
        def run():
            h_copy(i).wait()
            if first: m_copy[0].wait()
            @pl.loop(0, 8)
            def _(n):
                r = pl.ds(pl.multiple_of(n * 32, 32), 32)
                h = hb[i % 2, r, :]
                center = h - jnp.mean(h, axis=-1, keepdims=True)
                inv = lax.rsqrt(jnp.mean(center * center, axis=-1, keepdims=True) + EPS)
                nrm = center * inv
                gy = cotb[r, :].astype(F32) if first else g[r, :]
                a = gy * gains[2 - i, :][None]
                v = (a - jnp.mean(a, axis=-1, keepdims=True) - nrm * jnp.mean(a * nrm, axis=-1, keepdims=True)) * inv
                g[r, :] = v
                gb[r, :] = v.astype(BF)
            if i == 0: h_copy(2).start()
        return run

    def used(i):
        if i + NW < len(W_ORDER): w_copy(i + NW).start()

    def nt(lhs, i, fn):
        fn(dot_nt(lhs(), wbuf[i % NW]))

    def hidden_back(j):
        def run():
            w_copy(j).wait(); gp_copy(j).wait()
            def st(v):
                PB[8, j] = (gpb[j % 2] * v).astype(BF).reshape(2, 2, 2, 32, 1024)
            nt(lambda: gb[...], j, st)
            used(j)
            if j + 2 < 4: gp_copy(j + 2).start()
        return run

    def adapter_back():
        i = 4
        w_copy(i).wait(); m_copy[1].wait(); m_copy[2].wait()
        v = wbuf[i % NW, :, 512:1024].reshape(32, 32, 512)
        top, bot = v[:, :16].reshape(512, 512), v[:, 16:].reshape(512, 512)
        s = dot_nt(gb[:, 0:512], top) + dot_nt(gb[:, 512:1024], bot)
        gr[...] = (srb[...] * (4.0 * s)).astype(BF)
        wai = wbuf[i % NW, :, 0:512]
        g[...] = g[...] + dot_nt(gr[...], wai)
        used(i)

    def adapter_grads(zz):
        def run():
            if zz == 0:
                neighbours_in()
                for h in range(2):
                    v = 4.0 * dot(atb[...], gb[:, 512 * h:512 * h + 512])
                    PB[0, :, :, :, :, 16 * h:16 * h + 16, 512:1024] = v.astype(BF).reshape(4, 2, 2, 2, 16, 512)
                t_copy(0).wait()
            v = dot(tb[0, pl.ds(256 * zz, 256), :], gr[...])
            PB[0, zz, :, :, :, :, 0:512] = v.astype(BF).reshape(2, 2, 2, 32, 512)
            reds[0].sib(zz)
            if zz == 3: t_copy(3).start()
        return run

    def hidden_in_back(j):
        def run():
            i = 5 + j
            w_copy(i).wait()
            def st(v): g[...] = g[...] + v
            nt(lambda: PB[8, j].reshape(256, 1024), i, st)
            used(i)
        return run

    def grad_tile(t, ti, rhs, last, zz):
        def run():
            if zz == 0 and t in (1, 2, 4, 5, 6): t_copy(ti).wait()
            PB[t, zz] = dot(tb[ti % 3, pl.ds(256 * zz, 256), :], rhs()).astype(BF).reshape(2, 2, 2, 32, 1024)
            reds[t].sib(zz)
            if zz == 3 and last and ti + 3 < 6: t_copy(ti + 3).start()
        return run

    def mix_back(i):
        def run():
            w_copy(i).wait()
            def st(v): gx[...] = v.astype(BF)
            nt(lambda: gb[...], i, st)
            used(i)
        return run

    def attend_back(a, part):
        def run():
            if part == 0:
                p_copy(a).wait()
                for j in range(3): q_copy(a, j).wait()
            u = part // 2
            @pl.loop(0, 4)
            def _(n):
                pr = (part % 2) * 4 + n
                r, cc = pl.ds(u * 128, 128), cols(pr, 128)
                q, k, v = (PB[6 + a, j, u, :, :, :, cc].reshape(128, 128) for j in range(3))
                go = pair_up(gx[r, cc], lo, hi)
                prob = pb[u * 8 + pr]
                dp = dot_nt(go, v)
                ds = (prob * (dp - jnp.sum(prob * dp, axis=-1, keepdims=True))).astype(BF)
                gqkv[0, r, cc] = (dot(side(ds), pair_up(k, lo, hi)) * 0.125).astype(BF)
                gqkv[1, r, cc] = (dot_tn(ds, pair_up(q, lo, hi)) * 0.125).astype(BF)
                gqkv[2, r, cc] = dot_tn(prob.astype(BF), go).astype(BF)
            if part == 3 and a == 1: p_copy(0).start()
        return run

    def row_back(i, j, dst):
        def run():
            w_copy(i).wait()
            nt(lambda: gqkv[j], i, dst)
            used(i)
        return run
    def to_g(v): g[...] = g[...] + v
    cs = []
    me = p.x * 2 + p.c
    def context_back():
        i = 11
        w_copy(i).wait()
        def st(v): PB[8, 0] = (ctxf[...] + v).astype(BF).reshape(2, 2, 2, 32, 1024)
        nt(lambda: gqkv[2], i, st)
        used(i)
        for k, (dx, dc) in enumerate(((0, 1), (1, 0), (1, 1))):
            tx = (p.x + dx) % 2; tc = (p.c + dc) % 2
            c_ = pltpu.make_async_remote_copy(PB.at[8, 0, :, tx, tc], oen.at[0, me], csem.at[k], crsem.at[me], device_id=p.dev(x=tx, c=tc), device_id_type=MESH)
            c_.start(); cs.append(c_)
        c_ = pltpu.make_async_copy(PB.at[8, 0, :, p.x, p.c], oen.at[0, me], osem.at[0]); c_.start(); cs.append(c_)

    ctxf = gpb.at[0]
    def ctx_part(v): ctxf[...] = v
    def context_sent():
        for c_ in cs[:3]: c_.wait_send()
        cs[3].wait()
    def tokens_back():
        i = 16
        w_copy(i).wait()
        def st(v): gtok[...] = (g[...] + v).astype(BF)
        nt(lambda: gqkv[2], i, st)
        pltpu.make_async_copy(gtok, o_tok, osem.at[1]).start()

    def tile(t, ti, rhs, last):
        for zz in range(4): work(f"t{t}.{zz}", grad_tile(t, ti, rhs, last, zz))
    work("nb0", norm_back(0, True))
    for j in range(4): work(f"hb{j}", hidden_back(j))
    work("adb", adapter_back)
    for zz in range(4): work(f"adg.{zz}", adapter_grads(zz))
    for j in range(4): work(f"hi{j}", hidden_in_back(j))
    work("nb1", norm_back(1))
    tile(1, 1, lambda: gb[...], True)
    work("mb9", mix_back(9))
    for part in range(4): work(f"at1{part}", attend_back(1, part))
    tile(2, 2, lambda: gqkv[1], False)
    tile(3, 2, lambda: gqkv[2], True)
    tile(4, 3, lambda: gqkv[0], True)
    work("rb10", row_back(10, 1, ctx_part))
    work("cb", context_back)
    work("rb12", row_back(12, 0, to_g))
    work("nb2", norm_back(2))
    tile(5, 4, lambda: gb[...], True)
    work("mb13", mix_back(13))
    for part in range(4): work(f"at0{part}", attend_back(0, part))
    work("cs", context_sent)
    tile(6, 5, lambda: gqkv[1], False)
    tile(7, 5, lambda: gqkv[2], False)
    tile(8, 5, lambda: gqkv[0], True)
    work("rb14", row_back(14, 0, to_g))
    work("rb15", row_back(15, 1, to_g))
    work("tok", tokens_back)
    run_plan(PLAN_B, compute, reds, [p.z == z for z in range(4)])
    for r in reds: r.finish(None)
    for z in range(4):
        @pl.when(p.z == z)
        def _():
            for r in reds: r.finish(z)
    pltpu.make_async_copy(gtok, o_tok, osem.at[1]).wait()
    for k, (dx, dc) in enumerate(((0, 1), (1, 0), (1, 1))):
        tx = (p.x + dx) % 2; tc = (p.c + dc) % 2
        w = tx * 2 + tc
        pltpu.make_async_remote_copy(PB.at[8, 0, :, tx, tc], oen.at[0, w], csem.at[k], crsem.at[w], device_id=p.dev(), device_id_type=MESH).wait_recv()

def backward(gains, buf, gfo, qkv, P, H, T, AT, GP, SR, cot):
    any_ = pl.BlockSpec(memory_space=pl.ANY)
    vm = pl.BlockSpec(memory_space=pltpu.VMEM)
    V, S, D = pltpu.VMEM, jax.ShapeDtypeStruct, pltpu.SemaphoreType.DMA
    ops = (gains, buf.reshape(13, 1024, 1024), gfo.reshape(4, 1024, 1024), qkv.reshape(6, 2, 2, 2, 32, 1024), P, H, T, AT, GP, SR, cot)
    return pl.pallas_call(backward_kernel,
        out_shape=(S((256, 1024), BF), S((3, 32, 1024), F32), S((32, 1024), F32), S((3, 32, 1024), F32), S((32, 1024), F32), S((32, 512), F32), S((16, 1024), F32), S((1, 4, 2, 32, 1024), BF)),
        in_specs=[vm] + [any_] * 10, out_specs=(any_,) + (vm,) * 6 + (any_,),
        scratch_shapes=[V((NT, 4, 2, 2, 2, 32, 1024), BF), V((NT, 4, 2, 2, 32, 1024), BF), V((NT, 4, 2, 32, 1024), BF), V((3, 4, 32, 1024), BF),
                        V((6, 3, 2, 32, 1024), BF), V((6, 3, 2, 32, 1024), BF), V((3, 3, 32, 1024), BF), V((3, 3, 32, 1024), BF), V((NT, 32, 1024), BF),
                        V((NW, 1024, 1024), BF), V((2, 256, 1024), F32), V((2, 256, 1024), F32), V((3, 1024, 256), BF), V((512, 256), BF), V((256, 512), F32),
                        V((16, 256, 128), F32), V((256, 1024), BF), V((256, 1024), F32), V((256, 1024), BF), V((256, 512), BF), V((256, 1024), BF),
                        V((3, 256, 1024), BF), V((256, 1024), BF),
                        D((NT, NS)), D((NT, NR)), D((3,)), D((4,)), D((17,)), D((3,)), D((4,)), D((6,)), D((3,)), D((6,)), D((2,)), D((2,))],
        compiler_params=pltpu.CompilerParams(collective_id=1, has_side_effects=True, vmem_limit_bytes=63 << 20),
        name="backward")(*ops)


def finish_kernel(*refs):
    n = (len(refs) - 1) // 3
    ins, outs, held, sem = refs[:n], refs[n:2 * n], refs[2 * n:3 * n], refs[3 * n]
    first = [pltpu.make_async_copy(ins[k], held[k], sem.at[k]) for k in range(n)]
    last = [pltpu.make_async_copy(held[k], outs[k], sem.at[n + k]) for k in range(n)]
    for c in first: c.start()
    for k in range(n):
        first[k].wait()
        last[k].start()
    for c in last: c.wait()

def finish(*arrays):
    any_ = pl.BlockSpec(memory_space=pl.ANY)
    n = len(arrays)
    return pl.pallas_call(finish_kernel, out_shape=tuple(jax.ShapeDtypeStruct(a.shape, a.dtype) for a in arrays),
        in_specs=[any_] * n, out_specs=(any_,) * n,
        scratch_shapes=[pltpu.VMEM(a.shape, a.dtype) for a in arrays] + [pltpu.SemaphoreType.DMA((2 * n,))],
        compiler_params=pltpu.CompilerParams(vmem_limit_bytes=16 << 20), name="finish")(*arrays)


def device_program(tokens, encoder, dec_lengths, enc_lengths, gains, self_proj, self_out, cross_proj, cross_out, ffn_in, ffn_out, adapt_in, adapt_out, cotangent):
    shards = (self_proj, self_out, cross_proj, cross_out, ffn_in, ffn_out, adapt_in, adapt_out)
    buf, gfo, qkv, probs, hidden, turned, act_turned, gelu_slope, silu_slope, layer_out = forward(tokens, gains, dec_lengths, enc_lengths, shards, encoder)
    gtok, osp, oso, ocp, oco, oai, oao, oen = backward(gains, buf, gfo, qkv, probs, hidden, turned, act_turned, gelu_slope, silu_slope, cotangent)
    return finish(layer_out, gtok, oen, osp, oso, ocp, oco, oai, oao)


def solution(mesh):
    in_specs = (
        P(("seq", "enc"), None),
        P("seq", None, None, "enc", None),
        P(("seq", "enc"), None),
        P(("seq", "enc"), None),
        P(),
        P(None, ("seq", "enc"), None),
        P(("seq", "enc"), None),
        P(None, ("seq", "enc"), None),
        P(("seq", "enc"), None),
        P(("seq", "enc"), None),
        P(("seq", "enc"), None),
        P(("seq", "enc"), None),
        P(("seq", "enc"), None),
        P(("seq", "enc"), None),
    )
    out_specs = (
        P(("seq", "enc"), None),
        P(("seq", "enc"), None),
        P("seq", None, None, "enc", None),
        P(None, ("seq", "enc"), None),
        P(("seq", "enc"), None),
        P(None, ("seq", "enc"), None),
        P(("seq", "enc"), None),
        P(("seq", "enc"), None),
        P(("seq", "enc"), None),
    )
    fast = (mesh.shape["seq"], mesh.shape["enc"]) == (8, 4)
    return jax.shard_map(
        device_program if fast else per_device, mesh=mesh, in_specs=in_specs, out_specs=out_specs, check_vma=False
    )
```

```python
import jax
import jax.numpy as jnp
from jax import lax
from jax.experimental import pallas as pl
from jax.experimental.pallas import tpu as pltpu
from jax.sharding import PartitionSpec as P

HEADS = 16
ADAPT = 512
MICRO = 2


EPSILON = 1e-05
NEGATIVE = -1e30


def matmul(left, right):
    return jnp.dot(left, right, preferred_element_type=jnp.float32)


def matmul_tn(left, right):
    return lax.dot_general(
        left, right, (((0,), (0,)), ((), ())), preferred_element_type=jnp.float32
    )


def matmul_nt(left, right):
    return lax.dot_general(
        left, right, (((1,), (1,)), ((), ())), preferred_element_type=jnp.float32
    )


def layer_norm(hidden, gain):
    center = hidden - jnp.mean(hidden, axis=-1, keepdims=True)
    spread = jnp.mean(center * center, axis=-1, keepdims=True)
    return center * lax.rsqrt(spread + EPSILON) * gain


def norm_back(hidden, gain, grad_out):
    _, pullback = jax.vjp(lambda value: layer_norm(value, gain), hidden)
    return pullback(grad_out)[0]


def gelu_exact(value):
    return jax.nn.gelu(value, approximate=False)


def slot_masks(dec_row, enc_row, rows):
    half_rows = rows // 2
    places = lax.broadcasted_iota(jnp.int32, (rows,), 0)
    paired = dec_row[1] > 0
    second = jnp.logical_and(paired, places >= half_rows)
    anchor = jnp.where(second, half_rows, 0).astype(jnp.int32)
    dec_valid = jnp.where(second, dec_row[1], dec_row[0])
    enc_valid = jnp.where(second, enc_row[1], enc_row[0])
    key_live = places - anchor < dec_valid
    context_live = places - anchor < enc_valid
    same_slot = second[:, None] == second[None, :]
    causal = places[None, :] <= places[:, None]
    self_mask = same_slot & causal & key_live[None, :]
    cross_mask = same_slot & context_live[None, :]
    return (self_mask, cross_mask)


def split_heads(matrix):
    return matrix.reshape(matrix.shape[0], HEADS, matrix.shape[1] // HEADS)


def attend(queries, keys, values, allowed):
    depth = queries.shape[1] // HEADS
    scores = jnp.einsum(
        "qhd,khd->hqk", split_heads(queries), split_heads(keys), preferred_element_type=jnp.float32
    ) * float(depth) ** (-0.5)
    masked = jnp.where(allowed[None], scores, NEGATIVE)
    weights = jnp.exp(masked - jnp.max(masked, axis=-1, keepdims=True))
    probs = weights / jnp.sum(weights, axis=-1, keepdims=True)
    mixed = jnp.einsum(
        "hqk,khd->qhd",
        probs.astype(jnp.bfloat16),
        split_heads(values),
        preferred_element_type=jnp.float32,
    )
    return (mixed.reshape(queries.shape).astype(jnp.bfloat16), probs)


def attend_back(grad_mixed, queries, keys, values, probs):
    depth = queries.shape[1] // HEADS
    factor = float(depth) ** (-0.5)
    grad_heads = split_heads(grad_mixed)
    grad_probs = jnp.einsum(
        "qhd,khd->hqk", grad_heads, split_heads(values), preferred_element_type=jnp.float32
    )
    inner = jnp.sum(probs * grad_probs, axis=-1, keepdims=True)
    grad_scores = (probs * (grad_probs - inner)).astype(jnp.bfloat16)
    grad_query = (
        jnp.einsum(
            "hqk,khd->qhd", grad_scores, split_heads(keys), preferred_element_type=jnp.float32
        )
        * factor
    )
    grad_key = (
        jnp.einsum(
            "hqk,qhd->khd", grad_scores, split_heads(queries), preferred_element_type=jnp.float32
        )
        * factor
    )
    grad_value = jnp.einsum(
        "hqk,qhd->khd", probs.astype(jnp.bfloat16), grad_heads, preferred_element_type=jnp.float32
    )
    return (
        grad_query.reshape(queries.shape).astype(jnp.bfloat16),
        grad_key.reshape(keys.shape).astype(jnp.bfloat16),
        grad_value.reshape(values.shape).astype(jnp.bfloat16),
    )


def per_device(
    tokens,
    encoder,
    dec_lengths,
    enc_lengths,
    gains,
    self_proj,
    self_out,
    cross_proj,
    cross_out,
    ffn_in,
    ffn_out,
    adapt_in,
    adapt_out,
    cotangent,
):
    shards = (self_proj, self_out, cross_proj, cross_out, ffn_in, ffn_out, adapt_in, adapt_out)

    def obtain():
        return (
            lax.all_gather(shards[0], ("seq", "enc"), axis=1, tiled=True),
            lax.all_gather(shards[1], ("seq", "enc"), axis=0, tiled=True),
            lax.all_gather(shards[2], ("seq", "enc"), axis=1, tiled=True),
            lax.all_gather(shards[3], ("seq", "enc"), axis=0, tiled=True),
            lax.all_gather(shards[4], ("seq", "enc"), axis=0, tiled=True),
            lax.all_gather(shards[5], ("seq", "enc"), axis=0, tiled=True),
            lax.all_gather(shards[6], ("seq", "enc"), axis=0, tiled=True),
            lax.all_gather(shards[7], ("seq", "enc"), axis=0, tiled=True),
        )

    rows = tokens.shape[0] // MICRO
    width = tokens.shape[1]
    owner = lax.axis_index("enc")
    acc_self = jnp.zeros((width, 3, width), jnp.float32)
    acc_self_out = jnp.zeros((width, width), jnp.float32)
    acc_cross = jnp.zeros((width, 3, width), jnp.float32)
    acc_cross_out = jnp.zeros((width, width), jnp.float32)
    acc_adapt_in = jnp.zeros((width, ADAPT), jnp.float32)
    acc_adapt_out = jnp.zeros((ADAPT, width), jnp.float32)
    outputs = []
    grad_rows = []
    grad_contexts = []
    for micro_index in range(MICRO):
        w_self, w_self_out, w_cross, w_cross_out, w_ffn_in, w_ffn_out, w_adapt_in, w_adapt_out = (
            obtain()
        )
        lower = micro_index * rows
        token_rows = tokens[lower : lower + rows]
        self_mask, cross_mask = slot_masks(dec_lengths[micro_index], enc_lengths[micro_index], rows)
        pieces = encoder[0, :, micro_index]
        context = lax.dynamic_index_in_dim(
            lax.all_gather(pieces, "enc", axis=1, tiled=True), owner, 0, keepdims=False
        )
        self_query = matmul(token_rows, w_self[0]).astype(jnp.bfloat16)
        self_key = matmul(token_rows, w_self[1]).astype(jnp.bfloat16)
        self_value = matmul(token_rows, w_self[2]).astype(jnp.bfloat16)
        self_mix, self_probs = attend(self_query, self_key, self_value, self_mask)
        first_sum = token_rows.astype(jnp.float32) + matmul(self_mix, w_self_out)
        first_norm = layer_norm(first_sum, gains[0])
        first_low = first_norm.astype(jnp.bfloat16)
        cross_query = matmul(first_low, w_cross[0]).astype(jnp.bfloat16)
        cross_key = matmul(context, w_cross[1]).astype(jnp.bfloat16)
        cross_value = matmul(context, w_cross[2]).astype(jnp.bfloat16)
        cross_mix, cross_probs = attend(cross_query, cross_key, cross_value, cross_mask)
        second_sum = first_norm + matmul(cross_mix, w_cross_out)
        second_norm = layer_norm(second_sum, gains[1])
        second_low = second_norm.astype(jnp.bfloat16)
        ffn_pre = matmul(second_low, w_ffn_in)
        ffn_act = gelu_exact(ffn_pre).astype(jnp.bfloat16)
        adapt_pre = matmul(second_low, w_adapt_in)
        adapt_act = jax.nn.silu(adapt_pre).astype(jnp.bfloat16)
        third_sum = second_norm + matmul(ffn_act, w_ffn_out) + 4.0 * matmul(adapt_act, w_adapt_out)
        outputs.append(layer_norm(third_sum, gains[2]).astype(jnp.bfloat16))
        w_self, w_self_out, w_cross, w_cross_out, w_ffn_in, w_ffn_out, w_adapt_in, w_adapt_out = (
            obtain()
        )
        grad_third = norm_back(
            third_sum, gains[2], cotangent[lower : lower + rows].astype(jnp.float32)
        )
        grad_branch = grad_third.astype(jnp.bfloat16)
        _, gelu_pull = jax.vjp(gelu_exact, ffn_pre)
        grad_ffn_pre = gelu_pull(matmul_nt(grad_branch, w_ffn_out))[0].astype(jnp.bfloat16)
        grad_adapt_act = matmul_nt(grad_branch, w_adapt_out) * 4.0
        _, silu_pull = jax.vjp(jax.nn.silu, adapt_pre)
        grad_adapt_pre = silu_pull(grad_adapt_act)[0].astype(jnp.bfloat16)
        acc_adapt_out = acc_adapt_out + matmul_tn(adapt_act, grad_branch) * 4.0
        acc_adapt_in = acc_adapt_in + matmul_tn(second_low, grad_adapt_pre)
        grad_second = (
            grad_third + matmul_nt(grad_ffn_pre, w_ffn_in) + matmul_nt(grad_adapt_pre, w_adapt_in)
        )
        grad_second_sum = norm_back(second_sum, gains[1], grad_second)
        grad_cross_branch = grad_second_sum.astype(jnp.bfloat16)
        acc_cross_out = acc_cross_out + matmul_tn(cross_mix, grad_cross_branch)
        grad_cross_mix = matmul_nt(grad_cross_branch, w_cross_out).astype(jnp.bfloat16)
        grad_cq, grad_ck, grad_cv = attend_back(
            grad_cross_mix, cross_query, cross_key, cross_value, cross_probs
        )
        acc_cross = acc_cross + jnp.stack(
            [
                matmul_tn(first_low, grad_cq),
                matmul_tn(context, grad_ck),
                matmul_tn(context, grad_cv),
            ],
            axis=1,
        )
        grad_context = matmul_nt(grad_ck, w_cross[1]) + matmul_nt(grad_cv, w_cross[2])
        holder = jnp.zeros((lax.axis_size("enc"),) + grad_context.shape, jnp.float32)
        holder = lax.dynamic_update_index_in_dim(holder, grad_context, owner, 0)
        returned = lax.psum_scatter(
            holder.astype(jnp.bfloat16), "enc", scatter_dimension=1, tiled=True
        )
        grad_contexts.append(returned)
        grad_first = grad_second_sum + matmul_nt(grad_cq, w_cross[0])
        grad_first_sum = norm_back(first_sum, gains[0], grad_first)
        grad_self_branch = grad_first_sum.astype(jnp.bfloat16)
        acc_self_out = acc_self_out + matmul_tn(self_mix, grad_self_branch)
        grad_self_mix = matmul_nt(grad_self_branch, w_self_out).astype(jnp.bfloat16)
        grad_sq, grad_sk, grad_sv = attend_back(
            grad_self_mix, self_query, self_key, self_value, self_probs
        )
        acc_self = acc_self + jnp.stack(
            [
                matmul_tn(token_rows, grad_sq),
                matmul_tn(token_rows, grad_sk),
                matmul_tn(token_rows, grad_sv),
            ],
            axis=1,
        )
        grad_input = (
            grad_first_sum
            + matmul_nt(grad_sq, w_self[0])
            + matmul_nt(grad_sk, w_self[1])
            + matmul_nt(grad_sv, w_self[2])
        )
        grad_rows.append(grad_input.astype(jnp.bfloat16))
    summed = (
        lax.psum_scatter(acc_self, ("seq", "enc"), scatter_dimension=0, tiled=True),
        lax.psum_scatter(acc_self_out, ("seq", "enc"), scatter_dimension=0, tiled=True),
        lax.psum_scatter(acc_cross, ("seq", "enc"), scatter_dimension=0, tiled=True),
        lax.psum_scatter(acc_cross_out, ("seq", "enc"), scatter_dimension=0, tiled=True),
        lax.psum_scatter(acc_adapt_in, ("seq", "enc"), scatter_dimension=0, tiled=True),
        lax.psum_scatter(acc_adapt_out, ("seq", "enc"), scatter_dimension=0, tiled=True),
    )
    layer_out = jnp.concatenate(outputs, axis=0)
    grad_tokens = jnp.concatenate(grad_rows, axis=0)
    grad_encoder = jnp.stack(grad_contexts, axis=1)[None]
    grad_self_proj = jnp.transpose(summed[0], (1, 0, 2))
    grad_cross_proj = jnp.transpose(summed[2], (1, 0, 2))
    return (
        layer_out,
        grad_tokens,
        grad_encoder,
        grad_self_proj,
        summed[1],
        grad_cross_proj,
        summed[3],
        summed[4],
        summed[5],
    )


MESH = pl.DeviceIdType.MESH
class Place:
    def __init__(self):
        seq, enc = lax.axis_index("seq"), lax.axis_index("enc")
        self.z, self.y, self.x, self.c = seq // 2, seq % 2, enc // 2, enc % 2
        self.up, self.down = jnp.minimum(self.z + 1, 3), jnp.maximum(self.z - 1, 0)
        self.step = jnp.where(self.z < 2, 1, -1)
    def dev(self, z=None, y=None, x=None, c=None):
        z = self.z if z is None else z
        y = self.y if y is None else y
        x = self.x if x is None else x
        c = self.c if c is None else c
        return (z * 2 + y, x * 2 + c)

def entry_barrier(p):
    bar = pltpu.get_barrier_semaphore()
    def sig(d):
        pl.semaphore_signal(bar, inc=1, device_id=d, device_id_type=MESH)
    sig(p.dev(c=1 - p.c)); sig(p.dev(x=1 - p.x)); sig(p.dev(y=1 - p.y)); sig(p.dev(x=1 - p.x, c=1 - p.c))
    @pl.when(p.z < 3)
    def _(): sig(p.dev(z=p.up))
    @pl.when(p.z > 0)
    def _(): sig(p.dev(z=p.down))
    peers = 4 + (p.z < 3).astype(jnp.int32) + (p.z > 0).astype(jnp.int32)
    return lambda: pl.semaphore_wait(bar, peers)

ALL4 = pl.ds(0, 4)
ALL2 = pl.ds(0, 2)

class Stream:
    def __init__(self, p, own, view, order, ssem, rsem):
        self.p, self.own, self.view, self.order, self.ssem, self.rsem = p, own, view, order, ssem, rsem
        self.flat = order[0] == "z"
        self.b1, self.b2 = (order[1], order[2]) if self.flat else (order[0], order[2])
        self.me = {"x": p.x, "y": p.y}
        self.sends = [[], []]

    def source(self, r, kind):
        p = self.p
        return p.z - p.step if kind == 1 and r == 3 else p.z + p.step * r

    def unit(self, z, c=None, **where):
        w = dict(self.me) if self.flat else {**self.me, self.b1: ALL2}
        w.update(where)
        return self.view(z, w["y"], w["x"], self.p.c if c is None else c)

    def partner(self, b):
        return self.p.dev(**{b: 1 - self.me[b]})

    def copy(self, kind, slot, what):
        k = len(self.sends[kind])
        def make():
            src, dst, target = what()
            return pltpu.make_async_remote_copy(src, dst, self.ssem.at[k], self.rsem.at[slot()], device_id=target, device_id_type=MESH)
        make().start()
        self.sends[kind].append(make)

    def arrive(self, where, slot):
        pltpu.make_async_remote_copy(where, where, self.ssem.at[0], self.rsem.at[slot], device_id=self.p.dev(), device_id_type=MESH).wait_recv()

    def finish(self, kind):
        for make in self.sends[kind]: make().wait_send()

    def along(self, kind, r, way, src=None):
        p = self.p
        def what():
            u = self.unit(self.source(r, kind))
            return u if src is None else src, u, p.dev(z=p.z + way * p.step)
        self.copy(kind, lambda: self.source(r, kind), what)

    def across(self, kind, r, src=None):
        b = self.b1 if self.flat else self.b2
        def what():
            u = self.unit(self.source(r, kind))
            return u if src is None else src, u, self.partner(b)
        self.copy(kind, lambda: 4 + self.source(r, kind), what)

    def P0(self, r, kind):
        if self.flat:
            self.along(kind, 0, 1, self.own)
            if kind == 1: self.along(kind, 0, -1, self.own)
            self.across(kind, 0, self.own)
        else:
            self.copy(kind, lambda: 8, lambda: (self.own, self.unit(self.p.z, **self.me), self.partner(self.b1)))
    def E0(self, r, kind):
        self.arrive(self.unit(self.p.z, **{self.b1: 1 - self.me[self.b1]}), 8)
        self.along(kind, 0, 1)
        if kind == 1: self.along(kind, 0, -1)
        self.across(kind, 0)
    def H(self, r, kind):
        z = self.source(r, kind)
        self.arrive(self.unit(z), z)
        if kind == 1: self.along(kind, r, -1 if r < 3 else 1)
        self.across(kind, r)
    def E(self, r, kind):
        z = self.source(r, kind)
        self.arrive(self.unit(z, **{self.b1: 1 - self.me[self.b1]}), 4 + z)
        def what():
            u = self.unit(self.source(r, kind), **{self.b1: ALL2})
            return u, u, self.partner(self.b2)
        self.copy(kind, lambda: 8 + self.source(r, kind), what)
    def plane(self, far, c=None):
        return self.unit(ALL4, c, **{self.b1: ALL2, self.b2: 1 - self.me[self.b2] if far else self.me[self.b2]})
    def F0(self, r, kind):
        self.copy(kind, lambda: 12, lambda: (self.plane(False), self.plane(False), self.p.dev(c=1 - self.p.c)))
    def F5(self, r, kind):
        for zz in range(4):
            self.arrive(self.unit(zz, **{self.b1: ALL2, self.b2: 1 - self.me[self.b2]}), (8 if self.flat else 4) + zz)
        self.copy(kind, lambda: 13, lambda: (self.plane(True), self.plane(True), self.p.dev(c=1 - self.p.c)))
    def L(self, r, kind):
        self.arrive(self.plane(False, 1 - self.p.c), 12)
        self.arrive(self.plane(True, 1 - self.p.c), 13)

def run_plan(plan, compute, movers, guards):
    i = 0
    while i < len(plan):
        it = plan[i]
        if isinstance(it, str):
            compute[it]()
            i += 1
        elif it[3] is None:
            getattr(movers[it[0]], it[1])(it[2])
            i += 1
        else:
            j = i
            while j < len(plan) and not isinstance(plan[j], str) and plan[j][3] == it[3]: j += 1
            @pl.when(guards[it[3]])
            def _():
                for m, name, k, kind in plan[i:j]: getattr(movers[m], name)(k, kind)
            i = j


PLAN_F = [
    (0, "P0", 0, 0), (0, "P0", 0, 1), (1, "P0", 0, 0), (1, "P0", 0, 1), (2, "P0", 0, 0), (3, "P0", 0, 0), (2, "P0", 0, 1), (4, "P0", 0, 0),
    (3, "P0", 0, 1), (4, "P0", 0, 1), (5, "P0", 0, 0), (6, "P0", 0, 0), (5, "P0", 0, 1), (7, "P0", 0, 0), (8, "P0", 0, 0), (6, "P0", 0, 1),
    (9, "P0", 0, 0), (7, "P0", 0, 1), (0, "H", 1, 1), (0, "H", 1, 0), "staged", "own", (0, "E", 0, 0), (0, "H", 3, 1), (1, "E", 0, 0), (0, "E", 0, 1),
    (10, "P0", 0, 0), (1, "E", 0, 1), (11, "P0", 0, 0), (1, "H", 1, 1), (1, "H", 1, 0), (12, "P0", 0, 0), (1, "H", 3, 1), (13, "P0", 0, 0),
    (8, "P0", 0, 1), (2, "E0", 0, 0), (2, "E0", 0, 1), (4, "H", 1, 0), (3, "E0", 0, 0), (3, "E0", 0, 1), (14, "P0", 0, 0), (4, "E", 0, 0),
    (4, "H", 1, 1), (5, "H", 1, 0), (5, "E", 0, 0), (4, "H", 3, 1), (15, "P0", 0, 0), (4, "E", 0, 1), (16, "P0", 0, 0), (0, "H", 2, 1), (0, "H", 2, 0),
    (5, "H", 1, 1), (17, "P0", 0, 0), (5, "H", 3, 1), (18, "P0", 0, 0), (1, "H", 2, 0), (1, "H", 2, 1), (6, "E0", 0, 0), (5, "E", 0, 1),
    (7, "E0", 0, 0), (6, "E0", 0, 1), (19, "P0", 0, 0), (8, "H", 1, 0), (7, "E0", 0, 1), (8, "E", 0, 0), (9, "E", 0, 0), (0, "E", 1, 1),
    (20, "P0", 0, 0), (8, "H", 1, 1), (0, "E", 1, 0), (0, "E", 3, 1), (21, "P0", 0, 0), (8, "H", 3, 1), (22, "P0", 0, 0), (9, "P0", 0, 1),
    (23, "P0", 0, 0), (9, "H", 3, 1), (10, "P0", 0, 1), (1, "E", 1, 1), (11, "P0", 0, 1), (12, "P0", 0, 1), (1, "E", 3, 1), (12, "H", 3, 1),
    (2, "H", 1, 0), (2, "H", 1, 1), (11, "E0", 0, 0), (8, "E", 0, 1), (13, "P0", 0, 1), (10, "E0", 0, 0), (2, "H", 3, 1), (1, "E", 1, 0),
    (13, "H", 3, 1), (14, "P0", 0, 1), (12, "E", 0, 0), (15, "P0", 0, 1), (13, "E", 0, 0), (16, "P0", 0, 1), (17, "P0", 0, 1), (4, "E", 1, 0),
    (18, "P0", 0, 1), (19, "P0", 0, 1), (20, "P0", 0, 1), (3, "H", 1, 0), (3, "H", 1, 1), (21, "P0", 0, 1), (4, "H", 2, 0), (3, "H", 3, 1),
    (4, "H", 2, 1), (4, "E", 1, 1), (0, "H", 3, 0), (5, "H", 2, 1), (4, "E", 3, 1), (16, "H", 3, 1), (5, "E", 1, 1), (5, "H", 2, 0), (17, "H", 3, 1),
    (0, "E", 2, 1), (0, "F0", 0, 1), (5, "E", 3, 1), (1, "H", 3, 0), (22, "P0", 0, 1), (23, "P0", 0, 1), "flip0", (14, "E0", 0, 0), (1, "E", 2, 1),
    (1, "F0", 0, 1), (5, "E", 1, 0), "ctxsend", (6, "H", 1, 1), "masks", (6, "H", 3, 1), (15, "E0", 0, 0), (6, "H", 1, 0), (16, "E", 0, 0),
    (17, "E", 0, 0), (0, "E", 2, 0), (1, "E", 2, 0), (7, "H", 1, 1), (8, "E", 1, 1), (7, "H", 3, 1), (18, "E0", 0, 0), (8, "H", 2, 1), (8, "E", 3, 1),
    (9, "H", 1, 1), (7, "H", 1, 0), (20, "H", 3, 1), (9, "H", 2, 1), (8, "H", 2, 0), (10, "E0", 0, 1), (9, "E", 0, 1), (12, "H", 1, 1), (9, "H", 1, 0),
    (21, "H", 3, 1), (9, "E", 3, 1), (12, "H", 2, 1), (12, "H", 1, 0), (19, "E0", 0, 0), (13, "H", 1, 1), (8, "E", 1, 0), (12, "E", 0, 1),
    (11, "E0", 0, 1), (11, "H", 3, 1), (2, "H", 2, 0), (12, "E", 3, 1), (20, "E", 0, 0), (2, "H", 2, 1), (13, "H", 1, 0), (2, "F0", 0, 1),
    (21, "E", 0, 0), (22, "E0", 0, 0), (10, "H", 3, 1), (23, "E0", 0, 0), (16, "H", 1, 0), (13, "H", 2, 1), (14, "E0", 0, 1), (17, "H", 1, 0),
    (16, "H", 1, 1), (16, "E", 0, 1), (17, "H", 1, 1), (20, "H", 1, 0), (13, "E", 0, 1), (20, "H", 1, 1), (18, "E0", 0, 1), (14, "H", 3, 1),
    (20, "E", 0, 1), (21, "H", 1, 1), (3, "H", 2, 0), (21, "H", 1, 0), (13, "E", 3, 1), (3, "H", 2, 1), (4, "H", 3, 0), (3, "F0", 0, 1),
    (16, "H", 2, 1), (5, "H", 3, 0), (15, "E0", 0, 1), (15, "H", 3, 1), (17, "H", 2, 1), (17, "E", 0, 1), (18, "H", 3, 1), (19, "E0", 0, 1),
    (5, "E", 2, 0), (6, "H", 2, 0), (4, "E", 2, 1), (4, "F0", 0, 1), (21, "E", 0, 1), (1, "E", 3, 0), (6, "H", 2, 1), (1, "F0", 0, 0), (6, "F0", 0, 1),
    (16, "E", 3, 1), (19, "H", 3, 1), (5, "E", 2, 1), (5, "F0", 0, 1), (7, "H", 2, 0), (7, "H", 2, 1), (8, "H", 3, 0), (7, "F0", 0, 1),
    (20, "H", 2, 1), (9, "H", 2, 0), (17, "E", 3, 1), (22, "E0", 0, 1), (9, "H", 3, 0), (22, "H", 3, 1), (4, "E", 2, 0), (0, "E", 3, 0),
    (0, "F5", 0, 1), (0, "F0", 0, 0), (1, "F5", 0, 1), (23, "E0", 0, 1), (23, "H", 3, 1), (10, "H", 1, 1), (21, "H", 2, 1), (10, "H", 1, 0),
    (0, "L", 0, 1), (12, "H", 2, 0), (1, "L", 0, 1), (12, "H", 3, 0), (13, "H", 2, 0), (11, "H", 1, 1), "ctxin", "flip1", (9, "E", 1, 0),
    (11, "H", 1, 0), (11, "H", 2, 1), (11, "F0", 0, 1), (2, "H", 3, 0), (9, "E", 1, 1), (2, "F0", 0, 0), (10, "H", 2, 1), (13, "H", 3, 0),
    (9, "E", 2, 1), (9, "F0", 0, 1), (8, "E", 2, 0), (10, "F0", 0, 1), (12, "E", 1, 0), (8, "E", 2, 1), (8, "F0", 0, 1), (20, "E", 3, 1),
    (13, "E", 1, 0), (14, "H", 1, 1), (14, "H", 1, 0), (16, "H", 2, 0), (21, "E", 3, 1), (17, "H", 2, 0), (13, "E", 1, 1), (12, "E", 1, 1),
    (20, "H", 2, 0), (17, "E", 1, 0), (18, "H", 1, 1), (21, "E", 1, 0), (16, "E", 1, 0), (12, "E", 2, 1), (12, "F0", 0, 1), (5, "E", 3, 0),
    (5, "F0", 0, 0), (20, "E", 1, 0), (18, "H", 1, 0), (14, "H", 2, 1), (21, "H", 2, 0), (14, "F0", 0, 1), (2, "F5", 0, 1), (9, "E", 2, 0),
    (4, "E", 3, 0), (4, "F0", 0, 0), (15, "H", 1, 1), (9, "E", 3, 0), (3, "H", 3, 0), (3, "F0", 0, 0), (9, "F0", 0, 0), (16, "H", 3, 0),
    (2, "L", 0, 1), (16, "E", 1, 1), (13, "E", 2, 1), (13, "F0", 0, 1), (1, "F5", 0, 0), (0, "F5", 0, 0), (15, "H", 2, 1), (15, "F0", 0, 1),
    (15, "H", 1, 0), (20, "E", 1, 1), (17, "H", 3, 0), (1, "L", 0, 0), (0, "L", 0, 0), "w0", (18, "H", 2, 1), (18, "F0", 0, 1), (8, "E", 3, 0),
    (8, "F0", 0, 0), (13, "E", 2, 0), (12, "E", 2, 0), "proj0", (17, "E", 1, 1), (12, "E", 3, 0), (12, "F0", 0, 0), (19, "H", 1, 0), (3, "F5", 0, 1),
    (19, "H", 1, 1), (16, "E", 2, 1), (16, "F0", 0, 1), (2, "F5", 0, 0), (13, "E", 3, 0), (6, "H", 3, 0), (6, "F0", 0, 0), (13, "F0", 0, 0),
    (3, "L", 0, 1), (19, "H", 2, 1), (19, "F0", 0, 1), (2, "L", 0, 0), "w1", (7, "H", 3, 0), (7, "F0", 0, 0), "proj1", (16, "E", 2, 0),
    (20, "H", 3, 0), (22, "H", 1, 1), (20, "E", 2, 0), (22, "H", 1, 0), (17, "E", 2, 1), (17, "F0", 0, 1), (21, "E", 1, 1), (17, "E", 2, 0),
    (22, "H", 2, 1), (23, "H", 1, 0), (22, "F0", 0, 1), (23, "H", 1, 1), (23, "H", 2, 1), (23, "F0", 0, 1), (5, "F5", 0, 0), (10, "H", 2, 0),
    (21, "H", 3, 0), (4, "F5", 0, 1), (5, "L", 0, 0), (9, "F5", 0, 0), (4, "L", 0, 1), (21, "E", 2, 0), (11, "H", 2, 0), (6, "F5", 0, 1),
    (9, "L", 0, 0), (4, "F5", 0, 0), (3, "F5", 0, 0), (5, "F5", 0, 1), (17, "E", 3, 0), (17, "F0", 0, 0), (16, "E", 3, 0), (6, "L", 0, 1),
    (16, "F0", 0, 0), (11, "H", 3, 0), (11, "F0", 0, 0), (4, "L", 0, 0), (8, "F5", 0, 0), (5, "L", 0, 1), "w3", (3, "L", 0, 0), "w2", (7, "F5", 0, 1),
    (20, "E", 2, 1), (20, "F0", 0, 1), (10, "H", 3, 0), (10, "F0", 0, 0), "proj2", (12, "F5", 0, 0), "at00", (7, "L", 0, 1), (8, "L", 0, 0), "at01",
    (21, "E", 2, 1), (21, "F0", 0, 1), (6, "F5", 0, 0), (12, "L", 0, 0), (14, "H", 2, 0), "at02", (13, "F5", 0, 0), (18, "H", 2, 0), "at03",
    (10, "F5", 0, 1), (6, "L", 0, 0), "flip3", (13, "L", 0, 0), "branch3", (8, "F5", 0, 1), (11, "F5", 0, 1), (7, "F5", 0, 0), (14, "H", 3, 0),
    (14, "F0", 0, 0), "norm0", (10, "L", 0, 1), (8, "L", 0, 1), (20, "E", 3, 0), (20, "F0", 0, 0), "flip2", "w4", (7, "L", 0, 0), "w5",
    (11, "L", 0, 1), (9, "F5", 0, 1), (15, "H", 2, 0), (21, "E", 3, 0), (21, "F0", 0, 0), "proj4", (9, "L", 0, 1), "w6", (16, "F5", 0, 0), "proj5",
    (15, "H", 3, 0), "proj6", (15, "F0", 0, 0), "at10", (10, "F5", 0, 0), (16, "L", 0, 0), "at11", (17, "F5", 0, 0), (18, "H", 3, 0), (18, "F0", 0, 0),
    (12, "F5", 0, 1), (13, "F5", 0, 1), "at12", (10, "L", 0, 0), "at13", (11, "F5", 0, 0), (17, "L", 0, 0), (12, "L", 0, 1), (19, "H", 2, 0),
    (13, "L", 0, 1), (14, "F5", 0, 1), (15, "F5", 0, 1), "flip4", "w7", (19, "H", 3, 0), (19, "F0", 0, 0), "branch7", (14, "L", 0, 1), (11, "L", 0, 0),
    (21, "F5", 0, 0), "norm1", (15, "L", 0, 1), (14, "F5", 0, 0), (22, "H", 2, 0), "flip5", "w9", "w8", (21, "L", 0, 0), (18, "F5", 0, 1),
    (15, "F5", 0, 0), "hid0", (20, "F5", 0, 0), (22, "H", 3, 0), (22, "F0", 0, 0), (14, "L", 0, 0), (23, "H", 2, 0), "adapter", (16, "F5", 0, 1),
    (19, "F5", 0, 1), (23, "H", 3, 0), (18, "F5", 0, 0), (23, "F0", 0, 0), "adapter_out", (17, "F5", 0, 1), (18, "L", 0, 1), (15, "L", 0, 0), "w10",
    "w11", (20, "L", 0, 0), (16, "L", 0, 1), (19, "L", 0, 1), "hid1", (17, "L", 0, 1), "w12", (22, "F5", 0, 1), (23, "F5", 0, 1), (18, "L", 0, 0),
    (19, "F5", 0, 0), "hid2", (20, "F5", 0, 1), (21, "F5", 0, 1), (22, "F5", 0, 0), (23, "F5", 0, 0), "hid3", (22, "L", 0, 1), (23, "L", 0, 1), "w13",
    (19, "L", 0, 0), "w14", (22, "L", 0, 0), (20, "L", 0, 1), (21, "L", 0, 1), (23, "L", 0, 0), "out0", "out1", "w15", "w16", "out2", "out3", "norm2",
]

F32, BF = jnp.float32, jnp.bfloat16
NSLOT, NSEND = 14, 19
N_STREAM = 24
EPS = 1e-05

def dot(a, b):
    return jnp.dot(a, b, preferred_element_type=F32)

def dot_nt(a, b):
    return lax.dot_general(a, b, (((1,), (1,)), ((), ())), preferred_element_type=F32)

def dot_tn(a, b):
    return lax.dot_general(a, b, (((0,), (0,)), ((), ())), preferred_element_type=F32)

def cols(n, width):
    return pl.ds(pl.multiple_of(n * width, width), width)

def norm_rows(h):
    center = h - jnp.mean(h, axis=-1, keepdims=True)
    spread = jnp.mean(center * center, axis=-1, keepdims=True)
    return center * lax.rsqrt(spread + EPS)

def half_masks():
    lane = lax.broadcasted_iota(jnp.int32, (1, 128), 1)
    lo = jnp.where(lane < 64, 1.0, 0.0)
    return lo.astype(BF), (1.0 - lo).astype(BF)

def pair_up(m, lo, hi):
    return jnp.concatenate([m * lo, m * hi], axis=0)

def side(m):
    return jnp.concatenate([m[:128], m[128:]], axis=1)

def forward_kernel(x, gains, dlen, elen, sp, so, cp, co, fi, fo, ai, ao, en,
                   buf, gfo, o_qkv, o_p, o_h, o_t, o_at, o_gp, o_sr, o_out,
                   qkv, P, H, T, AT, GP, SR, OUT, ctx, wbuf, wo, own, ownf, y, yl, mix, af, ar, bias,
                   ssem, rsem, lsem, csem, crsem, wsem, osem):
    p = Place()
    neighbours_in = entry_barrier(p)
    loc = []
    def put(src, dst):
        c_ = pltpu.make_async_copy(src, dst, lsem.at[len(loc)]); c_.start(); loc.append(c_)
    for j, t in enumerate((0, 1, 2)): put(sp.at[j], own.at[t])
    put(so, own.at[3])
    for j, t in ((1, 4), (2, 5), (0, 6)): put(cp.at[j], own.at[t])
    put(co, own.at[7])
    put(ai, own.at[8, :, pl.ds(0, 512)])
    put(ao.at[:, pl.ds(0, 512)], own.at[8, pl.ds(0, 16), pl.ds(512, 512)])
    put(ao.at[:, pl.ds(512, 512)], own.at[8, pl.ds(16, 16), pl.ds(512, 512)])
    for j in range(4): put(fi.at[:, pl.ds(1024 * j, 1024)], own.at[9 + j])
    put(fo, ownf)
    me = p.x * 2 + p.c
    put(en.at[0, me], ctx.at[:, me])
    n_in = len(loc)
    c1 = pltpu.make_async_copy(own, buf.at[:, p.z, p.y, p.x, p.c], lsem.at[n_in])
    c2 = pltpu.make_async_copy(ownf, gfo.at[p.z, p.y, p.x, p.c], lsem.at[n_in + 1])
    def staged():
        for c_ in loc: c_.wait()
        c1.start(); c2.start()
    neighbours_in()
    streams = []
    for t in range(17):
        R = 32 if t < 13 else 128
        i = t % 3
        rows = [(0, R // 2, "zxy"), (R // 2, R // 2, "zyx")] if i == 0 else [(0, R, "xzy" if i == 1 else "yzx")]
        if t == 16: rows = [(0, 96, "xzy"), (96, 32, "yzx")]
        for r0, nr, order in rows:
            n = len(streams)
            if t < 13:
                arg = {0: sp.at[0], 1: sp.at[1], 2: sp.at[2], 3: so, 4: cp.at[1], 5: cp.at[2], 6: cp.at[0], 7: co, 8: own.at[8]}.get(t)
                mine = fi.at[pl.ds(r0, nr), pl.ds(1024 * (t - 9), 1024)] if t > 8 else arg.at[pl.ds(r0, nr)]
                view = lambda z, y_, x_, c, t=t, r0=r0, nr=nr: buf.at[t, z, y_, x_, c, pl.ds(r0, nr)]
            else:
                mine = fo.at[pl.ds(r0, nr), pl.ds(256 * (t - 13), 256)]
                view = lambda z, y_, x_, c, j=t - 13, r0=r0, nr=nr: gfo.at[z, y_, x_, c, pl.ds(r0, nr), pl.ds(256 * j, 256)]
            streams.append(Stream(p, mine, view, order, ssem.at[n], rsem.at[n]))
    ends = (p.z == 0) | (p.z == 3)
    guards = [ends, jnp.logical_not(ends)]

    def fetch(t):
        if t < 13: return pltpu.make_async_copy(buf.at[t], wbuf.at[t % 4], wsem.at[t])
        j = t - 13
        return pltpu.make_async_copy(gfo.at[:, :, :, :, :, pl.ds(256 * j, 256)], wo.at[j % 2], wsem.at[t])
    def start(t): return lambda: fetch(t).start()
    outs = []
    def keep(src, dst):
        c_ = pltpu.make_async_copy(src, dst, osem.at[len(outs)]); c_.start(); outs.append(c_)
    lo, hi = half_masks()

    def mm(lhs, t, fn):
        fn(dot(lhs[...], wbuf[t % 4].reshape(1024, 1024)))

    def proj(lhs, t, slot):
        def run():
            fetch(t).wait()
            def st(v): qkv[slot] = v.astype(BF)
            mm(lhs, t, st)
            keep(qkv.at[slot], o_qkv.at[slot])
        return run

    def flip(src, slot):
        def run():
            @pl.loop(0, 4)
            def _(n):
                T[slot, cols(n, 256), :] = src[:, cols(n, 256)].T
            keep(T.at[slot], o_t.at[slot])
        return run

    def attend(a, part):
        def run():
            u = part // 2
            @pl.loop(0, 4, unroll=4)
            def _(n):
                pr = (part % 2) * 4 + n
                r, cc = pl.ds(u * 128, 128), cols(pr, 128)
                q, k, v = (qkv[3 * a + j, r, cc] for j in range(3))
                b = bias[a, u]
                s = dot_nt(pair_up(q, lo, hi), k) * 0.125 + jnp.concatenate([b, b], axis=0)
                e = jnp.exp(s - jnp.max(s, axis=-1, keepdims=True))
                pr_ = e / jnp.sum(e, axis=-1, keepdims=True)
                P[a, u * 8 + pr] = pr_
                mix[r, cc] = dot(side(pr_.astype(BF)), pair_up(v, lo, hi)).astype(BF)
            if part == 3: keep(P.at[a], o_p.at[a])
        return run

    def branch(t, base, slot):
        def run():
            fetch(t).wait()
            def st(v): H[slot] = base[...].astype(F32) + v
            mm(mix, t, st)
        return run

    def norm(slot):
        def run():
            keep(H.at[slot], o_h.at[slot])
            @pl.loop(0, 4)
            def _(n):
                r = pl.ds(pl.multiple_of(n * 64, 64), 64)
                v = norm_rows(H[slot, r, :]) * gains[slot, :][None]
                if slot < 2:
                    y[r, :] = v
                    yl[r, :] = v.astype(BF)
                else:
                    OUT[r, :] = v.astype(BF)
            if slot == 2: keep(OUT, o_out)
        return run

    cs = []
    def context_out():
        for k, (dx, dc) in enumerate(((0, 1), (1, 0), (1, 1))):
            tx = (p.x + dx) % 2; tc = (p.c + dc) % 2
            c_ = pltpu.make_async_remote_copy(en.at[0, tx * 2 + tc], ctx.at[:, me], csem.at[k], crsem.at[me], device_id=p.dev(x=tx, c=tc), device_id_type=MESH)
            c_.start(); cs.append(c_)
    def context_in():
        for k, (dx, dc) in enumerate(((0, 1), (1, 0), (1, 1))):
            tx = (p.x + dx) % 2; tc = (p.c + dc) % 2
            w = tx * 2 + tc
            pltpu.make_async_remote_copy(en.at[0, w], ctx.at[:, w], csem.at[k], crsem.at[w], device_id=p.dev(), device_id_type=MESH).wait_recv()

    class Ctx:
        def __getitem__(self, idx):
            if idx is Ellipsis: return ctx[...].reshape(256, 1024)
            return ctx[:, :, :, idx[1]].reshape(256, -1)
    cref = Ctx()
    def adapter():
        fetch(8).wait()
        w = wbuf[0, :, :, :, :, :, pl.ds(0, 512)].reshape(1024, 512)
        r = dot(yl[...], w)
        s = 1.0 / (1.0 + jnp.exp(-r))
        a = (r * s).astype(BF)
        ar[...] = a
        SR[...] = s * (1.0 + r * (1.0 - s))
        AT[...] = a.T
        keep(SR, o_sr); keep(AT, o_at)
    def adapter_out():
        top = wbuf[0, :, :, :, :, pl.ds(0, 16), pl.ds(512, 512)].reshape(512, 512)
        bot = wbuf[0, :, :, :, :, pl.ds(16, 16), pl.ds(512, 512)].reshape(512, 512)
        H[2, :, 0:512] = y[:, 0:512] + 4.0 * dot(ar[...], top)
        H[2, :, 512:1024] = y[:, 512:1024] + 4.0 * dot(ar[...], bot)
    def hidden(j):
        def run():
            t = 9 + j
            fetch(t).wait()
            @pl.loop(0, 4)
            def _(n):
                ds = cols(n, 256)
                u = dot(yl[...], wbuf[t % 4, :, :, :, :, :, ds].reshape(1024, 256))
                half = 0.5 + 0.5 * lax.erf(u * 0.7071067811865476)
                af[j, :, ds] = (u * half).astype(BF)
                GP[j, :, ds] = half + u * (0.3989422804014327 * jnp.exp(-0.5 * u * u))
            keep(GP.at[j], o_gp.at[j])
        return run
    def out_cols(j):
        def run():
            fetch(13 + j).wait()
            acc = H[2, :, pl.ds(256 * j, 256)]
            for f in range(4):
                w = wo[j % 2, f].reshape(1024, 256)
                acc = acc + dot(af[f], w)
            H[2, :, pl.ds(256 * j, 256)] = acc
        return run

    def masks():
        row = lax.broadcasted_iota(jnp.int32, (128, 128), 0)
        col = lax.broadcasted_iota(jnp.int32, (128, 128), 1)
        for u in range(2):
            wide = lambda ref, j: jnp.broadcast_to(ref[u:u + 1, j:j + 1], (128, 128))
            paired = wide(dlen, 1) > 0
            far = jnp.where(paired, 64, 128)
            second = col >= far
            place = jnp.where(second, col - 64, col)
            same = (row >= far) == second
            dec = jnp.where(second, wide(dlen, 1), wide(dlen, 0))
            enc = jnp.where(second, wide(elen, 1), wide(elen, 0))
            bias[0, u] = jnp.where(same & (col <= row) & (place < dec), 0.0, -1e30)
            bias[1, u] = jnp.where(same & (place < enc), 0.0, -1e30)

    compute = {}
    for t in range(17): compute[f"w{t}"] = start(t)
    compute["masks"] = masks
    compute["staged"] = staged
    compute["own"] = lambda: (c1.wait(), c2.wait())
    for k, src in ((0, x), (1, cref), (2, yl), (3, mix), (4, mix), (5, yl)): compute[f"flip{k}"] = flip(src, k)
    for t, lhs, slot in ((0, x, 0), (1, x, 1), (2, x, 2), (4, cref, 4), (5, cref, 5), (6, yl, 3)): compute[f"proj{t}"] = proj(lhs, t, slot)
    for a in range(2):
        for part in range(4): compute[f"at{a}{part}"] = attend(a, part)
    compute.update(branch3=branch(3, x, 0), branch7=branch(7, y, 1), norm0=norm(0), norm1=norm(1), norm2=norm(2),
                   ctxsend=context_out, ctxin=context_in, adapter=adapter, adapter_out=adapter_out)
    for j in range(4): compute.update({f"hid{j}": hidden(j), f"out{j}": out_cols(j)})
    run_plan(PLAN_F, compute, streams, guards)
    for k in range(2):
        @pl.when(guards[k])
        def _():
            for s in streams: s.finish(k)
    for c_ in cs: c_.wait_send()
    for c_ in outs: c_.wait()

def forward(tokens, gains, dec_lengths, enc_lengths, shards, encoder):
    any_ = pl.BlockSpec(memory_space=pl.ANY)
    vm = pl.BlockSpec(memory_space=pltpu.VMEM)
    V, S, D = pltpu.VMEM, jax.ShapeDtypeStruct, pltpu.SemaphoreType.DMA
    tile = (4, 2, 2, 2, 32, 1024)
    return pl.pallas_call(forward_kernel,
        out_shape=(S((13,) + tile, BF), S((4, 2, 2, 2, 128, 1024), BF), S((6, 256, 1024), BF), S((2, 16, 256, 128), F32), S((3, 256, 1024), F32),
                   S((6, 1024, 256), BF), S((512, 256), BF), S((4, 256, 1024), F32), S((256, 512), F32), S((256, 1024), BF)),
        in_specs=[vm] * 4 + [any_] * 9, out_specs=(any_,) * 10,
        scratch_shapes=[V((6, 256, 1024), BF), V((2, 16, 256, 128), F32), V((3, 256, 1024), F32), V((6, 1024, 256), BF), V((512, 256), BF),
                        V((4, 256, 1024), F32), V((256, 512), F32), V((256, 1024), BF), V((2, 4, 32, 1024), BF), V((4,) + tile, BF),
                        V((2, 4, 2, 2, 2, 128, 256), BF), V((13, 32, 1024), BF), V((128, 1024), BF), V((256, 1024), F32), V((256, 1024), BF),
                        V((256, 1024), BF), V((4, 256, 1024), BF), V((256, 512), BF), V((2, 2, 128, 128), F32),
                        D((N_STREAM, NSEND)), D((N_STREAM, NSLOT)), D((20,)), D((3,)), D((4,)), D((17,)), D((26,))],
        compiler_params=pltpu.CompilerParams(collective_id=0, has_side_effects=True, vmem_limit_bytes=60 << 20),
        name="forward")(tokens, gains, dec_lengths, enc_lengths, *shards, encoder)

ORDERS = ["A", "xzy", "yzx", "A", "xzy", "yzx", "A", "xzy", "yzx"]
PLAN_B = [
    "nb0", "hb0", "hb1", "hb2", "hb3", "adb", "adg.0", "adg.1", "adg.2", "adg.3", "hi0", (0, "R1", 0, None), "hi1", (0, "R1", 1, None),
    (0, "R1", 2, None), (0, "R1", 3, None), "hi2", "hi3", (0, "R2", 0, None), "nb1", (0, "R2", 1, None), "t1.0", "t1.1", (0, "R2", 2, None), "t1.2",
    "t1.3", "mb9", (0, "R2", 3, None), (1, "R1", 0, None), (0, "R3", 0, None), (0, "U", 3, 0), (0, "D", 0, 3), "at10", (0, "R3", 1, None),
    (0, "R3", 2, None), (0, "D", 1, 3), (0, "U", 2, 0), (1, "R1", 1, None), (0, "D", 2, 3), (0, "U", 1, 0), (1, "R1", 2, None), (0, "R3", 3, None),
    (1, "R1", 3, None), "at11", (0, "U", 3, 1), (0, "D", 0, 2), "at12", (0, "D", 1, 2), (0, "U", 2, 1), (1, "R2", 0, None), (1, "U", 3, 0),
    (1, "D", 0, 3), "at13", (0, "D", 0, 1), (0, "U", 3, 2), "t2.0", "t2.1", "t2.2", "t2.3", (1, "R2", 1, None), (1, "D", 1, 3), (1, "U", 2, 0),
    (0, "FIN", 0, 2), (0, "FIN", 0, 1), "t3.0", "t3.1", "t3.2", "t3.3", (2, "R1", 0, None), "t4.0", (0, "FIN", 0, 3), (0, "FIN", 0, 0), (1, "D", 0, 2),
    (1, "U", 3, 1), (2, "R1", 1, None), "t4.1", (2, "R1", 2, None), "t4.2", (1, "R2", 2, None), (1, "D", 2, 3), (1, "U", 1, 0), (2, "R1", 3, None),
    "t4.3", (3, "R1", 0, None), "rb10", (1, "U", 2, 1), (1, "D", 1, 2), (3, "R1", 1, None), (3, "R1", 2, None), "cb", (3, "R1", 3, None),
    (1, "R2", 3, None), (2, "R2", 0, None), (2, "U", 3, 0), (2, "D", 0, 3), (1, "D", 0, 1), (1, "U", 3, 2), (4, "R1", 0, None), (4, "R1", 1, None),
    (4, "R1", 2, None), "rb12", (4, "R1", 3, None), (2, "R2", 1, None), (2, "D", 1, 3), (2, "U", 2, 0), "nb2", (1, "Z3", 0, 2), (1, "Z3", 0, 1),
    "t5.0", "t5.1", (2, "D", 0, 2), (2, "U", 3, 1), "t5.2", "t5.3", "mb13", (2, "R2", 2, None), (1, "Z3", 0, 3), (1, "Z3", 0, 0), (2, "D", 2, 3),
    (2, "U", 1, 0), "at00", (5, "R1", 0, None), (2, "D", 1, 2), (2, "U", 2, 1), (5, "R1", 1, None), (2, "R2", 3, None), (4, "R2", 0, None),
    (5, "R1", 2, None), (4, "U", 3, 0), (4, "D", 0, 3), (5, "R1", 3, None), "at01", (3, "R2", 0, None), (2, "D", 0, 1), (2, "U", 3, 2), "at02",
    (3, "R2", 1, None), (2, "Z3", 0, 2), (2, "Z3", 0, 1), (4, "R2", 1, None), (4, "U", 2, 0), (4, "D", 1, 3), "at03", (3, "R2", 2, None),
    (3, "R2", 3, None), "cs", "t6.0", (4, "R2", 2, None), (4, "D", 2, 3), (4, "U", 1, 0), (4, "D", 0, 2), (4, "U", 3, 1), (2, "Z3", 0, 0),
    (2, "Z3", 0, 3), "t6.1", "t6.2", (1, "FIN", 0, 3), (1, "FIN", 0, 0), (1, "FIN", 0, 2), (1, "FIN", 0, 1), "t6.3", "t7.0", (4, "D", 1, 2),
    (4, "U", 2, 1), "t7.1", (6, "R1", 0, None), "t7.2", (4, "R2", 3, None), (6, "R1", 1, None), "t7.3", "t8.0", (6, "R1", 2, None), (5, "R2", 0, None),
    (5, "U", 3, 0), (5, "D", 0, 3), (6, "R1", 3, None), "t8.1", (4, "D", 0, 1), (4, "U", 3, 2), (7, "R1", 0, None), (2, "FIN", 0, 1), (2, "FIN", 0, 2),
    "t8.2", (7, "R1", 1, None), "t8.3", "rb14", (7, "R1", 2, None), (2, "FIN", 0, 0), (2, "FIN", 0, 3), (5, "R2", 1, None), (5, "U", 2, 0),
    (5, "D", 1, 3), (7, "R1", 3, None), (8, "R1", 0, None), (4, "Z3", 0, 2), (4, "Z3", 0, 1), "rb15", (8, "R1", 1, None), (8, "R1", 2, None),
    (5, "U", 3, 1), (5, "D", 0, 2), "tok", (4, "Z3", 0, 0), (4, "Z3", 0, 3), (5, "R2", 2, None), (5, "D", 2, 3), (5, "U", 1, 0), (8, "R1", 3, None),
    (5, "U", 2, 1), (5, "D", 1, 2), (5, "R2", 3, None), (5, "D", 0, 1), (5, "U", 3, 2), (3, "R3", 0, None), (3, "D", 0, 3), (3, "U", 3, 0),
    (3, "R3", 1, None), (3, "U", 2, 0), (3, "D", 1, 3), (3, "R3", 2, None), (3, "D", 2, 3), (3, "U", 1, 0), (7, "R2", 0, None), (7, "D", 0, 3),
    (7, "U", 3, 0), (3, "R3", 3, None), (5, "Z3", 0, 2), (5, "Z3", 0, 1), (3, "U", 3, 1), (3, "D", 0, 2), (6, "R2", 0, None), (3, "U", 2, 1),
    (3, "D", 1, 2), (5, "Z3", 0, 3), (5, "Z3", 0, 0), (7, "R2", 1, None), (7, "D", 1, 3), (7, "U", 2, 0), (6, "R2", 1, None), (3, "U", 3, 2),
    (3, "D", 0, 1), (6, "R2", 2, None), (3, "FIN", 0, 2), (3, "FIN", 0, 1), (7, "R2", 2, None), (7, "D", 2, 3), (7, "U", 1, 0), (6, "R2", 3, None),
    (7, "D", 0, 2), (7, "U", 3, 1), (3, "FIN", 0, 3), (3, "FIN", 0, 0), (4, "FIN", 0, 2), (4, "FIN", 0, 1), (7, "R2", 3, None), (8, "R2", 0, None),
    (8, "D", 0, 3), (8, "U", 3, 0), (7, "D", 1, 2), (7, "U", 2, 1), (5, "FIN", 0, 1), (5, "FIN", 0, 2), (5, "FIN", 0, 0), (5, "FIN", 0, 3),
    (7, "U", 3, 2), (7, "D", 0, 1), (8, "R2", 1, None), (8, "U", 2, 0), (8, "D", 1, 3), (7, "Z3", 0, 1), (7, "Z3", 0, 2), (8, "R2", 2, None),
    (8, "D", 2, 3), (8, "U", 1, 0), (8, "D", 0, 2), (8, "U", 3, 1), (7, "Z3", 0, 0), (7, "Z3", 0, 3), (4, "FIN", 0, 0), (4, "FIN", 0, 3),
    (8, "D", 1, 2), (8, "U", 2, 1), (8, "R2", 3, None), (6, "R3", 0, None), (6, "D", 0, 3), (6, "U", 3, 0), (8, "D", 0, 1), (8, "U", 3, 2),
    (6, "R3", 1, None), (6, "D", 1, 3), (6, "U", 2, 0), (6, "R3", 2, None), (6, "D", 2, 3), (6, "U", 1, 0), (6, "R3", 3, None), (6, "D", 0, 2),
    (6, "U", 3, 1), (8, "Z3", 0, 2), (8, "Z3", 0, 1), (7, "FIN", 0, 3), (7, "FIN", 0, 0), (7, "FIN", 0, 2), (7, "FIN", 0, 1), (6, "D", 1, 2),
    (6, "U", 2, 1), (8, "Z3", 0, 0), (8, "Z3", 0, 3), (6, "D", 0, 1), (6, "U", 3, 2), (8, "FIN", 0, 2), (8, "FIN", 0, 1), (6, "FIN", 0, 2),
    (6, "FIN", 0, 1), (8, "FIN", 0, 3), (8, "FIN", 0, 0), (6, "FIN", 0, 0), (6, "FIN", 0, 3),
]


NT = 9
NS, NR = 27, 33

class Reduce:
    def __init__(self, p, t, order, PB, L0, L1, L2, UP, DN, LX, ssem, rsem, out):
        self.p, self.t, self.order = p, t, order
        self.PB, self.L0, self.L1, self.L2, self.UP, self.DN, self.LX = PB, L0, L1, L2, UP, DN, LX
        self.ssem, self.rsem, self.out = ssem, rsem, out
        self.sends = []
        self.me = {"x": p.x, "y": p.y}
        self.flat = order == "A"
        if not self.flat: self.b1, self.b2 = order[0], order[2]
    def partner(self, b):
        return self.p.dev(**{b: 1 - self.me[b]})
    def desc(self, src, dst, k, slot, target):
        return pltpu.make_async_remote_copy(src, dst, self.ssem.at[k], self.rsem.at[slot], device_id=target, device_id_type=MESH)
    def copy(self, what, k, slot, z=None):
        def make():
            src, dst, target = what()
            return self.desc(src, dst, k, slot, target)
        make().start()
        self.sends.append((make, z))
    def arrive(self, dst, slot):
        self.desc(dst, dst, 0, slot, self.p.dev()).wait_recv()
    def finish(self, z):
        for make, at in self.sends:
            if at == z: make().wait_send()
    def height(self, k):
        return jnp.where(self.p.z < 2, 3 - k, k)
    def sib(self, k):
        zz = self.height(k)
        self.copy(lambda: (self.PB.at[zz, :, :, 1 - self.p.c], self.L0.at[zz], self.p.dev(c=1 - self.p.c)), k, zz)
    def pair(self, zz, b2name, b2v, r=pl.ds(0, 32)):
        if b2name == "y": return self.PB.at[zz, b2v, :, self.p.c, r]
        return self.PB.at[zz, :, b2v, self.p.c, r]
    def block(self, zz, r=pl.ds(0, 32), **where):
        return self.PB.at[zz, where.get("y", self.p.y), where.get("x", self.p.x), self.p.c, r]
    def mine(self, zz):
        return self.block(zz) if self.flat else self.pair(zz, self.b2, self.me[self.b2])
    def halves(self):
        return [(h, b1, b2, pl.ds(16 * h, 16)) for h, (b1, b2) in enumerate((("x", "y"), ("y", "x")))]

    def R1(self, k):
        p, zz = self.p, self.height(k)
        self.arrive(self.L0.at[zz], zz)
        for yy in range(2):
            for xx in range(2):
                self.PB[zz, yy, xx, p.c] = self.PB[zz, yy, xx, p.c] + self.L0[zz, yy, xx]
        if self.flat:
            for h, b1, b2, r in self.halves():
                self.copy(lambda b2=b2, r=r: (self.pair(zz, b2, 1 - self.me[b2], r), self.L1.at[zz, :, r], self.partner(b2)), 4 + 4 * h + k, 17 + 4 * h + zz)
        else:
            self.copy(lambda: (self.pair(zz, self.b2, 1 - self.me[self.b2]), self.L1.at[zz], self.partner(self.b2)), 4 + k, 4 + zz)
    def R2(self, k):
        zz = self.height(k)
        if self.flat:
            for h, b1, b2, r in self.halves():
                self.arrive(self.L1.at[zz, :, r], 17 + 4 * h + zz)
                o = self.pair(zz, b2, self.me[b2], r)
                o[...] = o[...] + self.L1[zz, :, r]
                self.copy(lambda b1=b1, r=r: (self.block(zz, r, **{b1: 1 - self.me[b1]}), self.L2.at[zz, r], self.partner(b1)), 12 + 4 * h + k, 25 + 4 * h + zz)
        else:
            self.arrive(self.L1.at[zz], 4 + zz)
            o = self.mine(zz)
            o[...] = o[...] + self.L1[zz]
    def R3(self, k):
        zz = self.height(k)
        for h, b1, b2, r in self.halves():
            self.arrive(self.L2.at[zz, r], 25 + 4 * h + zz)
            o = self.block(zz, r)
            o[...] = o[...] + self.L2[zz, r]
    def U(self, zu, z):
        o, land = self.mine(zu), self.UP.at[zu - 1]
        if 0 < z <= zu:
            self.arrive(land, 8 + zu)
            o[...] = o[...] + land[...]
        if z < zu: self.copy(lambda: (self.mine(zu), self.UP.at[zu - 1], self.p.dev(z=z + 1)), 20 + zu - 1, 8 + zu, z)
    def D(self, zd, z):
        o, land = self.mine(zd), self.DN.at[zd]
        if zd <= z < 3:
            self.arrive(land, 12 + zd)
            o[...] = o[...] + land[...]
        if z > zd: self.copy(lambda: (self.mine(zd), self.DN.at[zd], self.p.dev(z=z - 1)), 23 + zd, 12 + zd, z)
    def Z3(self, k, z):
        if z > 0: self.U(z, z)
        if z < 3: self.D(z, z)
        self.copy(lambda: (self.block(z, **{self.b1: 1 - self.me[self.b1]}), self.LX, self.partner(self.b1)), 26, 16, z)
    def FIN(self, k, z):
        v = self.block(z)
        if self.flat:
            if z > 0: self.U(z, z)
            if z < 3: self.D(z, z)
            self.out(v[...].astype(F32))
        else:
            self.arrive(self.LX, 16)
            self.out(v[...].astype(F32) + self.LX[...].astype(F32))

W_ORDER = ["o0", "o1", "o2", "o3", 8, 9, 10, 11, 12, 7, 4, 5, 6, 3, 0, 1, 2]
T_ORDER = [5, 4, 1, 2, 3, 0]
NW = 3

def backward_kernel(gains, buf, gfo, qkv, P, H, T, AT, GP, SR, cot,
                    o_tok, osp, oso, ocp, oco, oai, oao, oen,
                    PB, L0, L1, L2, UPC, DNC, UPA, DNA, LX, wbuf, hb, gpb, tb, atb, srb, pb, cotb, g, gb, gr, gx, gqkv, gtok,
                    ssem, rsem, csem, crsem, wsem, hsem, gpsem, tsem, msem, qsem, psem, osem):
    p = Place()
    neighbours_in = entry_barrier(p)
    lo, hi = half_masks()
    def w_copy(i):
        n = W_ORDER[i]
        src = gfo.at[int(n[1])] if isinstance(n, str) else buf.at[n]
        return pltpu.make_async_copy(src, wbuf.at[i % NW], wsem.at[i])
    h_copy = lambda i: pltpu.make_async_copy(H.at[2 - i], hb.at[i % 2], hsem.at[i])
    gp_copy = lambda j: pltpu.make_async_copy(GP.at[j], gpb.at[j % 2], gpsem.at[j])
    t_copy = lambda i: pltpu.make_async_copy(T.at[T_ORDER[i]], tb.at[i % 3], tsem.at[i])
    q_copy = lambda a, j: pltpu.make_async_copy(qkv.at[3 * a + j], PB.at[6 + a, j], qsem.at[3 * a + j])
    p_copy = lambda a: pltpu.make_async_copy(P.at[a], pb, psem.at[a])
    m_copy = [pltpu.make_async_copy(cot, cotb, msem.at[0]), pltpu.make_async_copy(SR, srb, msem.at[1]), pltpu.make_async_copy(AT, atb, msem.at[2])]
    h_copy(0).start(); m_copy[0].start(); w_copy(0).start(); gp_copy(0).start(); w_copy(1).start(); gp_copy(1).start(); w_copy(2).start()
    h_copy(1).start(); m_copy[1].start(); m_copy[2].start()
    for i in range(3): t_copy(i).start()
    for j in range(3): q_copy(1, j).start()
    p_copy(1).start()
    for j in range(3): q_copy(0, j).start()

    def o_ad(v):
        oai[...] = v[:, :512]
        oao[:, 0:512] = v[0:16, 512:]
        oao[:, 512:1024] = v[16:32, 512:]
    def put(ref, j=None):
        def f(v):
            if j is None: ref[...] = v
            else: ref[j] = v
        return f
    finals = [o_ad, put(oco), put(ocp, 1), put(ocp, 2), put(ocp, 0), put(oso), put(osp, 1), put(osp, 2), put(osp, 0)]
    reds = []
    nc = na = 0
    for t in range(NT):
        if ORDERS[t] == "A":
            up, dn, l2 = UPA.at[na], DNA.at[na], L2.at[na]; na += 1
        else:
            up, dn, l2 = UPC.at[nc], DNC.at[nc], None; nc += 1
        reds.append(Reduce(p, t, ORDERS[t], PB.at[t], L0.at[t], L1.at[t], l2, up, dn, LX.at[t], ssem.at[t], rsem.at[t], finals[t]))

    compute = {}
    def work(name, fn): compute[name] = fn

    def norm_back(i, first=False):
        def run():
            h_copy(i).wait()
            if first: m_copy[0].wait()
            @pl.loop(0, 4)
            def _(n):
                r = pl.ds(pl.multiple_of(n * 64, 64), 64)
                h = hb[i % 2, r, :]
                center = h - jnp.mean(h, axis=-1, keepdims=True)
                inv = lax.rsqrt(jnp.mean(center * center, axis=-1, keepdims=True) + EPS)
                nrm = center * inv
                gy = cotb[r, :].astype(F32) if first else g[r, :]
                a = gy * gains[2 - i, :][None]
                v = (a - jnp.mean(a, axis=-1, keepdims=True) - nrm * jnp.mean(a * nrm, axis=-1, keepdims=True)) * inv
                g[r, :] = v
                gb[r, :] = v.astype(BF)
            if i == 0: h_copy(2).start()
        return run

    def used(i):
        if i + NW < len(W_ORDER): w_copy(i + NW).start()

    def nt(lhs, i, fn):
        fn(dot_nt(lhs(), wbuf[i % NW]))

    def hidden_back(j):
        def run():
            w_copy(j).wait(); gp_copy(j).wait()
            def st(v):
                PB[8, j] = (gpb[j % 2] * v).astype(BF).reshape(2, 2, 2, 32, 1024)
            nt(lambda: gb[...], j, st)
            used(j)
            if j + 2 < 4: gp_copy(j + 2).start()
        return run

    def adapter_back():
        i = 4
        w_copy(i).wait(); m_copy[1].wait(); m_copy[2].wait()
        v = wbuf[i % NW, :, 512:1024].reshape(32, 32, 512)
        top, bot = v[:, :16].reshape(512, 512), v[:, 16:].reshape(512, 512)
        s = dot_nt(gb[:, 0:512], top) + dot_nt(gb[:, 512:1024], bot)
        gr[...] = (srb[...] * (4.0 * s)).astype(BF)
        wai = wbuf[i % NW, :, 0:512]
        g[...] = g[...] + dot_nt(gr[...], wai)
        used(i)

    def rows_of(k):
        return pl.ds(pl.multiple_of(reds[0].height(k) * 256, 256), 256)
    def adapter_grads(k):
        def run():
            if k == 0:
                neighbours_in()
                for h in range(2):
                    v = 4.0 * dot(atb[...], gb[:, 512 * h:512 * h + 512])
                    PB[0, :, :, :, :, 16 * h:16 * h + 16, 512:1024] = v.astype(BF).reshape(4, 2, 2, 2, 16, 512)
                t_copy(0).wait()
            v = dot(tb[0, rows_of(k), :], gr[...])
            PB[0, reds[0].height(k), :, :, :, :, 0:512] = v.astype(BF).reshape(2, 2, 2, 32, 512)
            reds[0].sib(k)
            if k == 3: t_copy(3).start()
        return run

    def hidden_in_back(j):
        def run():
            i = 5 + j
            w_copy(i).wait()
            def st(v): g[...] = g[...] + v
            nt(lambda: PB[8, j].reshape(256, 1024), i, st)
            used(i)
        return run

    def grad_tile(t, ti, rhs, last, k):
        def run():
            if k == 0 and t in (1, 2, 4, 5, 6): t_copy(ti).wait()
            PB[t, reds[t].height(k)] = dot(tb[ti % 3, rows_of(k), :], rhs()).astype(BF).reshape(2, 2, 2, 32, 1024)
            reds[t].sib(k)
            if k == 3 and last and ti + 3 < 6: t_copy(ti + 3).start()
        return run

    def mix_back(i):
        def run():
            w_copy(i).wait()
            def st(v): gx[...] = v.astype(BF)
            nt(lambda: gb[...], i, st)
            used(i)
        return run

    def attend_back(a, part):
        def run():
            if part == 0:
                p_copy(a).wait()
                for j in range(3): q_copy(a, j).wait()
            u = part // 2
            @pl.loop(0, 4, unroll=4)
            def _(n):
                pr = (part % 2) * 4 + n
                r, cc = pl.ds(u * 128, 128), cols(pr, 128)
                q, k, v = (PB[6 + a, j, u, :, :, :, cc].reshape(128, 128) for j in range(3))
                go = pair_up(gx[r, cc], lo, hi)
                prob = pb[u * 8 + pr]
                dp = dot_nt(go, v)
                ds = (prob * (dp - jnp.sum(prob * dp, axis=-1, keepdims=True))).astype(BF)
                gqkv[0, r, cc] = (dot(side(ds), pair_up(k, lo, hi)) * 0.125).astype(BF)
                gqkv[1, r, cc] = (dot_tn(ds, pair_up(q, lo, hi)) * 0.125).astype(BF)
                gqkv[2, r, cc] = dot_tn(prob.astype(BF), go).astype(BF)
            if part == 3 and a == 1: p_copy(0).start()
        return run

    def row_back(i, j, dst):
        def run():
            w_copy(i).wait()
            nt(lambda: gqkv[j], i, dst)
            used(i)
        return run
    def to_g(v): g[...] = g[...] + v
    cs = []
    me = p.x * 2 + p.c
    def context_back():
        i = 11
        w_copy(i).wait()
        def st(v): PB[8, 0] = (ctxf[...] + v).astype(BF).reshape(2, 2, 2, 32, 1024)
        nt(lambda: gqkv[2], i, st)
        used(i)
        for k, (dx, dc) in enumerate(((0, 1), (1, 0), (1, 1))):
            tx = (p.x + dx) % 2; tc = (p.c + dc) % 2
            c_ = pltpu.make_async_remote_copy(PB.at[8, 0, :, tx, tc], oen.at[0, me], csem.at[k], crsem.at[me], device_id=p.dev(x=tx, c=tc), device_id_type=MESH)
            c_.start(); cs.append(c_)
        c_ = pltpu.make_async_copy(PB.at[8, 0, :, p.x, p.c], oen.at[0, me], osem.at[0]); c_.start(); cs.append(c_)

    ctxf = gpb.at[0]
    def ctx_part(v): ctxf[...] = v
    def context_sent():
        for c_ in cs[:3]: c_.wait_send()
        cs[3].wait()
    def tokens_back():
        i = 16
        w_copy(i).wait()
        def st(v): gtok[...] = (g[...] + v).astype(BF)
        nt(lambda: gqkv[2], i, st)
        pltpu.make_async_copy(gtok, o_tok, osem.at[1]).start()

    def tile(t, ti, rhs, last):
        for zz in range(4): work(f"t{t}.{zz}", grad_tile(t, ti, rhs, last, zz))
    work("nb0", norm_back(0, True))
    for j in range(4): work(f"hb{j}", hidden_back(j))
    work("adb", adapter_back)
    for zz in range(4): work(f"adg.{zz}", adapter_grads(zz))
    for j in range(4): work(f"hi{j}", hidden_in_back(j))
    work("nb1", norm_back(1))
    tile(1, 1, lambda: gb[...], True)
    work("mb9", mix_back(9))
    for part in range(4): work(f"at1{part}", attend_back(1, part))
    tile(2, 2, lambda: gqkv[1], False)
    tile(3, 2, lambda: gqkv[2], True)
    tile(4, 3, lambda: gqkv[0], True)
    work("rb10", row_back(10, 1, ctx_part))
    work("cb", context_back)
    work("rb12", row_back(12, 0, to_g))
    work("nb2", norm_back(2))
    tile(5, 4, lambda: gb[...], True)
    work("mb13", mix_back(13))
    for part in range(4): work(f"at0{part}", attend_back(0, part))
    work("cs", context_sent)
    tile(6, 5, lambda: gqkv[1], False)
    tile(7, 5, lambda: gqkv[2], False)
    tile(8, 5, lambda: gqkv[0], True)
    work("rb14", row_back(14, 0, to_g))
    work("rb15", row_back(15, 1, to_g))
    work("tok", tokens_back)
    run_plan(PLAN_B, compute, reds, [p.z == z for z in range(4)])
    for r in reds: r.finish(None)
    for z in range(4):
        @pl.when(p.z == z)
        def _():
            for r in reds: r.finish(z)
    pltpu.make_async_copy(gtok, o_tok, osem.at[1]).wait()
    for k, (dx, dc) in enumerate(((0, 1), (1, 0), (1, 1))):
        tx = (p.x + dx) % 2; tc = (p.c + dc) % 2
        w = tx * 2 + tc
        pltpu.make_async_remote_copy(PB.at[8, 0, :, tx, tc], oen.at[0, w], csem.at[k], crsem.at[w], device_id=p.dev(), device_id_type=MESH).wait_recv()

def backward(gains, buf, gfo, qkv, P, H, T, AT, GP, SR, cot):
    any_ = pl.BlockSpec(memory_space=pl.ANY)
    vm = pl.BlockSpec(memory_space=pltpu.VMEM)
    V, S, D = pltpu.VMEM, jax.ShapeDtypeStruct, pltpu.SemaphoreType.DMA
    ops = (gains, buf.reshape(13, 1024, 1024), gfo.reshape(4, 1024, 1024), qkv.reshape(6, 2, 2, 2, 32, 1024), P, H, T, AT, GP, SR, cot)
    return pl.pallas_call(backward_kernel,
        out_shape=(S((256, 1024), BF), S((3, 32, 1024), F32), S((32, 1024), F32), S((3, 32, 1024), F32), S((32, 1024), F32), S((32, 512), F32), S((16, 1024), F32), S((1, 4, 2, 32, 1024), BF)),
        in_specs=[vm] + [any_] * 10, out_specs=(any_,) + (vm,) * 6 + (any_,),
        scratch_shapes=[V((NT, 4, 2, 2, 2, 32, 1024), BF), V((NT, 4, 2, 2, 32, 1024), BF), V((NT, 4, 2, 32, 1024), BF), V((3, 4, 32, 1024), BF),
                        V((6, 3, 2, 32, 1024), BF), V((6, 3, 2, 32, 1024), BF), V((3, 3, 32, 1024), BF), V((3, 3, 32, 1024), BF), V((NT, 32, 1024), BF),
                        V((NW, 1024, 1024), BF), V((2, 256, 1024), F32), V((2, 256, 1024), F32), V((3, 1024, 256), BF), V((512, 256), BF), V((256, 512), F32),
                        V((16, 256, 128), F32), V((256, 1024), BF), V((256, 1024), F32), V((256, 1024), BF), V((256, 512), BF), V((256, 1024), BF),
                        V((3, 256, 1024), BF), V((256, 1024), BF),
                        D((NT, NS)), D((NT, NR)), D((3,)), D((4,)), D((17,)), D((3,)), D((4,)), D((6,)), D((3,)), D((6,)), D((2,)), D((2,))],
        compiler_params=pltpu.CompilerParams(collective_id=1, has_side_effects=True, vmem_limit_bytes=63 << 20),
        name="backward")(*ops)


def finish_kernel(*refs):
    n = (len(refs) - 1) // 3
    ins, outs, held, sem = refs[:n], refs[n:2 * n], refs[2 * n:3 * n], refs[3 * n]
    first = [pltpu.make_async_copy(ins[k], held[k], sem.at[k]) for k in range(n)]
    last = [pltpu.make_async_copy(held[k], outs[k], sem.at[n + k]) for k in range(n)]
    for c in first: c.start()
    for k in range(n):
        first[k].wait()
        last[k].start()
    for c in last: c.wait()

def finish(*arrays):
    any_ = pl.BlockSpec(memory_space=pl.ANY)
    n = len(arrays)
    return pl.pallas_call(finish_kernel, out_shape=tuple(jax.ShapeDtypeStruct(a.shape, a.dtype) for a in arrays),
        in_specs=[any_] * n, out_specs=(any_,) * n,
        scratch_shapes=[pltpu.VMEM(a.shape, a.dtype) for a in arrays] + [pltpu.SemaphoreType.DMA((2 * n,))],
        compiler_params=pltpu.CompilerParams(vmem_limit_bytes=62 << 20), name="finish")(*arrays)


def device_program(tokens, encoder, dec_lengths, enc_lengths, gains, self_proj, self_out, cross_proj, cross_out, ffn_in, ffn_out, adapt_in, adapt_out, cotangent):
    shards = (self_proj, self_out, cross_proj, cross_out, ffn_in, ffn_out, adapt_in, adapt_out)
    buf, gfo, qkv, probs, hidden, turned, act_turned, gelu_slope, silu_slope, layer_out = forward(tokens, gains, dec_lengths, enc_lengths, shards, encoder)
    gtok, osp, oso, ocp, oco, oai, oao, oen = backward(gains, buf, gfo, qkv, probs, hidden, turned, act_turned, gelu_slope, silu_slope, cotangent)
    return finish(layer_out, gtok, oen, osp, oso, ocp, oco, oai, oao)


def solution(mesh):
    in_specs = (
        P(("seq", "enc"), None),
        P("seq", None, None, "enc", None),
        P(("seq", "enc"), None),
        P(("seq", "enc"), None),
        P(),
        P(None, ("seq", "enc"), None),
        P(("seq", "enc"), None),
        P(None, ("seq", "enc"), None),
        P(("seq", "enc"), None),
        P(("seq", "enc"), None),
        P(("seq", "enc"), None),
        P(("seq", "enc"), None),
        P(("seq", "enc"), None),
        P(("seq", "enc"), None),
    )
    out_specs = (
        P(("seq", "enc"), None),
        P(("seq", "enc"), None),
        P("seq", None, None, "enc", None),
        P(None, ("seq", "enc"), None),
        P(("seq", "enc"), None),
        P(None, ("seq", "enc"), None),
        P(("seq", "enc"), None),
        P(("seq", "enc"), None),
        P(("seq", "enc"), None),
    )
    fast = (mesh.shape["seq"], mesh.shape["enc"]) == (8, 4)
    return jax.shard_map(
        device_program if fast else per_device, mesh=mesh, in_specs=in_specs, out_specs=out_specs, check_vma=False
    )
```

```python
import jax
import jax.numpy as jnp
from jax import lax
from jax.experimental import pallas as pl
from jax.experimental.pallas import tpu as pltpu
from jax.sharding import PartitionSpec as P

HEADS = 16
ADAPT = 512
MICRO = 2


EPSILON = 1e-05
NEGATIVE = -1e30


def matmul(left, right):
    return jnp.dot(left, right, preferred_element_type=jnp.float32)


def matmul_tn(left, right):
    return lax.dot_general(
        left, right, (((0,), (0,)), ((), ())), preferred_element_type=jnp.float32
    )


def matmul_nt(left, right):
    return lax.dot_general(
        left, right, (((1,), (1,)), ((), ())), preferred_element_type=jnp.float32
    )


def layer_norm(hidden, gain):
    center = hidden - jnp.mean(hidden, axis=-1, keepdims=True)
    spread = jnp.mean(center * center, axis=-1, keepdims=True)
    return center * lax.rsqrt(spread + EPSILON) * gain


def norm_back(hidden, gain, grad_out):
    _, pullback = jax.vjp(lambda value: layer_norm(value, gain), hidden)
    return pullback(grad_out)[0]


def gelu_exact(value):
    return jax.nn.gelu(value, approximate=False)


def slot_masks(dec_row, enc_row, rows):
    half_rows = rows // 2
    places = lax.broadcasted_iota(jnp.int32, (rows,), 0)
    paired = dec_row[1] > 0
    second = jnp.logical_and(paired, places >= half_rows)
    anchor = jnp.where(second, half_rows, 0).astype(jnp.int32)
    dec_valid = jnp.where(second, dec_row[1], dec_row[0])
    enc_valid = jnp.where(second, enc_row[1], enc_row[0])
    key_live = places - anchor < dec_valid
    context_live = places - anchor < enc_valid
    same_slot = second[:, None] == second[None, :]
    causal = places[None, :] <= places[:, None]
    self_mask = same_slot & causal & key_live[None, :]
    cross_mask = same_slot & context_live[None, :]
    return (self_mask, cross_mask)


def split_heads(matrix):
    return matrix.reshape(matrix.shape[0], HEADS, matrix.shape[1] // HEADS)


def attend(queries, keys, values, allowed):
    depth = queries.shape[1] // HEADS
    scores = jnp.einsum(
        "qhd,khd->hqk", split_heads(queries), split_heads(keys), preferred_element_type=jnp.float32
    ) * float(depth) ** (-0.5)
    masked = jnp.where(allowed[None], scores, NEGATIVE)
    weights = jnp.exp(masked - jnp.max(masked, axis=-1, keepdims=True))
    probs = weights / jnp.sum(weights, axis=-1, keepdims=True)
    mixed = jnp.einsum(
        "hqk,khd->qhd",
        probs.astype(jnp.bfloat16),
        split_heads(values),
        preferred_element_type=jnp.float32,
    )
    return (mixed.reshape(queries.shape).astype(jnp.bfloat16), probs)


def attend_back(grad_mixed, queries, keys, values, probs):
    depth = queries.shape[1] // HEADS
    factor = float(depth) ** (-0.5)
    grad_heads = split_heads(grad_mixed)
    grad_probs = jnp.einsum(
        "qhd,khd->hqk", grad_heads, split_heads(values), preferred_element_type=jnp.float32
    )
    inner = jnp.sum(probs * grad_probs, axis=-1, keepdims=True)
    grad_scores = (probs * (grad_probs - inner)).astype(jnp.bfloat16)
    grad_query = (
        jnp.einsum(
            "hqk,khd->qhd", grad_scores, split_heads(keys), preferred_element_type=jnp.float32
        )
        * factor
    )
    grad_key = (
        jnp.einsum(
            "hqk,qhd->khd", grad_scores, split_heads(queries), preferred_element_type=jnp.float32
        )
        * factor
    )
    grad_value = jnp.einsum(
        "hqk,qhd->khd", probs.astype(jnp.bfloat16), grad_heads, preferred_element_type=jnp.float32
    )
    return (
        grad_query.reshape(queries.shape).astype(jnp.bfloat16),
        grad_key.reshape(keys.shape).astype(jnp.bfloat16),
        grad_value.reshape(values.shape).astype(jnp.bfloat16),
    )


def per_device(
    tokens,
    encoder,
    dec_lengths,
    enc_lengths,
    gains,
    self_proj,
    self_out,
    cross_proj,
    cross_out,
    ffn_in,
    ffn_out,
    adapt_in,
    adapt_out,
    cotangent,
):
    shards = (self_proj, self_out, cross_proj, cross_out, ffn_in, ffn_out, adapt_in, adapt_out)

    def obtain():
        return (
            lax.all_gather(shards[0], ("seq", "enc"), axis=1, tiled=True),
            lax.all_gather(shards[1], ("seq", "enc"), axis=0, tiled=True),
            lax.all_gather(shards[2], ("seq", "enc"), axis=1, tiled=True),
            lax.all_gather(shards[3], ("seq", "enc"), axis=0, tiled=True),
            lax.all_gather(shards[4], ("seq", "enc"), axis=0, tiled=True),
            lax.all_gather(shards[5], ("seq", "enc"), axis=0, tiled=True),
            lax.all_gather(shards[6], ("seq", "enc"), axis=0, tiled=True),
            lax.all_gather(shards[7], ("seq", "enc"), axis=0, tiled=True),
        )

    rows = tokens.shape[0] // MICRO
    width = tokens.shape[1]
    owner = lax.axis_index("enc")
    acc_self = jnp.zeros((width, 3, width), jnp.float32)
    acc_self_out = jnp.zeros((width, width), jnp.float32)
    acc_cross = jnp.zeros((width, 3, width), jnp.float32)
    acc_cross_out = jnp.zeros((width, width), jnp.float32)
    acc_adapt_in = jnp.zeros((width, ADAPT), jnp.float32)
    acc_adapt_out = jnp.zeros((ADAPT, width), jnp.float32)
    outputs = []
    grad_rows = []
    grad_contexts = []
    for micro_index in range(MICRO):
        w_self, w_self_out, w_cross, w_cross_out, w_ffn_in, w_ffn_out, w_adapt_in, w_adapt_out = (
            obtain()
        )
        lower = micro_index * rows
        token_rows = tokens[lower : lower + rows]
        self_mask, cross_mask = slot_masks(dec_lengths[micro_index], enc_lengths[micro_index], rows)
        pieces = encoder[0, :, micro_index]
        context = lax.dynamic_index_in_dim(
            lax.all_gather(pieces, "enc", axis=1, tiled=True), owner, 0, keepdims=False
        )
        self_query = matmul(token_rows, w_self[0]).astype(jnp.bfloat16)
        self_key = matmul(token_rows, w_self[1]).astype(jnp.bfloat16)
        self_value = matmul(token_rows, w_self[2]).astype(jnp.bfloat16)
        self_mix, self_probs = attend(self_query, self_key, self_value, self_mask)
        first_sum = token_rows.astype(jnp.float32) + matmul(self_mix, w_self_out)
        first_norm = layer_norm(first_sum, gains[0])
        first_low = first_norm.astype(jnp.bfloat16)
        cross_query = matmul(first_low, w_cross[0]).astype(jnp.bfloat16)
        cross_key = matmul(context, w_cross[1]).astype(jnp.bfloat16)
        cross_value = matmul(context, w_cross[2]).astype(jnp.bfloat16)
        cross_mix, cross_probs = attend(cross_query, cross_key, cross_value, cross_mask)
        second_sum = first_norm + matmul(cross_mix, w_cross_out)
        second_norm = layer_norm(second_sum, gains[1])
        second_low = second_norm.astype(jnp.bfloat16)
        ffn_pre = matmul(second_low, w_ffn_in)
        ffn_act = gelu_exact(ffn_pre).astype(jnp.bfloat16)
        adapt_pre = matmul(second_low, w_adapt_in)
        adapt_act = jax.nn.silu(adapt_pre).astype(jnp.bfloat16)
        third_sum = second_norm + matmul(ffn_act, w_ffn_out) + 4.0 * matmul(adapt_act, w_adapt_out)
        outputs.append(layer_norm(third_sum, gains[2]).astype(jnp.bfloat16))
        w_self, w_self_out, w_cross, w_cross_out, w_ffn_in, w_ffn_out, w_adapt_in, w_adapt_out = (
            obtain()
        )
        grad_third = norm_back(
            third_sum, gains[2], cotangent[lower : lower + rows].astype(jnp.float32)
        )
        grad_branch = grad_third.astype(jnp.bfloat16)
        _, gelu_pull = jax.vjp(gelu_exact, ffn_pre)
        grad_ffn_pre = gelu_pull(matmul_nt(grad_branch, w_ffn_out))[0].astype(jnp.bfloat16)
        grad_adapt_act = matmul_nt(grad_branch, w_adapt_out) * 4.0
        _, silu_pull = jax.vjp(jax.nn.silu, adapt_pre)
        grad_adapt_pre = silu_pull(grad_adapt_act)[0].astype(jnp.bfloat16)
        acc_adapt_out = acc_adapt_out + matmul_tn(adapt_act, grad_branch) * 4.0
        acc_adapt_in = acc_adapt_in + matmul_tn(second_low, grad_adapt_pre)
        grad_second = (
            grad_third + matmul_nt(grad_ffn_pre, w_ffn_in) + matmul_nt(grad_adapt_pre, w_adapt_in)
        )
        grad_second_sum = norm_back(second_sum, gains[1], grad_second)
        grad_cross_branch = grad_second_sum.astype(jnp.bfloat16)
        acc_cross_out = acc_cross_out + matmul_tn(cross_mix, grad_cross_branch)
        grad_cross_mix = matmul_nt(grad_cross_branch, w_cross_out).astype(jnp.bfloat16)
        grad_cq, grad_ck, grad_cv = attend_back(
            grad_cross_mix, cross_query, cross_key, cross_value, cross_probs
        )
        acc_cross = acc_cross + jnp.stack(
            [
                matmul_tn(first_low, grad_cq),
                matmul_tn(context, grad_ck),
                matmul_tn(context, grad_cv),
            ],
            axis=1,
        )
        grad_context = matmul_nt(grad_ck, w_cross[1]) + matmul_nt(grad_cv, w_cross[2])
        holder = jnp.zeros((lax.axis_size("enc"),) + grad_context.shape, jnp.float32)
        holder = lax.dynamic_update_index_in_dim(holder, grad_context, owner, 0)
        returned = lax.psum_scatter(
            holder.astype(jnp.bfloat16), "enc", scatter_dimension=1, tiled=True
        )
        grad_contexts.append(returned)
        grad_first = grad_second_sum + matmul_nt(grad_cq, w_cross[0])
        grad_first_sum = norm_back(first_sum, gains[0], grad_first)
        grad_self_branch = grad_first_sum.astype(jnp.bfloat16)
        acc_self_out = acc_self_out + matmul_tn(self_mix, grad_self_branch)
        grad_self_mix = matmul_nt(grad_self_branch, w_self_out).astype(jnp.bfloat16)
        grad_sq, grad_sk, grad_sv = attend_back(
            grad_self_mix, self_query, self_key, self_value, self_probs
        )
        acc_self = acc_self + jnp.stack(
            [
                matmul_tn(token_rows, grad_sq),
                matmul_tn(token_rows, grad_sk),
                matmul_tn(token_rows, grad_sv),
            ],
            axis=1,
        )
        grad_input = (
            grad_first_sum
            + matmul_nt(grad_sq, w_self[0])
            + matmul_nt(grad_sk, w_self[1])
            + matmul_nt(grad_sv, w_self[2])
        )
        grad_rows.append(grad_input.astype(jnp.bfloat16))
    summed = (
        lax.psum_scatter(acc_self, ("seq", "enc"), scatter_dimension=0, tiled=True),
        lax.psum_scatter(acc_self_out, ("seq", "enc"), scatter_dimension=0, tiled=True),
        lax.psum_scatter(acc_cross, ("seq", "enc"), scatter_dimension=0, tiled=True),
        lax.psum_scatter(acc_cross_out, ("seq", "enc"), scatter_dimension=0, tiled=True),
        lax.psum_scatter(acc_adapt_in, ("seq", "enc"), scatter_dimension=0, tiled=True),
        lax.psum_scatter(acc_adapt_out, ("seq", "enc"), scatter_dimension=0, tiled=True),
    )
    layer_out = jnp.concatenate(outputs, axis=0)
    grad_tokens = jnp.concatenate(grad_rows, axis=0)
    grad_encoder = jnp.stack(grad_contexts, axis=1)[None]
    grad_self_proj = jnp.transpose(summed[0], (1, 0, 2))
    grad_cross_proj = jnp.transpose(summed[2], (1, 0, 2))
    return (
        layer_out,
        grad_tokens,
        grad_encoder,
        grad_self_proj,
        summed[1],
        grad_cross_proj,
        summed[3],
        summed[4],
        summed[5],
    )


MESH = pl.DeviceIdType.MESH
class Place:
    def __init__(self):
        seq, enc = lax.axis_index("seq"), lax.axis_index("enc")
        self.z, self.y, self.x, self.c = seq // 2, seq % 2, enc // 2, enc % 2
        self.up, self.down = jnp.minimum(self.z + 1, 3), jnp.maximum(self.z - 1, 0)
        self.step = jnp.where(self.z < 2, 1, -1)
    def dev(self, z=None, y=None, x=None, c=None):
        z = self.z if z is None else z
        y = self.y if y is None else y
        x = self.x if x is None else x
        c = self.c if c is None else c
        return (z * 2 + y, x * 2 + c)

def entry_barrier(p):
    bar = pltpu.get_barrier_semaphore()
    def sig(d):
        pl.semaphore_signal(bar, inc=1, device_id=d, device_id_type=MESH)
    sig(p.dev(c=1 - p.c)); sig(p.dev(x=1 - p.x)); sig(p.dev(y=1 - p.y)); sig(p.dev(x=1 - p.x, c=1 - p.c))
    @pl.when(p.z < 3)
    def _(): sig(p.dev(z=p.up))
    @pl.when(p.z > 0)
    def _(): sig(p.dev(z=p.down))
    peers = 4 + (p.z < 3).astype(jnp.int32) + (p.z > 0).astype(jnp.int32)
    return lambda: pl.semaphore_wait(bar, peers)

ALL4 = pl.ds(0, 4)
ALL2 = pl.ds(0, 2)

class Stream:
    def __init__(self, p, own, view, order, ssem, rsem):
        self.p, self.own, self.view, self.order, self.ssem, self.rsem = p, own, view, order, ssem, rsem
        self.flat = order[0] == "z"
        self.b1, self.b2 = (order[1], order[2]) if self.flat else (order[0], order[2])
        self.me = {"x": p.x, "y": p.y}
        self.sends = [[], []]

    def source(self, r, kind):
        p = self.p
        return p.z - p.step if kind == 1 and r == 3 else p.z + p.step * r

    def unit(self, z, c=None, **where):
        w = dict(self.me) if self.flat else {**self.me, self.b1: ALL2}
        w.update(where)
        return self.view(z, w["y"], w["x"], self.p.c if c is None else c)

    def partner(self, b):
        return self.p.dev(**{b: 1 - self.me[b]})

    def copy(self, kind, slot, what):
        k = len(self.sends[kind])
        def make():
            src, dst, target = what()
            return pltpu.make_async_remote_copy(src, dst, self.ssem.at[k], self.rsem.at[slot()], device_id=target, device_id_type=MESH)
        make().start()
        self.sends[kind].append(make)

    def arrive(self, where, slot):
        pltpu.make_async_remote_copy(where, where, self.ssem.at[0], self.rsem.at[slot], device_id=self.p.dev(), device_id_type=MESH).wait_recv()

    def finish(self, kind):
        for make in self.sends[kind]: make().wait_send()

    def along(self, kind, r, way, src=None):
        p = self.p
        def what():
            u = self.unit(self.source(r, kind))
            return u if src is None else src, u, p.dev(z=p.z + way * p.step)
        self.copy(kind, lambda: self.source(r, kind), what)

    def across(self, kind, r, src=None):
        b = self.b1 if self.flat else self.b2
        def what():
            u = self.unit(self.source(r, kind))
            return u if src is None else src, u, self.partner(b)
        self.copy(kind, lambda: 4 + self.source(r, kind), what)

    def P0(self, r, kind):
        if self.flat:
            self.along(kind, 0, 1, self.own)
            if kind == 1: self.along(kind, 0, -1, self.own)
            self.across(kind, 0, self.own)
        else:
            self.copy(kind, lambda: 8, lambda: (self.own, self.unit(self.p.z, **self.me), self.partner(self.b1)))
    def E0(self, r, kind):
        self.arrive(self.unit(self.p.z, **{self.b1: 1 - self.me[self.b1]}), 8)
        self.along(kind, 0, 1)
        if kind == 1: self.along(kind, 0, -1)
        self.across(kind, 0)
    def H(self, r, kind):
        z = self.source(r, kind)
        self.arrive(self.unit(z), z)
        if kind == 1: self.along(kind, r, -1 if r < 3 else 1)
        self.across(kind, r)
    def E(self, r, kind):
        z = self.source(r, kind)
        self.arrive(self.unit(z, **{self.b1: 1 - self.me[self.b1]}), 4 + z)
        def what():
            u = self.unit(self.source(r, kind), **{self.b1: ALL2})
            return u, u, self.partner(self.b2)
        self.copy(kind, lambda: 8 + self.source(r, kind), what)
    def plane(self, far, c=None):
        return self.unit(ALL4, c, **{self.b1: ALL2, self.b2: 1 - self.me[self.b2] if far else self.me[self.b2]})
    def F0(self, r, kind):
        self.copy(kind, lambda: 12, lambda: (self.plane(False), self.plane(False), self.p.dev(c=1 - self.p.c)))
    def F5(self, r, kind):
        for zz in range(4):
            self.arrive(self.unit(zz, **{self.b1: ALL2, self.b2: 1 - self.me[self.b2]}), (8 if self.flat else 4) + zz)
        self.copy(kind, lambda: 13, lambda: (self.plane(True), self.plane(True), self.p.dev(c=1 - self.p.c)))
    def L(self, r, kind):
        self.arrive(self.plane(False, 1 - self.p.c), 12)
        self.arrive(self.plane(True, 1 - self.p.c), 13)

def run_plan(plan, compute, movers, guards):
    i = 0
    while i < len(plan):
        it = plan[i]
        if isinstance(it, str):
            compute[it]()
            i += 1
        elif it[3] is None:
            getattr(movers[it[0]], it[1])(it[2])
            i += 1
        else:
            j = i
            while j < len(plan) and not isinstance(plan[j], str) and plan[j][3] == it[3]: j += 1
            @pl.when(guards[it[3]])
            def _():
                for m, name, k, kind in plan[i:j]: getattr(movers[m], name)(k, kind)
            i = j


PLAN_F = [
    (7, "P0", 0, 1), (6, "P0", 0, 0), (3, "P0", 0, 0), (10, "P0", 0, 1), (0, "P0", 0, 1), (1, "P0", 0, 1), (2, "P0", 0, 1), (3, "P0", 0, 1),
    (4, "P0", 0, 1), (0, "P0", 0, 0), (1, "P0", 0, 0), (5, "P0", 0, 1), (2, "P0", 0, 0), (6, "P0", 0, 1), (8, "P0", 0, 1), (4, "P0", 0, 0),
    (5, "P0", 0, 0), (9, "P0", 0, 1), (7, "P0", 0, 0), (8, "P0", 0, 0), "flip0", "ctxsend", "staged", "own", (0, "E", 0, 0), (1, "E", 0, 0), "masks",
    (0, "H", 1, 0), (3, "E0", 0, 0), (0, "H", 1, 1), (0, "H", 3, 1), (0, "E", 0, 1), (1, "H", 1, 0), (1, "H", 1, 1), (9, "P0", 0, 0), (4, "H", 1, 1),
    (1, "H", 3, 1), (1, "E", 0, 1), (7, "E0", 0, 1), (4, "E", 0, 0), (2, "E0", 0, 1), (4, "H", 1, 0), (10, "P0", 0, 0), (6, "E0", 0, 0),
    (5, "E", 0, 0), (3, "E0", 0, 1), (4, "H", 3, 1), (2, "E0", 0, 0), (5, "H", 1, 1), (4, "E", 0, 1), (5, "H", 1, 0), (5, "H", 3, 1), (5, "E", 0, 1),
    (8, "H", 1, 1), (8, "H", 3, 1), (8, "H", 1, 0), (9, "H", 1, 1), (6, "E0", 0, 1), (8, "E", 0, 0), (9, "H", 3, 1), (0, "H", 2, 1), (8, "E", 0, 1),
    (0, "H", 2, 0), (7, "E0", 0, 0), (9, "E", 0, 1), (1, "H", 2, 1), (1, "H", 2, 0), (4, "H", 2, 0), (10, "E0", 0, 1), (9, "H", 1, 0), (9, "E", 0, 0),
    (2, "H", 3, 1), (1, "E", 1, 1), (3, "H", 1, 1), (1, "E", 3, 1), (2, "H", 1, 1), (2, "H", 1, 0), (3, "H", 3, 1), (10, "E0", 0, 0), (3, "H", 1, 0),
    (1, "E", 1, 0), (5, "E", 1, 1), (5, "E", 1, 0), "ctxin", (5, "H", 2, 1), (5, "H", 2, 0), (7, "H", 3, 1), (6, "H", 3, 1), (8, "H", 2, 1),
    (8, "H", 2, 0), (0, "E", 3, 1), (9, "H", 2, 0), (5, "E", 3, 1), (4, "E", 1, 0), (9, "E", 1, 1), (4, "H", 2, 1), (4, "E", 1, 1), (0, "E", 1, 1),
    (7, "H", 1, 1), (6, "H", 1, 0), (1, "E", 2, 0), (9, "E", 1, 0), (0, "E", 1, 0), (9, "E", 3, 1), (10, "H", 3, 1), (0, "H", 3, 0), (4, "E", 3, 1),
    (8, "E", 1, 0), (9, "H", 2, 1), (7, "H", 1, 0), (1, "E", 2, 1), (10, "H", 1, 1), "flip1", (8, "E", 1, 1), (1, "H", 3, 0), (8, "E", 3, 1),
    (5, "H", 3, 0), (6, "H", 1, 1), (0, "E", 2, 0), (1, "F0", 0, 1), (4, "E", 2, 0), (5, "E", 2, 0), (11, "P0", 0, 1), (2, "H", 2, 1),
    (13, "P0", 0, 1), (0, "E", 2, 1), (2, "H", 2, 0), (10, "H", 1, 0), (3, "H", 2, 0), (14, "P0", 0, 1), (9, "E", 2, 0), (12, "P0", 0, 1),
    (3, "H", 2, 1), (0, "F0", 0, 1), (5, "E", 2, 1), (2, "F0", 0, 1), (4, "H", 3, 0), (16, "P0", 0, 1), (17, "P0", 0, 1), (6, "H", 2, 1),
    (7, "H", 2, 1), (8, "E", 2, 0), (1, "E", 3, 0), (3, "F0", 0, 1), (5, "F0", 0, 1), (1, "F0", 0, 0), (18, "P0", 0, 1), (6, "H", 2, 0),
    (20, "P0", 0, 1), (21, "P0", 0, 1), (6, "F0", 0, 1), (15, "P0", 0, 1), (10, "H", 2, 1), (7, "H", 2, 0), (4, "E", 2, 1), (0, "E", 3, 0),
    (4, "F0", 0, 1), (7, "F0", 0, 1), (13, "H", 1, 1), (8, "E", 2, 1), (8, "H", 3, 0), (0, "F0", 0, 0), (11, "P0", 0, 0), (16, "H", 1, 1),
    (17, "H", 1, 1), (20, "H", 1, 1), (12, "H", 1, 1), (9, "H", 3, 0), (10, "F0", 0, 1), (21, "H", 1, 1), (5, "E", 3, 0), (8, "F0", 0, 1),
    (5, "F0", 0, 0), (19, "P0", 0, 1), (12, "P0", 0, 0), (12, "H", 1, 0), (2, "H", 3, 0), (4, "E", 3, 0), (10, "H", 2, 0), (9, "E", 2, 1),
    (13, "P0", 0, 0), (8, "E", 3, 0), (4, "F0", 0, 0), (15, "P0", 0, 0), (13, "H", 1, 0), (3, "H", 3, 0), (3, "F0", 0, 0), (2, "F0", 0, 0),
    (13, "H", 3, 1), (9, "F0", 0, 1), (0, "F5", 0, 0), (14, "P0", 0, 0), (19, "P0", 0, 0), (8, "F0", 0, 0), (0, "L", 0, 0), (12, "H", 3, 1),
    (1, "F5", 0, 1), (12, "E", 0, 0), (9, "E", 3, 0), (13, "H", 2, 1), (11, "E0", 0, 0), (12, "E", 1, 0), (9, "F0", 0, 0), (1, "F5", 0, 0),
    (1, "L", 0, 0), (1, "L", 0, 1), (6, "H", 3, 0), (6, "F0", 0, 0), (5, "F5", 0, 0), (16, "P0", 0, 0), (12, "H", 2, 1), (16, "H", 1, 0),
    (17, "P0", 0, 0), (17, "H", 1, 0), (2, "F5", 0, 1), (3, "F5", 0, 1), (12, "E", 0, 1), (3, "F5", 0, 0), (5, "L", 0, 0), (0, "F5", 0, 1),
    (14, "E0", 0, 1), (2, "L", 0, 1), (16, "H", 3, 1), (7, "H", 3, 0), (3, "L", 0, 0), (13, "E", 0, 0), (11, "E0", 0, 1), (2, "F5", 0, 0),
    (7, "F0", 0, 0), (11, "H", 3, 1), (18, "P0", 0, 0), (17, "H", 3, 1), (5, "F5", 0, 1), (13, "E", 0, 1), (3, "L", 0, 1), (16, "E", 0, 1),
    (0, "L", 0, 1), "w0", (4, "F5", 0, 0), (5, "L", 0, 1), (7, "F5", 0, 1), "w2", (14, "E0", 0, 0), (2, "L", 0, 0), "w1", (9, "F5", 0, 0),
    (12, "H", 2, 0), (6, "F5", 0, 1), "proj0", "proj2", (15, "E0", 0, 0), (14, "H", 1, 1), (16, "H", 2, 1), (17, "E", 0, 1), "proj1", (20, "P0", 0, 0),
    (13, "E", 1, 0), (10, "H", 3, 0), (20, "H", 1, 0), (8, "F5", 0, 0), (10, "F0", 0, 0), (13, "H", 2, 0), (7, "L", 0, 1), (4, "L", 0, 0), "at00",
    (18, "E0", 0, 1), (20, "E", 0, 1), (6, "L", 0, 1), (16, "E", 0, 0), (16, "E", 1, 0), (19, "E0", 0, 1), (21, "P0", 0, 0), (21, "H", 1, 0),
    (16, "H", 2, 0), (17, "H", 2, 0), (11, "H", 1, 1), (12, "H", 3, 0), (8, "L", 0, 0), (14, "H", 3, 1), "at01", (19, "E0", 0, 0), (9, "L", 0, 0),
    (14, "H", 1, 0), (20, "E", 1, 1), (21, "E", 0, 1), (20, "H", 3, 1), (21, "H", 2, 0), "at02", (21, "H", 3, 1), (4, "F5", 0, 1), (20, "H", 2, 0),
    (15, "E0", 0, 1), (11, "H", 2, 1), (6, "F5", 0, 0), (9, "F5", 0, 1), (22, "P0", 0, 1), (23, "P0", 0, 1), (13, "H", 3, 0), (12, "E", 1, 1),
    (7, "F5", 0, 0), (17, "H", 2, 1), (16, "E", 1, 1), (13, "E", 1, 1), (17, "E", 0, 0), "at03", (10, "F5", 0, 1), (10, "L", 0, 1), (15, "H", 3, 1),
    (6, "L", 0, 0), (18, "E0", 0, 0), (8, "F5", 0, 1), (4, "L", 0, 1), (12, "E", 2, 1), (9, "L", 0, 1), "flip3", (12, "E", 3, 1), (17, "E", 1, 0),
    (17, "E", 1, 1), (18, "H", 1, 1), "w3", "w4", (7, "L", 0, 0), (11, "F0", 0, 1), (21, "E", 1, 1), "w5", (19, "H", 3, 1), (8, "L", 0, 1), "w6",
    (20, "E", 0, 0), (16, "E", 3, 1), (11, "H", 1, 0), (20, "E", 1, 0), (12, "E", 2, 0), "branch3", (13, "E", 3, 1), "norm0", (13, "E", 2, 1),
    (18, "H", 3, 1), (14, "H", 2, 0), (14, "H", 2, 1), (20, "H", 2, 1), (21, "H", 2, 1), "flip2", (18, "H", 1, 0), (16, "H", 3, 0), (16, "E", 2, 1),
    "proj4", (16, "F0", 0, 1), "proj5", (16, "E", 2, 0), (21, "E", 0, 0), "proj6", (10, "F5", 0, 0), (14, "F0", 0, 1), "at10", (15, "H", 1, 1),
    (12, "F0", 0, 1), (13, "E", 2, 0), (12, "E", 3, 0), (17, "E", 3, 1), "at11", (15, "H", 2, 1), (12, "F0", 0, 0), (10, "L", 0, 0), (13, "F0", 0, 1),
    "at12", (11, "H", 2, 0), (17, "E", 2, 0), (19, "H", 1, 1), (20, "E", 3, 1), (21, "E", 2, 0), "at13", (21, "E", 1, 0), (19, "H", 2, 1),
    (13, "E", 3, 0), (13, "F0", 0, 0), (20, "E", 2, 0), "flip4", "w7", (11, "H", 3, 0), (15, "F0", 0, 1), (11, "F0", 0, 0), (23, "P0", 0, 0),
    (22, "P0", 0, 0), (11, "F5", 0, 1), "branch7", (16, "E", 3, 0), "norm1", (15, "H", 1, 0), (16, "F0", 0, 0), (17, "H", 3, 0), (11, "L", 0, 1),
    "flip5", (19, "F0", 0, 1), (18, "H", 2, 1), (22, "E0", 0, 1), (18, "H", 2, 0), (18, "F0", 0, 1), (19, "H", 1, 0), (22, "H", 1, 1), (21, "E", 3, 1),
    (17, "E", 2, 1), (21, "H", 3, 0), (13, "F5", 0, 0), (20, "H", 3, 0), (23, "E0", 0, 1), (13, "L", 0, 0), (15, "H", 2, 0), (17, "F0", 0, 1),
    (14, "H", 3, 0), (14, "F0", 0, 0), (11, "F5", 0, 0), (12, "F5", 0, 1), (23, "H", 1, 1), (12, "F5", 0, 0), (12, "L", 0, 1), (11, "L", 0, 0),
    (15, "H", 3, 0), (22, "E0", 0, 0), (15, "F0", 0, 0), (12, "L", 0, 0), "w8", (23, "E0", 0, 0), (13, "F5", 0, 1), (16, "F5", 0, 0), "adapter",
    (17, "E", 3, 0), (20, "E", 2, 1), (22, "H", 3, 1), (19, "H", 2, 0), (17, "F0", 0, 0), (14, "F5", 0, 1), (13, "L", 0, 1), "w9", (16, "L", 0, 0),
    (23, "H", 3, 1), "hid0", (19, "H", 3, 0), (19, "F0", 0, 0), (20, "F0", 0, 1), (14, "L", 0, 1), (21, "E", 2, 1), "adapter_out", (22, "H", 2, 1),
    (20, "E", 3, 0), (20, "F0", 0, 0), (16, "F5", 0, 1), (16, "L", 0, 1), (14, "F5", 0, 0), (23, "H", 2, 1), (21, "E", 3, 0), (18, "H", 3, 0),
    (18, "F0", 0, 0), (15, "F5", 0, 1), (21, "F0", 0, 0), (21, "F0", 0, 1), (14, "L", 0, 0), "w10", (22, "F0", 0, 1), (15, "F5", 0, 0),
    (15, "L", 0, 1), (22, "H", 1, 0), (18, "F5", 0, 1), (23, "F0", 0, 1), "hid1", (23, "H", 1, 0), (17, "F5", 0, 0), (15, "L", 0, 0), "w11",
    (22, "H", 2, 0), (19, "F5", 0, 1), (23, "H", 2, 0), (18, "L", 0, 1), (17, "L", 0, 0), (18, "F5", 0, 0), "hid2", (20, "F5", 0, 0), (19, "L", 0, 1),
    (22, "H", 3, 0), (22, "F0", 0, 0), (20, "F5", 0, 1), (20, "L", 0, 0), (23, "H", 3, 0), (18, "L", 0, 0), (23, "F0", 0, 0), "w13", (17, "F5", 0, 1),
    (19, "F5", 0, 0), (20, "L", 0, 1), (17, "L", 0, 1), "w12", (21, "F5", 0, 0), (19, "L", 0, 0), "w14", "hid3", (21, "L", 0, 0), (23, "F5", 0, 0),
    (21, "F5", 0, 1), (22, "F5", 0, 0), (22, "F5", 0, 1), "out0", (23, "F5", 0, 1), "out1", (22, "L", 0, 0), (23, "L", 0, 0), (21, "L", 0, 1),
    (22, "L", 0, 1), "w15", (23, "L", 0, 1), "w16", "out2", "out3", "norm2",
]

F32, BF = jnp.float32, jnp.bfloat16
NSLOT, NSEND = 14, 19
N_STREAM = 24
EPS = 1e-05

def dot(a, b):
    return jnp.dot(a, b, preferred_element_type=F32)

def dot_nt(a, b):
    return lax.dot_general(a, b, (((1,), (1,)), ((), ())), preferred_element_type=F32)

def dot_tn(a, b):
    return lax.dot_general(a, b, (((0,), (0,)), ((), ())), preferred_element_type=F32)

def cols(n, width):
    return pl.ds(pl.multiple_of(n * width, width), width)

def norm_rows(h):
    center = h - jnp.mean(h, axis=-1, keepdims=True)
    spread = jnp.mean(center * center, axis=-1, keepdims=True)
    return center * lax.rsqrt(spread + EPS)

def half_masks():
    lane = lax.broadcasted_iota(jnp.int32, (1, 128), 1)
    lo = jnp.where(lane < 64, 1.0, 0.0)
    return lo.astype(BF), (1.0 - lo).astype(BF)

def pair_up(m, lo, hi):
    return jnp.concatenate([m * lo, m * hi], axis=0)

def side(m):
    return jnp.concatenate([m[:128], m[128:]], axis=1)

def forward_kernel(x, gains, dlen, elen, sp, so, cp, co, fi, fo, ai, ao, en,
                   buf, gfo, o_qkv, o_p, o_h, o_t, o_at, o_gp, o_sr, o_out,
                   qkv, P, H, T, AT, GP, SR, OUT, ctx, wbuf, wo, own, ownf, y, yl, mix, af, ar, bias,
                   ssem, rsem, lsem, csem, crsem, wsem, osem):
    p = Place()
    neighbours_in = entry_barrier(p)
    loc = []
    def put(src, dst):
        c_ = pltpu.make_async_copy(src, dst, lsem.at[len(loc)]); c_.start(); loc.append(c_)
    for j, t in enumerate((0, 1, 2)): put(sp.at[j], own.at[t])
    put(so, own.at[3])
    for j, t in ((1, 4), (2, 5), (0, 6)): put(cp.at[j], own.at[t])
    put(co, own.at[7])
    put(ai, own.at[8, :, pl.ds(0, 512)])
    put(ao.at[:, pl.ds(0, 512)], own.at[8, pl.ds(0, 16), pl.ds(512, 512)])
    put(ao.at[:, pl.ds(512, 512)], own.at[8, pl.ds(16, 16), pl.ds(512, 512)])
    for j in range(4): put(fi.at[:, pl.ds(1024 * j, 1024)], own.at[9 + j])
    put(fo, ownf)
    me = p.x * 2 + p.c
    put(en.at[0, me], ctx.at[:, me])
    n_in = len(loc)
    c1 = pltpu.make_async_copy(own, buf.at[:, p.z, p.y, p.x, p.c], lsem.at[n_in])
    c2 = pltpu.make_async_copy(ownf, gfo.at[p.z, p.y, p.x, p.c], lsem.at[n_in + 1])
    def staged():
        for c_ in loc: c_.wait()
        c1.start(); c2.start()
    neighbours_in()
    streams = []
    for t in range(17):
        R = 32 if t < 13 else 128
        i = t % 3
        rows = [(0, R // 2, "zxy"), (R // 2, R // 2, "zyx")] if i == 0 else [(0, R, "xzy" if i == 1 else "yzx")]
        if t == 16: rows = [(0, 96, "xzy"), (96, 32, "yzx")]
        for r0, nr, order in rows:
            n = len(streams)
            if t < 13:
                arg = {0: sp.at[0], 1: sp.at[1], 2: sp.at[2], 3: so, 4: cp.at[1], 5: cp.at[2], 6: cp.at[0], 7: co, 8: own.at[8]}.get(t)
                mine = fi.at[pl.ds(r0, nr), pl.ds(1024 * (t - 9), 1024)] if t > 8 else arg.at[pl.ds(r0, nr)]
                view = lambda z, y_, x_, c, t=t, r0=r0, nr=nr: buf.at[t, z, y_, x_, c, pl.ds(r0, nr)]
            else:
                mine = fo.at[pl.ds(r0, nr), pl.ds(256 * (t - 13), 256)]
                view = lambda z, y_, x_, c, j=t - 13, r0=r0, nr=nr: gfo.at[z, y_, x_, c, pl.ds(r0, nr), pl.ds(256 * j, 256)]
            streams.append(Stream(p, mine, view, order, ssem.at[n], rsem.at[n]))
    ends = (p.z == 0) | (p.z == 3)
    guards = [ends, jnp.logical_not(ends)]

    def fetch(t):
        if t < 13: return pltpu.make_async_copy(buf.at[t], wbuf.at[t % 4], wsem.at[t])
        j = t - 13
        return pltpu.make_async_copy(gfo.at[:, :, :, :, :, pl.ds(256 * j, 256)], wo.at[j % 2], wsem.at[t])
    def start(t): return lambda: fetch(t).start()
    outs = []
    def keep(src, dst):
        c_ = pltpu.make_async_copy(src, dst, osem.at[len(outs)]); c_.start(); outs.append(c_)
    lo, hi = half_masks()

    def mm(lhs, t, fn):
        fn(dot(lhs[...], wbuf[t % 4].reshape(1024, 1024)))

    def proj(lhs, t, slot):
        def run():
            fetch(t).wait()
            def st(v): qkv[slot] = v.astype(BF)
            mm(lhs, t, st)
            keep(qkv.at[slot], o_qkv.at[slot])
        return run

    def flip(src, slot):
        def run():
            @pl.loop(0, 4)
            def _(n):
                T[slot, cols(n, 256), :] = src[:, cols(n, 256)].T
            keep(T.at[slot], o_t.at[slot])
        return run

    def attend(a, part):
        def run():
            u = part // 2
            @pl.loop(0, 4, unroll=4)
            def _(n):
                pr = (part % 2) * 4 + n
                r, cc = pl.ds(u * 128, 128), cols(pr, 128)
                q, k, v = (qkv[3 * a + j, r, cc] for j in range(3))
                b = bias[a, u]
                s = dot_nt(pair_up(q, lo, hi), k) * 0.125 + jnp.concatenate([b, b], axis=0)
                e = jnp.exp(s - jnp.max(s, axis=-1, keepdims=True))
                pr_ = e / jnp.sum(e, axis=-1, keepdims=True)
                P[a, u * 8 + pr] = pr_
                mix[r, cc] = dot(side(pr_.astype(BF)), pair_up(v, lo, hi)).astype(BF)
            if part == 3: keep(P.at[a], o_p.at[a])
        return run

    def branch(t, base, slot):
        def run():
            fetch(t).wait()
            def st(v): H[slot] = base[...].astype(F32) + v
            mm(mix, t, st)
        return run

    def norm(slot):
        def run():
            keep(H.at[slot], o_h.at[slot])
            @pl.loop(0, 4)
            def _(n):
                r = pl.ds(pl.multiple_of(n * 64, 64), 64)
                v = norm_rows(H[slot, r, :]) * gains[slot, :][None]
                if slot < 2:
                    y[r, :] = v
                    yl[r, :] = v.astype(BF)
                else:
                    OUT[r, :] = v.astype(BF)
            if slot == 2: keep(OUT, o_out)
        return run

    cs = []
    def context_out():
        for k, (dx, dc) in enumerate(((0, 1), (1, 0), (1, 1))):
            tx = (p.x + dx) % 2; tc = (p.c + dc) % 2
            c_ = pltpu.make_async_remote_copy(en.at[0, tx * 2 + tc], ctx.at[:, me], csem.at[k], crsem.at[me], device_id=p.dev(x=tx, c=tc), device_id_type=MESH)
            c_.start(); cs.append(c_)
    def context_in():
        for k, (dx, dc) in enumerate(((0, 1), (1, 0), (1, 1))):
            tx = (p.x + dx) % 2; tc = (p.c + dc) % 2
            w = tx * 2 + tc
            pltpu.make_async_remote_copy(en.at[0, w], ctx.at[:, w], csem.at[k], crsem.at[w], device_id=p.dev(), device_id_type=MESH).wait_recv()

    class Ctx:
        def __getitem__(self, idx):
            if idx is Ellipsis: return ctx[...].reshape(256, 1024)
            return ctx[:, :, :, idx[1]].reshape(256, -1)
    cref = Ctx()
    def adapter():
        fetch(8).wait()
        w = wbuf[0, :, :, :, :, :, pl.ds(0, 512)].reshape(1024, 512)
        r = dot(yl[...], w)
        s = 1.0 / (1.0 + jnp.exp(-r))
        a = (r * s).astype(BF)
        ar[...] = a
        SR[...] = s * (1.0 + r * (1.0 - s))
        AT[...] = a.T
        keep(SR, o_sr); keep(AT, o_at)
    def adapter_out():
        top = wbuf[0, :, :, :, :, pl.ds(0, 16), pl.ds(512, 512)].reshape(512, 512)
        bot = wbuf[0, :, :, :, :, pl.ds(16, 16), pl.ds(512, 512)].reshape(512, 512)
        H[2, :, 0:512] = y[:, 0:512] + 4.0 * dot(ar[...], top)
        H[2, :, 512:1024] = y[:, 512:1024] + 4.0 * dot(ar[...], bot)
    def hidden(j):
        def run():
            t = 9 + j
            fetch(t).wait()
            @pl.loop(0, 4)
            def _(n):
                ds = cols(n, 256)
                u = dot(yl[...], wbuf[t % 4, :, :, :, :, :, ds].reshape(1024, 256))
                half = 0.5 + 0.5 * lax.erf(u * 0.7071067811865476)
                af[j, :, ds] = (u * half).astype(BF)
                GP[j, :, ds] = half + u * (0.3989422804014327 * jnp.exp(-0.5 * u * u))
            keep(GP.at[j], o_gp.at[j])
        return run
    def out_cols(j):
        def run():
            fetch(13 + j).wait()
            acc = H[2, :, pl.ds(256 * j, 256)]
            for f in range(4):
                w = wo[j % 2, f].reshape(1024, 256)
                acc = acc + dot(af[f], w)
            H[2, :, pl.ds(256 * j, 256)] = acc
        return run

    def masks():
        row = lax.broadcasted_iota(jnp.int32, (128, 128), 0)
        col = lax.broadcasted_iota(jnp.int32, (128, 128), 1)
        for u in range(2):
            wide = lambda ref, j: jnp.broadcast_to(ref[u:u + 1, j:j + 1], (128, 128))
            paired = wide(dlen, 1) > 0
            far = jnp.where(paired, 64, 128)
            second = col >= far
            place = jnp.where(second, col - 64, col)
            same = (row >= far) == second
            dec = jnp.where(second, wide(dlen, 1), wide(dlen, 0))
            enc = jnp.where(second, wide(elen, 1), wide(elen, 0))
            bias[0, u] = jnp.where(same & (col <= row) & (place < dec), 0.0, -1e30)
            bias[1, u] = jnp.where(same & (place < enc), 0.0, -1e30)

    compute = {}
    for t in range(17): compute[f"w{t}"] = start(t)
    compute["masks"] = masks
    compute["staged"] = staged
    compute["own"] = lambda: (c1.wait(), c2.wait())
    for k, src in ((0, x), (1, cref), (2, yl), (3, mix), (4, mix), (5, yl)): compute[f"flip{k}"] = flip(src, k)
    for t, lhs, slot in ((0, x, 0), (1, x, 1), (2, x, 2), (4, cref, 4), (5, cref, 5), (6, yl, 3)): compute[f"proj{t}"] = proj(lhs, t, slot)
    for a in range(2):
        for part in range(4): compute[f"at{a}{part}"] = attend(a, part)
    compute.update(branch3=branch(3, x, 0), branch7=branch(7, y, 1), norm0=norm(0), norm1=norm(1), norm2=norm(2),
                   ctxsend=context_out, ctxin=context_in, adapter=adapter, adapter_out=adapter_out)
    for j in range(4): compute.update({f"hid{j}": hidden(j), f"out{j}": out_cols(j)})
    run_plan(PLAN_F, compute, streams, guards)
    for k in range(2):
        @pl.when(guards[k])
        def _():
            for s in streams: s.finish(k)
    for c_ in cs: c_.wait_send()
    for c_ in outs: c_.wait()

def forward(tokens, gains, dec_lengths, enc_lengths, shards, encoder):
    any_ = pl.BlockSpec(memory_space=pl.ANY)
    vm = pl.BlockSpec(memory_space=pltpu.VMEM)
    V, S, D = pltpu.VMEM, jax.ShapeDtypeStruct, pltpu.SemaphoreType.DMA
    tile = (4, 2, 2, 2, 32, 1024)
    return pl.pallas_call(forward_kernel,
        out_shape=(S((13,) + tile, BF), S((4, 2, 2, 2, 128, 1024), BF), S((6, 256, 1024), BF), S((2, 16, 256, 128), F32), S((3, 256, 1024), F32),
                   S((6, 1024, 256), BF), S((512, 256), BF), S((4, 256, 1024), F32), S((256, 512), F32), S((256, 1024), BF)),
        in_specs=[vm] * 4 + [any_] * 9, out_specs=(any_,) * 10,
        scratch_shapes=[V((6, 256, 1024), BF), V((2, 16, 256, 128), F32), V((3, 256, 1024), F32), V((6, 1024, 256), BF), V((512, 256), BF),
                        V((4, 256, 1024), F32), V((256, 512), F32), V((256, 1024), BF), V((2, 4, 32, 1024), BF), V((4,) + tile, BF),
                        V((2, 4, 2, 2, 2, 128, 256), BF), V((13, 32, 1024), BF), V((128, 1024), BF), V((256, 1024), F32), V((256, 1024), BF),
                        V((256, 1024), BF), V((4, 256, 1024), BF), V((256, 512), BF), V((2, 2, 128, 128), F32),
                        D((N_STREAM, NSEND)), D((N_STREAM, NSLOT)), D((20,)), D((3,)), D((4,)), D((17,)), D((26,))],
        compiler_params=pltpu.CompilerParams(collective_id=0, has_side_effects=True, vmem_limit_bytes=60 << 20),
        name="forward")(tokens, gains, dec_lengths, enc_lengths, *shards, encoder)

ORDERS = ["xzy", "yzx", "A", "xzy", "yzx", "A", "xzy", "yzx", "A"]
PLAN_B = [
    "nb0", "hb0", "hb1", "hb2", "hb3", "adb", "adg.0", "adg.1", "adg.2", "adg.3", "hi0", (0, "R1", 0, None), "hi1", "hi2", (0, "R1", 1, None), "hi3",
    "nb1", "t1.0", "t1.1", "t1.2", "t1.3", "mb9", (0, "R2", 0, None), (1, "R1", 0, None), (0, "D", 0, 3), (0, "U", 3, 0), (0, "R1", 2, None), "at10",
    (1, "R1", 1, None), (0, "R2", 1, None), (0, "U", 2, 0), (0, "D", 0, 2), "at11", "at12", (0, "R1", 3, None), (0, "D", 1, 3), (1, "R2", 0, None),
    (1, "R1", 3, None), (0, "D", 1, 2), (1, "U", 3, 0), (0, "U", 3, 1), "at13", "t2.0", "t2.1", (0, "R2", 2, None), (0, "D", 2, 3), "t2.2", "t2.3",
    (1, "D", 0, 3), (1, "R1", 2, None), "t3.0", "t3.1", (1, "R2", 1, None), (1, "U", 2, 0), (1, "U", 3, 1), (2, "R1", 0, None), "t3.2", "t3.3",
    (2, "R1", 1, None), (0, "R2", 3, None), (0, "U", 3, 2), (0, "D", 0, 1), (1, "D", 0, 2), (2, "R1", 2, None), (3, "R1", 0, None), (3, "R1", 1, None),
    (0, "U", 2, 1), "t4.0", "t4.1", (1, "D", 1, 2), (4, "R1", 0, None), (1, "R2", 3, None), (1, "U", 3, 2), (1, "R2", 2, None), (1, "U", 1, 0),
    (2, "R1", 3, None), (1, "D", 1, 3), (0, "Z3", 0, 2), "t4.2", "t4.3", "rb10", "cb", "rb12", "nb2", (0, "Z3", 0, 1), (2, "R2", 1, None),
    (3, "R1", 2, None), (1, "D", 2, 3), (1, "D", 0, 1), (0, "U", 1, 0), "t5.0", (1, "Z3", 0, 1), (4, "R1", 2, None), (1, "U", 2, 1),
    (3, "R1", 3, None), (2, "R2", 0, None), (0, "Z3", 0, 0), (3, "R2", 0, None), (3, "D", 0, 3), (3, "U", 3, 1), (3, "U", 3, 0), (3, "D", 0, 2),
    (4, "R1", 1, None), (0, "Z3", 0, 3), "t5.1", "t5.2", "t5.3", "mb13", "at00", "at01", (5, "R1", 3, None), (4, "R2", 0, None), (3, "R2", 1, None),
    (3, "D", 1, 3), (3, "U", 2, 0), (5, "R1", 0, None), (4, "D", 0, 3), (4, "U", 3, 1), "at02", "at03", (3, "U", 2, 1), (3, "R2", 2, None),
    (5, "R1", 2, None), (4, "R1", 3, None), (4, "U", 3, 0), (2, "R2", 2, None), (4, "D", 0, 2), (3, "D", 1, 2), (2, "R3", 1, None), (2, "U", 2, 1),
    "cs", "t6.0", (2, "R3", 0, None), (2, "U", 3, 0), (2, "U", 3, 1), (4, "R2", 2, None), (2, "D", 0, 3), (2, "D", 0, 2), "t6.1", (2, "U", 2, 0),
    "t6.2", "t6.3", "t7.0", (0, "FIN", 0, 0), (6, "R1", 0, None), (2, "D", 1, 3), (2, "R2", 3, None), (6, "R1", 1, None), (3, "U", 1, 0),
    (5, "R1", 1, None), (3, "D", 2, 3), "t7.1", (3, "R2", 3, None), (3, "U", 3, 2), (3, "D", 0, 1), (6, "R1", 2, None), (1, "FIN", 0, 1),
    (1, "Z3", 0, 2), "t7.2", "t7.3", "t8.0", "t8.1", "t8.2", (7, "R1", 3, None), (2, "D", 1, 2), (7, "R1", 0, None), (6, "R1", 3, None),
    (4, "D", 2, 3), (4, "U", 1, 0), (0, "FIN", 0, 1), "t8.3", (1, "Z3", 0, 3), (4, "R2", 1, None), (4, "U", 2, 0), (4, "D", 1, 3), (4, "U", 2, 1),
    (1, "Z3", 0, 0), (7, "R1", 2, None), (8, "R1", 0, None), (7, "R1", 1, None), (0, "FIN", 0, 2), (6, "R2", 0, None), (6, "U", 3, 0), (6, "D", 0, 3),
    (6, "U", 3, 1), (4, "R2", 3, None), (4, "U", 3, 2), (0, "FIN", 0, 3), (2, "R3", 2, None), (2, "D", 2, 3), (4, "D", 1, 2), (3, "Z3", 0, 2), "rb14",
    "rb15", "tok", (1, "FIN", 0, 2), (3, "Z3", 0, 3), (4, "D", 0, 1), (6, "D", 0, 2), (3, "Z3", 0, 0), (8, "R1", 3, None), (6, "R2", 2, None),
    (6, "U", 1, 0), (8, "R1", 1, None), (6, "D", 2, 3), (2, "U", 1, 0), (6, "R2", 1, None), (6, "U", 2, 1), (6, "U", 2, 0), (6, "R2", 3, None),
    (6, "U", 3, 2), (6, "D", 1, 3), (7, "R2", 2, None), (4, "Z3", 0, 3), (6, "D", 0, 1), (6, "D", 1, 2), (5, "R2", 1, None), (2, "R3", 3, None),
    (2, "D", 0, 1), (5, "R2", 0, None), (8, "R1", 2, None), (7, "R2", 0, None), (7, "D", 0, 2), (7, "U", 3, 1), (7, "D", 0, 3), (7, "U", 3, 0),
    (7, "R2", 1, None), (7, "D", 1, 3), (7, "U", 2, 1), (7, "U", 2, 0), (6, "Z3", 0, 2), (7, "D", 1, 2), (1, "FIN", 0, 3), (6, "Z3", 0, 1),
    (7, "U", 1, 0), (7, "D", 2, 3), (1, "FIN", 0, 0), (2, "U", 3, 2), (8, "R2", 3, None), (5, "R3", 1, None), (5, "D", 1, 3), (5, "U", 2, 0),
    (7, "R2", 3, None), (7, "D", 0, 1), (8, "R2", 0, None), (5, "R2", 2, None), (5, "D", 1, 2), (8, "R2", 1, None), (5, "U", 2, 1), (4, "Z3", 0, 0),
    (5, "R2", 3, None), (3, "FIN", 0, 0), (3, "Z3", 0, 1), (7, "U", 3, 2), (5, "R3", 0, None), (5, "D", 0, 3), (5, "U", 3, 1), (5, "D", 0, 2),
    (6, "Z3", 0, 0), (4, "FIN", 0, 3), (6, "Z3", 0, 3), (5, "U", 3, 0), (4, "Z3", 0, 1), (4, "Z3", 0, 2), (8, "R2", 2, None), (8, "R3", 0, None),
    (8, "D", 0, 2), (8, "U", 3, 1), (8, "D", 0, 3), (8, "U", 3, 0), (4, "FIN", 0, 1), (7, "Z3", 0, 2), (5, "R3", 3, None), (5, "U", 3, 2),
    (7, "Z3", 0, 0), (5, "D", 0, 1), (6, "FIN", 0, 1), (8, "R3", 1, None), (8, "D", 1, 3), (8, "U", 2, 1), (8, "D", 1, 2), (8, "U", 2, 0),
    (6, "FIN", 0, 3), (3, "FIN", 0, 2), (5, "R3", 2, None), (5, "D", 2, 3), (5, "FIN", 0, 2), (6, "FIN", 0, 0), (7, "Z3", 0, 1), (5, "U", 1, 0),
    (6, "FIN", 0, 2), (8, "R3", 2, None), (8, "D", 2, 3), (4, "FIN", 0, 2), (4, "FIN", 0, 0), (2, "FIN", 0, 1), (8, "U", 1, 0), (2, "FIN", 0, 2),
    (7, "FIN", 0, 2), (2, "FIN", 0, 0), (7, "FIN", 0, 0), (7, "Z3", 0, 3), (2, "FIN", 0, 3), (8, "R3", 3, None), (8, "U", 3, 2), (8, "D", 0, 1),
    (3, "FIN", 0, 1), (5, "FIN", 0, 0), (8, "FIN", 0, 0), (7, "FIN", 0, 3), (8, "FIN", 0, 2), (7, "FIN", 0, 1), (5, "FIN", 0, 3), (5, "FIN", 0, 1),
    (3, "FIN", 0, 3), (8, "FIN", 0, 1), (8, "FIN", 0, 3),
]


NT = 9
NS, NR = 27, 33

class Reduce:
    def __init__(self, p, t, order, PB, L0, L1, L2, UP, DN, LX, ssem, rsem, out):
        self.p, self.t, self.order = p, t, order
        self.PB, self.L0, self.L1, self.L2, self.UP, self.DN, self.LX = PB, L0, L1, L2, UP, DN, LX
        self.ssem, self.rsem, self.out = ssem, rsem, out
        self.sends = []
        self.me = {"x": p.x, "y": p.y}
        self.flat = order == "A"
        if not self.flat: self.b1, self.b2 = order[0], order[2]
    def partner(self, b):
        return self.p.dev(**{b: 1 - self.me[b]})
    def desc(self, src, dst, k, slot, target):
        return pltpu.make_async_remote_copy(src, dst, self.ssem.at[k], self.rsem.at[slot], device_id=target, device_id_type=MESH)
    def copy(self, what, k, slot, z=None):
        def make():
            src, dst, target = what()
            return self.desc(src, dst, k, slot, target)
        make().start()
        self.sends.append((make, z))
    def arrive(self, dst, slot):
        self.desc(dst, dst, 0, slot, self.p.dev()).wait_recv()
    def finish(self, z):
        for make, at in self.sends:
            if at == z: make().wait_send()
    def height(self, k):
        return jnp.where(self.p.z < 2, 3 - k, k)
    def sib(self, k):
        zz = self.height(k)
        self.copy(lambda: (self.PB.at[zz, :, :, 1 - self.p.c], self.L0.at[zz], self.p.dev(c=1 - self.p.c)), k, zz)
    def pair(self, zz, b2name, b2v, r=pl.ds(0, 32)):
        if b2name == "y": return self.PB.at[zz, b2v, :, self.p.c, r]
        return self.PB.at[zz, :, b2v, self.p.c, r]
    def block(self, zz, r=pl.ds(0, 32), **where):
        return self.PB.at[zz, where.get("y", self.p.y), where.get("x", self.p.x), self.p.c, r]
    def mine(self, zz):
        return self.block(zz) if self.flat else self.pair(zz, self.b2, self.me[self.b2])
    def halves(self):
        return [(h, b1, b2, pl.ds(16 * h, 16)) for h, (b1, b2) in enumerate((("x", "y"), ("y", "x")))]

    def R1(self, k):
        p, zz = self.p, self.height(k)
        self.arrive(self.L0.at[zz], zz)
        for yy in range(2):
            for xx in range(2):
                self.PB[zz, yy, xx, p.c] = self.PB[zz, yy, xx, p.c] + self.L0[zz, yy, xx]
        if self.flat:
            for h, b1, b2, r in self.halves():
                self.copy(lambda b2=b2, r=r: (self.pair(zz, b2, 1 - self.me[b2], r), self.L1.at[zz, :, r], self.partner(b2)), 4 + 4 * h + k, 17 + 4 * h + zz)
        else:
            self.copy(lambda: (self.pair(zz, self.b2, 1 - self.me[self.b2]), self.L1.at[zz], self.partner(self.b2)), 4 + k, 4 + zz)
    def R2(self, k):
        zz = self.height(k)
        if self.flat:
            for h, b1, b2, r in self.halves():
                self.arrive(self.L1.at[zz, :, r], 17 + 4 * h + zz)
                o = self.pair(zz, b2, self.me[b2], r)
                o[...] = o[...] + self.L1[zz, :, r]
                self.copy(lambda b1=b1, r=r: (self.block(zz, r, **{b1: 1 - self.me[b1]}), self.L2.at[zz, r], self.partner(b1)), 12 + 4 * h + k, 25 + 4 * h + zz)
        else:
            self.arrive(self.L1.at[zz], 4 + zz)
            o = self.mine(zz)
            o[...] = o[...] + self.L1[zz]
    def R3(self, k):
        zz = self.height(k)
        for h, b1, b2, r in self.halves():
            self.arrive(self.L2.at[zz, r], 25 + 4 * h + zz)
            o = self.block(zz, r)
            o[...] = o[...] + self.L2[zz, r]
    def U(self, zu, z):
        o, land = self.mine(zu), self.UP.at[zu - 1]
        if 0 < z <= zu:
            self.arrive(land, 8 + zu)
            o[...] = o[...] + land[...]
        if z < zu: self.copy(lambda: (self.mine(zu), self.UP.at[zu - 1], self.p.dev(z=z + 1)), 20 + zu - 1, 8 + zu, z)
    def D(self, zd, z):
        o, land = self.mine(zd), self.DN.at[zd]
        if zd <= z < 3:
            self.arrive(land, 12 + zd)
            o[...] = o[...] + land[...]
        if z > zd: self.copy(lambda: (self.mine(zd), self.DN.at[zd], self.p.dev(z=z - 1)), 23 + zd, 12 + zd, z)
    def Z3(self, k, z):
        if z > 0: self.U(z, z)
        if z < 3: self.D(z, z)
        self.copy(lambda: (self.block(z, **{self.b1: 1 - self.me[self.b1]}), self.LX, self.partner(self.b1)), 26, 16, z)
    def FIN(self, k, z):
        v = self.block(z)
        if self.flat:
            if z > 0: self.U(z, z)
            if z < 3: self.D(z, z)
            self.out(v[...].astype(F32))
        else:
            self.arrive(self.LX, 16)
            self.out(v[...].astype(F32) + self.LX[...].astype(F32))

W_ORDER = ["o0", "o1", "o2", "o3", 8, 9, 10, 11, 12, 7, 4, 5, 6, 3, 0, 1, 2]
T_ORDER = [5, 4, 1, 2, 3, 0]
NW = 3

def backward_kernel(gains, buf, gfo, qkv, P, H, T, AT, GP, SR, cot,
                    o_tok, osp, oso, ocp, oco, oai, oao, oen,
                    PB, L0, L1, L2, UPC, DNC, UPA, DNA, LX, wbuf, hb, gpb, tb, atb, srb, pb, cotb, g, gb, gr, gx, gqkv, gtok,
                    ssem, rsem, csem, crsem, wsem, hsem, gpsem, tsem, msem, qsem, psem, osem):
    p = Place()
    neighbours_in = entry_barrier(p)
    lo, hi = half_masks()
    def w_copy(i):
        n = W_ORDER[i]
        src = gfo.at[int(n[1])] if isinstance(n, str) else buf.at[n]
        return pltpu.make_async_copy(src, wbuf.at[i % NW], wsem.at[i])
    h_copy = lambda i: pltpu.make_async_copy(H.at[2 - i], hb.at[i % 2], hsem.at[i])
    gp_copy = lambda j: pltpu.make_async_copy(GP.at[j], gpb.at[j % 2], gpsem.at[j])
    t_copy = lambda i: pltpu.make_async_copy(T.at[T_ORDER[i]], tb.at[i % 3], tsem.at[i])
    q_copy = lambda a, j: pltpu.make_async_copy(qkv.at[3 * a + j], PB.at[6 + a, j], qsem.at[3 * a + j])
    p_copy = lambda a: pltpu.make_async_copy(P.at[a], pb, psem.at[a])
    m_copy = [pltpu.make_async_copy(cot, cotb, msem.at[0]), pltpu.make_async_copy(SR, srb, msem.at[1]), pltpu.make_async_copy(AT, atb, msem.at[2])]
    h_copy(0).start(); m_copy[0].start(); w_copy(0).start(); gp_copy(0).start(); w_copy(1).start(); gp_copy(1).start(); w_copy(2).start()
    h_copy(1).start(); m_copy[1].start(); m_copy[2].start()
    for i in range(3): t_copy(i).start()
    for j in range(3): q_copy(1, j).start()
    p_copy(1).start()
    for j in range(3): q_copy(0, j).start()

    def o_ad(v):
        oai[...] = v[:, :512]
        oao[:, 0:512] = v[0:16, 512:]
        oao[:, 512:1024] = v[16:32, 512:]
    def put(ref, j=None):
        def f(v):
            if j is None: ref[...] = v
            else: ref[j] = v
        return f
    finals = [o_ad, put(oco), put(ocp, 1), put(ocp, 2), put(ocp, 0), put(oso), put(osp, 1), put(osp, 2), put(osp, 0)]
    reds = []
    nc = na = 0
    for t in range(NT):
        if ORDERS[t] == "A":
            up, dn, l2 = UPA.at[na], DNA.at[na], L2.at[na]; na += 1
        else:
            up, dn, l2 = UPC.at[nc], DNC.at[nc], None; nc += 1
        reds.append(Reduce(p, t, ORDERS[t], PB.at[t], L0.at[t], L1.at[t], l2, up, dn, LX.at[t], ssem.at[t], rsem.at[t], finals[t]))

    compute = {}
    def work(name, fn): compute[name] = fn

    def norm_back(i, first=False):
        def run():
            h_copy(i).wait()
            if first: m_copy[0].wait()
            @pl.loop(0, 4)
            def _(n):
                r = pl.ds(pl.multiple_of(n * 64, 64), 64)
                h = hb[i % 2, r, :]
                center = h - jnp.mean(h, axis=-1, keepdims=True)
                inv = lax.rsqrt(jnp.mean(center * center, axis=-1, keepdims=True) + EPS)
                nrm = center * inv
                gy = cotb[r, :].astype(F32) if first else g[r, :]
                a = gy * gains[2 - i, :][None]
                v = (a - jnp.mean(a, axis=-1, keepdims=True) - nrm * jnp.mean(a * nrm, axis=-1, keepdims=True)) * inv
                g[r, :] = v
                gb[r, :] = v.astype(BF)
            if i == 0: h_copy(2).start()
        return run

    def used(i):
        if i + NW < len(W_ORDER): w_copy(i + NW).start()

    def nt(lhs, i, fn):
        fn(dot_nt(lhs(), wbuf[i % NW]))

    def hidden_back(j):
        def run():
            w_copy(j).wait(); gp_copy(j).wait()
            def st(v):
                PB[8, j] = (gpb[j % 2] * v).astype(BF).reshape(2, 2, 2, 32, 1024)
            nt(lambda: gb[...], j, st)
            used(j)
            if j + 2 < 4: gp_copy(j + 2).start()
        return run

    def adapter_back():
        i = 4
        w_copy(i).wait(); m_copy[1].wait(); m_copy[2].wait()
        v = wbuf[i % NW, :, 512:1024].reshape(32, 32, 512)
        top, bot = v[:, :16].reshape(512, 512), v[:, 16:].reshape(512, 512)
        s = dot_nt(gb[:, 0:512], top) + dot_nt(gb[:, 512:1024], bot)
        gr[...] = (srb[...] * (4.0 * s)).astype(BF)
        wai = wbuf[i % NW, :, 0:512]
        g[...] = g[...] + dot_nt(gr[...], wai)
        used(i)

    def rows_of(k):
        return pl.ds(pl.multiple_of(reds[0].height(k) * 256, 256), 256)
    def adapter_grads(k):
        def run():
            if k == 0:
                neighbours_in()
                for h in range(2):
                    v = 4.0 * dot(atb[...], gb[:, 512 * h:512 * h + 512])
                    PB[0, :, :, :, :, 16 * h:16 * h + 16, 512:1024] = v.astype(BF).reshape(4, 2, 2, 2, 16, 512)
                t_copy(0).wait()
            v = dot(tb[0, rows_of(k), :], gr[...])
            PB[0, reds[0].height(k), :, :, :, :, 0:512] = v.astype(BF).reshape(2, 2, 2, 32, 512)
            reds[0].sib(k)
            if k == 3: t_copy(3).start()
        return run

    def hidden_in_back(j):
        def run():
            i = 5 + j
            w_copy(i).wait()
            def st(v): g[...] = g[...] + v
            nt(lambda: PB[8, j].reshape(256, 1024), i, st)
            used(i)
        return run

    def grad_tile(t, ti, rhs, last, k):
        def run():
            if k == 0 and t in (1, 2, 4, 5, 6): t_copy(ti).wait()
            PB[t, reds[t].height(k)] = dot(tb[ti % 3, rows_of(k), :], rhs()).astype(BF).reshape(2, 2, 2, 32, 1024)
            reds[t].sib(k)
            if k == 3 and last and ti + 3 < 6: t_copy(ti + 3).start()
        return run

    def mix_back(i):
        def run():
            w_copy(i).wait()
            def st(v): gx[...] = v.astype(BF)
            nt(lambda: gb[...], i, st)
            used(i)
        return run

    def attend_back(a, part):
        def run():
            if part == 0:
                p_copy(a).wait()
                for j in range(3): q_copy(a, j).wait()
            u = part // 2
            @pl.loop(0, 4, unroll=4)
            def _(n):
                pr = (part % 2) * 4 + n
                r, cc = pl.ds(u * 128, 128), cols(pr, 128)
                q, k, v = (PB[6 + a, j, u, :, :, :, cc].reshape(128, 128) for j in range(3))
                go = pair_up(gx[r, cc], lo, hi)
                prob = pb[u * 8 + pr]
                dp = dot_nt(go, v)
                ds = (prob * (dp - jnp.sum(prob * dp, axis=-1, keepdims=True))).astype(BF)
                gqkv[0, r, cc] = (dot(side(ds), pair_up(k, lo, hi)) * 0.125).astype(BF)
                gqkv[1, r, cc] = (dot_tn(ds, pair_up(q, lo, hi)) * 0.125).astype(BF)
                gqkv[2, r, cc] = dot_tn(prob.astype(BF), go).astype(BF)
            if part == 3 and a == 1: p_copy(0).start()
        return run

    def row_back(i, j, dst):
        def run():
            w_copy(i).wait()
            nt(lambda: gqkv[j], i, dst)
            used(i)
        return run
    def to_g(v): g[...] = g[...] + v
    cs = []
    me = p.x * 2 + p.c
    def context_back():
        i = 11
        w_copy(i).wait()
        def st(v): PB[8, 0] = (ctxf[...] + v).astype(BF).reshape(2, 2, 2, 32, 1024)
        nt(lambda: gqkv[2], i, st)
        used(i)
        for k, (dx, dc) in enumerate(((0, 1), (1, 0), (1, 1))):
            tx = (p.x + dx) % 2; tc = (p.c + dc) % 2
            c_ = pltpu.make_async_remote_copy(PB.at[8, 0, :, tx, tc], oen.at[0, me], csem.at[k], crsem.at[me], device_id=p.dev(x=tx, c=tc), device_id_type=MESH)
            c_.start(); cs.append(c_)
        c_ = pltpu.make_async_copy(PB.at[8, 0, :, p.x, p.c], oen.at[0, me], osem.at[0]); c_.start(); cs.append(c_)

    ctxf = gpb.at[0]
    def ctx_part(v): ctxf[...] = v
    def context_sent():
        for c_ in cs[:3]: c_.wait_send()
        cs[3].wait()
    def tokens_back():
        i = 16
        w_copy(i).wait()
        def st(v): gtok[...] = (g[...] + v).astype(BF)
        nt(lambda: gqkv[2], i, st)
        pltpu.make_async_copy(gtok, o_tok, osem.at[1]).start()

    def tile(t, ti, rhs, last):
        for zz in range(4): work(f"t{t}.{zz}", grad_tile(t, ti, rhs, last, zz))
    work("nb0", norm_back(0, True))
    for j in range(4): work(f"hb{j}", hidden_back(j))
    work("adb", adapter_back)
    for zz in range(4): work(f"adg.{zz}", adapter_grads(zz))
    for j in range(4): work(f"hi{j}", hidden_in_back(j))
    work("nb1", norm_back(1))
    tile(1, 1, lambda: gb[...], True)
    work("mb9", mix_back(9))
    for part in range(4): work(f"at1{part}", attend_back(1, part))
    tile(2, 2, lambda: gqkv[1], False)
    tile(3, 2, lambda: gqkv[2], True)
    tile(4, 3, lambda: gqkv[0], True)
    work("rb10", row_back(10, 1, ctx_part))
    work("cb", context_back)
    work("rb12", row_back(12, 0, to_g))
    work("nb2", norm_back(2))
    tile(5, 4, lambda: gb[...], True)
    work("mb13", mix_back(13))
    for part in range(4): work(f"at0{part}", attend_back(0, part))
    work("cs", context_sent)
    tile(6, 5, lambda: gqkv[1], False)
    tile(7, 5, lambda: gqkv[2], False)
    tile(8, 5, lambda: gqkv[0], True)
    work("rb14", row_back(14, 0, to_g))
    work("rb15", row_back(15, 1, to_g))
    work("tok", tokens_back)
    run_plan(PLAN_B, compute, reds, [p.z == z for z in range(4)])
    for r in reds: r.finish(None)
    for z in range(4):
        @pl.when(p.z == z)
        def _():
            for r in reds: r.finish(z)
    pltpu.make_async_copy(gtok, o_tok, osem.at[1]).wait()
    for k, (dx, dc) in enumerate(((0, 1), (1, 0), (1, 1))):
        tx = (p.x + dx) % 2; tc = (p.c + dc) % 2
        w = tx * 2 + tc
        pltpu.make_async_remote_copy(PB.at[8, 0, :, tx, tc], oen.at[0, w], csem.at[k], crsem.at[w], device_id=p.dev(), device_id_type=MESH).wait_recv()

def backward(gains, buf, gfo, qkv, P, H, T, AT, GP, SR, cot):
    any_ = pl.BlockSpec(memory_space=pl.ANY)
    vm = pl.BlockSpec(memory_space=pltpu.VMEM)
    V, S, D = pltpu.VMEM, jax.ShapeDtypeStruct, pltpu.SemaphoreType.DMA
    ops = (gains, buf.reshape(13, 1024, 1024), gfo.reshape(4, 1024, 1024), qkv.reshape(6, 2, 2, 2, 32, 1024), P, H, T, AT, GP, SR, cot)
    return pl.pallas_call(backward_kernel,
        out_shape=(S((256, 1024), BF), S((3, 32, 1024), F32), S((32, 1024), F32), S((3, 32, 1024), F32), S((32, 1024), F32), S((32, 512), F32), S((16, 1024), F32), S((1, 4, 2, 32, 1024), BF)),
        in_specs=[vm] + [any_] * 10, out_specs=(any_,) + (vm,) * 6 + (any_,),
        scratch_shapes=[V((NT, 4, 2, 2, 2, 32, 1024), BF), V((NT, 4, 2, 2, 32, 1024), BF), V((NT, 4, 2, 32, 1024), BF), V((3, 4, 32, 1024), BF),
                        V((6, 3, 2, 32, 1024), BF), V((6, 3, 2, 32, 1024), BF), V((3, 3, 32, 1024), BF), V((3, 3, 32, 1024), BF), V((NT, 32, 1024), BF),
                        V((NW, 1024, 1024), BF), V((2, 256, 1024), F32), V((2, 256, 1024), F32), V((3, 1024, 256), BF), V((512, 256), BF), V((256, 512), F32),
                        V((16, 256, 128), F32), V((256, 1024), BF), V((256, 1024), F32), V((256, 1024), BF), V((256, 512), BF), V((256, 1024), BF),
                        V((3, 256, 1024), BF), V((256, 1024), BF),
                        D((NT, NS)), D((NT, NR)), D((3,)), D((4,)), D((17,)), D((3,)), D((4,)), D((6,)), D((3,)), D((6,)), D((2,)), D((2,))],
        compiler_params=pltpu.CompilerParams(collective_id=1, has_side_effects=True, vmem_limit_bytes=63 << 20),
        name="backward")(*ops)


def finish_kernel(*refs):
    n = (len(refs) - 1) // 3
    ins, outs, held, sem = refs[:n], refs[n:2 * n], refs[2 * n:3 * n], refs[3 * n]
    first = [pltpu.make_async_copy(ins[k], held[k], sem.at[k]) for k in range(n)]
    last = [pltpu.make_async_copy(held[k], outs[k], sem.at[n + k]) for k in range(n)]
    for c in first: c.start()
    for k in range(n):
        first[k].wait()
        last[k].start()
    for c in last: c.wait()

def finish(*arrays):
    any_ = pl.BlockSpec(memory_space=pl.ANY)
    n = len(arrays)
    return pl.pallas_call(finish_kernel, out_shape=tuple(jax.ShapeDtypeStruct(a.shape, a.dtype) for a in arrays),
        in_specs=[any_] * n, out_specs=(any_,) * n,
        scratch_shapes=[pltpu.VMEM(a.shape, a.dtype) for a in arrays] + [pltpu.SemaphoreType.DMA((2 * n,))],
        compiler_params=pltpu.CompilerParams(vmem_limit_bytes=62 << 20), name="finish")(*arrays)


def device_program(tokens, encoder, dec_lengths, enc_lengths, gains, self_proj, self_out, cross_proj, cross_out, ffn_in, ffn_out, adapt_in, adapt_out, cotangent):
    shards = (self_proj, self_out, cross_proj, cross_out, ffn_in, ffn_out, adapt_in, adapt_out)
    buf, gfo, qkv, probs, hidden, turned, act_turned, gelu_slope, silu_slope, layer_out = forward(tokens, gains, dec_lengths, enc_lengths, shards, encoder)
    gtok, osp, oso, ocp, oco, oai, oao, oen = backward(gains, buf, gfo, qkv, probs, hidden, turned, act_turned, gelu_slope, silu_slope, cotangent)
    return finish(layer_out, gtok, oen, osp, oso, ocp, oco, oai, oao)


def solution(mesh):
    in_specs = (
        P(("seq", "enc"), None),
        P("seq", None, None, "enc", None),
        P(("seq", "enc"), None),
        P(("seq", "enc"), None),
        P(),
        P(None, ("seq", "enc"), None),
        P(("seq", "enc"), None),
        P(None, ("seq", "enc"), None),
        P(("seq", "enc"), None),
        P(("seq", "enc"), None),
        P(("seq", "enc"), None),
        P(("seq", "enc"), None),
        P(("seq", "enc"), None),
        P(("seq", "enc"), None),
    )
    out_specs = (
        P(("seq", "enc"), None),
        P(("seq", "enc"), None),
        P("seq", None, None, "enc", None),
        P(None, ("seq", "enc"), None),
        P(("seq", "enc"), None),
        P(None, ("seq", "enc"), None),
        P(("seq", "enc"), None),
        P(("seq", "enc"), None),
        P(("seq", "enc"), None),
    )
    fast = (mesh.shape["seq"], mesh.shape["enc"]) == (8, 4)
    return jax.shard_map(
        device_program if fast else per_device, mesh=mesh, in_specs=in_specs, out_specs=out_specs, check_vma=False
    )
```

```python
import jax
import jax.numpy as jnp
from jax import lax
from jax.experimental import pallas as pl
from jax.experimental.pallas import tpu as pltpu
from jax.sharding import PartitionSpec as P

HEADS = 16
ADAPT = 512
MICRO = 2


EPSILON = 1e-05
NEGATIVE = -1e30


def matmul(left, right):
    return jnp.dot(left, right, preferred_element_type=jnp.float32)


def matmul_tn(left, right):
    return lax.dot_general(
        left, right, (((0,), (0,)), ((), ())), preferred_element_type=jnp.float32
    )


def matmul_nt(left, right):
    return lax.dot_general(
        left, right, (((1,), (1,)), ((), ())), preferred_element_type=jnp.float32
    )


def layer_norm(hidden, gain):
    center = hidden - jnp.mean(hidden, axis=-1, keepdims=True)
    spread = jnp.mean(center * center, axis=-1, keepdims=True)
    return center * lax.rsqrt(spread + EPSILON) * gain


def norm_back(hidden, gain, grad_out):
    _, pullback = jax.vjp(lambda value: layer_norm(value, gain), hidden)
    return pullback(grad_out)[0]


def gelu_exact(value):
    return jax.nn.gelu(value, approximate=False)


def slot_masks(dec_row, enc_row, rows):
    half_rows = rows // 2
    places = lax.broadcasted_iota(jnp.int32, (rows,), 0)
    paired = dec_row[1] > 0
    second = jnp.logical_and(paired, places >= half_rows)
    anchor = jnp.where(second, half_rows, 0).astype(jnp.int32)
    dec_valid = jnp.where(second, dec_row[1], dec_row[0])
    enc_valid = jnp.where(second, enc_row[1], enc_row[0])
    key_live = places - anchor < dec_valid
    context_live = places - anchor < enc_valid
    same_slot = second[:, None] == second[None, :]
    causal = places[None, :] <= places[:, None]
    self_mask = same_slot & causal & key_live[None, :]
    cross_mask = same_slot & context_live[None, :]
    return (self_mask, cross_mask)


def split_heads(matrix):
    return matrix.reshape(matrix.shape[0], HEADS, matrix.shape[1] // HEADS)


def attend(queries, keys, values, allowed):
    depth = queries.shape[1] // HEADS
    scores = jnp.einsum(
        "qhd,khd->hqk", split_heads(queries), split_heads(keys), preferred_element_type=jnp.float32
    ) * float(depth) ** (-0.5)
    masked = jnp.where(allowed[None], scores, NEGATIVE)
    weights = jnp.exp(masked - jnp.max(masked, axis=-1, keepdims=True))
    probs = weights / jnp.sum(weights, axis=-1, keepdims=True)
    mixed = jnp.einsum(
        "hqk,khd->qhd",
        probs.astype(jnp.bfloat16),
        split_heads(values),
        preferred_element_type=jnp.float32,
    )
    return (mixed.reshape(queries.shape).astype(jnp.bfloat16), probs)


def attend_back(grad_mixed, queries, keys, values, probs):
    depth = queries.shape[1] // HEADS
    factor = float(depth) ** (-0.5)
    grad_heads = split_heads(grad_mixed)
    grad_probs = jnp.einsum(
        "qhd,khd->hqk", grad_heads, split_heads(values), preferred_element_type=jnp.float32
    )
    inner = jnp.sum(probs * grad_probs, axis=-1, keepdims=True)
    grad_scores = (probs * (grad_probs - inner)).astype(jnp.bfloat16)
    grad_query = (
        jnp.einsum(
            "hqk,khd->qhd", grad_scores, split_heads(keys), preferred_element_type=jnp.float32
        )
        * factor
    )
    grad_key = (
        jnp.einsum(
            "hqk,qhd->khd", grad_scores, split_heads(queries), preferred_element_type=jnp.float32
        )
        * factor
    )
    grad_value = jnp.einsum(
        "hqk,qhd->khd", probs.astype(jnp.bfloat16), grad_heads, preferred_element_type=jnp.float32
    )
    return (
        grad_query.reshape(queries.shape).astype(jnp.bfloat16),
        grad_key.reshape(keys.shape).astype(jnp.bfloat16),
        grad_value.reshape(values.shape).astype(jnp.bfloat16),
    )


def per_device(
    tokens,
    encoder,
    dec_lengths,
    enc_lengths,
    gains,
    self_proj,
    self_out,
    cross_proj,
    cross_out,
    ffn_in,
    ffn_out,
    adapt_in,
    adapt_out,
    cotangent,
):
    shards = (self_proj, self_out, cross_proj, cross_out, ffn_in, ffn_out, adapt_in, adapt_out)

    def obtain():
        return (
            lax.all_gather(shards[0], ("seq", "enc"), axis=1, tiled=True),
            lax.all_gather(shards[1], ("seq", "enc"), axis=0, tiled=True),
            lax.all_gather(shards[2], ("seq", "enc"), axis=1, tiled=True),
            lax.all_gather(shards[3], ("seq", "enc"), axis=0, tiled=True),
            lax.all_gather(shards[4], ("seq", "enc"), axis=0, tiled=True),
            lax.all_gather(shards[5], ("seq", "enc"), axis=0, tiled=True),
            lax.all_gather(shards[6], ("seq", "enc"), axis=0, tiled=True),
            lax.all_gather(shards[7], ("seq", "enc"), axis=0, tiled=True),
        )

    rows = tokens.shape[0] // MICRO
    width = tokens.shape[1]
    owner = lax.axis_index("enc")
    acc_self = jnp.zeros((width, 3, width), jnp.float32)
    acc_self_out = jnp.zeros((width, width), jnp.float32)
    acc_cross = jnp.zeros((width, 3, width), jnp.float32)
    acc_cross_out = jnp.zeros((width, width), jnp.float32)
    acc_adapt_in = jnp.zeros((width, ADAPT), jnp.float32)
    acc_adapt_out = jnp.zeros((ADAPT, width), jnp.float32)
    outputs = []
    grad_rows = []
    grad_contexts = []
    for micro_index in range(MICRO):
        w_self, w_self_out, w_cross, w_cross_out, w_ffn_in, w_ffn_out, w_adapt_in, w_adapt_out = (
            obtain()
        )
        lower = micro_index * rows
        token_rows = tokens[lower : lower + rows]
        self_mask, cross_mask = slot_masks(dec_lengths[micro_index], enc_lengths[micro_index], rows)
        pieces = encoder[0, :, micro_index]
        context = lax.dynamic_index_in_dim(
            lax.all_gather(pieces, "enc", axis=1, tiled=True), owner, 0, keepdims=False
        )
        self_query = matmul(token_rows, w_self[0]).astype(jnp.bfloat16)
        self_key = matmul(token_rows, w_self[1]).astype(jnp.bfloat16)
        self_value = matmul(token_rows, w_self[2]).astype(jnp.bfloat16)
        self_mix, self_probs = attend(self_query, self_key, self_value, self_mask)
        first_sum = token_rows.astype(jnp.float32) + matmul(self_mix, w_self_out)
        first_norm = layer_norm(first_sum, gains[0])
        first_low = first_norm.astype(jnp.bfloat16)
        cross_query = matmul(first_low, w_cross[0]).astype(jnp.bfloat16)
        cross_key = matmul(context, w_cross[1]).astype(jnp.bfloat16)
        cross_value = matmul(context, w_cross[2]).astype(jnp.bfloat16)
        cross_mix, cross_probs = attend(cross_query, cross_key, cross_value, cross_mask)
        second_sum = first_norm + matmul(cross_mix, w_cross_out)
        second_norm = layer_norm(second_sum, gains[1])
        second_low = second_norm.astype(jnp.bfloat16)
        ffn_pre = matmul(second_low, w_ffn_in)
        ffn_act = gelu_exact(ffn_pre).astype(jnp.bfloat16)
        adapt_pre = matmul(second_low, w_adapt_in)
        adapt_act = jax.nn.silu(adapt_pre).astype(jnp.bfloat16)
        third_sum = second_norm + matmul(ffn_act, w_ffn_out) + 4.0 * matmul(adapt_act, w_adapt_out)
        outputs.append(layer_norm(third_sum, gains[2]).astype(jnp.bfloat16))
        w_self, w_self_out, w_cross, w_cross_out, w_ffn_in, w_ffn_out, w_adapt_in, w_adapt_out = (
            obtain()
        )
        grad_third = norm_back(
            third_sum, gains[2], cotangent[lower : lower + rows].astype(jnp.float32)
        )
        grad_branch = grad_third.astype(jnp.bfloat16)
        _, gelu_pull = jax.vjp(gelu_exact, ffn_pre)
        grad_ffn_pre = gelu_pull(matmul_nt(grad_branch, w_ffn_out))[0].astype(jnp.bfloat16)
        grad_adapt_act = matmul_nt(grad_branch, w_adapt_out) * 4.0
        _, silu_pull = jax.vjp(jax.nn.silu, adapt_pre)
        grad_adapt_pre = silu_pull(grad_adapt_act)[0].astype(jnp.bfloat16)
        acc_adapt_out = acc_adapt_out + matmul_tn(adapt_act, grad_branch) * 4.0
        acc_adapt_in = acc_adapt_in + matmul_tn(second_low, grad_adapt_pre)
        grad_second = (
            grad_third + matmul_nt(grad_ffn_pre, w_ffn_in) + matmul_nt(grad_adapt_pre, w_adapt_in)
        )
        grad_second_sum = norm_back(second_sum, gains[1], grad_second)
        grad_cross_branch = grad_second_sum.astype(jnp.bfloat16)
        acc_cross_out = acc_cross_out + matmul_tn(cross_mix, grad_cross_branch)
        grad_cross_mix = matmul_nt(grad_cross_branch, w_cross_out).astype(jnp.bfloat16)
        grad_cq, grad_ck, grad_cv = attend_back(
            grad_cross_mix, cross_query, cross_key, cross_value, cross_probs
        )
        acc_cross = acc_cross + jnp.stack(
            [
                matmul_tn(first_low, grad_cq),
                matmul_tn(context, grad_ck),
                matmul_tn(context, grad_cv),
            ],
            axis=1,
        )
        grad_context = matmul_nt(grad_ck, w_cross[1]) + matmul_nt(grad_cv, w_cross[2])
        holder = jnp.zeros((lax.axis_size("enc"),) + grad_context.shape, jnp.float32)
        holder = lax.dynamic_update_index_in_dim(holder, grad_context, owner, 0)
        returned = lax.psum_scatter(
            holder.astype(jnp.bfloat16), "enc", scatter_dimension=1, tiled=True
        )
        grad_contexts.append(returned)
        grad_first = grad_second_sum + matmul_nt(grad_cq, w_cross[0])
        grad_first_sum = norm_back(first_sum, gains[0], grad_first)
        grad_self_branch = grad_first_sum.astype(jnp.bfloat16)
        acc_self_out = acc_self_out + matmul_tn(self_mix, grad_self_branch)
        grad_self_mix = matmul_nt(grad_self_branch, w_self_out).astype(jnp.bfloat16)
        grad_sq, grad_sk, grad_sv = attend_back(
            grad_self_mix, self_query, self_key, self_value, self_probs
        )
        acc_self = acc_self + jnp.stack(
            [
                matmul_tn(token_rows, grad_sq),
                matmul_tn(token_rows, grad_sk),
                matmul_tn(token_rows, grad_sv),
            ],
            axis=1,
        )
        grad_input = (
            grad_first_sum
            + matmul_nt(grad_sq, w_self[0])
            + matmul_nt(grad_sk, w_self[1])
            + matmul_nt(grad_sv, w_self[2])
        )
        grad_rows.append(grad_input.astype(jnp.bfloat16))
    summed = (
        lax.psum_scatter(acc_self, ("seq", "enc"), scatter_dimension=0, tiled=True),
        lax.psum_scatter(acc_self_out, ("seq", "enc"), scatter_dimension=0, tiled=True),
        lax.psum_scatter(acc_cross, ("seq", "enc"), scatter_dimension=0, tiled=True),
        lax.psum_scatter(acc_cross_out, ("seq", "enc"), scatter_dimension=0, tiled=True),
        lax.psum_scatter(acc_adapt_in, ("seq", "enc"), scatter_dimension=0, tiled=True),
        lax.psum_scatter(acc_adapt_out, ("seq", "enc"), scatter_dimension=0, tiled=True),
    )
    layer_out = jnp.concatenate(outputs, axis=0)
    grad_tokens = jnp.concatenate(grad_rows, axis=0)
    grad_encoder = jnp.stack(grad_contexts, axis=1)[None]
    grad_self_proj = jnp.transpose(summed[0], (1, 0, 2))
    grad_cross_proj = jnp.transpose(summed[2], (1, 0, 2))
    return (
        layer_out,
        grad_tokens,
        grad_encoder,
        grad_self_proj,
        summed[1],
        grad_cross_proj,
        summed[3],
        summed[4],
        summed[5],
    )


MESH = pl.DeviceIdType.MESH
class Place:
    def __init__(self):
        seq, enc = lax.axis_index("seq"), lax.axis_index("enc")
        self.z, self.y, self.x, self.c = seq // 2, seq % 2, enc // 2, enc % 2
        self.up, self.down = jnp.minimum(self.z + 1, 3), jnp.maximum(self.z - 1, 0)
        self.step = jnp.where(self.z < 2, 1, -1)
    def dev(self, z=None, y=None, x=None, c=None):
        z = self.z if z is None else z
        y = self.y if y is None else y
        x = self.x if x is None else x
        c = self.c if c is None else c
        return (z * 2 + y, x * 2 + c)

def entry_barrier(p):
    bar = pltpu.get_barrier_semaphore()
    def sig(d):
        pl.semaphore_signal(bar, inc=1, device_id=d, device_id_type=MESH)
    sig(p.dev(c=1 - p.c)); sig(p.dev(x=1 - p.x)); sig(p.dev(y=1 - p.y)); sig(p.dev(x=1 - p.x, c=1 - p.c))
    @pl.when(p.z < 3)
    def _(): sig(p.dev(z=p.up))
    @pl.when(p.z > 0)
    def _(): sig(p.dev(z=p.down))
    peers = 4 + (p.z < 3).astype(jnp.int32) + (p.z > 0).astype(jnp.int32)
    return lambda: pl.semaphore_wait(bar, peers)

ALL4 = pl.ds(0, 4)
ALL2 = pl.ds(0, 2)

class Stream:
    def __init__(self, p, own, view, order, ssem, rsem):
        self.p, self.own, self.view, self.order, self.ssem, self.rsem = p, own, view, order, ssem, rsem
        self.flat = order[0] == "z"
        self.b1, self.b2 = (order[1], order[2]) if self.flat else (order[0], order[2])
        self.me = {"x": p.x, "y": p.y}
        self.sends = [[], []]

    def source(self, r, kind):
        p = self.p
        return p.z - p.step if kind == 1 and r == 3 else p.z + p.step * r

    def unit(self, z, c=None, **where):
        w = dict(self.me) if self.flat else {**self.me, self.b1: ALL2}
        w.update(where)
        return self.view(z, w["y"], w["x"], self.p.c if c is None else c)

    def partner(self, b):
        return self.p.dev(**{b: 1 - self.me[b]})

    def copy(self, kind, slot, what):
        k = len(self.sends[kind])
        def make():
            src, dst, target = what()
            return pltpu.make_async_remote_copy(src, dst, self.ssem.at[k], self.rsem.at[slot()], device_id=target, device_id_type=MESH)
        make().start()
        self.sends[kind].append(make)

    def arrive(self, where, slot):
        pltpu.make_async_remote_copy(where, where, self.ssem.at[0], self.rsem.at[slot], device_id=self.p.dev(), device_id_type=MESH).wait_recv()

    def finish(self, kind):
        for make in self.sends[kind]: make().wait_send()

    def along(self, kind, r, way, src=None):
        p = self.p
        def what():
            u = self.unit(self.source(r, kind))
            return u if src is None else src, u, p.dev(z=p.z + way * p.step)
        self.copy(kind, lambda: self.source(r, kind), what)

    def across(self, kind, r, src=None):
        b = self.b1 if self.flat else self.b2
        def what():
            u = self.unit(self.source(r, kind))
            return u if src is None else src, u, self.partner(b)
        self.copy(kind, lambda: 4 + self.source(r, kind), what)

    def P0(self, r, kind):
        if self.flat:
            self.along(kind, 0, 1, self.own)
            if kind == 1: self.along(kind, 0, -1, self.own)
            self.across(kind, 0, self.own)
        else:
            self.copy(kind, lambda: 8, lambda: (self.own, self.unit(self.p.z, **self.me), self.partner(self.b1)))
    def E0(self, r, kind):
        self.arrive(self.unit(self.p.z, **{self.b1: 1 - self.me[self.b1]}), 8)
        self.along(kind, 0, 1)
        if kind == 1: self.along(kind, 0, -1)
        self.across(kind, 0)
    def H(self, r, kind):
        z = self.source(r, kind)
        self.arrive(self.unit(z), z)
        if kind == 1: self.along(kind, r, -1 if r < 3 else 1)
        self.across(kind, r)
    def E(self, r, kind):
        z = self.source(r, kind)
        self.arrive(self.unit(z, **{self.b1: 1 - self.me[self.b1]}), 4 + z)
        def what():
            u = self.unit(self.source(r, kind), **{self.b1: ALL2})
            return u, u, self.partner(self.b2)
        self.copy(kind, lambda: 8 + self.source(r, kind), what)
    def plane(self, far, c=None):
        return self.unit(ALL4, c, **{self.b1: ALL2, self.b2: 1 - self.me[self.b2] if far else self.me[self.b2]})
    def F0(self, r, kind):
        self.copy(kind, lambda: 12, lambda: (self.plane(False), self.plane(False), self.p.dev(c=1 - self.p.c)))
    def F5(self, r, kind):
        for zz in range(4):
            self.arrive(self.unit(zz, **{self.b1: ALL2, self.b2: 1 - self.me[self.b2]}), (8 if self.flat else 4) + zz)
        self.copy(kind, lambda: 13, lambda: (self.plane(True), self.plane(True), self.p.dev(c=1 - self.p.c)))
    def L(self, r, kind):
        self.arrive(self.plane(False, 1 - self.p.c), 12)
        self.arrive(self.plane(True, 1 - self.p.c), 13)

def run_plan(plan, compute, movers, guards):
    i = 0
    while i < len(plan):
        it = plan[i]
        if isinstance(it, str):
            compute[it]()
            i += 1
        elif it[3] is None:
            getattr(movers[it[0]], it[1])(it[2])
            i += 1
        else:
            j = i
            while j < len(plan) and not isinstance(plan[j], str) and plan[j][3] == it[3]: j += 1
            @pl.when(guards[it[3]])
            def _():
                for m, name, k, kind in plan[i:j]: getattr(movers[m], name)(k, kind)
            i = j


PLAN_F = [
    (7, "P0", 0, 1), (6, "P0", 0, 0), (3, "P0", 0, 0), (10, "P0", 0, 1), (0, "P0", 0, 1), (1, "P0", 0, 1), (2, "P0", 0, 1), (3, "P0", 0, 1),
    (4, "P0", 0, 1), (0, "P0", 0, 0), (1, "P0", 0, 0), (5, "P0", 0, 1), (2, "P0", 0, 0), (6, "P0", 0, 1), (8, "P0", 0, 1), (4, "P0", 0, 0),
    (5, "P0", 0, 0), (9, "P0", 0, 1), (7, "P0", 0, 0), (8, "P0", 0, 0), "flip0", "ctxsend", "staged", "own", (0, "E", 0, 0), (1, "E", 0, 0), "masks",
    (0, "H", 1, 0), (3, "E0", 0, 0), (0, "H", 1, 1), (0, "H", 3, 1), (0, "E", 0, 1), (1, "H", 1, 0), (1, "H", 1, 1), (9, "P0", 0, 0), (4, "H", 1, 1),
    (1, "H", 3, 1), (1, "E", 0, 1), (7, "E0", 0, 1), (4, "E", 0, 0), (2, "E0", 0, 1), (4, "H", 1, 0), (10, "P0", 0, 0), (6, "E0", 0, 0),
    (5, "E", 0, 0), (3, "E0", 0, 1), (4, "H", 3, 1), (2, "E0", 0, 0), (5, "H", 1, 1), (4, "E", 0, 1), (5, "H", 1, 0), (5, "H", 3, 1), (5, "E", 0, 1),
    (8, "H", 1, 1), (8, "H", 3, 1), (8, "H", 1, 0), (9, "H", 1, 1), (6, "E0", 0, 1), (8, "E", 0, 0), (9, "H", 3, 1), (0, "H", 2, 1), (8, "E", 0, 1),
    (0, "H", 2, 0), (7, "E0", 0, 0), (9, "E", 0, 1), (1, "H", 2, 1), (1, "H", 2, 0), (4, "H", 2, 0), (10, "E0", 0, 1), (9, "H", 1, 0), (9, "E", 0, 0),
    (2, "H", 3, 1), (1, "E", 1, 1), (3, "H", 1, 1), (1, "E", 3, 1), (2, "H", 1, 1), (2, "H", 1, 0), (3, "H", 3, 1), (10, "E0", 0, 0), (3, "H", 1, 0),
    (1, "E", 1, 0), (5, "E", 1, 1), (5, "E", 1, 0), "ctxin", (5, "H", 2, 1), (5, "H", 2, 0), (7, "H", 3, 1), (6, "H", 3, 1), (8, "H", 2, 1),
    (8, "H", 2, 0), (0, "E", 3, 1), (9, "H", 2, 0), (5, "E", 3, 1), (4, "E", 1, 0), (9, "E", 1, 1), (4, "H", 2, 1), (4, "E", 1, 1), (0, "E", 1, 1),
    (7, "H", 1, 1), (6, "H", 1, 0), (1, "E", 2, 0), (9, "E", 1, 0), (0, "E", 1, 0), (9, "E", 3, 1), (10, "H", 3, 1), (0, "H", 3, 0), (4, "E", 3, 1),
    (8, "E", 1, 0), (9, "H", 2, 1), (7, "H", 1, 0), (1, "E", 2, 1), (10, "H", 1, 1), "flip1", (8, "E", 1, 1), (1, "H", 3, 0), (8, "E", 3, 1),
    (5, "H", 3, 0), (6, "H", 1, 1), (0, "E", 2, 0), (1, "F0", 0, 1), (4, "E", 2, 0), (5, "E", 2, 0), (11, "P0", 0, 1), (2, "H", 2, 1),
    (13, "P0", 0, 1), (0, "E", 2, 1), (2, "H", 2, 0), (10, "H", 1, 0), (3, "H", 2, 0), (14, "P0", 0, 1), (9, "E", 2, 0), (12, "P0", 0, 1),
    (3, "H", 2, 1), (0, "F0", 0, 1), (5, "E", 2, 1), (2, "F0", 0, 1), (4, "H", 3, 0), (16, "P0", 0, 1), (17, "P0", 0, 1), (6, "H", 2, 1),
    (7, "H", 2, 1), (8, "E", 2, 0), (1, "E", 3, 0), (3, "F0", 0, 1), (5, "F0", 0, 1), (1, "F0", 0, 0), (18, "P0", 0, 1), (6, "H", 2, 0),
    (20, "P0", 0, 1), (21, "P0", 0, 1), (6, "F0", 0, 1), (15, "P0", 0, 1), (10, "H", 2, 1), (7, "H", 2, 0), (4, "E", 2, 1), (0, "E", 3, 0),
    (4, "F0", 0, 1), (7, "F0", 0, 1), (13, "H", 1, 1), (8, "E", 2, 1), (8, "H", 3, 0), (0, "F0", 0, 0), (11, "P0", 0, 0), (16, "H", 1, 1),
    (17, "H", 1, 1), (20, "H", 1, 1), (12, "H", 1, 1), (9, "H", 3, 0), (10, "F0", 0, 1), (21, "H", 1, 1), (5, "E", 3, 0), (8, "F0", 0, 1),
    (5, "F0", 0, 0), (19, "P0", 0, 1), (12, "P0", 0, 0), (12, "H", 1, 0), (2, "H", 3, 0), (4, "E", 3, 0), (10, "H", 2, 0), (9, "E", 2, 1),
    (13, "P0", 0, 0), (8, "E", 3, 0), (4, "F0", 0, 0), (15, "P0", 0, 0), (13, "H", 1, 0), (3, "H", 3, 0), (3, "F0", 0, 0), (2, "F0", 0, 0),
    (13, "H", 3, 1), (9, "F0", 0, 1), (0, "F5", 0, 0), (14, "P0", 0, 0), (19, "P0", 0, 0), (8, "F0", 0, 0), (0, "L", 0, 0), (12, "H", 3, 1),
    (1, "F5", 0, 1), (12, "E", 0, 0), (9, "E", 3, 0), (13, "H", 2, 1), (11, "E0", 0, 0), (12, "E", 1, 0), (9, "F0", 0, 0), (1, "F5", 0, 0),
    (1, "L", 0, 0), (1, "L", 0, 1), (6, "H", 3, 0), (6, "F0", 0, 0), (5, "F5", 0, 0), (16, "P0", 0, 0), (12, "H", 2, 1), (16, "H", 1, 0),
    (17, "P0", 0, 0), (17, "H", 1, 0), (2, "F5", 0, 1), (3, "F5", 0, 1), (12, "E", 0, 1), (3, "F5", 0, 0), (5, "L", 0, 0), (0, "F5", 0, 1),
    (14, "E0", 0, 1), (2, "L", 0, 1), (16, "H", 3, 1), (7, "H", 3, 0), (3, "L", 0, 0), (13, "E", 0, 0), (11, "E0", 0, 1), (2, "F5", 0, 0),
    (7, "F0", 0, 0), (11, "H", 3, 1), (18, "P0", 0, 0), (17, "H", 3, 1), (5, "F5", 0, 1), (13, "E", 0, 1), (3, "L", 0, 1), (16, "E", 0, 1),
    (0, "L", 0, 1), "w0", (4, "F5", 0, 0), (5, "L", 0, 1), (7, "F5", 0, 1), "w2", (14, "E0", 0, 0), (2, "L", 0, 0), "w1", (9, "F5", 0, 0),
    (12, "H", 2, 0), (6, "F5", 0, 1), "proj0", "proj2", (15, "E0", 0, 0), (14, "H", 1, 1), (16, "H", 2, 1), (17, "E", 0, 1), "proj1", (20, "P0", 0, 0),
    (13, "E", 1, 0), (10, "H", 3, 0), (20, "H", 1, 0), (8, "F5", 0, 0), (10, "F0", 0, 0), (13, "H", 2, 0), (7, "L", 0, 1), (4, "L", 0, 0), "at00",
    (18, "E0", 0, 1), (20, "E", 0, 1), (6, "L", 0, 1), (16, "E", 0, 0), (16, "E", 1, 0), (19, "E0", 0, 1), (21, "P0", 0, 0), (21, "H", 1, 0),
    (16, "H", 2, 0), (17, "H", 2, 0), (11, "H", 1, 1), (12, "H", 3, 0), (8, "L", 0, 0), (14, "H", 3, 1), "at01", (19, "E0", 0, 0), (9, "L", 0, 0),
    (14, "H", 1, 0), (20, "E", 1, 1), (21, "E", 0, 1), (20, "H", 3, 1), (21, "H", 2, 0), "at02", (21, "H", 3, 1), (4, "F5", 0, 1), (20, "H", 2, 0),
    (15, "E0", 0, 1), (11, "H", 2, 1), (6, "F5", 0, 0), (9, "F5", 0, 1), (22, "P0", 0, 1), (23, "P0", 0, 1), (13, "H", 3, 0), (12, "E", 1, 1),
    (7, "F5", 0, 0), (17, "H", 2, 1), (16, "E", 1, 1), (13, "E", 1, 1), (17, "E", 0, 0), "at03", (10, "F5", 0, 1), (10, "L", 0, 1), (15, "H", 3, 1),
    (6, "L", 0, 0), (18, "E0", 0, 0), (8, "F5", 0, 1), (4, "L", 0, 1), (12, "E", 2, 1), (9, "L", 0, 1), "flip3", (12, "E", 3, 1), (17, "E", 1, 0),
    (17, "E", 1, 1), (18, "H", 1, 1), "w3", "w4", (7, "L", 0, 0), (11, "F0", 0, 1), (21, "E", 1, 1), "w5", (19, "H", 3, 1), (8, "L", 0, 1), "w6",
    (20, "E", 0, 0), (16, "E", 3, 1), (11, "H", 1, 0), (20, "E", 1, 0), (12, "E", 2, 0), "branch3", (13, "E", 3, 1), "norm0", (13, "E", 2, 1),
    (18, "H", 3, 1), (14, "H", 2, 0), (14, "H", 2, 1), (20, "H", 2, 1), (21, "H", 2, 1), "flip2", (18, "H", 1, 0), (16, "H", 3, 0), (16, "E", 2, 1),
    "proj4", (16, "F0", 0, 1), "proj5", (16, "E", 2, 0), (21, "E", 0, 0), "proj6", (10, "F5", 0, 0), (14, "F0", 0, 1), "at10", (15, "H", 1, 1),
    (12, "F0", 0, 1), (13, "E", 2, 0), (12, "E", 3, 0), (17, "E", 3, 1), "at11", (15, "H", 2, 1), (12, "F0", 0, 0), (10, "L", 0, 0), (13, "F0", 0, 1),
    "at12", (11, "H", 2, 0), (17, "E", 2, 0), (19, "H", 1, 1), (20, "E", 3, 1), (21, "E", 2, 0), "at13", (21, "E", 1, 0), (19, "H", 2, 1),
    (13, "E", 3, 0), (13, "F0", 0, 0), (20, "E", 2, 0), "flip4", "w7", (11, "H", 3, 0), (15, "F0", 0, 1), (11, "F0", 0, 0), (23, "P0", 0, 0),
    (22, "P0", 0, 0), (11, "F5", 0, 1), "branch7", (16, "E", 3, 0), "norm1", (15, "H", 1, 0), (16, "F0", 0, 0), (17, "H", 3, 0), (11, "L", 0, 1),
    "flip5", (19, "F0", 0, 1), (18, "H", 2, 1), (22, "E0", 0, 1), (18, "H", 2, 0), (18, "F0", 0, 1), (19, "H", 1, 0), (22, "H", 1, 1), (21, "E", 3, 1),
    (17, "E", 2, 1), (21, "H", 3, 0), (13, "F5", 0, 0), (20, "H", 3, 0), (23, "E0", 0, 1), (13, "L", 0, 0), (15, "H", 2, 0), (17, "F0", 0, 1),
    (14, "H", 3, 0), (14, "F0", 0, 0), (11, "F5", 0, 0), (12, "F5", 0, 1), (23, "H", 1, 1), (12, "F5", 0, 0), (12, "L", 0, 1), (11, "L", 0, 0),
    (15, "H", 3, 0), (22, "E0", 0, 0), (15, "F0", 0, 0), (12, "L", 0, 0), "w8", (23, "E0", 0, 0), (13, "F5", 0, 1), (16, "F5", 0, 0), "adapter",
    (17, "E", 3, 0), (20, "E", 2, 1), (22, "H", 3, 1), (19, "H", 2, 0), (17, "F0", 0, 0), (14, "F5", 0, 1), (13, "L", 0, 1), "w9", (16, "L", 0, 0),
    (23, "H", 3, 1), "hid0", (19, "H", 3, 0), (19, "F0", 0, 0), (20, "F0", 0, 1), (14, "L", 0, 1), (21, "E", 2, 1), "adapter_out", (22, "H", 2, 1),
    (20, "E", 3, 0), (20, "F0", 0, 0), (16, "F5", 0, 1), (16, "L", 0, 1), (14, "F5", 0, 0), (23, "H", 2, 1), (21, "E", 3, 0), (18, "H", 3, 0),
    (18, "F0", 0, 0), (15, "F5", 0, 1), (21, "F0", 0, 0), (21, "F0", 0, 1), (14, "L", 0, 0), "w10", (22, "F0", 0, 1), (15, "F5", 0, 0),
    (15, "L", 0, 1), (22, "H", 1, 0), (18, "F5", 0, 1), (23, "F0", 0, 1), "hid1", (23, "H", 1, 0), (17, "F5", 0, 0), (15, "L", 0, 0), "w11",
    (22, "H", 2, 0), (19, "F5", 0, 1), (23, "H", 2, 0), (18, "L", 0, 1), (17, "L", 0, 0), (18, "F5", 0, 0), "hid2", (20, "F5", 0, 0), (19, "L", 0, 1),
    (22, "H", 3, 0), (22, "F0", 0, 0), (20, "F5", 0, 1), (20, "L", 0, 0), (23, "H", 3, 0), (18, "L", 0, 0), (23, "F0", 0, 0), "w13", (17, "F5", 0, 1),
    (19, "F5", 0, 0), (20, "L", 0, 1), (17, "L", 0, 1), "w12", (21, "F5", 0, 0), (19, "L", 0, 0), "w14", "hid3", (21, "L", 0, 0), (23, "F5", 0, 0),
    (21, "F5", 0, 1), (22, "F5", 0, 0), (22, "F5", 0, 1), "out0", (23, "F5", 0, 1), "out1", (22, "L", 0, 0), (23, "L", 0, 0), (21, "L", 0, 1),
    (22, "L", 0, 1), "w15", (23, "L", 0, 1), "w16", "out2", "out3", "norm2",
]

F32, BF = jnp.float32, jnp.bfloat16
NSLOT, NSEND = 14, 19
N_STREAM = 24
EPS = 1e-05

def dot(a, b):
    return jnp.dot(a, b, preferred_element_type=F32)

def dot_nt(a, b):
    return lax.dot_general(a, b, (((1,), (1,)), ((), ())), preferred_element_type=F32)

def dot_tn(a, b):
    return lax.dot_general(a, b, (((0,), (0,)), ((), ())), preferred_element_type=F32)

def cols(n, width):
    return pl.ds(pl.multiple_of(n * width, width), width)

def norm_rows(h):
    center = h - jnp.mean(h, axis=-1, keepdims=True)
    spread = jnp.mean(center * center, axis=-1, keepdims=True)
    return center * lax.rsqrt(spread + EPS)

def half_masks():
    lane = lax.broadcasted_iota(jnp.int32, (1, 128), 1)
    lo = jnp.where(lane < 64, 1.0, 0.0)
    return lo.astype(BF), (1.0 - lo).astype(BF)

def pair_up(m, lo, hi):
    return jnp.concatenate([m * lo, m * hi], axis=0)

def side(m):
    return jnp.concatenate([m[:128], m[128:]], axis=1)

def forward_kernel(tokens, gains, dlen, elen, sp, so, cp, co, fi, fo, ai, ao, en,
                   buf, gfo, o_qkv, o_p, o_h, o_t, o_at, o_gp, o_sr, o_out,
                   qkv, P, H, T, AT, GP, SR, OUT, ctx, wbuf, wo, own, ownf, y, yl, mix, af, ar, bias, x,
                   ssem, rsem, lsem, csem, crsem, wsem, osem):
    p = Place()
    neighbours_in = entry_barrier(p)
    loc = []
    x_in = pltpu.make_async_copy(tokens, x, lsem.at[19])
    def put(src, dst):
        c_ = pltpu.make_async_copy(src, dst, lsem.at[len(loc)]); c_.start(); loc.append(c_)
    for j, t in enumerate((0, 1, 2)): put(sp.at[j], own.at[t])
    put(so, own.at[3])
    for j, t in ((1, 4), (2, 5), (0, 6)): put(cp.at[j], own.at[t])
    put(co, own.at[7])
    put(ai, own.at[8, :, pl.ds(0, 512)])
    put(ao.at[:, pl.ds(0, 512)], own.at[8, pl.ds(0, 16), pl.ds(512, 512)])
    put(ao.at[:, pl.ds(512, 512)], own.at[8, pl.ds(16, 16), pl.ds(512, 512)])
    for j in range(4): put(fi.at[:, pl.ds(1024 * j, 1024)], own.at[9 + j])
    put(fo, ownf)
    me = p.x * 2 + p.c
    put(en.at[0, me], ctx.at[:, me])
    x_in.start()
    n_in = len(loc)
    c1 = pltpu.make_async_copy(own, buf.at[:, p.z, p.y, p.x, p.c], lsem.at[n_in])
    c2 = pltpu.make_async_copy(ownf, gfo.at[p.z, p.y, p.x, p.c], lsem.at[n_in + 1])
    def staged():
        for c_ in loc: c_.wait()
        c1.start(); c2.start()
    neighbours_in()
    streams = []
    for t in range(17):
        R = 32 if t < 13 else 128
        i = t % 3
        rows = [(0, R // 2, "zxy"), (R // 2, R // 2, "zyx")] if i == 0 else [(0, R, "xzy" if i == 1 else "yzx")]
        if t == 16: rows = [(0, 96, "xzy"), (96, 32, "yzx")]
        for r0, nr, order in rows:
            n = len(streams)
            if t < 13:
                arg = {0: sp.at[0], 1: sp.at[1], 2: sp.at[2], 3: so, 4: cp.at[1], 5: cp.at[2], 6: cp.at[0], 7: co, 8: own.at[8]}.get(t)
                mine = fi.at[pl.ds(r0, nr), pl.ds(1024 * (t - 9), 1024)] if t > 8 else arg.at[pl.ds(r0, nr)]
                view = lambda z, y_, x_, c, t=t, r0=r0, nr=nr: buf.at[t, z, y_, x_, c, pl.ds(r0, nr)]
            else:
                mine = fo.at[pl.ds(r0, nr), pl.ds(256 * (t - 13), 256)]
                view = lambda z, y_, x_, c, j=t - 13, r0=r0, nr=nr: gfo.at[z, y_, x_, c, pl.ds(r0, nr), pl.ds(256 * j, 256)]
            streams.append(Stream(p, mine, view, order, ssem.at[n], rsem.at[n]))
    ends = (p.z == 0) | (p.z == 3)
    guards = [ends, jnp.logical_not(ends)]

    def fetch(t):
        if t < 13: return pltpu.make_async_copy(buf.at[t], wbuf.at[t % 4], wsem.at[t])
        j = t - 13
        return pltpu.make_async_copy(gfo.at[:, :, :, :, :, pl.ds(256 * j, 256)], wo.at[j % 2], wsem.at[t])
    def start(t): return lambda: fetch(t).start()
    outs = []
    def keep(src, dst):
        c_ = pltpu.make_async_copy(src, dst, osem.at[len(outs)]); c_.start(); outs.append(c_)
    lo, hi = half_masks()

    def mm(lhs, t, fn):
        fn(dot(lhs[...], wbuf[t % 4].reshape(1024, 1024)))

    def proj(lhs, t, slot):
        def run():
            fetch(t).wait()
            def st(v): qkv[slot] = v.astype(BF)
            mm(lhs, t, st)
            keep(qkv.at[slot], o_qkv.at[slot])
        return run

    def flip(src, slot):
        def run():
            if slot == 0: x_in.wait()
            @pl.loop(0, 4)
            def _(n):
                T[slot, cols(n, 256), :] = src[:, cols(n, 256)].T
            keep(T.at[slot], o_t.at[slot])
        return run

    def attend(a, part):
        def run():
            u = part // 2
            @pl.loop(0, 4, unroll=4)
            def _(n):
                pr = (part % 2) * 4 + n
                r, cc = pl.ds(u * 128, 128), cols(pr, 128)
                q, k, v = (qkv[3 * a + j, r, cc] for j in range(3))
                b = bias[a, u]
                s = dot_nt(pair_up(q, lo, hi), k) * 0.125 + jnp.concatenate([b, b], axis=0)
                e = jnp.exp(s - jnp.max(s, axis=-1, keepdims=True))
                pr_ = e / jnp.sum(e, axis=-1, keepdims=True)
                P[a, u * 8 + pr] = pr_
                mix[r, cc] = dot(side(pr_.astype(BF)), pair_up(v, lo, hi)).astype(BF)
            if part == 3: keep(P.at[a], o_p.at[a])
        return run

    def branch(t, base, slot):
        def run():
            fetch(t).wait()
            def st(v): H[slot] = base[...].astype(F32) + v
            mm(mix, t, st)
        return run

    def norm(slot):
        def run():
            keep(H.at[slot], o_h.at[slot])
            @pl.loop(0, 4)
            def _(n):
                r = pl.ds(pl.multiple_of(n * 64, 64), 64)
                v = norm_rows(H[slot, r, :]) * gains[slot, :][None]
                if slot < 2:
                    y[r, :] = v
                    yl[r, :] = v.astype(BF)
                else:
                    OUT[r, :] = v.astype(BF)
            if slot == 2: keep(OUT, o_out)
        return run

    cs = []
    def context_out():
        for k, (dx, dc) in enumerate(((0, 1), (1, 0), (1, 1))):
            tx = (p.x + dx) % 2; tc = (p.c + dc) % 2
            c_ = pltpu.make_async_remote_copy(en.at[0, tx * 2 + tc], ctx.at[:, me], csem.at[k], crsem.at[me], device_id=p.dev(x=tx, c=tc), device_id_type=MESH)
            c_.start(); cs.append(c_)
    def context_in():
        for k, (dx, dc) in enumerate(((0, 1), (1, 0), (1, 1))):
            tx = (p.x + dx) % 2; tc = (p.c + dc) % 2
            w = tx * 2 + tc
            pltpu.make_async_remote_copy(en.at[0, w], ctx.at[:, w], csem.at[k], crsem.at[w], device_id=p.dev(), device_id_type=MESH).wait_recv()

    class Ctx:
        def __getitem__(self, idx):
            if idx is Ellipsis: return ctx[...].reshape(256, 1024)
            return ctx[:, :, :, idx[1]].reshape(256, -1)
    cref = Ctx()
    def adapter():
        fetch(8).wait()
        w = wbuf[0, :, :, :, :, :, pl.ds(0, 512)].reshape(1024, 512)
        r = dot(yl[...], w)
        s = 1.0 / (1.0 + jnp.exp(-r))
        a = (r * s).astype(BF)
        ar[...] = a
        SR[...] = s * (1.0 + r * (1.0 - s))
        AT[...] = a.T
        keep(SR, o_sr); keep(AT, o_at)
    def adapter_out():
        top = wbuf[0, :, :, :, :, pl.ds(0, 16), pl.ds(512, 512)].reshape(512, 512)
        bot = wbuf[0, :, :, :, :, pl.ds(16, 16), pl.ds(512, 512)].reshape(512, 512)
        H[2, :, 0:512] = y[:, 0:512] + 4.0 * dot(ar[...], top)
        H[2, :, 512:1024] = y[:, 512:1024] + 4.0 * dot(ar[...], bot)
    def hidden(j):
        def run():
            t = 9 + j
            fetch(t).wait()
            @pl.loop(0, 4)
            def _(n):
                ds = cols(n, 256)
                u = dot(yl[...], wbuf[t % 4, :, :, :, :, :, ds].reshape(1024, 256))
                half = 0.5 + 0.5 * lax.erf(u * 0.7071067811865476)
                af[j, :, ds] = (u * half).astype(BF)
                GP[j, :, ds] = half + u * (0.3989422804014327 * jnp.exp(-0.5 * u * u))
            keep(GP.at[j], o_gp.at[j])
        return run
    def out_cols(j):
        def run():
            fetch(13 + j).wait()
            acc = H[2, :, pl.ds(256 * j, 256)]
            for f in range(4):
                w = wo[j % 2, f].reshape(1024, 256)
                acc = acc + dot(af[f], w)
            H[2, :, pl.ds(256 * j, 256)] = acc
        return run

    def masks():
        row = lax.broadcasted_iota(jnp.int32, (128, 128), 0)
        col = lax.broadcasted_iota(jnp.int32, (128, 128), 1)
        for u in range(2):
            wide = lambda ref, j: jnp.broadcast_to(ref[u:u + 1, j:j + 1], (128, 128))
            paired = wide(dlen, 1) > 0
            far = jnp.where(paired, 64, 128)
            second = col >= far
            place = jnp.where(second, col - 64, col)
            same = (row >= far) == second
            dec = jnp.where(second, wide(dlen, 1), wide(dlen, 0))
            enc = jnp.where(second, wide(elen, 1), wide(elen, 0))
            bias[0, u] = jnp.where(same & (col <= row) & (place < dec), 0.0, -1e30)
            bias[1, u] = jnp.where(same & (place < enc), 0.0, -1e30)

    compute = {}
    for t in range(17): compute[f"w{t}"] = start(t)
    compute["masks"] = masks
    compute["staged"] = staged
    compute["own"] = lambda: (c1.wait(), c2.wait())
    for k, src in ((0, x), (1, cref), (2, yl), (3, mix), (4, mix), (5, yl)): compute[f"flip{k}"] = flip(src, k)
    for t, lhs, slot in ((0, x, 0), (1, x, 1), (2, x, 2), (4, cref, 4), (5, cref, 5), (6, yl, 3)): compute[f"proj{t}"] = proj(lhs, t, slot)
    for a in range(2):
        for part in range(4): compute[f"at{a}{part}"] = attend(a, part)
    compute.update(branch3=branch(3, x, 0), branch7=branch(7, y, 1), norm0=norm(0), norm1=norm(1), norm2=norm(2),
                   ctxsend=context_out, ctxin=context_in, adapter=adapter, adapter_out=adapter_out)
    for j in range(4): compute.update({f"hid{j}": hidden(j), f"out{j}": out_cols(j)})
    run_plan(PLAN_F, compute, streams, guards)
    for k in range(2):
        @pl.when(guards[k])
        def _():
            for s in streams: s.finish(k)
    for c_ in cs: c_.wait_send()
    for c_ in outs: c_.wait()

def forward(tokens, gains, dec_lengths, enc_lengths, shards, encoder):
    any_ = pl.BlockSpec(memory_space=pl.ANY)
    vm = pl.BlockSpec(memory_space=pltpu.VMEM)
    V, S, D = pltpu.VMEM, jax.ShapeDtypeStruct, pltpu.SemaphoreType.DMA
    tile = (4, 2, 2, 2, 32, 1024)
    return pl.pallas_call(forward_kernel,
        out_shape=(S((13,) + tile, BF), S((4, 2, 2, 2, 128, 1024), BF), S((6, 256, 1024), BF), S((2, 16, 256, 128), F32), S((3, 256, 1024), F32),
                   S((6, 1024, 256), BF), S((512, 256), BF), S((4, 256, 1024), F32), S((256, 512), F32), S((256, 1024), BF)),
        in_specs=[any_] + [vm] * 3 + [any_] * 9, out_specs=(any_,) * 10,
        scratch_shapes=[V((6, 256, 1024), BF), V((2, 16, 256, 128), F32), V((3, 256, 1024), F32), V((6, 1024, 256), BF), V((512, 256), BF),
                        V((4, 256, 1024), F32), V((256, 512), F32), V((256, 1024), BF), V((2, 4, 32, 1024), BF), V((4,) + tile, BF),
                        V((2, 4, 2, 2, 2, 128, 256), BF), V((13, 32, 1024), BF), V((128, 1024), BF), V((256, 1024), F32), V((256, 1024), BF),
                        V((256, 1024), BF), V((4, 256, 1024), BF), V((256, 512), BF), V((2, 2, 128, 128), F32), V((256, 1024), BF),
                        D((N_STREAM, NSEND)), D((N_STREAM, NSLOT)), D((20,)), D((3,)), D((4,)), D((17,)), D((26,))],
        compiler_params=pltpu.CompilerParams(collective_id=0, has_side_effects=True, vmem_limit_bytes=60 << 20),
        name="forward")(tokens, gains, dec_lengths, enc_lengths, *shards, encoder)

ORDERS = ["A", "yzx", "xzy", "xzy", "yzx", "A", "xzy", "yzx", "A"]
PLAN_B = [
    "nb0", "hb0", "hb1", "hb2", "hb3", "adb", "adg.0", "adg.1", "adg.2", "adg.3", "hi0", (0, "R1", 0, None), (0, "R1", 1, None), "hi1",
    (0, "R1", 2, None), (0, "R1", 3, None), "hi2", "hi3", "nb1", (0, "R2", 0, None), "t1.0", (0, "R2", 1, None), "t1.1", "t1.2", "t1.3", "mb9",
    (0, "R2", 2, None), (1, "R1", 0, None), "at10", (0, "R2", 3, None), (0, "R3", 0, None), (0, "U", 3, 0), (0, "D", 0, 3), (1, "R1", 1, None),
    (1, "R1", 2, None), (1, "R1", 3, None), "at11", (0, "R3", 1, None), (0, "R3", 2, None), (0, "D", 1, 3), (0, "U", 2, 0), "at12", (0, "D", 2, 3),
    (0, "U", 1, 0), "at13", (0, "U", 3, 1), (0, "D", 0, 2), (1, "R2", 0, None), "t2.0", (1, "D", 0, 3), (1, "U", 3, 0), "t2.1", (0, "R3", 3, None),
    "t2.2", (0, "D", 1, 2), (0, "U", 2, 1), "t2.3", "t3.0", "t3.1", "t3.2", (2, "R1", 0, None), "t3.3", "t4.0", (2, "R1", 1, None), "t4.1", "t4.2",
    (2, "R1", 2, None), (0, "D", 0, 1), (0, "U", 3, 2), (1, "R2", 1, None), (1, "U", 2, 0), (1, "D", 1, 3), "t4.3", (2, "R1", 3, None), "rb10",
    (0, "FIN", 0, 1), (0, "FIN", 0, 2), (3, "R1", 0, None), (1, "D", 0, 2), (1, "U", 3, 1), "cb", (3, "R1", 1, None), (3, "R1", 2, None),
    (1, "R2", 2, None), (1, "D", 2, 3), (1, "U", 1, 0), (3, "R1", 3, None), "rb12", (2, "R2", 0, None), (4, "R1", 0, None), (0, "FIN", 0, 0),
    (0, "FIN", 0, 3), (2, "D", 0, 3), (2, "U", 3, 0), (4, "R1", 1, None), "nb2", (4, "R1", 2, None), (1, "R2", 3, None), (1, "D", 1, 2),
    (1, "U", 2, 1), (2, "R2", 1, None), (2, "D", 1, 3), (2, "U", 2, 0), (1, "U", 3, 2), (1, "D", 0, 1), (4, "R1", 3, None), "t5.0", "t5.1", "t5.2",
    "t5.3", "mb13", "at00", (2, "R2", 2, None), (2, "D", 2, 3), (2, "U", 1, 0), (5, "R1", 0, None), (5, "R1", 1, None), (5, "R1", 2, None),
    (5, "R1", 3, None), "at01", (2, "U", 3, 1), (2, "D", 0, 2), (1, "Z3", 0, 0), (1, "Z3", 0, 3), (1, "Z3", 0, 2), (1, "Z3", 0, 1), "at02",
    (2, "R2", 3, None), "at03", (2, "D", 1, 2), (2, "U", 2, 1), (4, "R2", 0, None), (4, "U", 3, 0), (4, "D", 0, 3), (3, "R2", 0, None), (3, "U", 3, 0),
    (3, "D", 0, 3), "cs", "t6.0", "t6.1", (2, "D", 0, 1), (2, "U", 3, 2), "t6.2", "t6.3", "t7.0", "t7.1", "t7.2", (6, "R1", 0, None), "t7.3",
    (4, "R2", 1, None), (4, "D", 1, 3), (4, "U", 2, 0), "t8.0", (6, "R1", 1, None), (3, "R2", 1, None), "t8.1", (3, "D", 1, 3), (3, "U", 2, 0),
    (6, "R1", 2, None), "t8.2", (2, "Z3", 0, 2), (2, "Z3", 0, 1), "t8.3", (6, "R1", 3, None), "rb14", (7, "R1", 0, None), (4, "U", 3, 1),
    (4, "D", 0, 2), "rb15", (4, "R2", 2, None), (2, "Z3", 0, 0), (2, "Z3", 0, 3), (7, "R1", 1, None), (4, "D", 2, 3), (4, "U", 1, 0),
    (3, "R2", 2, None), (3, "D", 2, 3), (3, "U", 1, 0), (7, "R1", 2, None), (7, "R1", 3, None), "tok", (8, "R1", 0, None), (3, "D", 0, 2),
    (3, "U", 3, 1), (8, "R1", 1, None), (4, "R2", 3, None), (8, "R1", 2, None), (3, "R2", 3, None), (8, "R1", 3, None), (4, "D", 0, 1), (4, "U", 3, 2),
    (5, "R2", 0, None), (4, "D", 1, 2), (4, "U", 2, 1), (5, "R2", 1, None), (3, "D", 0, 1), (3, "U", 3, 2), (5, "R2", 2, None), (3, "D", 1, 2),
    (3, "U", 2, 1), (5, "R2", 3, None), (4, "Z3", 0, 0), (4, "Z3", 0, 3), (2, "FIN", 0, 2), (2, "FIN", 0, 1), (1, "FIN", 0, 2), (1, "FIN", 0, 1),
    (1, "FIN", 0, 0), (1, "FIN", 0, 3), (7, "R2", 0, None), (7, "U", 3, 0), (7, "D", 0, 3), (3, "Z3", 0, 3), (3, "Z3", 0, 0), (2, "FIN", 0, 0),
    (2, "FIN", 0, 3), (3, "Z3", 0, 2), (3, "Z3", 0, 1), (6, "R2", 0, None), (6, "U", 3, 0), (6, "D", 0, 3), (4, "Z3", 0, 2), (4, "Z3", 0, 1),
    (7, "R2", 1, None), (7, "D", 1, 3), (7, "U", 2, 0), (6, "R2", 1, None), (6, "U", 2, 0), (6, "D", 1, 3), (7, "U", 3, 1), (7, "D", 0, 2),
    (7, "R2", 2, None), (7, "D", 2, 3), (7, "U", 1, 0), (6, "R2", 2, None), (6, "U", 1, 0), (6, "D", 2, 3), (6, "D", 0, 2), (6, "U", 3, 1),
    (7, "R2", 3, None), (7, "D", 0, 1), (7, "U", 3, 2), (6, "R2", 3, None), (7, "D", 1, 2), (7, "U", 2, 1), (8, "R2", 0, None), (6, "U", 3, 2),
    (6, "D", 0, 1), (8, "R2", 1, None), (6, "D", 1, 2), (6, "U", 2, 1), (7, "Z3", 0, 0), (7, "Z3", 0, 3), (8, "R2", 2, None), (8, "R2", 3, None),
    (7, "Z3", 0, 1), (7, "Z3", 0, 2), (5, "R3", 0, None), (5, "D", 0, 3), (5, "U", 3, 0), (6, "Z3", 0, 0), (6, "Z3", 0, 3), (5, "R3", 1, None),
    (5, "D", 1, 3), (5, "U", 2, 0), (5, "R3", 2, None), (5, "U", 1, 0), (5, "D", 2, 3), (5, "R3", 3, None), (6, "Z3", 0, 2), (6, "Z3", 0, 1),
    (3, "FIN", 0, 1), (3, "FIN", 0, 0), (3, "FIN", 0, 3), (3, "FIN", 0, 2), (4, "FIN", 0, 1), (4, "FIN", 0, 2), (4, "FIN", 0, 0), (4, "FIN", 0, 3),
    (5, "U", 3, 1), (5, "D", 0, 2), (8, "R3", 0, None), (8, "U", 3, 0), (8, "D", 0, 3), (8, "R3", 1, None), (8, "U", 2, 0), (8, "D", 1, 3),
    (5, "U", 2, 1), (5, "D", 1, 2), (8, "R3", 2, None), (7, "FIN", 0, 0), (7, "FIN", 0, 3), (8, "R3", 3, None), (5, "U", 3, 2), (5, "D", 0, 1),
    (8, "D", 2, 3), (8, "U", 1, 0), (6, "FIN", 0, 0), (6, "FIN", 0, 3), (6, "FIN", 0, 2), (6, "FIN", 0, 1), (7, "FIN", 0, 2), (7, "FIN", 0, 1),
    (8, "D", 0, 2), (8, "U", 3, 1), (5, "FIN", 0, 1), (5, "FIN", 0, 2), (8, "D", 1, 2), (8, "U", 2, 1), (5, "FIN", 0, 0), (5, "FIN", 0, 3),
    (8, "D", 0, 1), (8, "U", 3, 2), (8, "FIN", 0, 2), (8, "FIN", 0, 1), (8, "FIN", 0, 0), (8, "FIN", 0, 3),
]


NT = 9
NS, NR = 27, 33

class Reduce:
    def __init__(self, p, t, order, PB, L0, L1, L2, UP, DN, LX, ssem, rsem, out):
        self.p, self.t, self.order = p, t, order
        self.PB, self.L0, self.L1, self.L2, self.UP, self.DN, self.LX = PB, L0, L1, L2, UP, DN, LX
        self.ssem, self.rsem, self.out = ssem, rsem, out
        self.sends = []
        self.me = {"x": p.x, "y": p.y}
        self.flat = order == "A"
        if not self.flat: self.b1, self.b2 = order[0], order[2]
    def partner(self, b):
        return self.p.dev(**{b: 1 - self.me[b]})
    def desc(self, src, dst, k, slot, target):
        return pltpu.make_async_remote_copy(src, dst, self.ssem.at[k], self.rsem.at[slot], device_id=target, device_id_type=MESH)
    def copy(self, what, k, slot, z=None):
        def make():
            src, dst, target = what()
            return self.desc(src, dst, k, slot, target)
        make().start()
        self.sends.append((make, z))
    def arrive(self, dst, slot):
        self.desc(dst, dst, 0, slot, self.p.dev()).wait_recv()
    def finish(self, z):
        for make, at in self.sends:
            if at == z: make().wait_send()
    def height(self, k):
        return jnp.where(self.p.z < 2, 3 - k, k)
    def sib(self, k):
        zz = self.height(k)
        self.copy(lambda: (self.PB.at[zz, :, :, 1 - self.p.c], self.L0.at[zz], self.p.dev(c=1 - self.p.c)), k, zz)
    def pair(self, zz, b2name, b2v, r=pl.ds(0, 32)):
        if b2name == "y": return self.PB.at[zz, b2v, :, self.p.c, r]
        return self.PB.at[zz, :, b2v, self.p.c, r]
    def block(self, zz, r=pl.ds(0, 32), **where):
        return self.PB.at[zz, where.get("y", self.p.y), where.get("x", self.p.x), self.p.c, r]
    def mine(self, zz):
        return self.block(zz) if self.flat else self.pair(zz, self.b2, self.me[self.b2])
    def halves(self):
        return [(h, b1, b2, pl.ds(16 * h, 16)) for h, (b1, b2) in enumerate((("x", "y"), ("y", "x")))]

    def R1(self, k):
        p, zz = self.p, self.height(k)
        self.arrive(self.L0.at[zz], zz)
        for yy in range(2):
            for xx in range(2):
                self.PB[zz, yy, xx, p.c] = self.PB[zz, yy, xx, p.c] + self.L0[zz, yy, xx]
        if self.flat:
            for h, b1, b2, r in self.halves():
                self.copy(lambda b2=b2, r=r: (self.pair(zz, b2, 1 - self.me[b2], r), self.L1.at[zz, :, r], self.partner(b2)), 4 + 4 * h + k, 17 + 4 * h + zz)
        else:
            self.copy(lambda: (self.pair(zz, self.b2, 1 - self.me[self.b2]), self.L1.at[zz], self.partner(self.b2)), 4 + k, 4 + zz)
    def R2(self, k):
        zz = self.height(k)
        if self.flat:
            for h, b1, b2, r in self.halves():
                self.arrive(self.L1.at[zz, :, r], 17 + 4 * h + zz)
                o = self.pair(zz, b2, self.me[b2], r)
                o[...] = o[...] + self.L1[zz, :, r]
                self.copy(lambda b1=b1, r=r: (self.block(zz, r, **{b1: 1 - self.me[b1]}), self.L2.at[zz, r], self.partner(b1)), 12 + 4 * h + k, 25 + 4 * h + zz)
        else:
            self.arrive(self.L1.at[zz], 4 + zz)
            o = self.mine(zz)
            o[...] = o[...] + self.L1[zz]
    def R3(self, k):
        zz = self.height(k)
        for h, b1, b2, r in self.halves():
            self.arrive(self.L2.at[zz, r], 25 + 4 * h + zz)
            o = self.block(zz, r)
            o[...] = o[...] + self.L2[zz, r]
    def U(self, zu, z):
        o, land = self.mine(zu), self.UP.at[zu - 1]
        if 0 < z <= zu:
            self.arrive(land, 8 + zu)
            o[...] = o[...] + land[...]
        if z < zu: self.copy(lambda: (self.mine(zu), self.UP.at[zu - 1], self.p.dev(z=z + 1)), 20 + zu - 1, 8 + zu, z)
    def D(self, zd, z):
        o, land = self.mine(zd), self.DN.at[zd]
        if zd <= z < 3:
            self.arrive(land, 12 + zd)
            o[...] = o[...] + land[...]
        if z > zd: self.copy(lambda: (self.mine(zd), self.DN.at[zd], self.p.dev(z=z - 1)), 23 + zd, 12 + zd, z)
    def Z3(self, k, z):
        if z > 0: self.U(z, z)
        if z < 3: self.D(z, z)
        self.copy(lambda: (self.block(z, **{self.b1: 1 - self.me[self.b1]}), self.LX, self.partner(self.b1)), 26, 16, z)
    def FIN(self, k, z):
        v = self.block(z)
        if self.flat:
            if z > 0: self.U(z, z)
            if z < 3: self.D(z, z)
            self.out(v[...].astype(F32))
        else:
            self.arrive(self.LX, 16)
            self.out(v[...].astype(F32) + self.LX[...].astype(F32))

W_ORDER = ["o0", "o1", "o2", "o3", 8, 9, 10, 11, 12, 7, 4, 5, 6, 3, 0, 1, 2]
T_ORDER = [5, 4, 1, 2, 3, 0]
NW = 3

def backward_kernel(gains, buf, gfo, qkv, P, H, T, AT, GP, SR, cot,
                    o_tok, osp, oso, ocp, oco, oai, oao, oen,
                    PB, L0, L1, L2, UPC, DNC, UPA, DNA, LX, wbuf, hb, gpb, tb, atb, srb, pb, cotb, g, gb, gr, gx, gqkv, gtok, vsp, vso, vcp, vco, vai, vao, fsem,
                    ssem, rsem, csem, crsem, wsem, hsem, gpsem, tsem, msem, qsem, psem, osem):
    p = Place()
    neighbours_in = entry_barrier(p)
    lo, hi = half_masks()
    def w_copy(i):
        n = W_ORDER[i]
        src = gfo.at[int(n[1])] if isinstance(n, str) else buf.at[n]
        return pltpu.make_async_copy(src, wbuf.at[i % NW], wsem.at[i])
    h_copy = lambda i: pltpu.make_async_copy(H.at[2 - i], hb.at[i % 2], hsem.at[i])
    gp_copy = lambda j: pltpu.make_async_copy(GP.at[j], gpb.at[j % 2], gpsem.at[j])
    t_copy = lambda i: pltpu.make_async_copy(T.at[T_ORDER[i]], tb.at[i % 3], tsem.at[i])
    q_copy = lambda a, j: pltpu.make_async_copy(qkv.at[3 * a + j], PB.at[6 + a, j], qsem.at[3 * a + j])
    p_copy = lambda a: pltpu.make_async_copy(P.at[a], pb, psem.at[a])
    m_copy = [pltpu.make_async_copy(cot, cotb, msem.at[0]), pltpu.make_async_copy(SR, srb, msem.at[1]), pltpu.make_async_copy(AT, atb, msem.at[2])]
    h_copy(0).start(); m_copy[0].start(); w_copy(0).start(); gp_copy(0).start(); w_copy(1).start(); gp_copy(1).start(); w_copy(2).start()
    def later(at):
        if at == "hb1": m_copy[1].start(); m_copy[2].start(); t_copy(0).start()
        if at == "hb3": h_copy(1).start()
        if at == "hi1":
            for i in (1, 2): t_copy(i).start()
            for j in range(3): q_copy(1, j).start()
        if at == "hi3":
            p_copy(1).start()
            for j in range(3): q_copy(0, j).start()

    def out_copy(held, ref, n): return pltpu.make_async_copy(held, ref, fsem.at[n])
    written = []
    def o_ad(v):
        vai[...] = v[:, :512]
        vao[:, 0:512] = v[0:16, 512:]
        vao[:, 512:1024] = v[16:32, 512:]
        out_copy(vai, oai, 0).start()
        out_copy(vao, oao, 1).start()
    def put(held, ref, n, j=None):
        written.append((held, ref, n, j))
        def f(v):
            if j is None:
                held[...] = v
                out_copy(held, ref, n).start()
            else:
                held[j] = v
                out_copy(held.at[j], ref.at[j], n).start()
        return f
    finals = [o_ad, put(vco, oco, 2), put(vcp, ocp, 3, 1), put(vcp, ocp, 4, 2), put(vcp, ocp, 5, 0), put(vso, oso, 6), put(vsp, osp, 7, 1), put(vsp, osp, 8, 2), put(vsp, osp, 9, 0)]
    reds = []
    nc = na = 0
    for t in range(NT):
        if ORDERS[t] == "A":
            up, dn, l2 = UPA.at[na], DNA.at[na], L2.at[na]; na += 1
        else:
            up, dn, l2 = UPC.at[nc], DNC.at[nc], None; nc += 1
        reds.append(Reduce(p, t, ORDERS[t], PB.at[t], L0.at[t], L1.at[t], l2, up, dn, LX.at[t], ssem.at[t], rsem.at[t], finals[t]))

    compute = {}
    def work(name, fn): compute[name] = fn

    def norm_back(i, first=False):
        def run():
            h_copy(i).wait()
            if first: m_copy[0].wait()
            @pl.loop(0, 4)
            def _(n):
                r = pl.ds(pl.multiple_of(n * 64, 64), 64)
                h = hb[i % 2, r, :]
                center = h - jnp.mean(h, axis=-1, keepdims=True)
                inv = lax.rsqrt(jnp.mean(center * center, axis=-1, keepdims=True) + EPS)
                nrm = center * inv
                gy = cotb[r, :].astype(F32) if first else g[r, :]
                a = gy * gains[2 - i, :][None]
                v = (a - jnp.mean(a, axis=-1, keepdims=True) - nrm * jnp.mean(a * nrm, axis=-1, keepdims=True)) * inv
                g[r, :] = v
                gb[r, :] = v.astype(BF)
            if i == 0: h_copy(2).start()
        return run

    def used(i):
        if i + NW < len(W_ORDER): w_copy(i + NW).start()

    def nt(lhs, i, fn):
        fn(dot_nt(lhs(), wbuf[i % NW]))

    def hidden_back(j):
        def run():
            w_copy(j).wait(); gp_copy(j).wait()
            def st(v):
                PB[8, j] = (gpb[j % 2] * v).astype(BF).reshape(2, 2, 2, 32, 1024)
            nt(lambda: gb[...], j, st)
            used(j)
            if j + 2 < 4: gp_copy(j + 2).start()
            later(f"hb{j}")
        return run

    def adapter_back():
        i = 4
        w_copy(i).wait(); m_copy[1].wait(); m_copy[2].wait()
        v = wbuf[i % NW, :, 512:1024].reshape(32, 32, 512)
        top, bot = v[:, :16].reshape(512, 512), v[:, 16:].reshape(512, 512)
        s = dot_nt(gb[:, 0:512], top) + dot_nt(gb[:, 512:1024], bot)
        gr[...] = (srb[...] * (4.0 * s)).astype(BF)
        wai = wbuf[i % NW, :, 0:512]
        g[...] = g[...] + dot_nt(gr[...], wai)
        used(i)

    def rows_of(k):
        return pl.ds(pl.multiple_of(reds[0].height(k) * 256, 256), 256)
    def adapter_grads(k):
        def run():
            if k == 0:
                neighbours_in()
                for h in range(2):
                    v = 4.0 * dot(atb[...], gb[:, 512 * h:512 * h + 512])
                    PB[0, :, :, :, :, 16 * h:16 * h + 16, 512:1024] = v.astype(BF).reshape(4, 2, 2, 2, 16, 512)
                t_copy(0).wait()
            v = dot(tb[0, rows_of(k), :], gr[...])
            PB[0, reds[0].height(k), :, :, :, :, 0:512] = v.astype(BF).reshape(2, 2, 2, 32, 512)
            reds[0].sib(k)
            if k == 3: t_copy(3).start()
        return run

    def hidden_in_back(j):
        def run():
            i = 5 + j
            w_copy(i).wait()
            def st(v): g[...] = g[...] + v
            nt(lambda: PB[8, j].reshape(256, 1024), i, st)
            used(i)
            later(f"hi{j}")
        return run

    def grad_tile(t, ti, rhs, last, k):
        def run():
            if k == 0 and t in (1, 2, 4, 5, 6): t_copy(ti).wait()
            PB[t, reds[t].height(k)] = dot(tb[ti % 3, rows_of(k), :], rhs()).astype(BF).reshape(2, 2, 2, 32, 1024)
            reds[t].sib(k)
            if k == 3 and last and ti + 3 < 6: t_copy(ti + 3).start()
        return run

    def mix_back(i):
        def run():
            w_copy(i).wait()
            def st(v): gx[...] = v.astype(BF)
            nt(lambda: gb[...], i, st)
            used(i)
        return run

    def attend_back(a, part):
        def run():
            if part == 0:
                p_copy(a).wait()
                for j in range(3): q_copy(a, j).wait()
            u = part // 2
            @pl.loop(0, 4, unroll=4)
            def _(n):
                pr = (part % 2) * 4 + n
                r, cc = pl.ds(u * 128, 128), cols(pr, 128)
                q, k, v = (PB[6 + a, j, u, :, :, :, cc].reshape(128, 128) for j in range(3))
                go = pair_up(gx[r, cc], lo, hi)
                prob = pb[u * 8 + pr]
                dp = dot_nt(go, v)
                ds = (prob * (dp - jnp.sum(prob * dp, axis=-1, keepdims=True))).astype(BF)
                gqkv[0, r, cc] = (dot(side(ds), pair_up(k, lo, hi)) * 0.125).astype(BF)
                gqkv[1, r, cc] = (dot_tn(ds, pair_up(q, lo, hi)) * 0.125).astype(BF)
                gqkv[2, r, cc] = dot_tn(prob.astype(BF), go).astype(BF)
            if part == 3 and a == 1: p_copy(0).start()
        return run

    def row_back(i, j, dst):
        def run():
            w_copy(i).wait()
            nt(lambda: gqkv[j], i, dst)
            used(i)
        return run
    def to_g(v): g[...] = g[...] + v
    cs = []
    me = p.x * 2 + p.c
    def context_back():
        i = 11
        w_copy(i).wait()
        def st(v): PB[8, 0] = (ctxf[...] + v).astype(BF).reshape(2, 2, 2, 32, 1024)
        nt(lambda: gqkv[2], i, st)
        used(i)
        for k, (dx, dc) in enumerate(((0, 1), (1, 0), (1, 1))):
            tx = (p.x + dx) % 2; tc = (p.c + dc) % 2
            c_ = pltpu.make_async_remote_copy(PB.at[8, 0, :, tx, tc], oen.at[0, me], csem.at[k], crsem.at[me], device_id=p.dev(x=tx, c=tc), device_id_type=MESH)
            c_.start(); cs.append(c_)
        c_ = pltpu.make_async_copy(PB.at[8, 0, :, p.x, p.c], oen.at[0, me], osem.at[0]); c_.start(); cs.append(c_)

    ctxf = gpb.at[0]
    def ctx_part(v): ctxf[...] = v
    def context_sent():
        for c_ in cs[:3]: c_.wait_send()
        cs[3].wait()
    def tokens_back():
        i = 16
        w_copy(i).wait()
        def st(v): gtok[...] = (g[...] + v).astype(BF)
        nt(lambda: gqkv[2], i, st)
        pltpu.make_async_copy(gtok, o_tok, osem.at[1]).start()

    def tile(t, ti, rhs, last):
        for zz in range(4): work(f"t{t}.{zz}", grad_tile(t, ti, rhs, last, zz))
    work("nb0", norm_back(0, True))
    for j in range(4): work(f"hb{j}", hidden_back(j))
    work("adb", adapter_back)
    for zz in range(4): work(f"adg.{zz}", adapter_grads(zz))
    for j in range(4): work(f"hi{j}", hidden_in_back(j))
    work("nb1", norm_back(1))
    tile(1, 1, lambda: gb[...], True)
    work("mb9", mix_back(9))
    for part in range(4): work(f"at1{part}", attend_back(1, part))
    tile(2, 2, lambda: gqkv[1], False)
    tile(3, 2, lambda: gqkv[2], True)
    tile(4, 3, lambda: gqkv[0], True)
    work("rb10", row_back(10, 1, ctx_part))
    work("cb", context_back)
    work("rb12", row_back(12, 0, to_g))
    work("nb2", norm_back(2))
    tile(5, 4, lambda: gb[...], True)
    work("mb13", mix_back(13))
    for part in range(4): work(f"at0{part}", attend_back(0, part))
    work("cs", context_sent)
    tile(6, 5, lambda: gqkv[1], False)
    tile(7, 5, lambda: gqkv[2], False)
    tile(8, 5, lambda: gqkv[0], True)
    work("rb14", row_back(14, 0, to_g))
    work("rb15", row_back(15, 1, to_g))
    work("tok", tokens_back)
    run_plan(PLAN_B, compute, reds, [p.z == z for z in range(4)])
    for r in reds: r.finish(None)
    for z in range(4):
        @pl.when(p.z == z)
        def _():
            for r in reds: r.finish(z)
    pltpu.make_async_copy(gtok, o_tok, osem.at[1]).wait()
    out_copy(vai, oai, 0).wait()
    out_copy(vao, oao, 1).wait()
    for held, ref, n, j in written:
        if j is None: out_copy(held, ref, n).wait()
        else: out_copy(held.at[j], ref.at[j], n).wait()
    for k, (dx, dc) in enumerate(((0, 1), (1, 0), (1, 1))):
        tx = (p.x + dx) % 2; tc = (p.c + dc) % 2
        w = tx * 2 + tc
        pltpu.make_async_remote_copy(PB.at[8, 0, :, tx, tc], oen.at[0, w], csem.at[k], crsem.at[w], device_id=p.dev(), device_id_type=MESH).wait_recv()

def backward(gains, buf, gfo, qkv, P, H, T, AT, GP, SR, cot):
    any_ = pl.BlockSpec(memory_space=pl.ANY)
    vm = pl.BlockSpec(memory_space=pltpu.VMEM)
    V, S, D = pltpu.VMEM, jax.ShapeDtypeStruct, pltpu.SemaphoreType.DMA
    ops = (gains, buf.reshape(13, 1024, 1024), gfo.reshape(4, 1024, 1024), qkv.reshape(6, 2, 2, 2, 32, 1024), P, H, T, AT, GP, SR, cot)
    return pl.pallas_call(backward_kernel,
        out_shape=(S((256, 1024), BF), S((3, 32, 1024), F32), S((32, 1024), F32), S((3, 32, 1024), F32), S((32, 1024), F32), S((32, 512), F32), S((16, 1024), F32), S((1, 4, 2, 32, 1024), BF)),
        in_specs=[vm] + [any_] * 10, out_specs=(any_,) * 8,
        scratch_shapes=[V((NT, 4, 2, 2, 2, 32, 1024), BF), V((NT, 4, 2, 2, 32, 1024), BF), V((NT, 4, 2, 32, 1024), BF), V((3, 4, 32, 1024), BF),
                        V((6, 3, 2, 32, 1024), BF), V((6, 3, 2, 32, 1024), BF), V((3, 3, 32, 1024), BF), V((3, 3, 32, 1024), BF), V((NT, 32, 1024), BF),
                        V((NW, 1024, 1024), BF), V((2, 256, 1024), F32), V((2, 256, 1024), F32), V((3, 1024, 256), BF), V((512, 256), BF), V((256, 512), F32),
                        V((16, 256, 128), F32), V((256, 1024), BF), V((256, 1024), F32), V((256, 1024), BF), V((256, 512), BF), V((256, 1024), BF),
                        V((3, 256, 1024), BF), V((256, 1024), BF),
                        V((3, 32, 1024), F32), V((32, 1024), F32), V((3, 32, 1024), F32), V((32, 1024), F32), V((32, 512), F32), V((16, 1024), F32), D((10,)),
                        D((NT, NS)), D((NT, NR)), D((3,)), D((4,)), D((17,)), D((3,)), D((4,)), D((6,)), D((3,)), D((6,)), D((2,)), D((2,))],
        compiler_params=pltpu.CompilerParams(collective_id=1, has_side_effects=True, vmem_limit_bytes=63 << 20),
        name="backward")(*ops)


def finish_kernel(*refs):
    n = (len(refs) - 1) // 3
    ins, outs, held, sem = refs[:n], refs[n:2 * n], refs[2 * n:3 * n], refs[3 * n]
    first = [pltpu.make_async_copy(ins[k], held[k], sem.at[k]) for k in range(n)]
    last = [pltpu.make_async_copy(held[k], outs[k], sem.at[n + k]) for k in range(n)]
    for c in first: c.start()
    for k in range(n):
        first[k].wait()
        last[k].start()
    for c in last: c.wait()

def finish(*arrays):
    any_ = pl.BlockSpec(memory_space=pl.ANY)
    n = len(arrays)
    return pl.pallas_call(finish_kernel, out_shape=tuple(jax.ShapeDtypeStruct(a.shape, a.dtype) for a in arrays),
        in_specs=[any_] * n, out_specs=(any_,) * n,
        scratch_shapes=[pltpu.VMEM(a.shape, a.dtype) for a in arrays] + [pltpu.SemaphoreType.DMA((2 * n,))],
        compiler_params=pltpu.CompilerParams(vmem_limit_bytes=62 << 20), name="finish")(*arrays)


def device_program(tokens, encoder, dec_lengths, enc_lengths, gains, self_proj, self_out, cross_proj, cross_out, ffn_in, ffn_out, adapt_in, adapt_out, cotangent):
    shards = (self_proj, self_out, cross_proj, cross_out, ffn_in, ffn_out, adapt_in, adapt_out)
    buf, gfo, qkv, probs, hidden, turned, act_turned, gelu_slope, silu_slope, layer_out = forward(tokens, gains, dec_lengths, enc_lengths, shards, encoder)
    gtok, osp, oso, ocp, oco, oai, oao, oen = backward(gains, buf, gfo, qkv, probs, hidden, turned, act_turned, gelu_slope, silu_slope, cotangent)
    return finish(layer_out, gtok, oen, osp, oso, ocp, oco, oai, oao)


def solution(mesh):
    in_specs = (
        P(("seq", "enc"), None),
        P("seq", None, None, "enc", None),
        P(("seq", "enc"), None),
        P(("seq", "enc"), None),
        P(),
        P(None, ("seq", "enc"), None),
        P(("seq", "enc"), None),
        P(None, ("seq", "enc"), None),
        P(("seq", "enc"), None),
        P(("seq", "enc"), None),
        P(("seq", "enc"), None),
        P(("seq", "enc"), None),
        P(("seq", "enc"), None),
        P(("seq", "enc"), None),
    )
    out_specs = (
        P(("seq", "enc"), None),
        P(("seq", "enc"), None),
        P("seq", None, None, "enc", None),
        P(None, ("seq", "enc"), None),
        P(("seq", "enc"), None),
        P(None, ("seq", "enc"), None),
        P(("seq", "enc"), None),
        P(("seq", "enc"), None),
        P(("seq", "enc"), None),
    )
    fast = (mesh.shape["seq"], mesh.shape["enc"]) == (8, 4)
    return jax.shard_map(
        device_program if fast else per_device, mesh=mesh, in_specs=in_specs, out_specs=out_specs, check_vma=False
    )
```

```python
import jax
import jax.numpy as jnp
from jax import lax
from jax.experimental import pallas as pl
from jax.experimental.pallas import tpu as pltpu
from jax.sharding import PartitionSpec as P

HEADS = 16
ADAPT = 512
MICRO = 2


EPSILON = 1e-05
NEGATIVE = -1e30


def matmul(left, right):
    return jnp.dot(left, right, preferred_element_type=jnp.float32)


def matmul_tn(left, right):
    return lax.dot_general(
        left, right, (((0,), (0,)), ((), ())), preferred_element_type=jnp.float32
    )


def matmul_nt(left, right):
    return lax.dot_general(
        left, right, (((1,), (1,)), ((), ())), preferred_element_type=jnp.float32
    )


def layer_norm(hidden, gain):
    center = hidden - jnp.mean(hidden, axis=-1, keepdims=True)
    spread = jnp.mean(center * center, axis=-1, keepdims=True)
    return center * lax.rsqrt(spread + EPSILON) * gain


def norm_back(hidden, gain, grad_out):
    _, pullback = jax.vjp(lambda value: layer_norm(value, gain), hidden)
    return pullback(grad_out)[0]


def gelu_exact(value):
    return jax.nn.gelu(value, approximate=False)


def slot_masks(dec_row, enc_row, rows):
    half_rows = rows // 2
    places = lax.broadcasted_iota(jnp.int32, (rows,), 0)
    paired = dec_row[1] > 0
    second = jnp.logical_and(paired, places >= half_rows)
    anchor = jnp.where(second, half_rows, 0).astype(jnp.int32)
    dec_valid = jnp.where(second, dec_row[1], dec_row[0])
    enc_valid = jnp.where(second, enc_row[1], enc_row[0])
    key_live = places - anchor < dec_valid
    context_live = places - anchor < enc_valid
    same_slot = second[:, None] == second[None, :]
    causal = places[None, :] <= places[:, None]
    self_mask = same_slot & causal & key_live[None, :]
    cross_mask = same_slot & context_live[None, :]
    return (self_mask, cross_mask)


def split_heads(matrix):
    return matrix.reshape(matrix.shape[0], HEADS, matrix.shape[1] // HEADS)


def attend(queries, keys, values, allowed):
    depth = queries.shape[1] // HEADS
    scores = jnp.einsum(
        "qhd,khd->hqk", split_heads(queries), split_heads(keys), preferred_element_type=jnp.float32
    ) * float(depth) ** (-0.5)
    masked = jnp.where(allowed[None], scores, NEGATIVE)
    weights = jnp.exp(masked - jnp.max(masked, axis=-1, keepdims=True))
    probs = weights / jnp.sum(weights, axis=-1, keepdims=True)
    mixed = jnp.einsum(
        "hqk,khd->qhd",
        probs.astype(jnp.bfloat16),
        split_heads(values),
        preferred_element_type=jnp.float32,
    )
    return (mixed.reshape(queries.shape).astype(jnp.bfloat16), probs)


def attend_back(grad_mixed, queries, keys, values, probs):
    depth = queries.shape[1] // HEADS
    factor = float(depth) ** (-0.5)
    grad_heads = split_heads(grad_mixed)
    grad_probs = jnp.einsum(
        "qhd,khd->hqk", grad_heads, split_heads(values), preferred_element_type=jnp.float32
    )
    inner = jnp.sum(probs * grad_probs, axis=-1, keepdims=True)
    grad_scores = (probs * (grad_probs - inner)).astype(jnp.bfloat16)
    grad_query = (
        jnp.einsum(
            "hqk,khd->qhd", grad_scores, split_heads(keys), preferred_element_type=jnp.float32
        )
        * factor
    )
    grad_key = (
        jnp.einsum(
            "hqk,qhd->khd", grad_scores, split_heads(queries), preferred_element_type=jnp.float32
        )
        * factor
    )
    grad_value = jnp.einsum(
        "hqk,qhd->khd", probs.astype(jnp.bfloat16), grad_heads, preferred_element_type=jnp.float32
    )
    return (
        grad_query.reshape(queries.shape).astype(jnp.bfloat16),
        grad_key.reshape(keys.shape).astype(jnp.bfloat16),
        grad_value.reshape(values.shape).astype(jnp.bfloat16),
    )


def per_device(
    tokens,
    encoder,
    dec_lengths,
    enc_lengths,
    gains,
    self_proj,
    self_out,
    cross_proj,
    cross_out,
    ffn_in,
    ffn_out,
    adapt_in,
    adapt_out,
    cotangent,
):
    shards = (self_proj, self_out, cross_proj, cross_out, ffn_in, ffn_out, adapt_in, adapt_out)

    def obtain():
        return (
            lax.all_gather(shards[0], ("seq", "enc"), axis=1, tiled=True),
            lax.all_gather(shards[1], ("seq", "enc"), axis=0, tiled=True),
            lax.all_gather(shards[2], ("seq", "enc"), axis=1, tiled=True),
            lax.all_gather(shards[3], ("seq", "enc"), axis=0, tiled=True),
            lax.all_gather(shards[4], ("seq", "enc"), axis=0, tiled=True),
            lax.all_gather(shards[5], ("seq", "enc"), axis=0, tiled=True),
            lax.all_gather(shards[6], ("seq", "enc"), axis=0, tiled=True),
            lax.all_gather(shards[7], ("seq", "enc"), axis=0, tiled=True),
        )

    rows = tokens.shape[0] // MICRO
    width = tokens.shape[1]
    owner = lax.axis_index("enc")
    acc_self = jnp.zeros((width, 3, width), jnp.float32)
    acc_self_out = jnp.zeros((width, width), jnp.float32)
    acc_cross = jnp.zeros((width, 3, width), jnp.float32)
    acc_cross_out = jnp.zeros((width, width), jnp.float32)
    acc_adapt_in = jnp.zeros((width, ADAPT), jnp.float32)
    acc_adapt_out = jnp.zeros((ADAPT, width), jnp.float32)
    outputs = []
    grad_rows = []
    grad_contexts = []
    for micro_index in range(MICRO):
        w_self, w_self_out, w_cross, w_cross_out, w_ffn_in, w_ffn_out, w_adapt_in, w_adapt_out = (
            obtain()
        )
        lower = micro_index * rows
        token_rows = tokens[lower : lower + rows]
        self_mask, cross_mask = slot_masks(dec_lengths[micro_index], enc_lengths[micro_index], rows)
        pieces = encoder[0, :, micro_index]
        context = lax.dynamic_index_in_dim(
            lax.all_gather(pieces, "enc", axis=1, tiled=True), owner, 0, keepdims=False
        )
        self_query = matmul(token_rows, w_self[0]).astype(jnp.bfloat16)
        self_key = matmul(token_rows, w_self[1]).astype(jnp.bfloat16)
        self_value = matmul(token_rows, w_self[2]).astype(jnp.bfloat16)
        self_mix, self_probs = attend(self_query, self_key, self_value, self_mask)
        first_sum = token_rows.astype(jnp.float32) + matmul(self_mix, w_self_out)
        first_norm = layer_norm(first_sum, gains[0])
        first_low = first_norm.astype(jnp.bfloat16)
        cross_query = matmul(first_low, w_cross[0]).astype(jnp.bfloat16)
        cross_key = matmul(context, w_cross[1]).astype(jnp.bfloat16)
        cross_value = matmul(context, w_cross[2]).astype(jnp.bfloat16)
        cross_mix, cross_probs = attend(cross_query, cross_key, cross_value, cross_mask)
        second_sum = first_norm + matmul(cross_mix, w_cross_out)
        second_norm = layer_norm(second_sum, gains[1])
        second_low = second_norm.astype(jnp.bfloat16)
        ffn_pre = matmul(second_low, w_ffn_in)
        ffn_act = gelu_exact(ffn_pre).astype(jnp.bfloat16)
        adapt_pre = matmul(second_low, w_adapt_in)
        adapt_act = jax.nn.silu(adapt_pre).astype(jnp.bfloat16)
        third_sum = second_norm + matmul(ffn_act, w_ffn_out) + 4.0 * matmul(adapt_act, w_adapt_out)
        outputs.append(layer_norm(third_sum, gains[2]).astype(jnp.bfloat16))
        w_self, w_self_out, w_cross, w_cross_out, w_ffn_in, w_ffn_out, w_adapt_in, w_adapt_out = (
            obtain()
        )
        grad_third = norm_back(
            third_sum, gains[2], cotangent[lower : lower + rows].astype(jnp.float32)
        )
        grad_branch = grad_third.astype(jnp.bfloat16)
        _, gelu_pull = jax.vjp(gelu_exact, ffn_pre)
        grad_ffn_pre = gelu_pull(matmul_nt(grad_branch, w_ffn_out))[0].astype(jnp.bfloat16)
        grad_adapt_act = matmul_nt(grad_branch, w_adapt_out) * 4.0
        _, silu_pull = jax.vjp(jax.nn.silu, adapt_pre)
        grad_adapt_pre = silu_pull(grad_adapt_act)[0].astype(jnp.bfloat16)
        acc_adapt_out = acc_adapt_out + matmul_tn(adapt_act, grad_branch) * 4.0
        acc_adapt_in = acc_adapt_in + matmul_tn(second_low, grad_adapt_pre)
        grad_second = (
            grad_third + matmul_nt(grad_ffn_pre, w_ffn_in) + matmul_nt(grad_adapt_pre, w_adapt_in)
        )
        grad_second_sum = norm_back(second_sum, gains[1], grad_second)
        grad_cross_branch = grad_second_sum.astype(jnp.bfloat16)
        acc_cross_out = acc_cross_out + matmul_tn(cross_mix, grad_cross_branch)
        grad_cross_mix = matmul_nt(grad_cross_branch, w_cross_out).astype(jnp.bfloat16)
        grad_cq, grad_ck, grad_cv = attend_back(
            grad_cross_mix, cross_query, cross_key, cross_value, cross_probs
        )
        acc_cross = acc_cross + jnp.stack(
            [
                matmul_tn(first_low, grad_cq),
                matmul_tn(context, grad_ck),
                matmul_tn(context, grad_cv),
            ],
            axis=1,
        )
        grad_context = matmul_nt(grad_ck, w_cross[1]) + matmul_nt(grad_cv, w_cross[2])
        holder = jnp.zeros((lax.axis_size("enc"),) + grad_context.shape, jnp.float32)
        holder = lax.dynamic_update_index_in_dim(holder, grad_context, owner, 0)
        returned = lax.psum_scatter(
            holder.astype(jnp.bfloat16), "enc", scatter_dimension=1, tiled=True
        )
        grad_contexts.append(returned)
        grad_first = grad_second_sum + matmul_nt(grad_cq, w_cross[0])
        grad_first_sum = norm_back(first_sum, gains[0], grad_first)
        grad_self_branch = grad_first_sum.astype(jnp.bfloat16)
        acc_self_out = acc_self_out + matmul_tn(self_mix, grad_self_branch)
        grad_self_mix = matmul_nt(grad_self_branch, w_self_out).astype(jnp.bfloat16)
        grad_sq, grad_sk, grad_sv = attend_back(
            grad_self_mix, self_query, self_key, self_value, self_probs
        )
        acc_self = acc_self + jnp.stack(
            [
                matmul_tn(token_rows, grad_sq),
                matmul_tn(token_rows, grad_sk),
                matmul_tn(token_rows, grad_sv),
            ],
            axis=1,
        )
        grad_input = (
            grad_first_sum
            + matmul_nt(grad_sq, w_self[0])
            + matmul_nt(grad_sk, w_self[1])
            + matmul_nt(grad_sv, w_self[2])
        )
        grad_rows.append(grad_input.astype(jnp.bfloat16))
    summed = (
        lax.psum_scatter(acc_self, ("seq", "enc"), scatter_dimension=0, tiled=True),
        lax.psum_scatter(acc_self_out, ("seq", "enc"), scatter_dimension=0, tiled=True),
        lax.psum_scatter(acc_cross, ("seq", "enc"), scatter_dimension=0, tiled=True),
        lax.psum_scatter(acc_cross_out, ("seq", "enc"), scatter_dimension=0, tiled=True),
        lax.psum_scatter(acc_adapt_in, ("seq", "enc"), scatter_dimension=0, tiled=True),
        lax.psum_scatter(acc_adapt_out, ("seq", "enc"), scatter_dimension=0, tiled=True),
    )
    layer_out = jnp.concatenate(outputs, axis=0)
    grad_tokens = jnp.concatenate(grad_rows, axis=0)
    grad_encoder = jnp.stack(grad_contexts, axis=1)[None]
    grad_self_proj = jnp.transpose(summed[0], (1, 0, 2))
    grad_cross_proj = jnp.transpose(summed[2], (1, 0, 2))
    return (
        layer_out,
        grad_tokens,
        grad_encoder,
        grad_self_proj,
        summed[1],
        grad_cross_proj,
        summed[3],
        summed[4],
        summed[5],
    )


MESH = pl.DeviceIdType.MESH
class Place:
    def __init__(self):
        seq, enc = lax.axis_index("seq"), lax.axis_index("enc")
        self.z, self.y, self.x, self.c = seq // 2, seq % 2, enc // 2, enc % 2
        self.up, self.down = jnp.minimum(self.z + 1, 3), jnp.maximum(self.z - 1, 0)
        self.step = jnp.where(self.z < 2, 1, -1)
    def dev(self, z=None, y=None, x=None, c=None):
        z = self.z if z is None else z
        y = self.y if y is None else y
        x = self.x if x is None else x
        c = self.c if c is None else c
        return (z * 2 + y, x * 2 + c)

def entry_barrier(p):
    bar = pltpu.get_barrier_semaphore()
    def sig(d):
        pl.semaphore_signal(bar, inc=1, device_id=d, device_id_type=MESH)
    sig(p.dev(c=1 - p.c)); sig(p.dev(x=1 - p.x)); sig(p.dev(y=1 - p.y)); sig(p.dev(x=1 - p.x, c=1 - p.c))
    @pl.when(p.z < 3)
    def _(): sig(p.dev(z=p.up))
    @pl.when(p.z > 0)
    def _(): sig(p.dev(z=p.down))
    peers = 4 + (p.z < 3).astype(jnp.int32) + (p.z > 0).astype(jnp.int32)
    return lambda: pl.semaphore_wait(bar, peers)

ALL4 = pl.ds(0, 4)
ALL2 = pl.ds(0, 2)

class Stream:
    def __init__(self, p, own, view, order, ssem, rsem):
        self.p, self.own, self.view, self.order, self.ssem, self.rsem = p, own, view, order, ssem, rsem
        self.flat = order[0] == "z"
        self.b1, self.b2 = (order[1], order[2]) if self.flat else (order[0], order[2])
        self.me = {"x": p.x, "y": p.y}
        self.sends = [[], []]

    def source(self, r, kind):
        p = self.p
        return p.z - p.step if kind == 1 and r == 3 else p.z + p.step * r

    def unit(self, z, c=None, **where):
        w = dict(self.me) if self.flat else {**self.me, self.b1: ALL2}
        w.update(where)
        return self.view(z, w["y"], w["x"], self.p.c if c is None else c)

    def partner(self, b):
        return self.p.dev(**{b: 1 - self.me[b]})

    def copy(self, kind, slot, what):
        k = len(self.sends[kind])
        def make():
            src, dst, target = what()
            return pltpu.make_async_remote_copy(src, dst, self.ssem.at[k], self.rsem.at[slot()], device_id=target, device_id_type=MESH)
        make().start()
        self.sends[kind].append(make)

    def arrive(self, where, slot):
        pltpu.make_async_remote_copy(where, where, self.ssem.at[0], self.rsem.at[slot], device_id=self.p.dev(), device_id_type=MESH).wait_recv()

    def finish(self, kind):
        for make in self.sends[kind]: make().wait_send()

    def along(self, kind, r, way, src=None):
        p = self.p
        def what():
            u = self.unit(self.source(r, kind))
            return u if src is None else src, u, p.dev(z=p.z + way * p.step)
        self.copy(kind, lambda: self.source(r, kind), what)

    def across(self, kind, r, src=None):
        b = self.b1 if self.flat else self.b2
        def what():
            u = self.unit(self.source(r, kind))
            return u if src is None else src, u, self.partner(b)
        self.copy(kind, lambda: 4 + self.source(r, kind), what)

    def P0(self, r, kind):
        if self.flat:
            self.along(kind, 0, 1, self.own)
            if kind == 1: self.along(kind, 0, -1, self.own)
            self.across(kind, 0, self.own)
        else:
            self.copy(kind, lambda: 8, lambda: (self.own, self.unit(self.p.z, **self.me), self.partner(self.b1)))
    def E0(self, r, kind):
        self.arrive(self.unit(self.p.z, **{self.b1: 1 - self.me[self.b1]}), 8)
        self.along(kind, 0, 1)
        if kind == 1: self.along(kind, 0, -1)
        self.across(kind, 0)
    def H(self, r, kind):
        z = self.source(r, kind)
        self.arrive(self.unit(z), z)
        if kind == 1: self.along(kind, r, -1 if r < 3 else 1)
        self.across(kind, r)
    def E(self, r, kind):
        z = self.source(r, kind)
        self.arrive(self.unit(z, **{self.b1: 1 - self.me[self.b1]}), 4 + z)
        def what():
            u = self.unit(self.source(r, kind), **{self.b1: ALL2})
            return u, u, self.partner(self.b2)
        self.copy(kind, lambda: 8 + self.source(r, kind), what)
    def plane(self, far, c=None):
        return self.unit(ALL4, c, **{self.b1: ALL2, self.b2: 1 - self.me[self.b2] if far else self.me[self.b2]})
    def F0(self, r, kind):
        self.copy(kind, lambda: 12, lambda: (self.plane(False), self.plane(False), self.p.dev(c=1 - self.p.c)))
    def F5(self, r, kind):
        for zz in range(4):
            self.arrive(self.unit(zz, **{self.b1: ALL2, self.b2: 1 - self.me[self.b2]}), (8 if self.flat else 4) + zz)
        self.copy(kind, lambda: 13, lambda: (self.plane(True), self.plane(True), self.p.dev(c=1 - self.p.c)))
    def L(self, r, kind):
        self.arrive(self.plane(False, 1 - self.p.c), 12)
        self.arrive(self.plane(True, 1 - self.p.c), 13)

def run_plan(plan, compute, movers, guards):
    i = 0
    while i < len(plan):
        it = plan[i]
        if isinstance(it, str):
            compute[it]()
            i += 1
        elif it[3] is None:
            getattr(movers[it[0]], it[1])(it[2])
            i += 1
        else:
            j = i
            while j < len(plan) and not isinstance(plan[j], str) and plan[j][3] == it[3]: j += 1
            @pl.when(guards[it[3]])
            def _():
                for m, name, k, kind in plan[i:j]: getattr(movers[m], name)(k, kind)
            i = j


GATHER = ["A", "xzy", "yzx", "yzx", "A", "xzy", "A", "xzy", "A", "A", "yzx", "yzx", "xzy", "A", "xzy", "yzx", "M"]
PLAN_F = [
    (0, "P0", 0, 0), (0, "P0", 0, 1), (1, "P0", 0, 0), (1, "P0", 0, 1), (2, "P0", 0, 0), (3, "P0", 0, 0), (2, "P0", 0, 1), (3, "P0", 0, 1),
    (4, "P0", 0, 0), (5, "P0", 0, 0), (4, "P0", 0, 1), (5, "P0", 0, 1), (6, "P0", 0, 0), (6, "P0", 0, 1), (7, "P0", 0, 0), (8, "P0", 0, 0),
    (7, "P0", 0, 1), (9, "P0", 0, 0), (8, "P0", 0, 1), (9, "P0", 0, 1), "flip0", "ctxsend", "masks", (0, "H", 1, 0), "staged", "own", (0, "E", 0, 0),
    (1, "E", 0, 0), (0, "H", 1, 1), (0, "H", 3, 1), (0, "E", 0, 1), (1, "E", 0, 1), (1, "H", 1, 0), (1, "H", 1, 1), (1, "H", 3, 1), (5, "H", 1, 1),
    (2, "E0", 0, 0), (2, "E0", 0, 1), (5, "H", 1, 0), (3, "E0", 0, 0), (3, "E0", 0, 1), (5, "H", 3, 1), (6, "H", 1, 1), (5, "E", 0, 0), (6, "H", 1, 0),
    (5, "E", 0, 1), (6, "H", 3, 1), (8, "H", 1, 1), (8, "H", 1, 0), (8, "H", 3, 1), (4, "E0", 0, 0), (4, "E0", 0, 1), (9, "H", 1, 1), (7, "E0", 0, 0),
    (7, "E0", 0, 1), (9, "H", 1, 0), (6, "E", 0, 0), (6, "E", 0, 1), (9, "H", 3, 1), (0, "H", 2, 1), (0, "H", 2, 0), (8, "E", 0, 1), (8, "E", 0, 0),
    (9, "E", 0, 0), (9, "E", 0, 1), (1, "H", 2, 1), (1, "H", 2, 0), (5, "H", 2, 0), (2, "H", 3, 1), (1, "E", 1, 0), (1, "E", 1, 1), (1, "E", 3, 1),
    (2, "H", 1, 1), (2, "H", 1, 0), (3, "H", 3, 1), "ctxin", "flip1", (3, "H", 1, 1), (0, "E", 1, 0), (0, "E", 1, 1), (6, "E", 1, 1), (5, "H", 2, 1),
    (3, "H", 1, 0), (0, "E", 3, 1), (6, "E", 1, 0), (4, "H", 3, 1), (6, "H", 2, 0), (6, "H", 2, 1), (8, "H", 2, 1), (5, "E", 1, 0), (8, "H", 2, 0),
    (6, "E", 3, 1), (5, "E", 1, 1), (9, "E", 1, 1), (7, "H", 3, 1), (9, "E", 1, 0), (4, "H", 1, 1), (4, "H", 1, 0), (8, "E", 1, 0), (9, "H", 2, 0),
    (5, "E", 3, 1), (1, "E", 2, 0), (9, "E", 3, 1), (8, "E", 1, 1), (7, "H", 1, 1), (8, "E", 3, 1), (9, "H", 2, 1), (7, "H", 1, 0), (1, "E", 2, 1),
    (1, "F0", 0, 1), (0, "H", 3, 0), (1, "H", 3, 0), (0, "E", 2, 0), (2, "H", 2, 1), (2, "F0", 0, 1), (6, "E", 2, 0), (11, "P0", 0, 1),
    (12, "P0", 0, 1), (2, "H", 2, 0), (0, "E", 2, 1), (5, "E", 2, 0), (0, "F0", 0, 1), (10, "P0", 0, 1), (3, "H", 2, 1), (3, "F0", 0, 1),
    (13, "P0", 0, 1), (14, "P0", 0, 1), (9, "E", 2, 0), (3, "H", 2, 0), (5, "H", 3, 0), (4, "H", 2, 1), (6, "H", 3, 0), (4, "F0", 0, 1),
    (15, "P0", 0, 1), (8, "H", 3, 0), (6, "E", 2, 1), (6, "F0", 0, 1), (1, "E", 3, 0), (1, "F0", 0, 0), (8, "E", 2, 0), (7, "H", 2, 1),
    (7, "F0", 0, 1), (17, "P0", 0, 1), (11, "H", 1, 1), (4, "H", 2, 0), (12, "H", 1, 1), (13, "H", 1, 1), (14, "H", 1, 1), (7, "H", 2, 0),
    (9, "H", 3, 0), (5, "E", 2, 1), (5, "F0", 0, 1), (6, "E", 3, 0), (16, "P0", 0, 1), (6, "F0", 0, 0), (0, "E", 3, 0), (0, "F0", 0, 0),
    (10, "P0", 0, 0), (2, "H", 3, 0), (2, "F0", 0, 0), (11, "P0", 0, 0), (12, "P0", 0, 0), (11, "H", 1, 0), (12, "H", 1, 0), (8, "E", 2, 1),
    (8, "F0", 0, 1), (11, "H", 3, 1), (9, "E", 3, 0), (9, "F0", 0, 0), (9, "E", 2, 1), (9, "F0", 0, 1), (18, "P0", 0, 1), (12, "H", 3, 1),
    (19, "P0", 0, 1), (3, "H", 3, 0), (3, "F0", 0, 0), (0, "F5", 0, 0), (13, "P0", 0, 0), (14, "P0", 0, 0), (5, "E", 3, 0), (5, "F0", 0, 0),
    (13, "H", 1, 0), (16, "P0", 0, 0), (11, "H", 2, 1), (8, "E", 3, 0), (8, "F0", 0, 0), (14, "H", 1, 0), (2, "F5", 0, 1), (18, "P0", 0, 0),
    (18, "H", 1, 1), (19, "P0", 0, 0), (12, "E", 0, 1), (12, "H", 2, 1), (0, "L", 0, 0), (1, "F5", 0, 0), (13, "H", 3, 1), (2, "F5", 0, 0),
    (19, "H", 1, 1), (14, "H", 3, 1), (12, "E", 0, 0), (2, "L", 0, 1), (0, "F5", 0, 1), (4, "H", 3, 0), (18, "H", 3, 1), (4, "F0", 0, 0),
    (12, "E", 1, 0), (14, "E", 0, 1), (15, "P0", 0, 0), (1, "L", 0, 0), (19, "H", 3, 1), (14, "E", 0, 0), (0, "L", 0, 1), (13, "H", 2, 1),
    (2, "L", 0, 0), "w1", (1, "F5", 0, 1), (11, "E", 0, 1), (14, "H", 2, 1), (15, "E0", 0, 1), (18, "H", 2, 1), (5, "F5", 0, 0), (6, "F5", 0, 0),
    (7, "H", 3, 0), (7, "F0", 0, 0), (19, "H", 2, 1), (17, "P0", 0, 0), "proj1", (10, "E0", 0, 1), (1, "L", 0, 1), "w0", (11, "H", 2, 0),
    (10, "E0", 0, 0), (5, "L", 0, 0), (12, "H", 2, 0), (7, "F5", 0, 1), (16, "E0", 0, 0), (11, "E", 0, 0), (6, "L", 0, 0), (8, "F5", 0, 0),
    (12, "E", 1, 1), (13, "H", 2, 0), "proj0", (11, "E", 1, 0), (14, "H", 2, 0), (14, "E", 1, 0), (14, "E", 1, 1), (18, "H", 1, 0), (3, "F5", 0, 1),
    (19, "E", 0, 0), (7, "L", 0, 1), (8, "L", 0, 0), (13, "E", 0, 1), (15, "H", 1, 1), (5, "F5", 0, 1), (9, "F5", 0, 0), (11, "H", 3, 0),
    (15, "E0", 0, 0), (19, "H", 1, 0), (18, "H", 2, 0), (3, "L", 0, 1), (5, "L", 0, 1), (12, "H", 3, 0), (10, "H", 3, 1), (9, "L", 0, 0),
    (16, "E0", 0, 1), (3, "F5", 0, 0), (4, "F5", 0, 1), (19, "H", 2, 0), (10, "H", 1, 1), (8, "F5", 0, 1), (13, "H", 3, 0), (13, "E", 0, 0),
    (7, "F5", 0, 0), (12, "E", 3, 1), (13, "E", 1, 0), (14, "H", 3, 0), (6, "F5", 0, 1), (3, "L", 0, 0), (18, "E", 0, 0), (4, "L", 0, 1), "w2",
    (16, "H", 3, 1), (12, "E", 2, 1), (12, "F0", 0, 1), (19, "E", 0, 1), (7, "L", 0, 0), "w5", (6, "L", 0, 1), "proj2", (8, "L", 0, 1),
    (10, "H", 2, 1), (10, "F0", 0, 1), (11, "E", 1, 1), (13, "E", 1, 1), (14, "E", 3, 1), (17, "E0", 0, 1), (12, "E", 2, 0), (19, "E", 1, 1),
    (15, "H", 1, 0), (15, "H", 3, 1), "at00", (19, "E", 3, 1), (11, "E", 3, 1), (20, "P0", 0, 1), (18, "H", 3, 0), (19, "H", 3, 0), "at01",
    (9, "F5", 0, 1), (4, "F5", 0, 0), "at02", (14, "E", 2, 1), (11, "E", 2, 1), (9, "L", 0, 1), (11, "F0", 0, 1), (14, "F0", 0, 1), (16, "H", 1, 1),
    (18, "E", 0, 1), (19, "E", 2, 1), (19, "F0", 0, 1), (18, "E", 1, 1), (21, "P0", 0, 1), (10, "H", 1, 0), (14, "E", 2, 0), (19, "E", 1, 0), "at03",
    (16, "H", 2, 1), (16, "F0", 0, 1), (4, "L", 0, 0), (12, "E", 3, 0), (12, "F0", 0, 0), (19, "E", 2, 0), (17, "E0", 0, 0), (13, "E", 3, 1), "flip3",
    "w4", "w3", "proj5", (18, "E", 3, 1), (11, "E", 2, 0), (15, "H", 2, 0), "w6", "branch3", (17, "H", 1, 1), (14, "E", 3, 0), (14, "F0", 0, 0),
    "norm0", (13, "E", 2, 1), (13, "F0", 0, 1), (22, "P0", 0, 1), (23, "P0", 0, 1), (16, "H", 1, 0), (13, "E", 2, 0), "proj4", "flip2",
    (15, "H", 2, 1), (15, "F0", 0, 1), (17, "H", 3, 1), "proj6", (19, "E", 3, 0), (19, "F0", 0, 0), "at10", (10, "H", 2, 0), (18, "E", 1, 0),
    (18, "E", 2, 1), (18, "F0", 0, 1), "at11", "at12", (10, "H", 3, 0), (10, "F0", 0, 0), (11, "E", 3, 0), (11, "F0", 0, 0), (20, "P0", 0, 0),
    (21, "P0", 0, 0), (10, "F5", 0, 1), (17, "H", 2, 1), (17, "F0", 0, 1), "at13", "flip4", (17, "H", 1, 0), (10, "L", 0, 1), (18, "E", 2, 0),
    (13, "E", 3, 0), (13, "F0", 0, 0), (22, "P0", 0, 0), (23, "P0", 0, 0), (16, "H", 2, 0), (16, "H", 3, 0), (16, "F0", 0, 0), (18, "E", 3, 0),
    (11, "F5", 0, 1), (18, "F0", 0, 0), (11, "L", 0, 1), (17, "H", 2, 0), (12, "F5", 0, 1), (10, "F5", 0, 0), (12, "F5", 0, 0), (12, "L", 0, 1),
    (11, "F5", 0, 0), (21, "E0", 0, 1), (10, "L", 0, 0), "w7", (15, "H", 3, 0), (12, "L", 0, 0), (15, "F0", 0, 0), (21, "E0", 0, 0), (11, "L", 0, 0),
    "w8", "branch7", "norm1", (17, "H", 3, 0), (17, "F0", 0, 0), "flip5", "adapter", (21, "H", 1, 1), (14, "F5", 0, 0), "adapter_out", (21, "H", 3, 1),
    (21, "H", 1, 0), (13, "F5", 0, 0), (13, "F5", 0, 1), (14, "L", 0, 0), (23, "E0", 0, 0), (23, "E0", 0, 1), (20, "E0", 0, 1), (13, "L", 0, 0),
    (13, "L", 0, 1), (18, "F5", 0, 0), (19, "F5", 0, 0), (14, "F5", 0, 1), (21, "H", 2, 0), (23, "H", 3, 1), (21, "H", 2, 1), (21, "F0", 0, 1),
    (18, "L", 0, 0), (14, "L", 0, 1), (19, "L", 0, 0), "w9", (20, "E0", 0, 0), (23, "H", 1, 0), (23, "H", 1, 1), (18, "F5", 0, 1), (22, "E0", 0, 0),
    "hid0", (20, "H", 1, 0), (18, "L", 0, 1), (19, "F5", 0, 1), (20, "H", 1, 1), (17, "F5", 0, 0), (17, "F5", 0, 1), (23, "H", 2, 1), (23, "F0", 0, 1),
    (19, "L", 0, 1), "w13", (20, "H", 3, 1), (21, "H", 3, 0), (21, "F0", 0, 0), (17, "L", 0, 0), (17, "L", 0, 1), (23, "H", 2, 0), "w12",
    (16, "F5", 0, 1), (16, "F5", 0, 0), (22, "E0", 0, 1), (22, "H", 3, 1), "hid3", (16, "L", 0, 1), (20, "H", 2, 0), (16, "L", 0, 0), "w11",
    (23, "H", 3, 0), (23, "F0", 0, 0), (15, "F5", 0, 0), (20, "H", 2, 1), (15, "F5", 0, 1), (20, "F0", 0, 1), "hid2", (22, "H", 1, 0), (15, "L", 0, 0),
    (22, "H", 1, 1), (15, "L", 0, 1), "w10", "hid1", (20, "H", 3, 0), (20, "F0", 0, 0), (22, "H", 2, 1), (22, "F0", 0, 1), "out0", (22, "H", 2, 0),
    (22, "H", 3, 0), (22, "F0", 0, 0), (20, "F5", 0, 1), (20, "F5", 0, 0), (20, "L", 0, 1), (20, "L", 0, 0), "w14", (21, "F5", 0, 0), (21, "F5", 0, 1),
    (22, "F5", 0, 0), "out1", (22, "F5", 0, 1), (23, "F5", 0, 1), (21, "L", 0, 0), (21, "L", 0, 1), (23, "F5", 0, 0), "w15", (22, "L", 0, 0),
    (22, "L", 0, 1), (23, "L", 0, 0), (23, "L", 0, 1), "w16", "out2", "out3", "norm2",
]

F32, BF = jnp.float32, jnp.bfloat16
NSLOT, NSEND = 14, 19
N_STREAM = 24
EPS = 1e-05

def dot(a, b):
    return jnp.dot(a, b, preferred_element_type=F32)

def dot_nt(a, b):
    return lax.dot_general(a, b, (((1,), (1,)), ((), ())), preferred_element_type=F32)

def dot_tn(a, b):
    return lax.dot_general(a, b, (((0,), (0,)), ((), ())), preferred_element_type=F32)

def cols(n, width):
    return pl.ds(pl.multiple_of(n * width, width), width)

def norm_rows(h):
    center = h - jnp.mean(h, axis=-1, keepdims=True)
    spread = jnp.mean(center * center, axis=-1, keepdims=True)
    return center * lax.rsqrt(spread + EPS)

def half_masks():
    lane = lax.broadcasted_iota(jnp.int32, (1, 128), 1)
    lo = jnp.where(lane < 64, 1.0, 0.0)
    return lo.astype(BF), (1.0 - lo).astype(BF)

def pair_up(m, lo, hi):
    return jnp.concatenate([m * lo, m * hi], axis=0)

def side(m):
    return jnp.concatenate([m[:128], m[128:]], axis=1)

def forward_kernel(tokens, gains, dlen, elen, sp, so, cp, co, fi, fo, ai, ao, en,
                   buf, gfo, o_qkv, o_p, o_h, o_t, o_at, o_gp, o_sr, o_out,
                   qkv, P, H, T, AT, GP, SR, OUT, ctx, wbuf, wo, own, ownf, y, yl, mix, af, ar, bias, x,
                   ssem, rsem, lsem, csem, crsem, wsem, osem):
    p = Place()
    neighbours_in = entry_barrier(p)
    loc = []
    x_in = pltpu.make_async_copy(tokens, x, lsem.at[19])
    def put(src, dst):
        c_ = pltpu.make_async_copy(src, dst, lsem.at[len(loc)]); c_.start(); loc.append(c_)
    for j, t in enumerate((0, 1, 2)): put(sp.at[j], own.at[t])
    put(so, own.at[3])
    for j, t in ((1, 4), (2, 5), (0, 6)): put(cp.at[j], own.at[t])
    put(co, own.at[7])
    put(ai, own.at[8, :, pl.ds(0, 512)])
    put(ao.at[:, pl.ds(0, 512)], own.at[8, pl.ds(0, 16), pl.ds(512, 512)])
    put(ao.at[:, pl.ds(512, 512)], own.at[8, pl.ds(16, 16), pl.ds(512, 512)])
    for j in range(4): put(fi.at[:, pl.ds(1024 * j, 1024)], own.at[9 + j])
    put(fo, ownf)
    me = p.x * 2 + p.c
    put(en.at[0, me], ctx.at[:, me])
    x_in.start()
    n_in = len(loc)
    c1 = pltpu.make_async_copy(own, buf.at[:, p.z, p.y, p.x, p.c], lsem.at[n_in])
    c2 = pltpu.make_async_copy(ownf, gfo.at[p.z, p.y, p.x, p.c], lsem.at[n_in + 1])
    def staged():
        for c_ in loc: c_.wait()
        c1.start(); c2.start()
    neighbours_in()
    streams = []
    for t in range(17):
        R = 32 if t < 13 else 128
        kind = GATHER[t]
        rows = {"A": [(0, R // 2, "zxy"), (R // 2, R // 2, "zyx")], "M": [(0, R * 3 // 4, "xzy"), (R * 3 // 4, R // 4, "yzx")]}.get(kind, [(0, R, kind)])
        for r0, nr, order in rows:
            n = len(streams)
            if t < 13:
                arg = {0: sp.at[0], 1: sp.at[1], 2: sp.at[2], 3: so, 4: cp.at[1], 5: cp.at[2], 6: cp.at[0], 7: co, 8: own.at[8]}.get(t)
                mine = fi.at[pl.ds(r0, nr), pl.ds(1024 * (t - 9), 1024)] if t > 8 else arg.at[pl.ds(r0, nr)]
                view = lambda z, y_, x_, c, t=t, r0=r0, nr=nr: buf.at[t, z, y_, x_, c, pl.ds(r0, nr)]
            else:
                mine = fo.at[pl.ds(r0, nr), pl.ds(256 * (t - 13), 256)]
                view = lambda z, y_, x_, c, j=t - 13, r0=r0, nr=nr: gfo.at[z, y_, x_, c, pl.ds(r0, nr), pl.ds(256 * j, 256)]
            streams.append(Stream(p, mine, view, order, ssem.at[n], rsem.at[n]))
    ends = (p.z == 0) | (p.z == 3)
    guards = [ends, jnp.logical_not(ends)]

    def fetch(t):
        if t < 13: return pltpu.make_async_copy(buf.at[t], wbuf.at[t % 4], wsem.at[t])
        j = t - 13
        return pltpu.make_async_copy(gfo.at[:, :, :, :, :, pl.ds(256 * j, 256)], wo.at[j % 2], wsem.at[t])
    def start(t): return lambda: fetch(t).start()
    outs = []
    def keep(src, dst):
        c_ = pltpu.make_async_copy(src, dst, osem.at[len(outs)]); c_.start(); outs.append(c_)
    lo, hi = half_masks()

    def mm(lhs, t, fn):
        fn(dot(lhs[...], wbuf[t % 4].reshape(1024, 1024)))

    def proj(lhs, t, slot):
        def run():
            fetch(t).wait()
            def st(v): qkv[slot] = v.astype(BF)
            mm(lhs, t, st)
            keep(qkv.at[slot], o_qkv.at[slot])
        return run

    def flip(src, slot):
        def run():
            if slot == 0: x_in.wait()
            @pl.loop(0, 4)
            def _(n):
                T[slot, cols(n, 256), :] = src[:, cols(n, 256)].T
            keep(T.at[slot], o_t.at[slot])
        return run

    def attend(a, part):
        def run():
            u = part // 2
            @pl.loop(0, 4, unroll=4)
            def _(n):
                pr = (part % 2) * 4 + n
                r, cc = pl.ds(u * 128, 128), cols(pr, 128)
                q, k, v = (qkv[3 * a + j, r, cc] for j in range(3))
                b = bias[a, u]
                s = dot_nt(pair_up(q, lo, hi), k) * 0.125 + jnp.concatenate([b, b], axis=0)
                e = jnp.exp(s - jnp.max(s, axis=-1, keepdims=True))
                pr_ = e / jnp.sum(e, axis=-1, keepdims=True)
                P[a, u * 8 + pr] = pr_
                mix[r, cc] = dot(side(pr_.astype(BF)), pair_up(v, lo, hi)).astype(BF)
            if part == 3: keep(P.at[a], o_p.at[a])
        return run

    def branch(t, base, slot):
        def run():
            fetch(t).wait()
            def st(v): H[slot] = base[...].astype(F32) + v
            mm(mix, t, st)
        return run

    def norm(slot):
        def run():
            keep(H.at[slot], o_h.at[slot])
            @pl.loop(0, 4)
            def _(n):
                r = pl.ds(pl.multiple_of(n * 64, 64), 64)
                v = norm_rows(H[slot, r, :]) * gains[slot, :][None]
                if slot < 2:
                    y[r, :] = v
                    yl[r, :] = v.astype(BF)
                else:
                    OUT[r, :] = v.astype(BF)
            if slot == 2: keep(OUT, o_out)
        return run

    cs = []
    def context_out():
        for k, (dx, dc) in enumerate(((0, 1), (1, 0), (1, 1))):
            tx = (p.x + dx) % 2; tc = (p.c + dc) % 2
            c_ = pltpu.make_async_remote_copy(en.at[0, tx * 2 + tc], ctx.at[:, me], csem.at[k], crsem.at[me], device_id=p.dev(x=tx, c=tc), device_id_type=MESH)
            c_.start(); cs.append(c_)
    def context_in():
        for k, (dx, dc) in enumerate(((0, 1), (1, 0), (1, 1))):
            tx = (p.x + dx) % 2; tc = (p.c + dc) % 2
            w = tx * 2 + tc
            pltpu.make_async_remote_copy(en.at[0, w], ctx.at[:, w], csem.at[k], crsem.at[w], device_id=p.dev(), device_id_type=MESH).wait_recv()

    class Ctx:
        def __getitem__(self, idx):
            if idx is Ellipsis: return ctx[...].reshape(256, 1024)
            return ctx[:, :, :, idx[1]].reshape(256, -1)
    cref = Ctx()
    def adapter():
        fetch(8).wait()
        w = wbuf[0, :, :, :, :, :, pl.ds(0, 512)].reshape(1024, 512)
        r = dot(yl[...], w)
        s = 1.0 / (1.0 + jnp.exp(-r))
        a = (r * s).astype(BF)
        ar[...] = a
        SR[...] = s * (1.0 + r * (1.0 - s))
        AT[...] = a.T
        keep(SR, o_sr); keep(AT, o_at)
    def adapter_out():
        top = wbuf[0, :, :, :, :, pl.ds(0, 16), pl.ds(512, 512)].reshape(512, 512)
        bot = wbuf[0, :, :, :, :, pl.ds(16, 16), pl.ds(512, 512)].reshape(512, 512)
        H[2, :, 0:512] = y[:, 0:512] + 4.0 * dot(ar[...], top)
        H[2, :, 512:1024] = y[:, 512:1024] + 4.0 * dot(ar[...], bot)
    def hidden(j):
        def run():
            t = 9 + j
            fetch(t).wait()
            @pl.loop(0, 4)
            def _(n):
                ds = cols(n, 256)
                u = dot(yl[...], wbuf[t % 4, :, :, :, :, :, ds].reshape(1024, 256))
                half = 0.5 + 0.5 * lax.erf(u * 0.7071067811865476)
                af[j, :, ds] = (u * half).astype(BF)
                GP[j, :, ds] = half + u * (0.3989422804014327 * jnp.exp(-0.5 * u * u))
            keep(GP.at[j], o_gp.at[j])
        return run
    def out_cols(j):
        def run():
            fetch(13 + j).wait()
            acc = H[2, :, pl.ds(256 * j, 256)]
            for f in range(4):
                w = wo[j % 2, f].reshape(1024, 256)
                acc = acc + dot(af[f], w)
            H[2, :, pl.ds(256 * j, 256)] = acc
        return run

    def masks():
        row = lax.broadcasted_iota(jnp.int32, (128, 128), 0)
        col = lax.broadcasted_iota(jnp.int32, (128, 128), 1)
        for u in range(2):
            wide = lambda ref, j: jnp.broadcast_to(ref[u:u + 1, j:j + 1], (128, 128))
            paired = wide(dlen, 1) > 0
            far = jnp.where(paired, 64, 128)
            second = col >= far
            place = jnp.where(second, col - 64, col)
            same = (row >= far) == second
            dec = jnp.where(second, wide(dlen, 1), wide(dlen, 0))
            enc = jnp.where(second, wide(elen, 1), wide(elen, 0))
            bias[0, u] = jnp.where(same & (col <= row) & (place < dec), 0.0, -1e30)
            bias[1, u] = jnp.where(same & (place < enc), 0.0, -1e30)

    compute = {}
    for t in range(17): compute[f"w{t}"] = start(t)
    compute["masks"] = masks
    compute["staged"] = staged
    compute["own"] = lambda: (c1.wait(), c2.wait())
    for k, src in ((0, x), (1, cref), (2, yl), (3, mix), (4, mix), (5, yl)): compute[f"flip{k}"] = flip(src, k)
    for t, lhs, slot in ((0, x, 0), (1, x, 1), (2, x, 2), (4, cref, 4), (5, cref, 5), (6, yl, 3)): compute[f"proj{t}"] = proj(lhs, t, slot)
    for a in range(2):
        for part in range(4): compute[f"at{a}{part}"] = attend(a, part)
    compute.update(branch3=branch(3, x, 0), branch7=branch(7, y, 1), norm0=norm(0), norm1=norm(1), norm2=norm(2),
                   ctxsend=context_out, ctxin=context_in, adapter=adapter, adapter_out=adapter_out)
    for j in range(4): compute.update({f"hid{j}": hidden(j), f"out{j}": out_cols(j)})
    run_plan(PLAN_F, compute, streams, guards)
    for k in range(2):
        @pl.when(guards[k])
        def _():
            for s in streams: s.finish(k)
    for c_ in cs: c_.wait_send()
    for c_ in outs: c_.wait()

def forward(tokens, gains, dec_lengths, enc_lengths, shards, encoder):
    any_ = pl.BlockSpec(memory_space=pl.ANY)
    vm = pl.BlockSpec(memory_space=pltpu.VMEM)
    V, S, D = pltpu.VMEM, jax.ShapeDtypeStruct, pltpu.SemaphoreType.DMA
    tile = (4, 2, 2, 2, 32, 1024)
    return pl.pallas_call(forward_kernel,
        out_shape=(S((13,) + tile, BF), S((4, 2, 2, 2, 128, 1024), BF), S((6, 256, 1024), BF), S((2, 16, 256, 128), F32), S((3, 256, 1024), F32),
                   S((6, 1024, 256), BF), S((512, 256), BF), S((4, 256, 1024), F32), S((256, 512), F32), S((256, 1024), BF)),
        in_specs=[any_] + [vm] * 3 + [any_] * 9, out_specs=(any_,) * 10,
        scratch_shapes=[V((6, 256, 1024), BF), V((2, 16, 256, 128), F32), V((3, 256, 1024), F32), V((6, 1024, 256), BF), V((512, 256), BF),
                        V((4, 256, 1024), F32), V((256, 512), F32), V((256, 1024), BF), V((2, 4, 32, 1024), BF), V((4,) + tile, BF),
                        V((2, 4, 2, 2, 2, 128, 256), BF), V((13, 32, 1024), BF), V((128, 1024), BF), V((256, 1024), F32), V((256, 1024), BF),
                        V((256, 1024), BF), V((4, 256, 1024), BF), V((256, 512), BF), V((2, 2, 128, 128), F32), V((256, 1024), BF),
                        D((N_STREAM, NSEND)), D((N_STREAM, NSLOT)), D((20,)), D((3,)), D((4,)), D((17,)), D((26,))],
        compiler_params=pltpu.CompilerParams(collective_id=0, has_side_effects=True, vmem_limit_bytes=60 << 20),
        name="forward")(tokens, gains, dec_lengths, enc_lengths, *shards, encoder)

ORDERS = ["A", "yzx", "xzy", "xzy", "yzx", "A", "xzy", "yzx", "A"]
PLAN_B = [
    "nb0", "hb0", "hb1", "hb2", "hb3", "adb", "adg.0", "adg.1", "adg.2", "adg.3", "hi0", (0, "R1", 0, None), (0, "R1", 1, None), "hi1",
    (0, "R1", 2, None), (0, "R1", 3, None), "hi2", "hi3", "nb1", (0, "R2", 0, None), "t1.0", (0, "R2", 1, None), "t1.1", "t1.2", "t1.3", "mb9",
    (0, "R2", 2, None), (1, "R1", 0, None), "at10", (0, "R2", 3, None), (0, "R3", 0, None), (0, "U", 3, 0), (0, "D", 0, 3), (1, "R1", 1, None),
    (1, "R1", 2, None), (1, "R1", 3, None), "at11", (0, "R3", 1, None), (0, "R3", 2, None), (0, "D", 1, 3), (0, "U", 2, 0), "at12", (0, "D", 2, 3),
    (0, "U", 1, 0), "at13", (0, "U", 3, 1), (0, "D", 0, 2), (1, "R2", 0, None), "t2.0", (1, "D", 0, 3), (1, "U", 3, 0), "t2.1", (0, "R3", 3, None),
    "t2.2", (0, "D", 1, 2), (0, "U", 2, 1), "t2.3", "t3.0", "t3.1", "t3.2", (2, "R1", 0, None), "t3.3", "t4.0", (2, "R1", 1, None), "t4.1", "t4.2",
    (2, "R1", 2, None), (0, "D", 0, 1), (0, "U", 3, 2), (1, "R2", 1, None), (1, "U", 2, 0), (1, "D", 1, 3), "t4.3", (2, "R1", 3, None), "rb10",
    (0, "FIN", 0, 1), (0, "FIN", 0, 2), (3, "R1", 0, None), (1, "D", 0, 2), (1, "U", 3, 1), "cb", (3, "R1", 1, None), (3, "R1", 2, None),
    (1, "R2", 2, None), (1, "D", 2, 3), (1, "U", 1, 0), (3, "R1", 3, None), "rb12", (2, "R2", 0, None), (4, "R1", 0, None), (0, "FIN", 0, 0),
    (0, "FIN", 0, 3), (2, "D", 0, 3), (2, "U", 3, 0), (4, "R1", 1, None), "nb2", (4, "R1", 2, None), (1, "R2", 3, None), (1, "D", 1, 2),
    (1, "U", 2, 1), (2, "R2", 1, None), (2, "D", 1, 3), (2, "U", 2, 0), (1, "U", 3, 2), (1, "D", 0, 1), (4, "R1", 3, None), "t5.0", "t5.1", "t5.2",
    "t5.3", "mb13", "at00", (2, "R2", 2, None), (2, "D", 2, 3), (2, "U", 1, 0), (5, "R1", 0, None), (5, "R1", 1, None), (5, "R1", 2, None),
    (5, "R1", 3, None), "at01", (2, "U", 3, 1), (2, "D", 0, 2), (1, "Z3", 0, 0), (1, "Z3", 0, 3), (1, "Z3", 0, 2), (1, "Z3", 0, 1), "at02",
    (2, "R2", 3, None), "at03", (2, "D", 1, 2), (2, "U", 2, 1), (4, "R2", 0, None), (4, "U", 3, 0), (4, "D", 0, 3), (3, "R2", 0, None), (3, "U", 3, 0),
    (3, "D", 0, 3), "cs", "t6.0", "t6.1", (2, "D", 0, 1), (2, "U", 3, 2), "t6.2", "t6.3", "t7.0", "t7.1", "t7.2", (6, "R1", 0, None), "t7.3",
    (4, "R2", 1, None), (4, "D", 1, 3), (4, "U", 2, 0), "t8.0", (6, "R1", 1, None), (3, "R2", 1, None), "t8.1", (3, "D", 1, 3), (3, "U", 2, 0),
    (6, "R1", 2, None), "t8.2", (2, "Z3", 0, 2), (2, "Z3", 0, 1), "t8.3", (6, "R1", 3, None), "rb14", (7, "R1", 0, None), (4, "U", 3, 1),
    (4, "D", 0, 2), "rb15", (4, "R2", 2, None), (2, "Z3", 0, 0), (2, "Z3", 0, 3), (7, "R1", 1, None), (4, "D", 2, 3), (4, "U", 1, 0),
    (3, "R2", 2, None), (3, "D", 2, 3), (3, "U", 1, 0), (7, "R1", 2, None), (7, "R1", 3, None), "tok", (8, "R1", 0, None), (3, "D", 0, 2),
    (3, "U", 3, 1), (8, "R1", 1, None), (4, "R2", 3, None), (8, "R1", 2, None), (3, "R2", 3, None), (8, "R1", 3, None), (4, "D", 0, 1), (4, "U", 3, 2),
    (5, "R2", 0, None), (4, "D", 1, 2), (4, "U", 2, 1), (5, "R2", 1, None), (3, "D", 0, 1), (3, "U", 3, 2), (5, "R2", 2, None), (3, "D", 1, 2),
    (3, "U", 2, 1), (5, "R2", 3, None), (4, "Z3", 0, 0), (4, "Z3", 0, 3), (2, "FIN", 0, 2), (2, "FIN", 0, 1), (1, "FIN", 0, 2), (1, "FIN", 0, 1),
    (1, "FIN", 0, 0), (1, "FIN", 0, 3), (7, "R2", 0, None), (7, "U", 3, 0), (7, "D", 0, 3), (3, "Z3", 0, 3), (3, "Z3", 0, 0), (2, "FIN", 0, 0),
    (2, "FIN", 0, 3), (3, "Z3", 0, 2), (3, "Z3", 0, 1), (6, "R2", 0, None), (6, "U", 3, 0), (6, "D", 0, 3), (4, "Z3", 0, 2), (4, "Z3", 0, 1),
    (7, "R2", 1, None), (7, "D", 1, 3), (7, "U", 2, 0), (6, "R2", 1, None), (6, "U", 2, 0), (6, "D", 1, 3), (7, "U", 3, 1), (7, "D", 0, 2),
    (7, "R2", 2, None), (7, "D", 2, 3), (7, "U", 1, 0), (6, "R2", 2, None), (6, "U", 1, 0), (6, "D", 2, 3), (6, "D", 0, 2), (6, "U", 3, 1),
    (7, "R2", 3, None), (7, "D", 0, 1), (7, "U", 3, 2), (6, "R2", 3, None), (7, "D", 1, 2), (7, "U", 2, 1), (8, "R2", 0, None), (6, "U", 3, 2),
    (6, "D", 0, 1), (8, "R2", 1, None), (6, "D", 1, 2), (6, "U", 2, 1), (7, "Z3", 0, 0), (7, "Z3", 0, 3), (8, "R2", 2, None), (8, "R2", 3, None),
    (7, "Z3", 0, 1), (7, "Z3", 0, 2), (5, "R3", 0, None), (5, "D", 0, 3), (5, "U", 3, 0), (6, "Z3", 0, 0), (6, "Z3", 0, 3), (5, "R3", 1, None),
    (5, "D", 1, 3), (5, "U", 2, 0), (5, "R3", 2, None), (5, "U", 1, 0), (5, "D", 2, 3), (5, "R3", 3, None), (6, "Z3", 0, 2), (6, "Z3", 0, 1),
    (3, "FIN", 0, 1), (3, "FIN", 0, 0), (3, "FIN", 0, 3), (3, "FIN", 0, 2), (4, "FIN", 0, 1), (4, "FIN", 0, 2), (4, "FIN", 0, 0), (4, "FIN", 0, 3),
    (5, "U", 3, 1), (5, "D", 0, 2), (8, "R3", 0, None), (8, "U", 3, 0), (8, "D", 0, 3), (8, "R3", 1, None), (8, "U", 2, 0), (8, "D", 1, 3),
    (5, "U", 2, 1), (5, "D", 1, 2), (8, "R3", 2, None), (7, "FIN", 0, 0), (7, "FIN", 0, 3), (8, "R3", 3, None), (5, "U", 3, 2), (5, "D", 0, 1),
    (8, "D", 2, 3), (8, "U", 1, 0), (6, "FIN", 0, 0), (6, "FIN", 0, 3), (6, "FIN", 0, 2), (6, "FIN", 0, 1), (7, "FIN", 0, 2), (7, "FIN", 0, 1),
    (8, "D", 0, 2), (8, "U", 3, 1), (5, "FIN", 0, 1), (5, "FIN", 0, 2), (8, "D", 1, 2), (8, "U", 2, 1), (5, "FIN", 0, 0), (5, "FIN", 0, 3),
    (8, "D", 0, 1), (8, "U", 3, 2), (8, "FIN", 0, 2), (8, "FIN", 0, 1), (8, "FIN", 0, 0), (8, "FIN", 0, 3),
]


NT = 9
NS, NR = 27, 33

class Reduce:
    def __init__(self, p, t, order, PB, L0, L1, L2, UP, DN, LX, ssem, rsem, out):
        self.p, self.t, self.order = p, t, order
        self.PB, self.L0, self.L1, self.L2, self.UP, self.DN, self.LX = PB, L0, L1, L2, UP, DN, LX
        self.ssem, self.rsem, self.out = ssem, rsem, out
        self.sends = []
        self.me = {"x": p.x, "y": p.y}
        self.flat = order == "A"
        if not self.flat: self.b1, self.b2 = order[0], order[2]
    def partner(self, b):
        return self.p.dev(**{b: 1 - self.me[b]})
    def desc(self, src, dst, k, slot, target):
        return pltpu.make_async_remote_copy(src, dst, self.ssem.at[k], self.rsem.at[slot], device_id=target, device_id_type=MESH)
    def copy(self, what, k, slot, z=None):
        def make():
            src, dst, target = what()
            return self.desc(src, dst, k, slot, target)
        make().start()
        self.sends.append((make, z))
    def arrive(self, dst, slot):
        self.desc(dst, dst, 0, slot, self.p.dev()).wait_recv()
    def finish(self, z):
        for make, at in self.sends:
            if at == z: make().wait_send()
    def height(self, k):
        return jnp.where(self.p.z < 2, 3 - k, k)
    def sib(self, k):
        zz = self.height(k)
        self.copy(lambda: (self.PB.at[zz, :, :, 1 - self.p.c], self.L0.at[zz], self.p.dev(c=1 - self.p.c)), k, zz)
    def pair(self, zz, b2name, b2v, r=pl.ds(0, 32)):
        if b2name == "y": return self.PB.at[zz, b2v, :, self.p.c, r]
        return self.PB.at[zz, :, b2v, self.p.c, r]
    def block(self, zz, r=pl.ds(0, 32), **where):
        return self.PB.at[zz, where.get("y", self.p.y), where.get("x", self.p.x), self.p.c, r]
    def mine(self, zz):
        return self.block(zz) if self.flat else self.pair(zz, self.b2, self.me[self.b2])
    def halves(self):
        return [(h, b1, b2, pl.ds(16 * h, 16)) for h, (b1, b2) in enumerate((("x", "y"), ("y", "x")))]

    def R1(self, k):
        p, zz = self.p, self.height(k)
        self.arrive(self.L0.at[zz], zz)
        if self.flat:
            for yy in range(2):
                for xx in range(2):
                    self.PB[zz, yy, xx, p.c] = self.PB[zz, yy, xx, p.c] + self.L0[zz, yy, xx]
            for h, b1, b2, r in self.halves():
                self.copy(lambda b2=b2, r=r: (self.pair(zz, b2, 1 - self.me[b2], r), self.L1.at[zz, :, r], self.partner(b2)), 4 + 4 * h + k, 17 + 4 * h + zz)
        else:
            def merge(side):
                o = self.pair(zz, self.b2, side)
                land = self.L0.at[zz, side] if self.b2 == "y" else self.L0.at[zz, :, side]
                o[...] = o[...] + land[...]
            merge(1 - self.me[self.b2])
            self.copy(lambda: (self.pair(zz, self.b2, 1 - self.me[self.b2]), self.L1.at[zz], self.partner(self.b2)), 4 + k, 4 + zz)
            merge(self.me[self.b2])
    def R2(self, k):
        zz = self.height(k)
        if self.flat:
            for h, b1, b2, r in self.halves():
                self.arrive(self.L1.at[zz, :, r], 17 + 4 * h + zz)
                o = self.pair(zz, b2, self.me[b2], r)
                o[...] = o[...] + self.L1[zz, :, r]
                self.copy(lambda b1=b1, r=r: (self.block(zz, r, **{b1: 1 - self.me[b1]}), self.L2.at[zz, r], self.partner(b1)), 12 + 4 * h + k, 25 + 4 * h + zz)
        else:
            self.arrive(self.L1.at[zz], 4 + zz)
            o = self.mine(zz)
            o[...] = o[...] + self.L1[zz]
    def R3(self, k):
        zz = self.height(k)
        for h, b1, b2, r in self.halves():
            self.arrive(self.L2.at[zz, r], 25 + 4 * h + zz)
            o = self.block(zz, r)
            o[...] = o[...] + self.L2[zz, r]
    def U(self, zu, z):
        o, land = self.mine(zu), self.UP.at[zu - 1]
        if 0 < z <= zu:
            self.arrive(land, 8 + zu)
            o[...] = o[...] + land[...]
        if z < zu: self.copy(lambda: (self.mine(zu), self.UP.at[zu - 1], self.p.dev(z=z + 1)), 20 + zu - 1, 8 + zu, z)
    def D(self, zd, z):
        o, land = self.mine(zd), self.DN.at[zd]
        if zd <= z < 3:
            self.arrive(land, 12 + zd)
            o[...] = o[...] + land[...]
        if z > zd: self.copy(lambda: (self.mine(zd), self.DN.at[zd], self.p.dev(z=z - 1)), 23 + zd, 12 + zd, z)
    def Z3(self, k, z):
        if z > 0: self.U(z, z)
        if z < 3: self.D(z, z)
        self.copy(lambda: (self.block(z, **{self.b1: 1 - self.me[self.b1]}), self.LX, self.partner(self.b1)), 26, 16, z)
    def FIN(self, k, z):
        v = self.block(z)
        if self.flat:
            if z > 0: self.U(z, z)
            if z < 3: self.D(z, z)
            self.out(v[...].astype(F32))
        else:
            self.arrive(self.LX, 16)
            self.out(v[...].astype(F32) + self.LX[...].astype(F32))

W_ORDER = ["o0", "o1", "o2", "o3", 8, 9, 10, 11, 12, 7, 4, 5, 6, 3, 0, 1, 2]
T_ORDER = [5, 4, 1, 2, 3, 0]
NW = 3

def backward_kernel(gains, buf, gfo, qkv, P, H, T, AT, GP, SR, cot,
                    o_tok, osp, oso, ocp, oco, oai, oao, oen,
                    PB, L0, L1, L2, UPC, DNC, UPA, DNA, LX, wbuf, hb, gpb, tb, atb, srb, pb, cotb, g, gb, gr, gx, gqkv, gtok, vsp, vso, vcp, vco, vai, vao, fsem,
                    ssem, rsem, csem, crsem, wsem, hsem, gpsem, tsem, msem, qsem, psem, osem):
    p = Place()
    neighbours_in = entry_barrier(p)
    lo, hi = half_masks()
    def w_copy(i):
        n = W_ORDER[i]
        src = gfo.at[int(n[1])] if isinstance(n, str) else buf.at[n]
        return pltpu.make_async_copy(src, wbuf.at[i % NW], wsem.at[i])
    h_copy = lambda i: pltpu.make_async_copy(H.at[2 - i], hb.at[i % 2], hsem.at[i])
    gp_copy = lambda j: pltpu.make_async_copy(GP.at[j], gpb.at[j % 2], gpsem.at[j])
    t_copy = lambda i: pltpu.make_async_copy(T.at[T_ORDER[i]], tb.at[i % 3], tsem.at[i])
    q_copy = lambda a, j: pltpu.make_async_copy(qkv.at[3 * a + j], PB.at[6 + a, j], qsem.at[3 * a + j])
    p_copy = lambda a: pltpu.make_async_copy(P.at[a], pb, psem.at[a])
    m_copy = [pltpu.make_async_copy(cot, cotb, msem.at[0]), pltpu.make_async_copy(SR, srb, msem.at[1]), pltpu.make_async_copy(AT, atb, msem.at[2])]
    h_copy(0).start(); m_copy[0].start(); w_copy(0).start(); gp_copy(0).start(); w_copy(1).start(); gp_copy(1).start(); w_copy(2).start()
    def later(at):
        if at == "hb1": m_copy[1].start(); m_copy[2].start(); t_copy(0).start()
        if at == "hb3": h_copy(1).start()
        if at == "hi1":
            for i in (1, 2): t_copy(i).start()
            for j in range(3): q_copy(1, j).start()
        if at == "hi3":
            p_copy(1).start()
            for j in range(3): q_copy(0, j).start()

    def out_copy(held, ref, n): return pltpu.make_async_copy(held, ref, fsem.at[n])
    written = []
    def o_ad(v):
        vai[...] = v[:, :512]
        vao[:, 0:512] = v[0:16, 512:]
        vao[:, 512:1024] = v[16:32, 512:]
        out_copy(vai, oai, 0).start()
        out_copy(vao, oao, 1).start()
    def put(held, ref, n, j=None):
        written.append((held, ref, n, j))
        def f(v):
            if j is None:
                held[...] = v
                out_copy(held, ref, n).start()
            else:
                held[j] = v
                out_copy(held.at[j], ref.at[j], n).start()
        return f
    finals = [o_ad, put(vco, oco, 2), put(vcp, ocp, 3, 1), put(vcp, ocp, 4, 2), put(vcp, ocp, 5, 0), put(vso, oso, 6), put(vsp, osp, 7, 1), put(vsp, osp, 8, 2), put(vsp, osp, 9, 0)]
    reds = []
    nc = na = 0
    for t in range(NT):
        if ORDERS[t] == "A":
            up, dn, l2 = UPA.at[na], DNA.at[na], L2.at[na]; na += 1
        else:
            up, dn, l2 = UPC.at[nc], DNC.at[nc], None; nc += 1
        reds.append(Reduce(p, t, ORDERS[t], PB.at[t], L0.at[t], L1.at[t], l2, up, dn, LX.at[t], ssem.at[t], rsem.at[t], finals[t]))

    compute = {}
    def work(name, fn): compute[name] = fn

    def norm_back(i, first=False):
        def run():
            h_copy(i).wait()
            if first: m_copy[0].wait()
            @pl.loop(0, 4)
            def _(n):
                r = pl.ds(pl.multiple_of(n * 64, 64), 64)
                h = hb[i % 2, r, :]
                center = h - jnp.mean(h, axis=-1, keepdims=True)
                inv = lax.rsqrt(jnp.mean(center * center, axis=-1, keepdims=True) + EPS)
                nrm = center * inv
                gy = cotb[r, :].astype(F32) if first else g[r, :]
                a = gy * gains[2 - i, :][None]
                v = (a - jnp.mean(a, axis=-1, keepdims=True) - nrm * jnp.mean(a * nrm, axis=-1, keepdims=True)) * inv
                g[r, :] = v
                gb[r, :] = v.astype(BF)
            if i == 0: h_copy(2).start()
        return run

    def used(i):
        if i + NW < len(W_ORDER): w_copy(i + NW).start()

    def nt(lhs, i, fn):
        fn(dot_nt(lhs(), wbuf[i % NW]))

    def hidden_back(j):
        def run():
            w_copy(j).wait(); gp_copy(j).wait()
            def st(v):
                PB[8, j] = (gpb[j % 2] * v).astype(BF).reshape(2, 2, 2, 32, 1024)
            nt(lambda: gb[...], j, st)
            used(j)
            if j + 2 < 4: gp_copy(j + 2).start()
            later(f"hb{j}")
        return run

    def adapter_back():
        i = 4
        w_copy(i).wait(); m_copy[1].wait(); m_copy[2].wait()
        v = wbuf[i % NW, :, 512:1024].reshape(32, 32, 512)
        top, bot = v[:, :16].reshape(512, 512), v[:, 16:].reshape(512, 512)
        s = dot_nt(gb[:, 0:512], top) + dot_nt(gb[:, 512:1024], bot)
        gr[...] = (srb[...] * (4.0 * s)).astype(BF)
        wai = wbuf[i % NW, :, 0:512]
        g[...] = g[...] + dot_nt(gr[...], wai)
        used(i)

    def rows_of(k):
        return pl.ds(pl.multiple_of(reds[0].height(k) * 256, 256), 256)
    def adapter_grads(k):
        def run():
            if k == 0:
                neighbours_in()
                for h in range(2):
                    v = 4.0 * dot(atb[...], gb[:, 512 * h:512 * h + 512])
                    PB[0, :, :, :, :, 16 * h:16 * h + 16, 512:1024] = v.astype(BF).reshape(4, 2, 2, 2, 16, 512)
                t_copy(0).wait()
            v = dot(tb[0, rows_of(k), :], gr[...])
            PB[0, reds[0].height(k), :, :, :, :, 0:512] = v.astype(BF).reshape(2, 2, 2, 32, 512)
            reds[0].sib(k)
            if k == 3: t_copy(3).start()
        return run

    def hidden_in_back(j):
        def run():
            i = 5 + j
            w_copy(i).wait()
            def st(v): g[...] = g[...] + v
            nt(lambda: PB[8, j].reshape(256, 1024), i, st)
            used(i)
            later(f"hi{j}")
        return run

    def grad_tile(t, ti, rhs, last, k):
        def run():
            if k == 0 and t in (1, 2, 4, 5, 6): t_copy(ti).wait()
            PB[t, reds[t].height(k)] = dot(tb[ti % 3, rows_of(k), :], rhs()).astype(BF).reshape(2, 2, 2, 32, 1024)
            reds[t].sib(k)
            if k == 3 and last and ti + 3 < 6: t_copy(ti + 3).start()
        return run

    def mix_back(i):
        def run():
            w_copy(i).wait()
            def st(v): gx[...] = v.astype(BF)
            nt(lambda: gb[...], i, st)
            used(i)
        return run

    def attend_back(a, part):
        def run():
            if part == 0:
                p_copy(a).wait()
                for j in range(3): q_copy(a, j).wait()
            u = part // 2
            @pl.loop(0, 4, unroll=4)
            def _(n):
                pr = (part % 2) * 4 + n
                r, cc = pl.ds(u * 128, 128), cols(pr, 128)
                q, k, v = (PB[6 + a, j, u, :, :, :, cc].reshape(128, 128) for j in range(3))
                go = pair_up(gx[r, cc], lo, hi)
                prob = pb[u * 8 + pr]
                dp = dot_nt(go, v)
                ds = (prob * (dp - jnp.sum(prob * dp, axis=-1, keepdims=True))).astype(BF)
                gqkv[0, r, cc] = (dot(side(ds), pair_up(k, lo, hi)) * 0.125).astype(BF)
                gqkv[1, r, cc] = (dot_tn(ds, pair_up(q, lo, hi)) * 0.125).astype(BF)
                gqkv[2, r, cc] = dot_tn(prob.astype(BF), go).astype(BF)
            if part == 3 and a == 1: p_copy(0).start()
        return run

    def row_back(i, j, dst):
        def run():
            w_copy(i).wait()
            nt(lambda: gqkv[j], i, dst)
            used(i)
        return run
    def to_g(v): g[...] = g[...] + v
    cs = []
    me = p.x * 2 + p.c
    def context_back():
        i = 11
        w_copy(i).wait()
        def st(v): PB[8, 0] = (ctxf[...] + v).astype(BF).reshape(2, 2, 2, 32, 1024)
        nt(lambda: gqkv[2], i, st)
        used(i)
        for k, (dx, dc) in enumerate(((0, 1), (1, 0), (1, 1))):
            tx = (p.x + dx) % 2; tc = (p.c + dc) % 2
            c_ = pltpu.make_async_remote_copy(PB.at[8, 0, :, tx, tc], oen.at[0, me], csem.at[k], crsem.at[me], device_id=p.dev(x=tx, c=tc), device_id_type=MESH)
            c_.start(); cs.append(c_)
        c_ = pltpu.make_async_copy(PB.at[8, 0, :, p.x, p.c], oen.at[0, me], osem.at[0]); c_.start(); cs.append(c_)

    ctxf = gpb.at[0]
    def ctx_part(v): ctxf[...] = v
    def context_sent():
        for c_ in cs[:3]: c_.wait_send()
        cs[3].wait()
    def tokens_back():
        i = 16
        w_copy(i).wait()
        def st(v): gtok[...] = (g[...] + v).astype(BF)
        nt(lambda: gqkv[2], i, st)
        pltpu.make_async_copy(gtok, o_tok, osem.at[1]).start()

    def tile(t, ti, rhs, last):
        for zz in range(4): work(f"t{t}.{zz}", grad_tile(t, ti, rhs, last, zz))
    work("nb0", norm_back(0, True))
    for j in range(4): work(f"hb{j}", hidden_back(j))
    work("adb", adapter_back)
    for zz in range(4): work(f"adg.{zz}", adapter_grads(zz))
    for j in range(4): work(f"hi{j}", hidden_in_back(j))
    work("nb1", norm_back(1))
    tile(1, 1, lambda: gb[...], True)
    work("mb9", mix_back(9))
    for part in range(4): work(f"at1{part}", attend_back(1, part))
    tile(2, 2, lambda: gqkv[1], False)
    tile(3, 2, lambda: gqkv[2], True)
    tile(4, 3, lambda: gqkv[0], True)
    work("rb10", row_back(10, 1, ctx_part))
    work("cb", context_back)
    work("rb12", row_back(12, 0, to_g))
    work("nb2", norm_back(2))
    tile(5, 4, lambda: gb[...], True)
    work("mb13", mix_back(13))
    for part in range(4): work(f"at0{part}", attend_back(0, part))
    work("cs", context_sent)
    tile(6, 5, lambda: gqkv[1], False)
    tile(7, 5, lambda: gqkv[2], False)
    tile(8, 5, lambda: gqkv[0], True)
    work("rb14", row_back(14, 0, to_g))
    work("rb15", row_back(15, 1, to_g))
    work("tok", tokens_back)
    run_plan(PLAN_B, compute, reds, [p.z == z for z in range(4)])
    for r in reds: r.finish(None)
    for z in range(4):
        @pl.when(p.z == z)
        def _():
            for r in reds: r.finish(z)
    pltpu.make_async_copy(gtok, o_tok, osem.at[1]).wait()
    out_copy(vai, oai, 0).wait()
    out_copy(vao, oao, 1).wait()
    for held, ref, n, j in written:
        if j is None: out_copy(held, ref, n).wait()
        else: out_copy(held.at[j], ref.at[j], n).wait()
    for k, (dx, dc) in enumerate(((0, 1), (1, 0), (1, 1))):
        tx = (p.x + dx) % 2; tc = (p.c + dc) % 2
        w = tx * 2 + tc
        pltpu.make_async_remote_copy(PB.at[8, 0, :, tx, tc], oen.at[0, w], csem.at[k], crsem.at[w], device_id=p.dev(), device_id_type=MESH).wait_recv()

def backward(gains, buf, gfo, qkv, P, H, T, AT, GP, SR, cot):
    any_ = pl.BlockSpec(memory_space=pl.ANY)
    vm = pl.BlockSpec(memory_space=pltpu.VMEM)
    V, S, D = pltpu.VMEM, jax.ShapeDtypeStruct, pltpu.SemaphoreType.DMA
    ops = (gains, buf.reshape(13, 1024, 1024), gfo.reshape(4, 1024, 1024), qkv.reshape(6, 2, 2, 2, 32, 1024), P, H, T, AT, GP, SR, cot)
    return pl.pallas_call(backward_kernel,
        out_shape=(S((256, 1024), BF), S((3, 32, 1024), F32), S((32, 1024), F32), S((3, 32, 1024), F32), S((32, 1024), F32), S((32, 512), F32), S((16, 1024), F32), S((1, 4, 2, 32, 1024), BF)),
        in_specs=[vm] + [any_] * 10, out_specs=(any_,) * 8,
        scratch_shapes=[V((NT, 4, 2, 2, 2, 32, 1024), BF), V((NT, 4, 2, 2, 32, 1024), BF), V((NT, 4, 2, 32, 1024), BF), V((3, 4, 32, 1024), BF),
                        V((6, 3, 2, 32, 1024), BF), V((6, 3, 2, 32, 1024), BF), V((3, 3, 32, 1024), BF), V((3, 3, 32, 1024), BF), V((NT, 32, 1024), BF),
                        V((NW, 1024, 1024), BF), V((2, 256, 1024), F32), V((2, 256, 1024), F32), V((3, 1024, 256), BF), V((512, 256), BF), V((256, 512), F32),
                        V((16, 256, 128), F32), V((256, 1024), BF), V((256, 1024), F32), V((256, 1024), BF), V((256, 512), BF), V((256, 1024), BF),
                        V((3, 256, 1024), BF), V((256, 1024), BF),
                        V((3, 32, 1024), F32), V((32, 1024), F32), V((3, 32, 1024), F32), V((32, 1024), F32), V((32, 512), F32), V((16, 1024), F32), D((10,)),
                        D((NT, NS)), D((NT, NR)), D((3,)), D((4,)), D((17,)), D((3,)), D((4,)), D((6,)), D((3,)), D((6,)), D((2,)), D((2,))],
        compiler_params=pltpu.CompilerParams(collective_id=1, has_side_effects=True, vmem_limit_bytes=63 << 20),
        name="backward")(*ops)


def finish_kernel(*refs):
    n = (len(refs) - 1) // 3
    ins, outs, held, sem = refs[:n], refs[n:2 * n], refs[2 * n:3 * n], refs[3 * n]
    first = [pltpu.make_async_copy(ins[k], held[k], sem.at[k]) for k in range(n)]
    last = [pltpu.make_async_copy(held[k], outs[k], sem.at[n + k]) for k in range(n)]
    for c in first: c.start()
    for k in range(n):
        first[k].wait()
        last[k].start()
    for c in last: c.wait()

def finish(*arrays):
    any_ = pl.BlockSpec(memory_space=pl.ANY)
    n = len(arrays)
    return pl.pallas_call(finish_kernel, out_shape=tuple(jax.ShapeDtypeStruct(a.shape, a.dtype) for a in arrays),
        in_specs=[any_] * n, out_specs=(any_,) * n,
        scratch_shapes=[pltpu.VMEM(a.shape, a.dtype) for a in arrays] + [pltpu.SemaphoreType.DMA((2 * n,))],
        compiler_params=pltpu.CompilerParams(vmem_limit_bytes=62 << 20), name="finish")(*arrays)


def device_program(tokens, encoder, dec_lengths, enc_lengths, gains, self_proj, self_out, cross_proj, cross_out, ffn_in, ffn_out, adapt_in, adapt_out, cotangent):
    shards = (self_proj, self_out, cross_proj, cross_out, ffn_in, ffn_out, adapt_in, adapt_out)
    buf, gfo, qkv, probs, hidden, turned, act_turned, gelu_slope, silu_slope, layer_out = forward(tokens, gains, dec_lengths, enc_lengths, shards, encoder)
    gtok, osp, oso, ocp, oco, oai, oao, oen = backward(gains, buf, gfo, qkv, probs, hidden, turned, act_turned, gelu_slope, silu_slope, cotangent)
    return finish(layer_out, gtok, oen, osp, oso, ocp, oco, oai, oao)


def solution(mesh):
    in_specs = (
        P(("seq", "enc"), None),
        P("seq", None, None, "enc", None),
        P(("seq", "enc"), None),
        P(("seq", "enc"), None),
        P(),
        P(None, ("seq", "enc"), None),
        P(("seq", "enc"), None),
        P(None, ("seq", "enc"), None),
        P(("seq", "enc"), None),
        P(("seq", "enc"), None),
        P(("seq", "enc"), None),
        P(("seq", "enc"), None),
        P(("seq", "enc"), None),
        P(("seq", "enc"), None),
    )
    out_specs = (
        P(("seq", "enc"), None),
        P(("seq", "enc"), None),
        P("seq", None, None, "enc", None),
        P(None, ("seq", "enc"), None),
        P(("seq", "enc"), None),
        P(None, ("seq", "enc"), None),
        P(("seq", "enc"), None),
        P(("seq", "enc"), None),
        P(("seq", "enc"), None),
    )
    fast = (mesh.shape["seq"], mesh.shape["enc"]) == (8, 4)
    return jax.shard_map(
        device_program if fast else per_device, mesh=mesh, in_specs=in_specs, out_specs=out_specs, check_vma=False
    )
```
